32 devices in a mesh: dp: 2 (over y), wide: 16 (over z, x, core).
Axes of the slice: x: 2, y: 2, z: 4, core: 2. Of those that a mesh axis runs over, the one named last changes fastest.
Arguments:
- inputs: bfloat16 [16384, 1024], P(('dp', 'wide')), may hold values from -6 to 6
- out_grad: bfloat16 [16384, 1024], P(('dp', 'wide')), may hold values from -6 to 6
- doc_lengths: int32 [2, 16], replicated, may hold values from 1 to 1024, 8192 in all within a row
- step_count: int32 [1], replicated, may hold values from 2 to 20
- qkv_weight: float32 [1024, 3072], P('wide'), may hold values from -0.1875 to 0.1875
- qkv_first: float32 [1024, 3072], P('wide'), may hold values from -0.00018310547 to 0.00018310547
- qkv_second: float32 [1024, 3072], P('wide'), may hold values from 8.0917345e-10 to 1.2930909e-08
- out_weight: float32 [1024, 1024], P('wide'), may hold values from -0.375 to 0.375
- out_first: float32 [1024, 1024], P('wide'), may hold values from -0.00018310547 to 0.00018310547
- out_second: float32 [1024, 1024], P('wide'), may hold values from 8.0917345e-10 to 1.2930909e-08
- fc1_weight: float32 [1024, 4096], P(None, 'wide'), may hold values from -0.1875 to 0.1875
- fc1_first: float32 [1024, 4096], P(None, 'wide'), may hold values from -0.00018310547 to 0.00018310547
- fc1_second: float32 [1024, 4096], P(None, 'wide'), may hold values from 8.0917345e-10 to 1.2930909e-08
- fc2_weight: float32 [4096, 1024], P('wide'), may hold values from -0.09375 to 0.09375
- fc2_first: float32 [4096, 1024], P('wide'), may hold values from -0.00018310547 to 0.00018310547
- fc2_second: float32 [4096, 1024], P('wide'), may hold values from 8.0917345e-10 to 1.2930909e-08
- model_vectors: float32 [10, 1024], P(None, 'wide'), may hold values from -0.4 to 1.3
- vectors_first: float32 [10, 1024], P(None, 'wide'), may hold values from -0.00018310547 to 0.00018310547
- vectors_second: float32 [10, 1024], P(None, 'wide'), may hold values from 8.0917345e-10 to 1.2930909e-08
- hidden_vectors: float32 [3, 4096], P(None, 'wide'), may hold values from -0.4 to 1.3
- hidden_first: float32 [3, 4096], P(None, 'wide'), may hold values from -0.00018310547 to 0.00018310547
- hidden_second: float32 [3, 4096], P(None, 'wide'), may hold values from 8.0917345e-10 to 1.2930909e-08
- head_scale: float32 [16], replicated, may hold values from 0.5 to 1.5
- head_first: float32 [16], replicated, may hold values from -0.00018310547 to 0.00018310547
- head_second: float32 [16], replicated, may hold values from 8.0917345e-10 to 1.2930909e-08
Outputs:
- output: bfloat16 [16384, 1024], P(('dp', 'wide'))
- input_grad: float32 [16384, 1024], P(('dp', 'wide'))
- grad_norm: float32 [1], replicated
- qkv_first_new: float32 [1024, 3072], P('wide')
- qkv_second_new: float32 [1024, 3072], P('wide')
- qkv_weight_new: float32 [1024, 3072], P('wide')
- out_first_new: float32 [1024, 1024], P('wide')
- out_second_new: float32 [1024, 1024], P('wide')
- out_weight_new: float32 [1024, 1024], P('wide')
- fc1_first_new: float32 [1024, 4096], P(None, 'wide')
- fc1_second_new: float32 [1024, 4096], P(None, 'wide')
- fc1_weight_new: float32 [1024, 4096], P(None, 'wide')
- fc2_first_new: float32 [4096, 1024], P('wide')
- fc2_second_new: float32 [4096, 1024], P('wide')
- fc2_weight_new: float32 [4096, 1024], P('wide')
- vectors_first_new: float32 [10, 1024], P(None, 'wide')
- vectors_second_new: float32 [10, 1024], P(None, 'wide')
- vectors_new: float32 [10, 1024], P(None, 'wide')
- hidden_first_new: float32 [3, 4096], P(None, 'wide')
- hidden_second_new: float32 [3, 4096], P(None, 'wide')
- hidden_new: float32 [3, 4096], P(None, 'wide')
- head_first_new: float32 [16], replicated
- head_second_new: float32 [16], replicated
- head_new: float32 [16], replicated
The draws below stay inside these ranges and needn't reach their ends.
Inputs may be any that keep to these rules, and one draw needn't show every extreme that they name: `doc_lengths`: each row's 16 lengths sum to 8192, and the longest of each row is 1024.
All inputs are finite; a program needn't handle non-finite values.
Results may differ from the reference program's by a relative error of at most 0.0095.
The reference program's roundings to bfloat16 on the way count: a program that leaves them out, or rounds other values in their place, can miss the bound.
Values may be sent and summed in bfloat16 or wider, within the bound.
A program may use at most 256 MiB of HBM per device.

```python
import math
import jax
import jax.numpy as jnp
import numpy as np
from jax import lax

D = 1024
HEADS = 16
HEAD_DIM = 64
FF = 4096
DOC_MOST = 1024
LENGTH = 8192
DOCS = 16
TOKENS = 16384
ROWS = 2
NPARAM = 12605456


def draw_model_vectors(key, part):
    first_key, second_key = jax.random.split(jax.random.fold_in(key, 11))
    gains = 1.0 + 0.1 * jnp.clip(jax.random.normal(first_key, (3, D), jnp.float32), -3.0, 3.0)
    biases = 0.1 * jnp.clip(jax.random.normal(second_key, (7, D), jnp.float32), -4.0, 4.0)
    return jnp.concatenate([gains, biases], axis=0)


def draw_hidden_vectors(key, part):
    first_key, second_key = jax.random.split(jax.random.fold_in(key, 23))
    gains = 1.0 + 0.1 * jnp.clip(jax.random.normal(first_key, (1, FF), jnp.float32), -3.0, 3.0)
    biases = 0.1 * jnp.clip(jax.random.normal(second_key, (2, FF), jnp.float32), -4.0, 4.0)
    return jnp.concatenate([gains, biases], axis=0)


def levels(rng, dims, cuts, smallest, largest):
    def one(position, shards_of):
        heights = jax.random.uniform(jax.random.fold_in(jax.random.fold_in(rng, 6), position), (shards_of,), jnp.float32, smallest / len(cuts), largest / len(cuts))
        return jnp.repeat(jnp.exp(heights), dims[position] // shards_of).reshape((-1,) + (1,) * (len(dims) - position - 1))

    loudness = one(*cuts[0])
    for cut in cuts[1:]:
        loudness = loudness * one(*cut)
    return loudness


def length_profile(amount, total, bound, lean):
    loads = [(1 << 20) // math.isqrt(grade ** lean) + 1 for grade in range(2, amount + 1)]
    surplus, counts = total - bound - (amount - 1), [1] * (amount - 1)
    while surplus > 0:
        free = [i for i in range(amount - 1) if counts[i] < bound]
        pool, left = sum([loads[i] for i in free]), surplus
        for i in free:
            more = min(bound - counts[i], max(1, left * loads[i] // pool), surplus)
            counts[i] = counts[i] + more
            surplus = surplus - more
    return np.array([bound] + counts)


def uneven_parts(key, count, total, reach, lean):
    if count == 2:
        one = jax.random.randint(key, (), max(1, total - reach), min(reach, total - 1) + 1)
        return jnp.stack([one, total - one])
    sizes = jnp.asarray(length_profile(count, total, reach, lean), jnp.int32)
    pairs = (count - 1) // 2
    giver, taker = sizes[1:1 + 2 * pairs:2], sizes[2:2 + 2 * pairs:2]
    slack = jnp.minimum(giver - 1, reach - taker)
    shifted = jax.random.randint(jax.random.fold_in(key, 1), (pairs,), 0, 1 << 20) % (slack + 1)
    sizes = sizes.at[1:1 + 2 * pairs:2].set(giver - shifted).at[2:2 + 2 * pairs:2].set(taker + shifted)
    return sizes[jax.random.permutation(jax.random.fold_in(key, 2), count)]


def noise(key, dims, width, most, cuts=(), kind=jnp.bfloat16):
    entries = jax.random.normal(key, dims, jnp.float32) * width
    if len(cuts) > 0:
        entries = levels(key, dims, cuts, -0.22, 0.18) * entries
    return jnp.clip(entries, min=-most, max=most).astype(kind)


def setup_inputs(seed: int = 0) -> dict:
    splits = jax.random.split(jax.random.key(seed), 26)
    inputs = noise(splits[0], (TOKENS, D), 1.0, 6.0, ((0, 32),))
    out_grad = noise(splits[1], (TOKENS, D), 1.0, 6.0, ((0, 32),))
    doc_lengths = jax.vmap(lambda own: uneven_parts(own, DOCS, LENGTH, DOC_MOST, 2))(jax.random.split(splits[2], ROWS)).reshape((ROWS, DOCS)).astype(jnp.int32)
    step_count = jax.random.randint(splits[3], (1,), 2, 21).astype(jnp.int32)
    qkv_weight = noise(splits[4], (D, 3 * D), D ** -0.5, 0.1875, ((0, 16),), jnp.float32)
    qkv_first = noise(splits[5], (D, 3 * D), (0.111 * NPARAM ** -0.5), 0.00018310547, ((0, 16),), jnp.float32)
    qkv_second = jnp.clip(jnp.exp(math.log(1.293090878817793e-08) - 2.7713625 * jax.random.uniform(splits[6], (D, 3 * D), jnp.float32) ** levels(splits[6], (D, 3 * D), ((0, 16),), -0.2, 0.2)), 8.091734504667158e-10, 1.293090878817793e-08)
    out_weight = noise(splits[7], (D, D), (D // 4) ** -0.5, 0.375, ((0, 16),), jnp.float32)
    out_first = noise(splits[8], (D, D), (0.111 * NPARAM ** -0.5), 0.00018310547, ((0, 16),), jnp.float32)
    out_second = jnp.clip(jnp.exp(math.log(1.293090878817793e-08) - 2.7713625 * jax.random.uniform(splits[9], (D, D), jnp.float32) ** levels(splits[9], (D, D), ((0, 16),), -0.2, 0.2)), 8.091734504667158e-10, 1.293090878817793e-08)
    fc1_weight = noise(splits[10], (D, FF), D ** -0.5, 0.1875, ((1, 16),), jnp.float32)
    fc1_first = noise(splits[11], (D, FF), (0.111 * NPARAM ** -0.5), 0.00018310547, ((1, 16),), jnp.float32)
    fc1_second = jnp.clip(jnp.exp(math.log(1.293090878817793e-08) - 2.7713625 * jax.random.uniform(splits[12], (D, FF), jnp.float32) ** levels(splits[12], (D, FF), ((1, 16),), -0.2, 0.2)), 8.091734504667158e-10, 1.293090878817793e-08)
    fc2_weight = noise(splits[13], (FF, D), FF ** -0.5, 0.09375, ((0, 16),), jnp.float32)
    fc2_first = noise(splits[14], (FF, D), (0.111 * NPARAM ** -0.5), 0.00018310547, ((0, 16),), jnp.float32)
    fc2_second = jnp.clip(jnp.exp(math.log(1.293090878817793e-08) - 2.7713625 * jax.random.uniform(splits[15], (FF, D), jnp.float32) ** levels(splits[15], (FF, D), ((0, 16),), -0.2, 0.2)), 8.091734504667158e-10, 1.293090878817793e-08)
    model_vectors = draw_model_vectors(jax.random.fold_in(splits[25], 71), 0)
    vectors_first = noise(splits[17], (10, D), (0.111 * NPARAM ** -0.5), 0.00018310547, ((1, 16),), jnp.float32)
    vectors_second = jnp.clip(jnp.exp(math.log(1.293090878817793e-08) - 2.7713625 * jax.random.uniform(splits[18], (10, D), jnp.float32) ** levels(splits[18], (10, D), ((1, 16),), -0.2, 0.2)), 8.091734504667158e-10, 1.293090878817793e-08)
    hidden_vectors = draw_hidden_vectors(jax.random.fold_in(splits[25], 71), 0)
    hidden_first = noise(splits[20], (3, FF), (0.111 * NPARAM ** -0.5), 0.00018310547, ((1, 16),), jnp.float32)
    hidden_second = jnp.clip(jnp.exp(math.log(1.293090878817793e-08) - 2.7713625 * jax.random.uniform(splits[21], (3, FF), jnp.float32) ** levels(splits[21], (3, FF), ((1, 16),), -0.2, 0.2)), 8.091734504667158e-10, 1.293090878817793e-08)
    head_scale = jnp.clip(1.0 + 0.1 * jax.random.normal(splits[22], (HEADS,), jnp.float32), 0.5, 1.5)
    head_first = noise(splits[23], (HEADS,), (0.111 * NPARAM ** -0.5), 0.00018310547, (), jnp.float32)
    head_second = jnp.clip(jnp.exp(jax.random.uniform(splits[24], (HEADS,), jnp.float32, math.log(8.091734504667158e-10), math.log(1.293090878817793e-08))), 8.091734504667158e-10, 1.293090878817793e-08)
    return dict(inputs=inputs, out_grad=out_grad, doc_lengths=doc_lengths, step_count=step_count, qkv_weight=qkv_weight, qkv_first=qkv_first, qkv_second=qkv_second, out_weight=out_weight, out_first=out_first, out_second=out_second, fc1_weight=fc1_weight, fc1_first=fc1_first, fc1_second=fc1_second, fc2_weight=fc2_weight, fc2_first=fc2_first, fc2_second=fc2_second, model_vectors=model_vectors, vectors_first=vectors_first, vectors_second=vectors_second, hidden_vectors=hidden_vectors, hidden_first=hidden_first, hidden_second=hidden_second, head_scale=head_scale, head_first=head_first, head_second=head_second)


norm_epsilon = 1e-05
clip_limit = 1.0
first_decay = 0.9
second_decay = 0.98
adam_epsilon = 1e-08
matrix_rate = 0.1
vector_rate = 0.4
weight_decay = 0.1
masked_score = -1e+30

@jax.custom_vjp
def low(v):
    return lax.optimization_barrier(v.astype(jnp.bfloat16)).astype(jnp.float32)

@jax.custom_vjp
def low_back(v):
    return v

def low_keep(v):
    return (low(v), None)

def low_pass(kept, grad):
    return (grad,)

def back_keep(v):
    return (v, None)

def back_low(kept, grad):
    return (low(grad),)
low.defvjp(low_keep, low_pass)
low_back.defvjp(back_keep, back_low)

def dense(left, right):
    return jnp.dot(left, right, precision=lax.Precision.HIGHEST)

def layer_norm(values_in, gain, shift):
    center = values_in - lax.optimization_barrier(jnp.mean(values_in, axis=-1, keepdims=True))
    variance = lax.optimization_barrier(jnp.mean(center * center, axis=-1, keepdims=True))
    return center * lax.rsqrt(variance + norm_epsilon) * gain + shift

def middle_norm(values_in, gain, shift):
    first_mean = lax.optimization_barrier(jnp.mean(values_in, axis=-1, keepdims=True))
    second_mean = lax.optimization_barrier(jnp.mean(values_in * values_in, axis=-1, keepdims=True))
    scale = lax.rsqrt(second_mean - first_mean * first_mean + norm_epsilon)
    return (values_in - first_mean) * scale * gain + shift

def attend_block(queries, start, keys, values, labels):
    length_here = queries.shape[0]
    places = start + jnp.arange(length_here, dtype=jnp.int32)
    query_labels = lax.dynamic_slice_in_dim(labels, start, length_here, 0)
    key_places = jnp.arange(LENGTH, dtype=jnp.int32)
    scores = jnp.einsum('qhd,khd->hqk', queries, keys, precision=lax.Precision.HIGHEST) * HEAD_DIM ** (-0.5)
    scores = low_back(scores)
    allowed = (query_labels[:, None] == labels[None, :]) & (key_places[None, :] <= places[:, None])
    masked = jnp.where(allowed[None], scores, masked_score)
    probs = jax.nn.softmax(masked, axis=-1)
    return jnp.einsum('hqk,khd->qhd', low(probs), values, precision=lax.Precision.HIGHEST)

def attend_row(row_data):
    queries, keys, values, labels = row_data
    block_rows = min(512, LENGTH)
    block_count = LENGTH // block_rows
    query_blocks = queries.reshape(block_count, block_rows, HEADS, HEAD_DIM)
    starts = jnp.arange(block_count, dtype=jnp.int32) * block_rows

    def one_block(member):
        return attend_block(member[0], member[1], keys, values, labels)
    outputs = lax.map(jax.checkpoint(one_block), (query_blocks, starts))
    return outputs.reshape(LENGTH, HEADS, HEAD_DIM)

def forward(tokens, labels, qkv_w, out_w, fc1_w, fc2_w, vectors, hidden, heads_gain):
    qkv_w = low(qkv_w)
    out_w = low(out_w)
    fc1_w = low(fc1_w)
    fc2_w = low(fc2_w)
    vectors = low(vectors)
    hidden = low(hidden)
    heads_gain = low(heads_gain)
    normed = low(layer_norm(tokens, vectors[0], vectors[3]))
    projected = dense(normed, qkv_w)
    queries = low(low_back(projected[:, :D] + vectors[4]))
    keys = low(low_back(projected[:, D:2 * D]))
    values = low(low_back(projected[:, 2 * D:] + vectors[5]))
    shape_rows = (ROWS, LENGTH, HEADS, HEAD_DIM)
    attended = lax.map(jax.checkpoint(attend_row), (queries.reshape(shape_rows), keys.reshape(shape_rows), values.reshape(shape_rows), labels))
    attended = low_back(attended.reshape(TOKENS, HEADS, HEAD_DIM))
    mixed = low(attended * heads_gain[None, :, None]).reshape(TOKENS, D)
    proj_out = low_back(dense(mixed, out_w) + vectors[6])
    residual = tokens + layer_norm(proj_out, vectors[1], vectors[7])
    normed_two = low(layer_norm(residual, vectors[2], vectors[8]))
    pre_act = low_back(dense(normed_two, fc1_w) + hidden[2])
    activated = jax.nn.gelu(pre_act, approximate=False)
    middle = low(middle_norm(activated, hidden[0], hidden[1]))
    ffn_out = low_back(dense(middle, fc2_w) + vectors[9])
    return residual + ffn_out

def adam_step(grad, weight, first, second, step, rate, decay):
    first_new = first_decay * first + (1.0 - first_decay) * grad
    second_new = second_decay * second + (1.0 - second_decay) * grad * grad
    fix_one = 1.0 - jnp.power(jnp.float32(first_decay), step)
    fix_two = 1.0 - jnp.power(jnp.float32(second_decay), step)
    direction = first_new / fix_one / (jnp.sqrt(second_new / fix_two) + adam_epsilon)
    weight_new = weight - rate * (direction + decay * weight)
    return (first_new, second_new, weight_new)

def reference(inputs, out_grad, doc_lengths, step_count, qkv_weight, qkv_first, qkv_second, out_weight, out_first, out_second, fc1_weight, fc1_first, fc1_second, fc2_weight, fc2_first, fc2_second, model_vectors, vectors_first, vectors_second, hidden_vectors, hidden_first, hidden_second, head_scale, head_first, head_second):
    ends = jnp.cumsum(doc_lengths, axis=1)
    places = jnp.arange(LENGTH, dtype=jnp.int32)
    labels = lax.optimization_barrier(jnp.sum((places[None, :, None] >= ends[:, None, :]).astype(jnp.int32), axis=2)).astype(jnp.int32)
    params = (qkv_weight, out_weight, fc1_weight, fc2_weight, model_vectors, hidden_vectors, head_scale)

    def run_layer(tokens, *weights):
        return forward(tokens, labels, *weights)
    result, pullback = jax.vjp(run_layer, inputs.astype(jnp.float32), *params)
    grads = pullback(out_grad.astype(jnp.float32))
    input_grad = grads[0]
    squares = sum((jnp.sum(part * part) for part in grads[1:]))
    grad_norm = jnp.sqrt(squares)
    factor = jnp.minimum(1.0, clip_limit / (grad_norm + 1e-06))
    step = step_count[0].astype(jnp.float32)
    firsts = (qkv_first, out_first, fc1_first, fc2_first, vectors_first, hidden_first, head_first)
    seconds = (qkv_second, out_second, fc1_second, fc2_second, vectors_second, hidden_second, head_second)
    rates = (matrix_rate, matrix_rate, matrix_rate, matrix_rate, vector_rate, vector_rate, vector_rate)
    decays = (weight_decay, weight_decay, weight_decay, weight_decay, 0.0, 0.0, 0.0)
    updated = []
    for number in range(7):
        updated.extend(adam_step(grads[number + 1] * factor, params[number], firsts[number], seconds[number], step, rates[number], decays[number]))
    return (result.astype(jnp.bfloat16), input_grad, grad_norm.reshape(1), updated[0], updated[1], updated[2], updated[3], updated[4], updated[5], updated[6], updated[7], updated[8], updated[9], updated[10], updated[11], updated[12], updated[13], updated[14], updated[15], updated[16], updated[17], updated[18], updated[19], updated[20])
```

```python
import functools

import jax
import jax.numpy as jnp
from jax import lax
from jax.experimental import pallas as pl
from jax.experimental.pallas import tpu as pltpu
from jax.sharding import PartitionSpec as P

DOC_MOST = 1024
MESH = pl.DeviceIdType.MESH
HBM = pl.BlockSpec(memory_space=pltpu.HBM)
VMEM = pl.BlockSpec(memory_space=pltpu.VMEM)
BF16 = jnp.bfloat16
F32 = jnp.float32

norm_epsilon = 1e-05
clip_limit = 1.0
first_decay = 0.9
second_decay = 0.98
adam_epsilon = 1e-08
matrix_rate = 0.1
vector_rate = 0.4
weight_decay = 0.1
masked_score = -1e30


def layer_norm(values_in, gain, shift):
    center = values_in - jnp.mean(values_in, axis=-1, keepdims=True)
    variance = jnp.mean(center * center, axis=-1, keepdims=True)
    scale = lax.rsqrt(variance + norm_epsilon)
    normed = center * scale
    return (normed * gain + shift, normed, scale)


def norm_back(grad, normed, scale, gain):
    scaled = grad * gain
    mean_plain = jnp.mean(scaled, axis=-1, keepdims=True)
    mean_cross = jnp.mean(scaled * normed, axis=-1, keepdims=True)
    return scale * (scaled - mean_plain - normed * mean_cross)


def middle_forward(activated, first_mean, second_mean, gain, shift):
    scale = lax.rsqrt(second_mean - first_mean * first_mean + norm_epsilon)
    normed = (activated - first_mean) * scale
    return (normed * gain + shift, normed, scale)


def exact_gelu(values_in):
    return jax.nn.gelu(values_in, approximate=False)


def doc_labels(doc_lengths, start, count, row_length):
    doc_count = doc_lengths.shape[1]
    places = start + jnp.arange(count, dtype=jnp.int32)
    row_number = start // row_length
    ends = jnp.cumsum(doc_lengths, axis=1)
    row_ends = lax.dynamic_slice_in_dim(ends, jnp.maximum(row_number, 0), 1, 0)[0]
    within = places - row_number * row_length
    document = jnp.sum((within[:, None] >= row_ends[None, :]).astype(jnp.int32), axis=1)
    return (row_number * doc_count + document, places)


def adam_step(grad, weight, first, second, step, rate, decay):
    first_new = first_decay * first + (1.0 - first_decay) * grad
    second_new = second_decay * second + (1.0 - second_decay) * grad * grad
    fix_one = 1.0 - jnp.power(jnp.float32(first_decay), step)
    fix_two = 1.0 - jnp.power(jnp.float32(second_decay), step)
    direction = first_new / fix_one / (jnp.sqrt(second_new / fix_two) + adam_epsilon)
    weight_new = weight - rate * (direction + decay * weight)
    return (first_new, second_new, weight_new)


def from_behind(shard, axis, by):
    count = lax.axis_size(axis)
    pairs = [(i, i + by) for i in range(count) if 0 <= i + by < count]
    return lax.ppermute(shard, axis, pairs)


class Place:
    def __init__(self):
        self.y = lax.axis_index("dp")
        self.w = lax.axis_index("wide")
        self.z = self.w // 4
        self.x = (self.w // 2) % 2
        self.c = self.w % 2

    def slab(self, z, x, c):
        return z * 4 + x * 2 + c

    def wide(self, w):
        return (self.y, w)

    def core_mate(self):
        return self.wide(self.slab(self.z, self.x, 1 - self.c))

    def x_mate(self):
        return self.wide(self.slab(self.z, 1 - self.x, self.c))

    def y_mate(self):
        return (1 - self.y, self.w)

    def up(self):
        return self.wide(lax.rem(self.w + 4, 16))

    def down(self):
        return self.wide(lax.rem(self.w + 12, 16))


def greet(me, extra=()):
    barrier = pltpu.get_barrier_semaphore()

    def hello(target):
        pl.semaphore_signal(barrier, inc=1, device_id=target, device_id_type=MESH)

    always = [me.core_mate(), me.x_mate(), me.y_mate(), *extra]
    sometimes = [
        (me.z < 3, me.up()),
        (me.z > 0, me.down()),
        (me.w < 14, me.wide(lax.rem(me.w + 2, 16))),
        (me.w >= 2, me.wide(lax.rem(me.w + 14, 16))),
    ]
    for target in always:
        hello(target)
    for holds, target in sometimes:
        pl.when(holds)(functools.partial(hello, target))
    count = len(always) + sum(holds.astype(jnp.int32) for holds, _ in sometimes)
    pl.semaphore_wait(barrier, count)


class Wire:
    def __init__(self, send, recv):
        self.send, self.recv = send, recv
        self.started = []

    def copy(self, source, target, index, device):
        return pltpu.make_async_remote_copy(
            src_ref=source,
            dst_ref=target,
            send_sem=self.send.at[index],
            recv_sem=self.recv.at[index],
            device_id=device,
            device_id_type=MESH,
        )

    def put(self, source, target, index, device, holds=None):
        moved = self.copy(source, target, index, device)
        if holds is None:
            moved.start()
        else:
            pl.when(holds)(moved.start)
        self.started.append((holds, moved))

    def got(self, target, index, device):
        self.copy(target, target, index, device).wait_recv()

    def finish(self):
        for holds, moved in self.started:
            if holds is None:
                moved.wait_send()
            else:
                pl.when(holds)(moved.wait_send)


def both(*conditions):
    held = [one for one in conditions if one is not None]
    total = held[0] if held else None
    for one in held[1:]:
        total = jnp.logical_and(total, one)
    return total


def when(holds, action):
    if holds is None:
        action()
    else:
        pl.when(holds)(action)


def ag_steps(me, wire, base, own, full, third):
    rows = own.shape[0]
    plane = (
        pl.ds(pl.multiple_of(me.y * third, 16), rows - third) if third else pl.ds(0, rows)
    )
    share = pl.ds(pl.multiple_of(me.y * (rows - third), 16), third) if third else None
    other = pl.ds(pl.multiple_of((1 - me.y) * (rows - third), 16), third) if third else None
    my_slab = me.slab(me.z, me.x, me.c)
    ups, downs, xs, ys, cs, ts = (base + k for k in (0, 4, 8, 12, 20, 28))

    def pass_on(z, x, holds):
        slab = me.slab(z, x, me.c)
        place = z * 2 + x
        block = full.at[slab, plane]
        if third:
            piece = full.at[slab, share]
            wire.put(piece, piece, ys + place, me.y_mate(), holds)
        wire.put(block, block, cs + place, me.core_mate(), holds)

    wire.put(own.at[plane], full.at[my_slab, plane], ups + me.z, me.up(), me.z < 3)
    wire.put(own.at[plane], full.at[my_slab, plane], downs + me.z, me.down(), me.z > 0)
    wire.put(own.at[plane], full.at[my_slab, plane], xs + me.z, me.x_mate())
    wire.put(own, full.at[my_slab], cs + me.z * 2 + me.x, me.core_mate())
    yield
    for tick in range(1, 5):
        if tick < 4:
            for away, holds, onward, follow, sems in (
                (me.z - tick, me.z - tick >= 0, me.up(), me.z < 3, ups),
                (me.z + tick, me.z + tick <= 3, me.down(), me.z > 0, downs),
            ):
                safe = lax.rem(away + 4, 4)
                block = full.at[me.slab(safe, me.x, me.c), plane]
                pl.when(holds)(functools.partial(wire.got, block, sems + safe, onward))
                wire.put(block, block, sems + safe, onward, both(holds, follow))
                wire.put(block, block, xs + safe, me.x_mate(), holds)
                pass_on(safe, me.x, holds)
        before = tick - 1
        for away, holds in (
            ((me.z, None),)
            if before == 0
            else (
                (me.z - before, me.z - before >= 0),
                (me.z + before, me.z + before <= 3),
            )
        ):
            safe = lax.rem(away + 4, 4)
            block = full.at[me.slab(safe, 1 - me.x, me.c), plane]
            when(holds, functools.partial(wire.got, block, xs + safe, me.x_mate()))
            pass_on(safe, 1 - me.x, holds)
        yield
    if third:
        for k in range(1, 8):
            place = lax.rem(me.z * 2 + me.x + k, 8)
            piece = full.at[me.slab(place // 2, place % 2, me.c), other]
            wire.got(piece, ys + place, me.y_mate())
            wire.put(piece, piece, ts + place, me.core_mate())
        yield
    mine = me.z * 2 + me.x
    wire.got(full.at[me.slab(me.z, me.x, 1 - me.c)], cs + mine, me.core_mate())
    for k in range(1, 8):
        place = lax.rem(mine + k, 8)
        slab = me.slab(place // 2, place % 2, 1 - me.c)
        wire.got(full.at[slab, plane], cs + place, me.core_mate())
        if third:
            wire.got(full.at[slab, other], ts + place, me.core_mate())
    yield


AG_SEMS = 36


def run_all(steps):
    waiting, active = list(steps), []
    while waiting or active:
        if waiting:
            active.append(waiting.pop(0))
        active = [one for one in reversed(active) if next(one, active) is not active][::-1]


def gather_kernel(thirds, *refs):
    count = len(thirds)
    owns, tokens = refs[:count], refs[count]
    fulls, halo = refs[count + 1 : 2 * count + 1], refs[2 * count + 1]
    blank, send, recv, local = refs[2 * count + 2 :]
    me = Place()
    first, second = AG_SEMS * count, AG_SEMS * count + 1
    keep = [
        pltpu.make_async_copy(own, full.at[me.w], local.at[k])
        for k, (own, full) in enumerate(zip(owns, fulls))
    ]
    for one in keep:
        one.start()
    blank[...] = jnp.zeros_like(blank)
    clear = [
        (me.w < 2, pltpu.make_async_copy(blank, halo.at[0], local.at[count])),
        (me.w < 1, pltpu.make_async_copy(blank, halo.at[1], local.at[count + 1])),
    ]
    for holds, one in clear:
        pl.when(holds)(one.start)
    greet(me)
    wire = Wire(send, recv)
    wire.put(tokens, halo.at[0], first, me.wide(lax.rem(me.w + 2, 16)), me.w < 14)
    wire.put(tokens, halo.at[1], second, me.core_mate(), me.c == 0)

    def halo_steps():
        yield
        yield
        pl.when(me.w >= 2)(functools.partial(wire.got, halo.at[0], first, me.core_mate()))
        wire.put(
            halo.at[0], halo.at[1], second, me.core_mate(), both(me.c == 1, me.w >= 2)
        )
        pl.when(me.w >= 1)(functools.partial(wire.got, halo.at[1], second, me.core_mate()))
        yield

    run_all(
        [
            ag_steps(me, wire, AG_SEMS * k, own, full, third)
            for k, (own, full, third) in enumerate(zip(owns, fulls, thirds))
        ]
        + [halo_steps()]
    )
    wire.finish()
    for one in keep:
        one.wait()
    for holds, one in clear:
        pl.when(holds)(one.wait)


def gather_all(shards, thirds, tokens):
    count = len(shards)
    wide = lax.axis_size("wide")
    if lax.axis_size("dp") == 2 and wide == 16:
        out_shape = [jax.ShapeDtypeStruct((wide, *one.shape), one.dtype) for one in shards]
        out_shape.append(jax.ShapeDtypeStruct((2, *tokens.shape), tokens.dtype))
        sems = AG_SEMS * count + 2
        return pl.pallas_call(
            functools.partial(gather_kernel, thirds),
            out_shape=out_shape,
            in_specs=[VMEM] * (count + 1),
            out_specs=[HBM] * (count + 1),
            scratch_shapes=[
                pltpu.VMEM(tokens.shape, tokens.dtype),
                pltpu.SemaphoreType.DMA((sems,)),
                pltpu.SemaphoreType.DMA((sems,)),
                pltpu.SemaphoreType.DMA((count + 2,)),
            ],
            compiler_params=pltpu.CompilerParams(
                collective_id=0, has_side_effects=True, vmem_limit_bytes=24 << 20
            ),
            name="gather_all",
        )(*shards, tokens)
    fulls = [lax.all_gather(one, "wide", axis=0, tiled=False) for one in shards]
    halo = jnp.stack([from_behind(tokens, "wide", 2), from_behind(tokens, "wide", 1)])
    return [*fulls, halo]


def row_chunk(rows, columns, most):
    chunk = min(rows, max(16, most // columns // 16 * 16))
    while rows % chunk:
        chunk -= 16
    return chunk


def accumulate(target, source):
    *lead, rows, columns = source.shape
    chunk = row_chunk(rows, columns, 65536)
    per = rows // chunk
    many = per
    for size in lead:
        many *= size

    def step(number, carry):
        part = pl.ds(pl.multiple_of(lax.rem(number, per) * chunk, 16), chunk)
        rest, index = number // per, []
        for size in reversed(lead):
            index.insert(0, lax.rem(rest, size))
            rest = rest // size
        at = (*index, part)
        target[at] = (target[at].astype(F32) + source[at].astype(F32)).astype(target.dtype)
        return carry

    lax.fori_loop(0, many, step, 0)


RS_SEMS = 12


def rs_steps(me, wire, base, local, grad, quarter, held, bufs, final, squares, limit):
    from_core, from_y, from_x, from_down, from_up, from_last = bufs
    count, columns = held.shape[-2:]
    take = pltpu.make_async_copy(grad.at[:, :, me.c], held, local)
    take.start()
    wire.put(grad.at[:, :, 1 - me.c], from_core, base, me.core_mate())
    yield
    take.wait()
    wire.got(from_core, base, me.core_mate())
    accumulate(held, from_core)
    inside = count - quarter
    plane = pl.ds(pl.multiple_of(me.y * quarter, 16), inside) if quarter else pl.ds(0, count)
    if quarter:
        share = pl.ds(pl.multiple_of(me.y * inside, 16), quarter)
        other = pl.ds(pl.multiple_of((1 - me.y) * inside, 16), quarter)
        wire.put(held.at[:, :, other], from_y, base + 1, me.y_mate())
        yield
        wire.got(from_y, base + 1, me.y_mate())
        accumulate(held.at[:, :, share], from_y)
    mine = held.at[:, me.x, plane]
    wire.put(held.at[:, 1 - me.x, plane], from_x, base + 2, me.x_mate())
    yield
    wire.got(from_x, base + 2, me.x_mate())
    accumulate(mine, from_x)
    for tick in range(4):
        for place, sign, source, sems, onward, back in (
            (me.z, 1, from_down, 4, me.up(), me.down()),
            (3 - me.z, -1, from_up, 8, me.down(), me.up()),
        ):
            goal = me.z if tick == 3 else lax.rem(me.z + sign * (3 - tick) + 8, 4)
            sends = None if tick == 3 else both(place <= tick, place < 3)
            block, arrived = mine.at[goal], source.at[goal]

            def take_in(block=block, arrived=arrived, index=base + sems + goal, back=back):
                wire.got(arrived, index, back)
                accumulate(block, arrived)

            pl.when(both(sends, place > 0))(take_in)
            if sends is not None:
                wire.put(block, arrived, base + sems + goal, onward, sends)
        if tick < 3:
            yield
    wire.put(mine.at[me.z], from_last, base + 3, me.y_mate())
    yield
    wire.got(from_last, base + 3, me.y_mate())
    own = held.at[me.z, me.x]
    middle = count - 2 * quarter
    chunk = row_chunk(middle, columns, 32768)

    def add_planes(number, carry):
        at = pl.multiple_of(quarter + number * chunk, 16)
        there = pl.multiple_of(at - (1 - me.y) * quarter, 16)
        final[pl.ds(at, chunk)] = own[pl.ds(at, chunk)].astype(F32) + from_last[
            pl.ds(there, chunk)
        ].astype(F32)
        return carry

    lax.fori_loop(0, middle // chunk, add_planes, 0)
    if quarter:
        for plane_of, at, there in ((0, 0, 0), (1, count - quarter, count - 2 * quarter)):

            def from_held(at=at):
                final[pl.ds(at, quarter)] = own[pl.ds(at, quarter)].astype(F32)

            def from_mate(at=at, there=there):
                final[pl.ds(at, quarter)] = from_last[pl.ds(there, quarter)].astype(F32)

            pl.when(me.y == plane_of)(from_held)
            pl.when(me.y != plane_of)(from_mate)

    def square(number, total):
        value = final[pl.ds(pl.multiple_of(number * 8, 8), 8)]
        power = value * value
        if limit % 8:
            place = number * 8 + lax.broadcasted_iota(jnp.int32, power.shape, 0)
            power = jnp.where(place < limit, power, 0.0)
        folded = power[:, :128]
        for lane in range(128, columns, 128):
            folded = folded + power[:, lane : lane + 128]
        return total + folded

    squares[...] = squares[...] + lax.fori_loop(
        0, (limit + 7) // 8, square, jnp.zeros((8, 128), F32)
    )
    yield


def reduce_kernel(pieces, *refs):
    refs = list(refs)
    arrays = 1 + max(piece[0] for piece in pieces)
    count = len(pieces)
    grads, halo = refs[:arrays], refs[arrays]
    finals, back, norm = refs[arrays + 1 : 2 * arrays + 1], refs[2 * arrays + 1], refs[2 * arrays + 2]
    scratch = refs[2 * arrays + 3 :]
    blank, passing, joined, tiles, send, recv, local = scratch[-7:]
    me = Place()
    ending = RS_SEMS * count
    blank[...] = jnp.zeros_like(blank)
    tiles[...] = jnp.zeros_like(tiles)
    clear = [
        (me.w >= 14, pltpu.make_async_copy(blank, back.at[0], local.at[count])),
        (me.c == 1, pltpu.make_async_copy(blank, back.at[1], local.at[count + 1])),
    ]
    for holds, one in clear:
        pl.when(holds)(one.start)
    rounds = [me.wide(jnp.bitwise_xor(me.w, bit)) for bit in (1, 2, 4, 8)]
    greet(me, rounds[2:])
    wire = Wire(send, recv)

    def halo_steps():
        far = me.wide(lax.rem(me.w + 14, 16))
        inner = me.w >= 2
        wire.put(halo.at[0], back.at[0], ending, far, both(me.c == 0, inner))
        wire.put(halo.at[1], back.at[1], ending + 1, me.core_mate(), me.c == 1)
        wire.put(halo.at[1], passing, ending + 2, me.core_mate(), both(me.c == 0, inner))
        load = pltpu.make_async_copy(halo.at[0], joined, local.at[count + 2])
        joins = both(me.c == 1, inner)
        pl.when(joins)(load.start)
        yield

        def join():
            load.wait()
            wire.got(passing, ending + 2, me.core_mate())
            accumulate(joined, passing)

        pl.when(joins)(join)
        wire.put(joined, back.at[0], ending, far, joins)
        for _ in range(6):
            yield
        pl.when(me.w < 14)(functools.partial(wire.got, back.at[0], ending, far))
        pl.when(me.c == 0)(functools.partial(wire.got, back.at[1], ending + 1, me.core_mate()))
        yield

    sequences = []
    for k, (number, first, rows, quarter, limit) in enumerate(pieces):
        here = pl.ds(first, rows)
        sequences.append(
            rs_steps(
                me, wire, RS_SEMS * k, local.at[k],
                grads[number].at[:, :, :, here], quarter, scratch[7 * k],
                scratch[7 * k + 1 : 7 * k + 7], finals[number].at[here], tiles.at[0], limit,
            )
        )
    run_all([sequences[0], halo_steps(), *sequences[1:]])
    for k, partner in enumerate(rounds):
        index = ending + 3 + k
        moved = wire.copy(tiles.at[k], tiles.at[5 + k], index, partner)
        moved.start()
        moved.wait()
        tiles[k + 1] = tiles[k] + tiles[5 + k]
    norm[...] = tiles[4]
    wire.finish()
    for holds, one in clear:
        pl.when(holds)(one.wait)


def piece_buffers(rows, columns, quarter, dtype):
    inside = rows - quarter
    some = (4, 2, quarter, columns) if quarter else (1, 1, 16, 128)
    shapes = [
        (4, 2, rows, columns),
        (4, 2, rows, columns),
        some,
        (4, inside, columns),
        (4, inside, columns),
        (4, inside, columns),
        (inside, columns),
    ]
    return [pltpu.VMEM(shape, dtype) for shape in shapes]


def reduce_all(grads, halo, pieces):
    wide = lax.axis_size("wide")
    if lax.axis_size("dp") == 2 and wide == 16:
        count = len(pieces)
        tokens = halo.shape[1:]
        out_shape = [jax.ShapeDtypeStruct(one.shape[1:], F32) for one in grads]
        out_shape.append(jax.ShapeDtypeStruct(halo.shape, halo.dtype))
        out_shape.append(jax.ShapeDtypeStruct((8, 128), F32))
        scratch = []
        for number, _, rows, quarter, _ in pieces:
            one = grads[number]
            scratch += piece_buffers(rows, one.shape[2], quarter, one.dtype)
        sems = RS_SEMS * count + 7
        return pl.pallas_call(
            functools.partial(reduce_kernel, pieces),
            out_shape=out_shape,
            in_specs=[HBM] * (len(grads) + 1),
            out_specs=[VMEM] * len(grads) + [HBM, VMEM],
            scratch_shapes=scratch
            + [
                pltpu.VMEM(tokens, BF16),
                pltpu.VMEM(tokens, BF16),
                pltpu.VMEM(tokens, BF16),
                pltpu.VMEM((9, 8, 128), F32),
                pltpu.SemaphoreType.DMA((sems,)),
                pltpu.SemaphoreType.DMA((sems,)),
                pltpu.SemaphoreType.DMA((count + 3,)),
            ],
            compiler_params=pltpu.CompilerParams(
                collective_id=1, has_side_effects=True, vmem_limit_bytes=60 << 20
            ),
            name="reduce_all",
        )(*[one.reshape(4, 2, 2, *one.shape[1:]) for one in grads], halo)
    totals = [
        lax.psum(
            lax.psum_scatter(one.astype(F32), "wide", scatter_dimension=0, tiled=False), "dp"
        )
        for one in grads
    ]
    back = jnp.stack([from_behind(halo[0], "wide", -2), from_behind(halo[1], "wide", -1)])
    squares = jnp.float32(0.0)
    for number, first, rows, _, limit in pieces:
        part = totals[number][first : first + limit]
        squares = squares + jnp.sum(part * part)
    norm = jnp.zeros((8, 128), F32).at[0, 0].set(lax.psum(squares, "wide"))
    return [*totals, back, norm]


def pack(parts):
    flat = jnp.concatenate(parts, axis=1)
    size = -(-flat.shape[1] // 2048) * 2048
    return jnp.pad(flat, ((0, 0), (0, size - flat.shape[1]))).reshape(flat.shape[0], -1, 128)


def to_slabs(rows, wide):
    count, columns = rows.shape
    return rows.reshape(count, wide, -1).transpose(1, 0, 2).reshape(wide, -1)


def unpack(slabs, count):
    return slabs.reshape(slabs.shape[0], count, -1).transpose(1, 0, 2).reshape(count, -1)


def body(
    inputs,
    out_grad,
    doc_lengths,
    step_count,
    qkv_weight,
    qkv_first,
    qkv_second,
    out_weight,
    out_first,
    out_second,
    fc1_weight,
    fc1_first,
    fc1_second,
    fc2_weight,
    fc2_first,
    fc2_second,
    model_vectors,
    vectors_first,
    vectors_second,
    hidden_vectors,
    hidden_first,
    hidden_second,
    head_scale,
    head_first,
    head_second,
):
    tokens_dev = inputs.shape[0]
    width = inputs.shape[1]
    heads_count = head_scale.shape[0]
    head_size = width // heads_count
    wide = lax.axis_size("wide")
    row_length = tokens_dev * wide
    score_scale = head_size ** (-0.5)
    block_index = lax.axis_index("dp") * wide + lax.axis_index("wide")
    first_token = block_index * tokens_dev
    hidden_width = hidden_vectors.shape[1] * wide
    vector_rows, hidden_rows = model_vectors.shape[0], hidden_vectors.shape[0]
    vector_size, hidden_size = model_vectors.size, hidden_vectors.size

    small = pack(
        [model_vectors.astype(BF16).reshape(1, -1), hidden_vectors.astype(BF16).reshape(1, -1)]
    )[0]
    small_full, qkv_full, out_full, fc1_full, fc2_full, halo = gather_all(
        [
            small,
            qkv_weight.astype(BF16),
            out_weight.astype(BF16),
            fc1_weight.astype(BF16),
            fc2_weight.astype(BF16),
        ],
        (0, 16, 16, 256, 64),
        inputs,
    )
    flat = small_full.reshape(wide, -1)
    vectors = unpack(flat[:, :vector_size], vector_rows).astype(F32)
    hidden_par = unpack(flat[:, vector_size : vector_size + hidden_size], hidden_rows).astype(F32)
    qkv_full = qkv_full.reshape(width, 3 * width)
    out_full = out_full.reshape(width, width)
    fc2_full = fc2_full.reshape(hidden_width, width)
    heads_low = lax.optimization_barrier(head_scale.astype(BF16)).astype(F32)

    tokens_in = inputs.astype(F32)
    tokens_all = jnp.concatenate([halo.reshape(-1, width), inputs], axis=0)
    normed_in, hat_in, scale_in = layer_norm(tokens_all.astype(F32), vectors[0], vectors[3])
    normed_low = normed_in.astype(BF16)
    own = slice(2 * tokens_dev, None)
    queries = (
        jnp.dot(normed_low[own], qkv_full[:, :width], preferred_element_type=F32) + vectors[4]
    ).astype(BF16)
    projected = jnp.dot(normed_low, qkv_full[:, width:], preferred_element_type=F32)
    keys_all = projected[:, :width].astype(BF16).reshape(-1, heads_count, head_size)
    values_all = (
        (projected[:, width:] + vectors[5]).astype(BF16).reshape(-1, heads_count, head_size)
    )
    labels, places = [], []
    for back in (2, 1, 0):
        labels_here, places_here = doc_labels(
            doc_lengths, first_token - back * tokens_dev, tokens_dev, row_length
        )
        labels.append(labels_here)
        places.append(places_here)
    allowed = (labels[2][:, None] == jnp.concatenate(labels)[None, :]) & (
        jnp.concatenate(places)[None, :] <= places[2][:, None]
    )
    queries_split = queries.reshape(tokens_dev, heads_count, head_size)

    def masked_scores():
        raw = (
            jnp.einsum("qhd,khd->hqk", queries_split, keys_all, preferred_element_type=F32)
            * score_scale
        )
        return jnp.where(allowed[None], raw, masked_score)

    scores = masked_scores()
    highest = jnp.max(scores, axis=-1, keepdims=True)
    weights_exp = jnp.exp(scores - highest)
    totals = jnp.sum(weights_exp, axis=-1, keepdims=True)
    log_totals = highest + jnp.log(totals)
    probs_low = (weights_exp / totals).astype(BF16)
    attended = jnp.einsum("hqk,khd->qhd", probs_low, values_all, preferred_element_type=F32)
    mixed_low = (attended * heads_low[None, :, None]).astype(BF16).reshape(tokens_dev, width)
    proj_out = jnp.dot(mixed_low, out_full, preferred_element_type=F32) + vectors[6]
    normed_post, hat_post, scale_post = layer_norm(proj_out, vectors[1], vectors[7])
    residual = tokens_in + normed_post
    normed_two, hat_two, scale_two = layer_norm(residual, vectors[2], vectors[8])
    rows_low = normed_two.astype(BF16)
    grad_in = out_grad.astype(F32)

    pre_act = (
        jnp.einsum("td,wdf->twf", rows_low, fc1_full, preferred_element_type=F32).reshape(
            tokens_dev, hidden_width
        )
        + hidden_par[2]
    )
    activated, gelu_back = jax.vjp(exact_gelu, pre_act)
    first_mean = jnp.mean(activated, axis=-1, keepdims=True)
    second_mean = jnp.mean(activated * activated, axis=-1, keepdims=True)
    middle, hat_mid, scale_mid = middle_forward(
        activated, first_mean, second_mean, hidden_par[0], hidden_par[1]
    )
    middle_low = middle.astype(BF16)
    ffn_out = jnp.dot(middle_low, fc2_full, preferred_element_type=F32)
    output = (residual + (ffn_out + vectors[9])).astype(BF16)
    fc2_grad = jnp.einsum("tf,td->fd", middle_low, out_grad, preferred_element_type=F32)
    middle_grad = jnp.einsum("td,fd->tf", out_grad, fc2_full, preferred_element_type=F32)
    mid_gain_grad = jnp.sum(middle_grad * hat_mid, axis=0)
    mid_bias_grad = jnp.sum(middle_grad, axis=0)
    scaled_mid = middle_grad * hidden_par[0]
    plain_mean = jnp.mean(scaled_mid, axis=-1, keepdims=True)
    cross_mean = jnp.mean(scaled_mid * hat_mid, axis=-1, keepdims=True)
    act_grad = scale_mid * (scaled_mid - plain_mean - hat_mid * cross_mean)
    pre_low = gelu_back(act_grad)[0].astype(BF16)
    fc1_bias_grad = jnp.sum(pre_low.astype(F32), axis=0)
    pre_split = pre_low.reshape(tokens_dev, wide, -1)
    fc1_grad = jnp.einsum("td,twf->wdf", rows_low, pre_split, preferred_element_type=F32)
    rows_grad = jnp.einsum("twf,wdf->td", pre_split, fc1_full, preferred_element_type=F32)
    hidden_grad = jnp.stack([mid_gain_grad, mid_bias_grad, fc1_bias_grad])
    out_bias_total = jnp.sum(grad_in, axis=0)
    residual_grad = grad_in + norm_back(rows_grad, hat_two, scale_two, vectors[2])
    gain_two_grad = jnp.sum(rows_grad * hat_two, axis=0)
    bias_two_grad = jnp.sum(rows_grad, axis=0)
    gain_post_grad = jnp.sum(residual_grad * hat_post, axis=0)
    bias_post_grad = jnp.sum(residual_grad, axis=0)
    proj_low = norm_back(residual_grad, hat_post, scale_post, vectors[1]).astype(BF16)
    proj_bias_grad = jnp.sum(proj_low.astype(F32), axis=0)
    out_weight_grad = jnp.einsum("td,te->de", mixed_low, proj_low, preferred_element_type=F32)
    mixed_grad = jnp.einsum(
        "te,de->td", proj_low, out_full, preferred_element_type=F32
    ).reshape(tokens_dev, heads_count, head_size)
    head_grad = jnp.sum(mixed_grad * attended, axis=(0, 2))
    attended_low = (mixed_grad * heads_low[None, :, None]).astype(BF16)
    probs = jnp.exp(masked_scores() - log_totals)
    probs_grad = jnp.einsum("qhd,khd->hqk", attended_low, values_all, preferred_element_type=F32)
    delta = jnp.transpose(jnp.sum(attended_low.astype(F32) * attended, axis=-1))[:, :, None]
    scores_low = (probs * (probs_grad - delta)).astype(BF16)
    query_grad = (
        (
            jnp.einsum("hqk,khd->qhd", scores_low, keys_all, preferred_element_type=F32)
            * score_scale
        )
        .astype(BF16)
        .reshape(tokens_dev, width)
    )
    key_grad = (
        jnp.einsum("hqk,qhd->khd", scores_low, queries_split, preferred_element_type=F32)
        * score_scale
    )
    value_grad = jnp.einsum(
        "hqk,qhd->khd", probs.astype(BF16), attended_low, preferred_element_type=F32
    )
    pair_low = jnp.concatenate(
        [key_grad.reshape(-1, width), value_grad.reshape(-1, width)], axis=1
    ).astype(BF16)
    query_bias_grad = jnp.sum(query_grad.astype(F32), axis=0)
    value_bias_grad = jnp.sum(pair_low[:, width:].astype(F32), axis=0)
    qkv_grad = jnp.concatenate(
        [
            jnp.einsum("td,te->de", normed_low[own], query_grad, preferred_element_type=F32),
            jnp.einsum("td,te->de", normed_low, pair_low, preferred_element_type=F32),
        ],
        axis=1,
    )
    normed_grad = jnp.einsum("te,de->td", pair_low, qkv_full[:, width:], preferred_element_type=F32)
    halo_grad = normed_grad[: 2 * tokens_dev]
    own_grad = normed_grad[own] + jnp.einsum(
        "te,de->td", query_grad, qkv_full[:, :width], preferred_element_type=F32
    )
    gain_in_grad = jnp.sum(halo_grad * hat_in[: 2 * tokens_dev], axis=0) + jnp.sum(
        own_grad * hat_in[own], axis=0
    )
    bias_in_grad = jnp.sum(halo_grad, axis=0) + jnp.sum(own_grad, axis=0)
    vector_grad = jnp.stack(
        [
            gain_in_grad,
            gain_post_grad,
            gain_two_grad,
            bias_in_grad,
            query_bias_grad,
            value_bias_grad,
            proj_bias_grad,
            bias_post_grad,
            bias_two_grad,
            out_bias_total,
        ]
    )
    small_grad = pack(
        [
            to_slabs(vector_grad, wide),
            to_slabs(hidden_grad, wide),
            jnp.broadcast_to(head_grad[None], (wide, heads_count)),
        ]
    )
    counted = (vector_size + hidden_size) // 128
    fc1_rows, fc2_rows = fc1_weight.shape[0], fc2_weight.shape[0]
    qkv_rows, out_rows = qkv_weight.shape[0], out_weight.shape[0]
    small_part, qkv_part, out_part, fc1_part, fc2_part, halo_back, norm_tile = reduce_all(
        [
            small_grad,
            qkv_grad.astype(BF16).reshape(wide, -1, 3 * width),
            out_weight_grad.astype(BF16).reshape(wide, -1, width),
            fc1_grad.astype(BF16),
            fc2_grad.astype(BF16).reshape(wide, -1, width),
        ],
        halo_grad.astype(BF16).reshape(2, tokens_dev, width),
        (
            (3, 0, fc1_rows // 2, fc1_rows // 8, fc1_rows // 2),
            (3, fc1_rows // 2, fc1_rows // 2, fc1_rows // 8, fc1_rows // 2),
            (4, 0, fc2_rows // 2, fc2_rows // 8, fc2_rows // 2),
            (4, fc2_rows // 2, fc2_rows // 2, fc2_rows // 8, fc2_rows // 2),
            (0, 0, small_grad.shape[1], 0, counted),
            (1, 0, qkv_rows, qkv_rows // 4, qkv_rows),
            (2, 0, out_rows, out_rows // 4, out_rows),
        ),
    )
    total_grad = own_grad + halo_back[0].astype(F32) + halo_back[1].astype(F32)
    input_grad = residual_grad + norm_back(total_grad, hat_in[own], scale_in[own], vectors[0])
    flat = small_part.reshape(-1)
    vector_part = flat[:vector_size].reshape(model_vectors.shape)
    hidden_part = flat[vector_size : vector_size + hidden_size].reshape(hidden_vectors.shape)
    head_total = flat[vector_size + hidden_size :][:heads_count]
    grad_norm = jnp.sqrt(jnp.sum(norm_tile) + jnp.sum(head_total * head_total))
    factor = jnp.minimum(1.0, clip_limit / (grad_norm + 1e-06))
    step = step_count[0].astype(F32)
    grads = (qkv_part, out_part, fc1_part, fc2_part, vector_part, hidden_part, head_total)
    params = (
        qkv_weight,
        out_weight,
        fc1_weight,
        fc2_weight,
        model_vectors,
        hidden_vectors,
        head_scale,
    )
    firsts = (qkv_first, out_first, fc1_first, fc2_first, vectors_first, hidden_first, head_first)
    seconds = (
        qkv_second,
        out_second,
        fc1_second,
        fc2_second,
        vectors_second,
        hidden_second,
        head_second,
    )
    rates = (
        matrix_rate,
        matrix_rate,
        matrix_rate,
        matrix_rate,
        vector_rate,
        vector_rate,
        vector_rate,
    )
    decays = (weight_decay, weight_decay, weight_decay, weight_decay, 0.0, 0.0, 0.0)
    updated = []
    for number in range(7):
        updated.extend(
            adam_step(
                grads[number] * factor,
                params[number],
                firsts[number],
                seconds[number],
                step,
                rates[number],
                decays[number],
            )
        )
    return (
        output,
        input_grad,
        grad_norm.reshape(1),
        updated[0],
        updated[1],
        updated[2],
        updated[3],
        updated[4],
        updated[5],
        updated[6],
        updated[7],
        updated[8],
        updated[9],
        updated[10],
        updated[11],
        updated[12],
        updated[13],
        updated[14],
        updated[15],
        updated[16],
        updated[17],
        updated[18],
        updated[19],
        updated[20],
    )


def solution(mesh):
    placed = (
        P(("dp", "wide"), None),
        P(("dp", "wide"), None),
        P(),
        P(),
        P("wide", None),
        P("wide", None),
        P("wide", None),
        P("wide", None),
        P("wide", None),
        P("wide", None),
        P(None, "wide"),
        P(None, "wide"),
        P(None, "wide"),
        P("wide", None),
        P("wide", None),
        P("wide", None),
        P(None, "wide"),
        P(None, "wide"),
        P(None, "wide"),
        P(None, "wide"),
        P(None, "wide"),
        P(None, "wide"),
        P(),
        P(),
        P(),
    )
    return jax.shard_map(
        body,
        mesh=mesh,
        in_specs=placed,
        out_specs=(
            P(("dp", "wide"), None),
            P(("dp", "wide"), None),
            P(),
            P("wide", None),
            P("wide", None),
            P("wide", None),
            P("wide", None),
            P("wide", None),
            P("wide", None),
            P(None, "wide"),
            P(None, "wide"),
            P(None, "wide"),
            P("wide", None),
            P("wide", None),
            P("wide", None),
            P(None, "wide"),
            P(None, "wide"),
            P(None, "wide"),
            P(None, "wide"),
            P(None, "wide"),
            P(None, "wide"),
            P(),
            P(),
            P(),
        ),
        check_vma=False,
    )
```

```python
import functools

import jax
import jax.numpy as jnp
from jax import lax
from jax.experimental import pallas as pl
from jax.experimental.pallas import tpu as pltpu
from jax.sharding import PartitionSpec as P

DOC_MOST = 1024
MESH = pl.DeviceIdType.MESH
HBM = pl.BlockSpec(memory_space=pltpu.HBM)
VMEM = pl.BlockSpec(memory_space=pltpu.VMEM)
BF16 = jnp.bfloat16
F32 = jnp.float32

norm_epsilon = 1e-05
clip_limit = 1.0
first_decay = 0.9
second_decay = 0.98
adam_epsilon = 1e-08
matrix_rate = 0.1
vector_rate = 0.4
weight_decay = 0.1
masked_score = -1e30


def layer_norm(values_in, gain, shift):
    center = values_in - jnp.mean(values_in, axis=-1, keepdims=True)
    variance = jnp.mean(center * center, axis=-1, keepdims=True)
    scale = lax.rsqrt(variance + norm_epsilon)
    normed = center * scale
    return (normed * gain + shift, normed, scale)


def norm_back(grad, normed, scale, gain):
    scaled = grad * gain
    mean_plain = jnp.mean(scaled, axis=-1, keepdims=True)
    mean_cross = jnp.mean(scaled * normed, axis=-1, keepdims=True)
    return scale * (scaled - mean_plain - normed * mean_cross)


def middle_forward(activated, first_mean, second_mean, gain, shift):
    scale = lax.rsqrt(second_mean - first_mean * first_mean + norm_epsilon)
    normed = (activated - first_mean) * scale
    return (normed * gain + shift, normed, scale)


def exact_gelu(values_in):
    return jax.nn.gelu(values_in, approximate=False)


def doc_starts(doc_lengths, row, first, count):
    ends = lax.dynamic_slice_in_dim(jnp.cumsum(doc_lengths, axis=1), row, 1, 0)[0]
    places = first + jnp.arange(count, dtype=jnp.int32)
    return jnp.max(jnp.where(ends[None, :] <= places[:, None], ends[None, :], 0), axis=1)


def adam_step(grad, weight, first, second, step, rate, decay):
    first_new = first_decay * first + (1.0 - first_decay) * grad
    second_new = second_decay * second + (1.0 - second_decay) * grad * grad
    fix_one = 1.0 - jnp.power(jnp.float32(first_decay), step)
    fix_two = 1.0 - jnp.power(jnp.float32(second_decay), step)
    direction = first_new / fix_one / (jnp.sqrt(second_new / fix_two) + adam_epsilon)
    weight_new = weight - rate * (direction + decay * weight)
    return (first_new, second_new, weight_new)


def from_behind(shard, axis, by):
    count = lax.axis_size(axis)
    pairs = [(i, i + by) for i in range(count) if 0 <= i + by < count]
    return lax.ppermute(shard, axis, pairs)


class Place:
    def __init__(self):
        self.y = lax.axis_index("dp")
        self.w = lax.axis_index("wide")
        self.z = self.w // 4
        self.x = (self.w // 2) % 2
        self.c = self.w % 2

    def slab(self, z, x, c):
        return z * 4 + x * 2 + c

    def wide(self, w):
        return (self.y, w)

    def core_mate(self):
        return self.wide(self.slab(self.z, self.x, 1 - self.c))

    def x_mate(self):
        return self.wide(self.slab(self.z, 1 - self.x, self.c))

    def y_mate(self):
        return (1 - self.y, self.w)

    def up(self):
        return self.wide(lax.rem(self.w + 4, 16))

    def down(self):
        return self.wide(lax.rem(self.w + 12, 16))


def greet(me, extra=()):
    barrier = pltpu.get_barrier_semaphore()

    def hello(target):
        pl.semaphore_signal(barrier, inc=1, device_id=target, device_id_type=MESH)

    always = [me.core_mate(), me.x_mate(), me.y_mate(), *extra]
    sometimes = [
        (me.z < 3, me.up()),
        (me.z > 0, me.down()),
        (me.w < 14, me.wide(lax.rem(me.w + 2, 16))),
        (me.w >= 2, me.wide(lax.rem(me.w + 14, 16))),
    ]
    for target in always:
        hello(target)
    for holds, target in sometimes:
        pl.when(holds)(functools.partial(hello, target))
    count = len(always) + sum(holds.astype(jnp.int32) for holds, _ in sometimes)
    pl.semaphore_wait(barrier, count)


class Wire:
    def __init__(self, send, recv):
        self.send, self.recv = send, recv
        self.started = []

    def copy(self, source, target, index, device):
        return pltpu.make_async_remote_copy(
            src_ref=source,
            dst_ref=target,
            send_sem=self.send.at[index],
            recv_sem=self.recv.at[index],
            device_id=device,
            device_id_type=MESH,
        )

    def put(self, source, target, index, device, holds=None):
        moved = self.copy(source, target, index, device)
        if holds is None:
            moved.start()
        else:
            pl.when(holds)(moved.start)
        self.started.append((holds, moved))

    def got(self, target, index, device):
        self.copy(target, target, index, device).wait_recv()

    def finish(self):
        for holds, moved in self.started:
            if holds is None:
                moved.wait_send()
            else:
                pl.when(holds)(moved.wait_send)


def both(*conditions):
    held = [one for one in conditions if one is not None]
    total = held[0] if held else None
    for one in held[1:]:
        total = jnp.logical_and(total, one)
    return total


def when(holds, action):
    if holds is None:
        action()
    else:
        pl.when(holds)(action)


def ag_steps(me, wire, base, own, full, third):
    rows = own.shape[0]
    plane = (
        pl.ds(pl.multiple_of(me.y * third, 16), rows - third) if third else pl.ds(0, rows)
    )
    share = pl.ds(pl.multiple_of(me.y * (rows - third), 16), third) if third else None
    other = pl.ds(pl.multiple_of((1 - me.y) * (rows - third), 16), third) if third else None
    my_slab = me.slab(me.z, me.x, me.c)
    ups, downs, xs, ys, cs, ts = (base + k for k in (0, 4, 8, 12, 20, 28))

    def pass_on(z, x, holds):
        slab = me.slab(z, x, me.c)
        place = z * 2 + x
        block = full.at[slab, plane]
        if third:
            piece = full.at[slab, share]
            wire.put(piece, piece, ys + place, me.y_mate(), holds)
        wire.put(block, block, cs + place, me.core_mate(), holds)

    wire.put(own.at[plane], full.at[my_slab, plane], ups + me.z, me.up(), me.z < 3)
    wire.put(own.at[plane], full.at[my_slab, plane], downs + me.z, me.down(), me.z > 0)
    wire.put(own.at[plane], full.at[my_slab, plane], xs + me.z, me.x_mate())
    wire.put(own, full.at[my_slab], cs + me.z * 2 + me.x, me.core_mate())
    yield
    for tick in range(1, 5):
        if tick < 4:
            for away, holds, onward, follow, sems in (
                (me.z - tick, me.z - tick >= 0, me.up(), me.z < 3, ups),
                (me.z + tick, me.z + tick <= 3, me.down(), me.z > 0, downs),
            ):
                safe = lax.rem(away + 4, 4)
                block = full.at[me.slab(safe, me.x, me.c), plane]
                pl.when(holds)(functools.partial(wire.got, block, sems + safe, onward))
                wire.put(block, block, sems + safe, onward, both(holds, follow))
                wire.put(block, block, xs + safe, me.x_mate(), holds)
                pass_on(safe, me.x, holds)
        before = tick - 1
        for away, holds in (
            ((me.z, None),)
            if before == 0
            else (
                (me.z - before, me.z - before >= 0),
                (me.z + before, me.z + before <= 3),
            )
        ):
            safe = lax.rem(away + 4, 4)
            block = full.at[me.slab(safe, 1 - me.x, me.c), plane]
            when(holds, functools.partial(wire.got, block, xs + safe, me.x_mate()))
            pass_on(safe, 1 - me.x, holds)
        yield
    if third:
        for k in range(1, 8):
            place = lax.rem(me.z * 2 + me.x + k, 8)
            piece = full.at[me.slab(place // 2, place % 2, me.c), other]
            wire.got(piece, ys + place, me.y_mate())
            wire.put(piece, piece, ts + place, me.core_mate())
        yield
    mine = me.z * 2 + me.x
    wire.got(full.at[me.slab(me.z, me.x, 1 - me.c)], cs + mine, me.core_mate())
    for k in range(1, 8):
        place = lax.rem(mine + k, 8)
        slab = me.slab(place // 2, place % 2, 1 - me.c)
        wire.got(full.at[slab, plane], cs + place, me.core_mate())
        if third:
            wire.got(full.at[slab, other], ts + place, me.core_mate())
    yield


AG_SEMS = 36


def run_all(steps, at_once):
    waiting, active = list(steps), []
    while waiting or active:
        active = waiting[:at_once] + active
        del waiting[:at_once]
        active = [one for one in active if next(one, active) is not active]


def gather_kernel(thirds, *refs):
    count = len(thirds)
    owns, tokens = refs[:count], refs[count]
    fulls, halo = refs[count + 1 : 2 * count + 1], refs[2 * count + 1]
    blank, send, recv, local = refs[2 * count + 2 :]
    me = Place()
    first, second = AG_SEMS * count, AG_SEMS * count + 1
    keep = [
        pltpu.make_async_copy(own, full.at[me.w], local.at[k])
        for k, (own, full) in enumerate(zip(owns, fulls))
    ]
    for one in keep:
        one.start()
    blank[...] = jnp.zeros_like(blank)
    clear = [
        (me.w < 2, pltpu.make_async_copy(blank, halo.at[0], local.at[count])),
        (me.w < 1, pltpu.make_async_copy(blank, halo.at[1], local.at[count + 1])),
    ]
    for holds, one in clear:
        pl.when(holds)(one.start)
    greet(me)
    wire = Wire(send, recv)
    wire.put(tokens, halo.at[0], first, me.wide(lax.rem(me.w + 2, 16)), me.w < 14)
    wire.put(tokens, halo.at[1], second, me.core_mate(), me.c == 0)

    def halo_steps():
        yield
        yield
        pl.when(me.w >= 2)(functools.partial(wire.got, halo.at[0], first, me.core_mate()))
        wire.put(
            halo.at[0], halo.at[1], second, me.core_mate(), both(me.c == 1, me.w >= 2)
        )
        pl.when(me.w >= 1)(functools.partial(wire.got, halo.at[1], second, me.core_mate()))
        yield

    run_all(
        [
            ag_steps(me, wire, AG_SEMS * k, own, full, third)
            for k, (own, full, third) in enumerate(zip(owns, fulls, thirds))
        ]
        + [halo_steps()],
        count + 1,
    )
    wire.finish()
    for one in keep:
        one.wait()
    for holds, one in clear:
        pl.when(holds)(one.wait)


def gather_all(shards, thirds, tokens):
    count = len(shards)
    wide = lax.axis_size("wide")
    if lax.axis_size("dp") == 2 and wide == 16:
        out_shape = [jax.ShapeDtypeStruct((wide, *one.shape), one.dtype) for one in shards]
        out_shape.append(jax.ShapeDtypeStruct((2, *tokens.shape), tokens.dtype))
        sems = AG_SEMS * count + 2
        return pl.pallas_call(
            functools.partial(gather_kernel, thirds),
            out_shape=out_shape,
            in_specs=[VMEM] * (count + 1),
            out_specs=[HBM] * (count + 1),
            scratch_shapes=[
                pltpu.VMEM(tokens.shape, tokens.dtype),
                pltpu.SemaphoreType.DMA((sems,)),
                pltpu.SemaphoreType.DMA((sems,)),
                pltpu.SemaphoreType.DMA((count + 2,)),
            ],
            compiler_params=pltpu.CompilerParams(
                collective_id=0, has_side_effects=True, vmem_limit_bytes=24 << 20
            ),
            name="gather_all",
        )(*shards, tokens)
    fulls = [lax.all_gather(one, "wide", axis=0, tiled=False) for one in shards]
    halo = jnp.stack([from_behind(tokens, "wide", 2), from_behind(tokens, "wide", 1)])
    return [*fulls, halo]


def row_chunk(rows, columns, most):
    chunk = min(rows, max(16, most // columns // 16 * 16))
    while rows % chunk:
        chunk -= 16
    return chunk


def accumulate(target, source):
    *lead, rows, columns = source.shape
    chunk = row_chunk(rows, columns, 65536)
    per = rows // chunk
    many = per
    for size in lead:
        many *= size

    def step(number, carry):
        part = pl.ds(pl.multiple_of(lax.rem(number, per) * chunk, 16), chunk)
        rest, index = number // per, []
        for size in reversed(lead):
            index.insert(0, lax.rem(rest, size))
            rest = rest // size
        at = (*index, part)
        target[at] = (target[at].astype(F32) + source[at].astype(F32)).astype(target.dtype)
        return carry

    lax.fori_loop(0, many, step, 0)


RS_SEMS = 12


def rs_steps(me, wire, base, local, grad, quarter, held, bufs, final, squares, limit):
    from_core, from_y, from_x, from_down, from_up, from_last = bufs
    count, columns = held.shape[-2:]
    take = pltpu.make_async_copy(grad.at[:, :, me.c], held, local)
    take.start()
    wire.put(grad.at[:, :, 1 - me.c], from_core, base, me.core_mate())
    yield
    take.wait()
    wire.got(from_core, base, me.core_mate())
    accumulate(held, from_core)
    inside = count - quarter
    plane = pl.ds(pl.multiple_of(me.y * quarter, 16), inside) if quarter else pl.ds(0, count)
    if quarter:
        share = pl.ds(pl.multiple_of(me.y * inside, 16), quarter)
        other = pl.ds(pl.multiple_of((1 - me.y) * inside, 16), quarter)
        wire.put(held.at[:, :, other], from_y, base + 1, me.y_mate())
        yield
        wire.got(from_y, base + 1, me.y_mate())
        accumulate(held.at[:, :, share], from_y)
    mine = held.at[:, me.x, plane]
    wire.put(held.at[:, 1 - me.x, plane], from_x, base + 2, me.x_mate())
    yield
    wire.got(from_x, base + 2, me.x_mate())
    accumulate(mine, from_x)
    for tick in range(4):
        for place, sign, source, sems, onward, back in (
            (me.z, 1, from_down, 4, me.up(), me.down()),
            (3 - me.z, -1, from_up, 8, me.down(), me.up()),
        ):
            goal = me.z if tick == 3 else lax.rem(me.z + sign * (3 - tick) + 8, 4)
            sends = None if tick == 3 else both(place <= tick, place < 3)
            block, arrived = mine.at[goal], source.at[goal]

            def take_in(block=block, arrived=arrived, index=base + sems + goal, back=back):
                wire.got(arrived, index, back)
                accumulate(block, arrived)

            pl.when(both(sends, place > 0))(take_in)
            if sends is not None:
                wire.put(block, arrived, base + sems + goal, onward, sends)
        if tick < 3:
            yield
    wire.put(mine.at[me.z], from_last, base + 3, me.y_mate())
    yield
    wire.got(from_last, base + 3, me.y_mate())
    own = held.at[me.z, me.x]
    middle = count - 2 * quarter
    chunk = row_chunk(middle, columns, 32768)

    def add_planes(number, carry):
        at = pl.multiple_of(quarter + number * chunk, 16)
        there = pl.multiple_of(at - (1 - me.y) * quarter, 16)
        final[pl.ds(at, chunk)] = own[pl.ds(at, chunk)].astype(F32) + from_last[
            pl.ds(there, chunk)
        ].astype(F32)
        return carry

    lax.fori_loop(0, middle // chunk, add_planes, 0)
    if quarter:
        for plane_of, at, there in ((0, 0, 0), (1, count - quarter, count - 2 * quarter)):

            def from_held(at=at):
                final[pl.ds(at, quarter)] = own[pl.ds(at, quarter)].astype(F32)

            def from_mate(at=at, there=there):
                final[pl.ds(at, quarter)] = from_last[pl.ds(there, quarter)].astype(F32)

            pl.when(me.y == plane_of)(from_held)
            pl.when(me.y != plane_of)(from_mate)

    def square(number, total):
        value = final[pl.ds(pl.multiple_of(number * 8, 8), 8)]
        power = value * value
        if limit % 8:
            place = number * 8 + lax.broadcasted_iota(jnp.int32, power.shape, 0)
            power = jnp.where(place < limit, power, 0.0)
        folded = power[:, :128]
        for lane in range(128, columns, 128):
            folded = folded + power[:, lane : lane + 128]
        return total + folded

    squares[...] = squares[...] + lax.fori_loop(
        0, (limit + 7) // 8, square, jnp.zeros((8, 128), F32)
    )
    yield


def reduce_kernel(pieces, *refs):
    refs = list(refs)
    arrays = 1 + max(piece[0] for piece in pieces)
    results = 1 + max(piece[5] for piece in pieces)
    count = len(pieces)
    grads, halo = refs[:arrays], refs[arrays]
    finals, (back, norm) = refs[arrays + 1 :][:results], refs[arrays + 1 + results :][:2]
    scratch = refs[arrays + 3 + results :]
    blank, passing, joined, tiles, send, recv, local = scratch[-7:]
    me = Place()
    ending = RS_SEMS * count
    blank[...] = jnp.zeros_like(blank)
    tiles[...] = jnp.zeros_like(tiles)
    clear = [
        (me.w >= 14, pltpu.make_async_copy(blank, back.at[0], local.at[count])),
        (me.c == 1, pltpu.make_async_copy(blank, back.at[1], local.at[count + 1])),
    ]
    for holds, one in clear:
        pl.when(holds)(one.start)
    rounds = [me.wide(jnp.bitwise_xor(me.w, bit)) for bit in (1, 2, 4, 8)]
    greet(me, rounds[2:])
    wire = Wire(send, recv)

    def halo_steps():
        far = me.wide(lax.rem(me.w + 14, 16))
        inner = me.w >= 2
        wire.put(halo.at[0], back.at[0], ending, far, both(me.c == 0, inner))
        wire.put(halo.at[1], back.at[1], ending + 1, me.core_mate(), me.c == 1)
        wire.put(halo.at[1], passing, ending + 2, me.core_mate(), both(me.c == 0, inner))
        load = pltpu.make_async_copy(halo.at[0], joined, local.at[count + 2])
        joins = both(me.c == 1, inner)
        pl.when(joins)(load.start)
        yield

        def join():
            load.wait()
            wire.got(passing, ending + 2, me.core_mate())
            accumulate(joined, passing)

        pl.when(joins)(join)
        wire.put(joined, back.at[0], ending, far, joins)
        for _ in range(6):
            yield
        pl.when(me.w < 14)(functools.partial(wire.got, back.at[0], ending, far))
        pl.when(me.c == 0)(functools.partial(wire.got, back.at[1], ending + 1, me.core_mate()))
        yield

    sequences = []
    for k, (number, first, rows, quarter, limit, result, column) in enumerate(pieces):
        here = pl.ds(first, rows)
        final = finals[result].at[here, pl.ds(column, grads[number].shape[-1])]
        sequences.append(
            rs_steps(
                me, wire, RS_SEMS * k, local.at[k],
                grads[number].at[:, :, :, here], quarter, scratch[7 * k],
                scratch[7 * k + 1 : 7 * k + 7], final, tiles.at[0], limit,
            )
        )
    run_all([sequences[0], halo_steps(), *sequences[1:]], 1)
    for k, partner in enumerate(rounds):
        index = ending + 3 + k
        moved = wire.copy(tiles.at[k], tiles.at[5 + k], index, partner)
        moved.start()
        moved.wait()
        tiles[k + 1] = tiles[k] + tiles[5 + k]
    norm[...] = tiles[4]
    wire.finish()
    for holds, one in clear:
        pl.when(holds)(one.wait)


def piece_buffers(rows, columns, quarter, dtype):
    inside = rows - quarter
    some = (4, 2, quarter, columns) if quarter else (1, 1, 16, 128)
    shapes = [
        (4, 2, rows, columns),
        (4, 2, rows, columns),
        some,
        (4, inside, columns),
        (4, inside, columns),
        (4, inside, columns),
        (inside, columns),
    ]
    return [pltpu.VMEM(shape, dtype) for shape in shapes]


def reduce_all(grads, halo, pieces):
    wide = lax.axis_size("wide")
    if lax.axis_size("dp") == 2 and wide == 16:
        count = len(pieces)
        tokens = halo.shape[1:]
        sizes = {}
        for number, _, _, _, _, result, column in pieces:
            _, rows, columns = grads[number].shape
            sizes[result] = (rows, max(column + columns, sizes.get(result, (0, 0))[1]))
        out_shape = [jax.ShapeDtypeStruct(sizes[k], F32) for k in range(len(sizes))]
        out_shape.append(jax.ShapeDtypeStruct(halo.shape, halo.dtype))
        out_shape.append(jax.ShapeDtypeStruct((8, 128), F32))
        scratch = []
        for number, _, rows, quarter, *_ in pieces:
            one = grads[number]
            scratch += piece_buffers(rows, one.shape[2], quarter, one.dtype)
        sems = RS_SEMS * count + 7
        return pl.pallas_call(
            functools.partial(reduce_kernel, pieces),
            out_shape=out_shape,
            in_specs=[HBM] * (len(grads) + 1),
            out_specs=[VMEM] * len(sizes) + [HBM, VMEM],
            scratch_shapes=scratch
            + [
                pltpu.VMEM(tokens, BF16),
                pltpu.VMEM(tokens, BF16),
                pltpu.VMEM(tokens, BF16),
                pltpu.VMEM((9, 8, 128), F32),
                pltpu.SemaphoreType.DMA((sems,)),
                pltpu.SemaphoreType.DMA((sems,)),
                pltpu.SemaphoreType.DMA((count + 3,)),
            ],
            compiler_params=pltpu.CompilerParams(
                collective_id=1, has_side_effects=True, vmem_limit_bytes=60 << 20
            ),
            name="reduce_all",
        )(*[one.reshape(4, 2, 2, *one.shape[1:]) for one in grads], halo)
    whole = [
        lax.psum(
            lax.psum_scatter(one.astype(F32), "wide", scatter_dimension=0, tiled=False), "dp"
        )
        for one in grads
    ]
    totals = []
    for result in range(1 + max(piece[5] for piece in pieces)):
        columns = {piece[6]: whole[piece[0]] for piece in pieces if piece[5] == result}
        totals.append(jnp.concatenate([columns[key] for key in sorted(columns)], axis=1))
    back = jnp.stack([from_behind(halo[0], "wide", -2), from_behind(halo[1], "wide", -1)])
    squares = jnp.float32(0.0)
    for number, first, _, _, limit, *_ in pieces:
        part = whole[number][first : first + limit]
        squares = squares + jnp.sum(part * part)
    norm = jnp.zeros((8, 128), F32).at[0, 0].set(lax.psum(squares, "wide"))
    return [*totals, back, norm]


def dot(a, b, left=1, right=0):
    return lax.dot_general(
        a, b, (((left,), (right,)), ((), ())), preferred_element_type=F32
    )


Q_TILE = 256


def split_pair(pair, size):
    lane = lax.broadcasted_iota(jnp.int32, pair.shape, 1)
    zero = jnp.zeros_like(pair)
    return jnp.where(lane < size, pair, zero), jnp.where(lane < size, zero, pair)


def fill_mask(starts, bias, tokens, span, keys_before):
    for tile in range(tokens // Q_TILE):
        query = lax.broadcasted_iota(jnp.int32, (span, Q_TILE), 1) + tile * Q_TILE + keys_before
        key = lax.broadcasted_iota(jnp.int32, (span, Q_TILE), 0) + tile * Q_TILE
        first = starts[:, tile * Q_TILE : (tile + 1) * Q_TILE]
        seen = jnp.logical_and(key <= query, key >= first)
        bias[tile] = jnp.where(seen, 0.0, masked_score)


def attend_kernel(size, starts, scale_ref, q_ref, k_ref, v_ref, o_ref, c_ref, lse_ref, bias, vt, ot):
    tokens, window = q_ref.shape[0], k_ref.shape[0]
    before = window - tokens
    span = before + Q_TILE

    @pl.when(pl.program_id(0) == 0)
    def _():
        fill_mask(starts, bias, tokens, span, before)

    vt[...] = v_ref[...].T
    for tile in range(tokens // Q_TILE):
        rows = slice(tile * Q_TILE, (tile + 1) * Q_TILE)
        keys = slice(tile * Q_TILE, tile * Q_TILE + span)
        k_pair = k_ref[keys, :]
        for head, q_one in enumerate(split_pair(q_ref[rows, :], size)):
            scores = dot(k_pair, q_one, 1, 1) + bias[tile]
            highest = jnp.max(scores, axis=0, keepdims=True)
            powers = jnp.exp(scores - highest)
            total = jnp.sum(powers, axis=0, keepdims=True)
            probs = (powers * (1.0 / total)).astype(BF16)
            lse_ref[0, head : head + 1, rows] = highest + jnp.log(total)
            part = slice(head * size, (head + 1) * size)
            ot[part, rows] = dot(vt[part, keys], probs)
    attended = ot[...].T
    o_ref[...] = attended
    c_ref[...] = (attended * scale_ref[...]).astype(BF16)


def attend(queries, keys, values, starts, scales, heads):
    tokens, width = queries.shape
    window = keys.shape[0]
    pairs = heads // 2
    lanes = width // pairs
    span = window - tokens + Q_TILE
    by_rows = lambda rows: pl.BlockSpec((rows, lanes), lambda p: (0, p))
    return pl.pallas_call(
        functools.partial(attend_kernel, width // heads),
        grid=(pairs,),
        in_specs=[
            pl.BlockSpec((1, tokens), lambda p: (0, 0)),
            by_rows(1),
            by_rows(tokens),
            by_rows(window),
            by_rows(window),
        ],
        out_specs=[
            by_rows(tokens),
            by_rows(tokens),
            pl.BlockSpec((1, 2, tokens), lambda p: (p, 0, 0)),
        ],
        out_shape=[
            jax.ShapeDtypeStruct((tokens, width), F32),
            jax.ShapeDtypeStruct((tokens, width), BF16),
            jax.ShapeDtypeStruct((pairs, 2, tokens), F32),
        ],
        scratch_shapes=[
            pltpu.VMEM((tokens // Q_TILE, span, Q_TILE), F32),
            pltpu.VMEM((lanes, window), BF16),
            pltpu.VMEM((lanes, tokens), F32),
        ],
        compiler_params=pltpu.CompilerParams(vmem_limit_bytes=40 << 20),
        name="attend",
    )(starts, scales, queries, keys, values)


def attend_back_kernel(
    size, starts, q_ref, k_ref, v_ref, do_ref, lse_ref, delta_ref,
    dq_ref, dk_ref, dv_ref, bias, dk_sum, dv_sum, kt, dqt,
):
    tokens, window = q_ref.shape[0], k_ref.shape[0]
    before = window - tokens
    span = before + Q_TILE

    @pl.when(pl.program_id(0) == 0)
    def _():
        fill_mask(starts, bias, tokens, span, before)

    kt[...] = k_ref[...].T
    dk_sum[...] = jnp.zeros_like(dk_sum)
    dv_sum[...] = jnp.zeros_like(dv_sum)
    for tile in range(tokens // Q_TILE):
        rows = slice(tile * Q_TILE, (tile + 1) * Q_TILE)
        keys = slice(tile * Q_TILE, tile * Q_TILE + span)
        k_pair, v_pair = k_ref[keys, :], v_ref[keys, :]
        for head, (q_one, do_one) in enumerate(
            zip(split_pair(q_ref[rows, :], size), split_pair(do_ref[rows, :], size))
        ):
            scores = dot(k_pair, q_one, 1, 1) + bias[tile]
            probs = jnp.exp(scores - lse_ref[0, head : head + 1, rows])
            grads = dot(v_pair, do_one, 1, 1) - delta_ref[0, head : head + 1, rows]
            low = (probs * grads).astype(BF16)
            dv_sum[keys, :] += dot(probs.astype(BF16), do_one)
            dk_sum[keys, :] += dot(low, q_one)
            part = slice(head * size, (head + 1) * size)
            dqt[part, rows] = dot(kt[part, keys], low)
    dq_ref[...] = (dqt[...].T * size ** (-0.5)).astype(BF16)
    dk_ref[...] = dk_sum[...].astype(BF16)
    dv_ref[...] = dv_sum[...].astype(BF16)


def attend_back(queries, keys, values, outs_grad, lse, delta, starts, heads):
    tokens, width = queries.shape
    window = keys.shape[0]
    pairs = heads // 2
    lanes = width // pairs
    span = window - tokens + Q_TILE
    by_rows = lambda rows: pl.BlockSpec((rows, lanes), lambda p: (0, p))
    stats = pl.BlockSpec((1, 2, tokens), lambda p: (p, 0, 0))
    return pl.pallas_call(
        functools.partial(attend_back_kernel, width // heads),
        grid=(pairs,),
        in_specs=[
            pl.BlockSpec((1, tokens), lambda p: (0, 0)),
            by_rows(tokens),
            by_rows(window),
            by_rows(window),
            by_rows(tokens),
            stats,
            stats,
        ],
        out_specs=[
            by_rows(tokens),
            by_rows(window),
            by_rows(window),
        ],
        out_shape=[
            jax.ShapeDtypeStruct((tokens, width), BF16),
            jax.ShapeDtypeStruct((window, width), BF16),
            jax.ShapeDtypeStruct((window, width), BF16),
        ],
        scratch_shapes=[
            pltpu.VMEM((tokens // Q_TILE, span, Q_TILE), F32),
            pltpu.VMEM((window, lanes), F32),
            pltpu.VMEM((window, lanes), F32),
            pltpu.VMEM((lanes, window), BF16),
            pltpu.VMEM((lanes, tokens), F32),
        ],
        compiler_params=pltpu.CompilerParams(vmem_limit_bytes=40 << 20),
        name="attend_back",
    )(starts, queries, keys, values, outs_grad, lse, delta)


def plane_share(rows):
    return rows // 16 * 3 // 8 * 16


def pack(parts):
    flat = jnp.concatenate(parts, axis=1)
    size = -(-flat.shape[1] // 2048) * 2048
    return jnp.pad(flat, ((0, 0), (0, size - flat.shape[1]))).reshape(flat.shape[0], -1, 128)


def to_slabs(rows, wide):
    count, columns = rows.shape
    return rows.reshape(count, wide, -1).transpose(1, 0, 2).reshape(wide, -1)


def unpack(slabs, count):
    return slabs.reshape(slabs.shape[0], count, -1).transpose(1, 0, 2).reshape(count, -1)


def body(
    inputs,
    out_grad,
    doc_lengths,
    step_count,
    qkv_weight,
    qkv_first,
    qkv_second,
    out_weight,
    out_first,
    out_second,
    fc1_weight,
    fc1_first,
    fc1_second,
    fc2_weight,
    fc2_first,
    fc2_second,
    model_vectors,
    vectors_first,
    vectors_second,
    hidden_vectors,
    hidden_first,
    hidden_second,
    head_scale,
    head_first,
    head_second,
):
    tokens_dev = inputs.shape[0]
    width = inputs.shape[1]
    heads_count = head_scale.shape[0]
    head_size = width // heads_count
    wide = lax.axis_size("wide")
    score_scale = head_size ** (-0.5)
    hidden_width = hidden_vectors.shape[1] * wide
    vector_rows, hidden_rows = model_vectors.shape[0], hidden_vectors.shape[0]
    vector_size, hidden_size = model_vectors.size, hidden_vectors.size

    fc1_rows, fc2_rows = fc1_weight.shape[0], fc2_weight.shape[0]
    qkv_rows, out_rows = qkv_weight.shape[0], out_weight.shape[0]
    small = pack(
        [model_vectors.astype(BF16).reshape(1, -1), hidden_vectors.astype(BF16).reshape(1, -1)]
    )[0]
    small_full, qkv_full, out_full, fc1_full, fc2_full, halo = gather_all(
        [
            small,
            qkv_weight.astype(BF16),
            out_weight.astype(BF16),
            fc1_weight.astype(BF16),
            fc2_weight.astype(BF16),
        ],
        tuple(plane_share(one) for one in (0, qkv_rows, out_rows, fc1_rows, fc2_rows)),
        inputs,
    )
    flat = small_full.reshape(wide, -1)
    vectors = unpack(flat[:, :vector_size], vector_rows).astype(F32)
    hidden_par = unpack(flat[:, vector_size : vector_size + hidden_size], hidden_rows).astype(F32)
    qkv_full = qkv_full.reshape(width, 3 * width)
    out_full = out_full.reshape(width, width)
    fc2_full = fc2_full.reshape(hidden_width, width)
    heads_low = lax.optimization_barrier(head_scale.astype(BF16)).astype(F32)

    tokens_in = inputs.astype(F32)
    tokens_all = jnp.concatenate([halo.reshape(-1, width), inputs], axis=0)
    normed_in, hat_in, scale_in = layer_norm(tokens_all.astype(F32), vectors[0], vectors[3])
    normed_low = normed_in.astype(BF16)
    own = slice(2 * tokens_dev, None)
    queries = (
        jnp.dot(normed_low[own], qkv_full[:, :width], preferred_element_type=F32) + vectors[4]
    ).astype(BF16) * jnp.asarray(score_scale, BF16)
    projected = jnp.dot(normed_low, qkv_full[:, width:], preferred_element_type=F32)
    keys_all = projected[:, :width].astype(BF16)
    values_all = (projected[:, width:] + vectors[5]).astype(BF16)
    starts = doc_starts(
        doc_lengths, lax.axis_index("dp"), lax.axis_index("wide") * tokens_dev, tokens_dev
    )
    starts = jnp.maximum(starts - (lax.axis_index("wide") - 2) * tokens_dev, 0).reshape(1, -1)
    scales = jnp.repeat(heads_low, head_size).reshape(1, width)
    attended, mixed_low, log_totals = attend(
        queries, keys_all, values_all, starts, scales, heads_count
    )
    proj_out = jnp.dot(mixed_low, out_full, preferred_element_type=F32) + vectors[6]
    normed_post, hat_post, scale_post = layer_norm(proj_out, vectors[1], vectors[7])
    residual = tokens_in + normed_post
    normed_two, hat_two, scale_two = layer_norm(residual, vectors[2], vectors[8])
    rows_low = normed_two.astype(BF16)
    grad_in = out_grad.astype(F32)

    pre_act = (
        jnp.einsum("td,wdf->twf", rows_low, fc1_full, preferred_element_type=F32).reshape(
            tokens_dev, hidden_width
        )
        + hidden_par[2]
    )
    activated, gelu_back = jax.vjp(exact_gelu, pre_act)
    first_mean = jnp.mean(activated, axis=-1, keepdims=True)
    second_mean = jnp.mean(activated * activated, axis=-1, keepdims=True)
    middle, hat_mid, scale_mid = middle_forward(
        activated, first_mean, second_mean, hidden_par[0], hidden_par[1]
    )
    middle_low = middle.astype(BF16)
    ffn_out = jnp.dot(middle_low, fc2_full, preferred_element_type=F32)
    output = (residual + (ffn_out + vectors[9])).astype(BF16)
    fc2_grad = jnp.einsum("tf,td->fd", middle_low, out_grad, preferred_element_type=F32)
    middle_grad = jnp.einsum("td,fd->tf", out_grad, fc2_full, preferred_element_type=F32)
    mid_gain_grad = jnp.sum(middle_grad * hat_mid, axis=0)
    mid_bias_grad = jnp.sum(middle_grad, axis=0)
    scaled_mid = middle_grad * hidden_par[0]
    plain_mean = jnp.mean(scaled_mid, axis=-1, keepdims=True)
    cross_mean = jnp.mean(scaled_mid * hat_mid, axis=-1, keepdims=True)
    act_grad = scale_mid * (scaled_mid - plain_mean - hat_mid * cross_mean)
    pre_low = gelu_back(act_grad)[0].astype(BF16)
    fc1_bias_grad = jnp.sum(pre_low.astype(F32), axis=0)
    pre_split = pre_low.reshape(tokens_dev, wide, -1)
    fc1_grad = jnp.einsum("td,twf->wdf", rows_low, pre_split, preferred_element_type=F32)
    rows_grad = jnp.einsum("twf,wdf->td", pre_split, fc1_full, preferred_element_type=F32)
    hidden_grad = jnp.stack([mid_gain_grad, mid_bias_grad, fc1_bias_grad])
    out_bias_total = jnp.sum(grad_in, axis=0)
    residual_grad = grad_in + norm_back(rows_grad, hat_two, scale_two, vectors[2])
    gain_two_grad = jnp.sum(rows_grad * hat_two, axis=0)
    bias_two_grad = jnp.sum(rows_grad, axis=0)
    gain_post_grad = jnp.sum(residual_grad * hat_post, axis=0)
    bias_post_grad = jnp.sum(residual_grad, axis=0)
    proj_low = norm_back(residual_grad, hat_post, scale_post, vectors[1]).astype(BF16)
    proj_bias_grad = jnp.sum(proj_low.astype(F32), axis=0)
    out_weight_grad = jnp.einsum("td,te->de", mixed_low, proj_low, preferred_element_type=F32)
    mixed_grad = jnp.einsum("te,de->td", proj_low, out_full, preferred_element_type=F32)
    head_grad = jnp.sum((mixed_grad * attended).reshape(tokens_dev, heads_count, -1), axis=(0, 2))
    attended_low = (mixed_grad * scales).astype(BF16)
    delta = (
        jnp.sum((attended_low.astype(F32) * attended).reshape(tokens_dev, heads_count, -1), axis=-1)
        .transpose(1, 0)
        .reshape(heads_count // 2, 2, tokens_dev)
    )
    query_grad, key_grad, value_grad = attend_back(
        queries, keys_all, values_all, attended_low, log_totals, delta, starts, heads_count
    )
    query_bias_grad = jnp.sum(query_grad.astype(F32), axis=0)
    value_bias_grad = jnp.sum(value_grad.astype(F32), axis=0)
    query_part = jnp.einsum("td,te->de", normed_low[own], query_grad, preferred_element_type=F32)
    key_part = jnp.einsum("td,te->de", normed_low, key_grad, preferred_element_type=F32)
    value_part = jnp.einsum("td,te->de", normed_low, value_grad, preferred_element_type=F32)
    normed_grad = jnp.einsum(
        "te,de->td", key_grad, qkv_full[:, width : 2 * width], preferred_element_type=F32
    ) + jnp.einsum("te,de->td", value_grad, qkv_full[:, 2 * width :], preferred_element_type=F32)
    halo_grad = normed_grad[: 2 * tokens_dev]
    own_grad = normed_grad[own] + jnp.einsum(
        "te,de->td", query_grad, qkv_full[:, :width], preferred_element_type=F32
    )
    gain_in_grad = jnp.sum(halo_grad * hat_in[: 2 * tokens_dev], axis=0) + jnp.sum(
        own_grad * hat_in[own], axis=0
    )
    bias_in_grad = jnp.sum(halo_grad, axis=0) + jnp.sum(own_grad, axis=0)
    vector_grad = jnp.stack(
        [
            gain_in_grad,
            gain_post_grad,
            gain_two_grad,
            bias_in_grad,
            query_bias_grad,
            value_bias_grad,
            proj_bias_grad,
            bias_post_grad,
            bias_two_grad,
            out_bias_total,
        ]
    )
    small_grad = pack(
        [
            to_slabs(vector_grad, wide),
            to_slabs(hidden_grad, wide),
            jnp.broadcast_to(head_grad[None], (wide, heads_count)),
        ]
    )
    counted = (vector_size + hidden_size) // 128
    small_part, qkv_part, out_part, fc1_part, fc2_part, halo_back, norm_tile = reduce_all(
        [
            small_grad,
            query_part.astype(BF16).reshape(wide, -1, width),
            key_part.astype(BF16).reshape(wide, -1, width),
            value_part.astype(BF16).reshape(wide, -1, width),
            out_weight_grad.astype(BF16).reshape(wide, -1, width),
            fc1_grad.astype(BF16),
            fc2_grad.astype(BF16).reshape(wide, -1, width),
        ],
        halo_grad.astype(BF16).reshape(2, tokens_dev, width),
        tuple(
            (6, k * (fc2_rows // 4), fc2_rows // 4, fc2_rows // 16, fc2_rows // 4, 4, 0)
            for k in range(4)
        )
        + tuple(
            (5, k * (fc1_rows // 4), fc1_rows // 4, plane_share(fc1_rows // 4), fc1_rows // 4, 3, 0)
            for k in range(4)
        )
        + (
            (4, 0, out_rows, out_rows // 4, out_rows, 2, 0),
            (0, 0, small_grad.shape[1], 0, counted, 0, 0),
            (1, 0, qkv_rows, qkv_rows // 4, qkv_rows, 1, 0),
            (2, 0, qkv_rows, qkv_rows // 4, qkv_rows, 1, width),
            (3, 0, qkv_rows, qkv_rows // 4, qkv_rows, 1, 2 * width),
        ),
    )
    total_grad = own_grad + halo_back[0].astype(F32) + halo_back[1].astype(F32)
    input_grad = residual_grad + norm_back(total_grad, hat_in[own], scale_in[own], vectors[0])
    flat = small_part.reshape(-1)
    vector_part = flat[:vector_size].reshape(model_vectors.shape)
    hidden_part = flat[vector_size : vector_size + hidden_size].reshape(hidden_vectors.shape)
    head_total = flat[vector_size + hidden_size :][:heads_count]
    grad_norm = jnp.sqrt(jnp.sum(norm_tile) + jnp.sum(head_total * head_total))
    factor = jnp.minimum(1.0, clip_limit / (grad_norm + 1e-06))
    step = step_count[0].astype(F32)
    grads = (qkv_part, out_part, fc1_part, fc2_part, vector_part, hidden_part, head_total)
    params = (
        qkv_weight,
        out_weight,
        fc1_weight,
        fc2_weight,
        model_vectors,
        hidden_vectors,
        head_scale,
    )
    firsts = (qkv_first, out_first, fc1_first, fc2_first, vectors_first, hidden_first, head_first)
    seconds = (
        qkv_second,
        out_second,
        fc1_second,
        fc2_second,
        vectors_second,
        hidden_second,
        head_second,
    )
    rates = (
        matrix_rate,
        matrix_rate,
        matrix_rate,
        matrix_rate,
        vector_rate,
        vector_rate,
        vector_rate,
    )
    decays = (weight_decay, weight_decay, weight_decay, weight_decay, 0.0, 0.0, 0.0)
    updated = []
    for number in range(7):
        updated.extend(
            adam_step(
                grads[number] * factor,
                params[number],
                firsts[number],
                seconds[number],
                step,
                rates[number],
                decays[number],
            )
        )
    return (
        output,
        input_grad,
        grad_norm.reshape(1),
        updated[0],
        updated[1],
        updated[2],
        updated[3],
        updated[4],
        updated[5],
        updated[6],
        updated[7],
        updated[8],
        updated[9],
        updated[10],
        updated[11],
        updated[12],
        updated[13],
        updated[14],
        updated[15],
        updated[16],
        updated[17],
        updated[18],
        updated[19],
        updated[20],
    )


def solution(mesh):
    placed = (
        P(("dp", "wide"), None),
        P(("dp", "wide"), None),
        P(),
        P(),
        P("wide", None),
        P("wide", None),
        P("wide", None),
        P("wide", None),
        P("wide", None),
        P("wide", None),
        P(None, "wide"),
        P(None, "wide"),
        P(None, "wide"),
        P("wide", None),
        P("wide", None),
        P("wide", None),
        P(None, "wide"),
        P(None, "wide"),
        P(None, "wide"),
        P(None, "wide"),
        P(None, "wide"),
        P(None, "wide"),
        P(),
        P(),
        P(),
    )
    return jax.shard_map(
        body,
        mesh=mesh,
        in_specs=placed,
        out_specs=(
            P(("dp", "wide"), None),
            P(("dp", "wide"), None),
            P(),
            P("wide", None),
            P("wide", None),
            P("wide", None),
            P("wide", None),
            P("wide", None),
            P("wide", None),
            P(None, "wide"),
            P(None, "wide"),
            P(None, "wide"),
            P("wide", None),
            P("wide", None),
            P("wide", None),
            P(None, "wide"),
            P(None, "wide"),
            P(None, "wide"),
            P(None, "wide"),
            P(None, "wide"),
            P(None, "wide"),
            P(),
            P(),
            P(),
        ),
        check_vma=False,
    )
```

```python
import functools

import jax
import jax.numpy as jnp
from jax import lax
from jax.experimental import pallas as pl
from jax.experimental.pallas import tpu as pltpu
from jax.sharding import PartitionSpec as P

DOC_MOST = 1024
MESH = pl.DeviceIdType.MESH
HBM = pl.BlockSpec(memory_space=pltpu.HBM)
VMEM = pl.BlockSpec(memory_space=pltpu.VMEM)
BF16 = jnp.bfloat16
F32 = jnp.float32

norm_epsilon = 1e-05
clip_limit = 1.0
first_decay = 0.9
second_decay = 0.98
adam_epsilon = 1e-08
matrix_rate = 0.1
vector_rate = 0.4
weight_decay = 0.1
masked_score = -1e30


def layer_norm(values_in, gain, shift):
    center = values_in - jnp.mean(values_in, axis=-1, keepdims=True)
    variance = jnp.mean(center * center, axis=-1, keepdims=True)
    scale = lax.rsqrt(variance + norm_epsilon)
    normed = center * scale
    return (normed * gain + shift, normed, scale)


def norm_back(grad, normed, scale, gain):
    scaled = grad * gain
    mean_plain = jnp.mean(scaled, axis=-1, keepdims=True)
    mean_cross = jnp.mean(scaled * normed, axis=-1, keepdims=True)
    return scale * (scaled - mean_plain - normed * mean_cross)


def doc_starts(doc_lengths, row, first, count):
    ends = lax.dynamic_slice_in_dim(jnp.cumsum(doc_lengths, axis=1), row, 1, 0)[0]
    places = first + jnp.arange(count, dtype=jnp.int32)
    return jnp.max(jnp.where(ends[None, :] <= places[:, None], ends[None, :], 0), axis=1)


def adam_step(grad, weight, first, second, step, rate, decay):
    first_new = first_decay * first + (1.0 - first_decay) * grad
    second_new = second_decay * second + (1.0 - second_decay) * grad * grad
    fix_one = 1.0 - jnp.power(jnp.float32(first_decay), step)
    fix_two = 1.0 - jnp.power(jnp.float32(second_decay), step)
    direction = first_new / fix_one / (jnp.sqrt(second_new / fix_two) + adam_epsilon)
    weight_new = weight - rate * (direction + decay * weight)
    return (first_new, second_new, weight_new)


def from_behind(shard, axis, by):
    count = lax.axis_size(axis)
    pairs = [(i, i + by) for i in range(count) if 0 <= i + by < count]
    return lax.ppermute(shard, axis, pairs)


def dot(a, b, left=1, right=0):
    return lax.dot_general(
        a, b, (((left,), (right,)), ((), ())), preferred_element_type=F32
    )


Q_TILE = 256


def split_pair(pair, size):
    lane = lax.broadcasted_iota(jnp.int32, pair.shape, 1)
    zero = jnp.zeros_like(pair)
    return jnp.where(lane < size, pair, zero), jnp.where(lane < size, zero, pair)


def fill_mask(starts, bias, tokens, span, keys_before):
    for tile in range(tokens // Q_TILE):
        query = lax.broadcasted_iota(jnp.int32, (span, Q_TILE), 1) + tile * Q_TILE + keys_before
        key = lax.broadcasted_iota(jnp.int32, (span, Q_TILE), 0) + tile * Q_TILE
        first = starts[:, tile * Q_TILE : (tile + 1) * Q_TILE]
        seen = jnp.logical_and(key <= query, key >= first)
        bias[tile] = jnp.where(seen, 0.0, masked_score)


def attend_pair(size, q_ref, k_ref, v_ref, scale_ref, o_ref, c_ref, lse_ref, bias, vt, ot):
    tokens, window = q_ref.shape[0], k_ref.shape[0]
    span = window - tokens + Q_TILE
    vt[...] = v_ref[...].T
    for tile in range(tokens // Q_TILE):
        rows = slice(tile * Q_TILE, (tile + 1) * Q_TILE)
        keys = slice(tile * Q_TILE, tile * Q_TILE + span)
        k_pair = k_ref[keys, :]
        for head, q_one in enumerate(split_pair(q_ref[rows, :], size)):
            scores = dot(k_pair, q_one, 1, 1) + bias[tile]
            highest = jnp.max(scores, axis=0, keepdims=True)
            powers = jnp.exp(scores - highest)
            total = jnp.sum(powers, axis=0, keepdims=True)
            probs = (powers * (1.0 / total)).astype(BF16)
            lse_ref[head : head + 1, rows] = highest + jnp.log(total)
            part = slice(head * size, (head + 1) * size)
            ot[part, rows] = dot(vt[part, keys], probs)
    attended = ot[...].T
    o_ref[...] = attended
    c_ref[...] = (attended * scale_ref[...]).astype(BF16)


def attend_kernel(size, starts, scale_ref, q_ref, k_ref, v_ref, o_ref, c_ref, lse_ref, bias, vt, ot):
    tokens, window = q_ref.shape[0], k_ref.shape[0]
    before = window - tokens

    @pl.when(pl.program_id(0) == 0)
    def _():
        fill_mask(starts, bias, tokens, before + Q_TILE, before)

    attend_pair(size, q_ref, k_ref, v_ref, scale_ref, o_ref, c_ref, lse_ref.at[0], bias, vt, ot)


def attend(queries, keys, values, starts, scales, heads):
    tokens, width = queries.shape
    window = keys.shape[0]
    pairs = heads // 2
    lanes = width // pairs
    span = window - tokens + Q_TILE
    by_rows = lambda rows: pl.BlockSpec((rows, lanes), lambda p: (0, p))
    return pl.pallas_call(
        functools.partial(attend_kernel, width // heads),
        grid=(pairs,),
        in_specs=[
            pl.BlockSpec((1, tokens), lambda p: (0, 0)),
            by_rows(1),
            by_rows(tokens),
            by_rows(window),
            by_rows(window),
        ],
        out_specs=[
            by_rows(tokens),
            by_rows(tokens),
            pl.BlockSpec((1, 2, tokens), lambda p: (p, 0, 0)),
        ],
        out_shape=[
            jax.ShapeDtypeStruct((tokens, width), F32),
            jax.ShapeDtypeStruct((tokens, width), BF16),
            jax.ShapeDtypeStruct((pairs, 2, tokens), F32),
        ],
        scratch_shapes=[
            pltpu.VMEM((tokens // Q_TILE, span, Q_TILE), F32),
            pltpu.VMEM((lanes, window), BF16),
            pltpu.VMEM((lanes, tokens), F32),
        ],
        compiler_params=pltpu.CompilerParams(vmem_limit_bytes=40 << 20),
        name="attend",
    )(starts, scales, queries, keys, values)


def attend_back_kernel(
    size, starts, q_ref, k_ref, v_ref, do_ref, lse_ref, delta_ref,
    dq_ref, dk_ref, dv_ref, bias, dk_sum, dv_sum, kt, dqt,
):
    tokens, window = q_ref.shape[0], k_ref.shape[0]
    before = window - tokens
    span = before + Q_TILE

    @pl.when(pl.program_id(0) == 0)
    def _():
        fill_mask(starts, bias, tokens, span, before)

    kt[...] = k_ref[...].T
    dk_sum[...] = jnp.zeros_like(dk_sum)
    dv_sum[...] = jnp.zeros_like(dv_sum)
    for tile in range(tokens // Q_TILE):
        rows = slice(tile * Q_TILE, (tile + 1) * Q_TILE)
        keys = slice(tile * Q_TILE, tile * Q_TILE + span)
        k_pair, v_pair = k_ref[keys, :], v_ref[keys, :]
        for head, (q_one, do_one) in enumerate(
            zip(split_pair(q_ref[rows, :], size), split_pair(do_ref[rows, :], size))
        ):
            scores = dot(k_pair, q_one, 1, 1) + bias[tile]
            probs = jnp.exp(scores - lse_ref[0, head : head + 1, rows])
            grads = dot(v_pair, do_one, 1, 1) - delta_ref[0, head : head + 1, rows]
            low = (probs * grads).astype(BF16)
            dv_sum[keys, :] += dot(probs.astype(BF16), do_one)
            dk_sum[keys, :] += dot(low, q_one)
            part = slice(head * size, (head + 1) * size)
            dqt[part, rows] = dot(kt[part, keys], low)
    dq_ref[...] = (dqt[...].T * size ** (-0.5)).astype(BF16)
    dk_ref[...] = dk_sum[...].astype(BF16)
    dv_ref[...] = dv_sum[...].astype(BF16)


def attend_back(queries, keys, values, outs_grad, lse, delta, starts, heads):
    tokens, width = queries.shape
    window = keys.shape[0]
    pairs = heads // 2
    lanes = width // pairs
    span = window - tokens + Q_TILE
    by_rows = lambda rows: pl.BlockSpec((rows, lanes), lambda p: (0, p))
    stats = pl.BlockSpec((1, 2, tokens), lambda p: (p, 0, 0))
    return pl.pallas_call(
        functools.partial(attend_back_kernel, width // heads),
        grid=(pairs,),
        in_specs=[
            pl.BlockSpec((1, tokens), lambda p: (0, 0)),
            by_rows(tokens),
            by_rows(window),
            by_rows(window),
            by_rows(tokens),
            stats,
            stats,
        ],
        out_specs=[
            by_rows(tokens),
            by_rows(window),
            by_rows(window),
        ],
        out_shape=[
            jax.ShapeDtypeStruct((tokens, width), BF16),
            jax.ShapeDtypeStruct((window, width), BF16),
            jax.ShapeDtypeStruct((window, width), BF16),
        ],
        scratch_shapes=[
            pltpu.VMEM((tokens // Q_TILE, span, Q_TILE), F32),
            pltpu.VMEM((window, lanes), F32),
            pltpu.VMEM((window, lanes), F32),
            pltpu.VMEM((lanes, window), BF16),
            pltpu.VMEM((lanes, tokens), F32),
        ],
        compiler_params=pltpu.CompilerParams(vmem_limit_bytes=40 << 20),
        name="attend_back",
    )(starts, queries, keys, values, outs_grad, lse, delta)


class Place:
    def __init__(self):
        self.y = lax.axis_index("dp")
        self.w = lax.axis_index("wide")
        self.z = self.w // 4
        self.x = (self.w // 2) % 2
        self.c = self.w % 2

    def slab(self, z, x, c):
        return z * 4 + x * 2 + c

    def wide(self, w):
        return (self.y, w)

    def core_mate(self):
        return self.wide(self.slab(self.z, self.x, 1 - self.c))

    def x_mate(self):
        return self.wide(self.slab(self.z, 1 - self.x, self.c))

    def y_mate(self):
        return (1 - self.y, self.w)

    def up(self):
        return self.wide(lax.rem(self.w + 4, 16))

    def down(self):
        return self.wide(lax.rem(self.w + 12, 16))


def greet(me, extra=()):
    barrier = pltpu.get_barrier_semaphore()

    def hello(target):
        pl.semaphore_signal(barrier, inc=1, device_id=target, device_id_type=MESH)

    always = [me.core_mate(), me.x_mate(), me.y_mate(), *extra]
    sometimes = [
        (me.z < 3, me.up()),
        (me.z > 0, me.down()),
        (me.w < 14, me.wide(lax.rem(me.w + 2, 16))),
        (me.w >= 2, me.wide(lax.rem(me.w + 14, 16))),
    ]
    for target in always:
        hello(target)
    for holds, target in sometimes:
        pl.when(holds)(functools.partial(hello, target))
    count = len(always) + sum(holds.astype(jnp.int32) for holds, _ in sometimes)
    pl.semaphore_wait(barrier, count)


class Wire:
    def __init__(self, send, recv):
        self.send, self.recv = send, recv
        self.planned = []

    def copy(self, source, target, index, device):
        return pltpu.make_async_remote_copy(
            src_ref=source,
            dst_ref=target,
            send_sem=self.send.at[index],
            recv_sem=self.recv.at[index],
            device_id=device,
            device_id_type=MESH,
        )

    def put(self, source, target, index, device, holds=None):
        moved = self.copy(source, target, index, device)
        self.planned.append((holds, moved))
        return lambda: when(holds, moved.start)

    def got(self, target, index, device, holds=None):
        moved = self.copy(target, target, index, device)
        return lambda: when(holds, moved.wait_recv)

    def finish(self):
        for holds, moved in self.planned:
            when(holds, moved.wait_send)


def act(actions):
    for one in actions:
        one()


def both(*conditions):
    held = [one for one in conditions if one is not None]
    total = held[0] if held else None
    for one in held[1:]:
        total = jnp.logical_and(total, one)
    return total


def when(holds, action):
    if holds is None:
        action()
    else:
        pl.when(holds)(action)


def gather_ticks(me, wire, base, own, full, third):
    rows = own.shape[0]
    plane = (
        pl.ds(pl.multiple_of(me.y * third, 16), rows - third) if third else pl.ds(0, rows)
    )
    share = pl.ds(pl.multiple_of(me.y * (rows - third), 16), third) if third else None
    other = pl.ds(pl.multiple_of((1 - me.y) * (rows - third), 16), third) if third else None
    my_slab = me.slab(me.z, me.x, me.c)
    ups, downs, xs, ys, cs, ts = (base + k for k in (0, 4, 8, 12, 20, 28))
    mine = me.z * 2 + me.x

    def pass_on(z, x, holds):
        slab = me.slab(z, x, me.c)
        place = z * 2 + x
        block = full.at[slab, plane]
        actions = []
        if third:
            piece = full.at[slab, share]
            actions.append(wire.put(piece, piece, ys + place, me.y_mate(), holds))
        actions.append(wire.put(block, block, cs + place, me.core_mate(), holds))
        return actions

    goal = full.at[my_slab, plane]
    ticks = [
        [
            wire.put(own.at[plane], goal, ups + me.z, me.up(), me.z < 3),
            wire.put(own.at[plane], goal, downs + me.z, me.down(), me.z > 0),
            wire.put(own.at[plane], goal, xs + me.z, me.x_mate()),
            wire.put(own, full.at[my_slab], cs + mine, me.core_mate()),
        ]
    ]
    for tick in range(1, 5):
        actions = []
        if tick < 4:
            for away, holds, onward, follow, sems in (
                (me.z - tick, me.z - tick >= 0, me.up(), me.z < 3, ups),
                (me.z + tick, me.z + tick <= 3, me.down(), me.z > 0, downs),
            ):
                safe = lax.rem(away + 4, 4)
                block = full.at[me.slab(safe, me.x, me.c), plane]
                actions.append(wire.got(block, sems + safe, onward, holds))
                actions.append(wire.put(block, block, sems + safe, onward, both(holds, follow)))
                actions.append(wire.put(block, block, xs + safe, me.x_mate(), holds))
                actions += pass_on(safe, me.x, holds)
        before = tick - 1
        for away, holds in (
            ((me.z, None),)
            if before == 0
            else (
                (me.z - before, me.z - before >= 0),
                (me.z + before, me.z + before <= 3),
            )
        ):
            safe = lax.rem(away + 4, 4)
            block = full.at[me.slab(safe, 1 - me.x, me.c), plane]
            actions.append(wire.got(block, xs + safe, me.x_mate(), holds))
            actions += pass_on(safe, 1 - me.x, holds)
        ticks.append(actions)
    actions = []
    if third:
        for k in range(1, 8):
            place = lax.rem(mine + k, 8)
            piece = full.at[me.slab(place // 2, place % 2, me.c), other]
            actions.append(wire.got(piece, ys + place, me.y_mate()))
            actions.append(wire.put(piece, piece, ts + place, me.core_mate()))
    ticks.append(actions)
    actions = [wire.got(full.at[me.slab(me.z, me.x, 1 - me.c)], cs + mine, me.core_mate())]
    for k in range(1, 8):
        place = lax.rem(mine + k, 8)
        slab = me.slab(place // 2, place % 2, 1 - me.c)
        actions.append(wire.got(full.at[slab, plane], cs + place, me.core_mate()))
        if third:
            actions.append(wire.got(full.at[slab, other], ts + place, me.core_mate()))
    ticks.append(actions)
    return ticks


AG_SEMS = 36


FRONT_BLOCK = 256


def front_kernel(thirds, head_size, *refs):
    owns, (tokens, starts, scale_ref) = refs[:5], refs[5:8]
    fulls, outs = refs[8:13], refs[13:20]
    xs_out, a_out, q_out, k_out, v_out, o_out, c_out = outs
    lse_ref = refs[20]
    (xs, a_all, qkv, q_all, k_all, v_all, o_all, c_all, vecs, small, bias, vt, ot, send, recv, local) = refs[21:]
    me = Place()
    count = len(owns)
    width = tokens.shape[1]
    rows = tokens.shape[0]
    window = 3 * rows
    before = window - rows
    span = before + Q_TILE
    landings = (small, qkv, *fulls[2:])
    keep = [
        pltpu.make_async_copy(own, full.at[me.w], local.at[k])
        for k, (own, full) in enumerate(zip(owns, landings))
    ] + [pltpu.make_async_copy(tokens, xs.at[2], local.at[count])]
    for one in keep:
        one.start()

    def clear(slot):
        xs[slot] = jnp.zeros((rows, width), BF16)

    pl.when(me.w < 2)(functools.partial(clear, 0))
    pl.when(me.w < 1)(functools.partial(clear, 1))
    wire = Wire(send, recv)
    first, second = AG_SEMS * count, AG_SEMS * count + 1
    ticks = [
        gather_ticks(me, wire, AG_SEMS * k, own, landing, third)
        for k, (own, landing, third) in enumerate(zip(owns, landings, thirds))
    ]
    send_block = wire.put(tokens, xs.at[0], first, me.wide(lax.rem(me.w + 2, 16)), me.w < 14)
    send_near = wire.put(tokens, xs.at[1], second, me.core_mate(), me.c == 0)
    get_block = wire.got(xs.at[0], first, me.core_mate(), me.w >= 2)
    pass_block = wire.put(xs.at[0], xs.at[1], second, me.core_mate(), both(me.c == 1, me.w >= 2))
    get_near = wire.got(xs.at[1], second, me.core_mate(), me.w >= 1)
    greet(me)
    early, late = ticks[:2], ticks[2:]
    act(early[0][0] + early[1][0])
    send_block()
    send_near()
    for tick in range(1, 4):
        act(early[0][tick] + early[1][tick])
    for one in late:
        act(one[0])
    get_block()
    pass_block()
    fill_mask(starts, bias, rows, span, before)
    for tick in range(4, 7):
        act(early[0][tick] + early[1][tick])
    get_near()
    for one in keep:
        one.wait()
    shared = [
        pltpu.make_async_copy(small, fulls[0], local.at[0]),
        pltpu.make_async_copy(qkv, fulls[1], local.at[1]),
        pltpu.make_async_copy(xs, xs_out, local.at[2]),
    ]
    for one in shared:
        one.start()

    lane = lax.broadcasted_iota(jnp.int32, (16, 128), 1)
    for pair in range(8):
        even = small[2 * pair].astype(F32)
        odd = pltpu.roll(small[2 * pair + 1].astype(F32), 64, 1)
        vecs[:, pair * 128 : (pair + 1) * 128] = jnp.where(lane < 64, even, odd)

    def project(first_column, column, a_rows):
        weights = qkv[:, :, pl.ds(first_column + column, FRONT_BLOCK)].reshape(width, FRONT_BLOCK)
        return dot(a_rows, weights)

    per = rows // FRONT_BLOCK

    def normalize(number, carry):
        here = pl.ds(pl.multiple_of(lax.rem(number, per) * FRONT_BLOCK, FRONT_BLOCK), FRONT_BLOCK)
        there = pl.ds(pl.multiple_of(number * FRONT_BLOCK, FRONT_BLOCK), FRONT_BLOCK)
        value, _, _ = layer_norm(xs[number // per, here].astype(F32), vecs[0:1], vecs[3:4])
        low = value.astype(BF16)
        a_all[there] = low
        for column in range(0, width, FRONT_BLOCK):
            columns = slice(column, column + FRONT_BLOCK)
            k_all[there, columns] = project(width, column, low).astype(BF16)
            v_all[there, columns] = (
                project(2 * width, column, low) + vecs[5:6, columns]
            ).astype(BF16)
        return carry

    lax.fori_loop(0, window // FRONT_BLOCK, normalize, 0)
    for number in range(per):
        here = pl.ds(number * FRONT_BLOCK, FRONT_BLOCK)
        low = a_all[before + number * FRONT_BLOCK : before + (number + 1) * FRONT_BLOCK]
        for column in range(0, width, FRONT_BLOCK):
            columns = slice(column, column + FRONT_BLOCK)
            query = (project(0, column, low) + vecs[4:5, columns]).astype(BF16)
            q_all[here, columns] = query * jnp.asarray(head_size ** (-0.5), BF16)
    kept = [
        pltpu.make_async_copy(one, out, local.at[3 + k])
        for k, (one, out) in enumerate(
            ((a_all, a_out), (q_all, q_out), (k_all, k_out), (v_all, v_out))
        )
    ]
    for one in kept:
        one.start()

    def pair_step(pair, carry):
        lanes = pl.ds(pl.multiple_of(pair * 128, 128), 128)
        attend_pair(
            head_size, q_all.at[:, lanes], k_all.at[:, lanes], v_all.at[:, lanes],
            scale_ref.at[:, lanes], o_all.at[:, lanes], c_all.at[:, lanes], lse_ref.at[pair], bias, vt, ot,
        )
        for tick, when_done in ((1, 0), (2, 4)):
            pl.when(pair == when_done)(
                lambda tick=tick: act([action for one in late for action in one[tick]])
            )
        return carry

    lax.fori_loop(0, width // 128, pair_step, 0)
    results = [
        pltpu.make_async_copy(o_all, o_out, local.at[7]),
        pltpu.make_async_copy(c_all, c_out, local.at[8]),
    ]
    for one in results:
        one.start()
    for tick in range(3, 7):
        for one in late:
            act(one[tick])
    wire.finish()
    for one in shared + kept + results:
        one.wait()


def plain_front(shards, tokens, starts, scales, heads):
    width = tokens.shape[1]
    fulls = [lax.all_gather(one, "wide", axis=0, tiled=False) for one in shards]
    each = width // fulls[0].shape[0]
    vectors = fulls[0][:, :10, :each].transpose(1, 0, 2).reshape(10, width).astype(F32)
    window = jnp.stack([from_behind(tokens, "wide", 2), from_behind(tokens, "wide", 1), tokens])
    normed, _, _ = layer_norm(window.reshape(-1, width).astype(F32), vectors[0], vectors[3])
    low = normed.astype(BF16)
    weights = fulls[1].reshape(width, 3 * width)
    queries = dot(low[-tokens.shape[0] :], weights[:, :width]) + vectors[4]
    queries = queries.astype(BF16) * jnp.asarray((width // heads) ** (-0.5), BF16)
    keys = dot(low, weights[:, width : 2 * width]).astype(BF16)
    values = (dot(low, weights[:, 2 * width :]) + vectors[5]).astype(BF16)
    attended = attend(queries, keys, values, starts, scales, heads)
    return [*fulls, window, low, queries, keys, values, *attended]


def front(shards, thirds, tokens, starts, scales, heads):
    rows, width = tokens.shape
    wide = lax.axis_size("wide")
    if lax.axis_size("dp") != 2 or wide != 16:
        return plain_front(shards, tokens, starts, scales, heads)
    window = 3 * rows
    like = jax.ShapeDtypeStruct
    out_shape = [like((wide, *one.shape), one.dtype) for one in shards] + [
        like((3, rows, width), BF16),
        like((window, width), BF16),
        like((rows, width), BF16),
        like((window, width), BF16),
        like((window, width), BF16),
        like((rows, width), F32),
        like((rows, width), BF16),
        like((heads // 2, 2, rows), F32),
    ]
    sems = AG_SEMS * len(shards) + 2
    scratch = [
        ((3, rows, width), BF16),
        ((window, width), BF16),
        ((wide, *shards[1].shape), BF16),
        ((rows, width), BF16),
        ((window, width), BF16),
        ((window, width), BF16),
        ((rows, width), F32),
        ((rows, width), BF16),
        ((16, width), F32),
        ((wide, *shards[0].shape), BF16),
        ((rows // Q_TILE, window - rows + Q_TILE, Q_TILE), F32),
        ((128, window), BF16),
        ((128, rows), F32),
    ]
    return pl.pallas_call(
        functools.partial(front_kernel, thirds, width // heads),
        out_shape=out_shape,
        in_specs=[VMEM] * 8,
        out_specs=[HBM] * 12 + [VMEM],
        scratch_shapes=[pltpu.VMEM(shape, dtype) for shape, dtype in scratch]
        + [
            pltpu.SemaphoreType.DMA((sems,)),
            pltpu.SemaphoreType.DMA((sems,)),
            pltpu.SemaphoreType.DMA((9,)),
        ],
        compiler_params=pltpu.CompilerParams(
            collective_id=0, has_side_effects=True, vmem_limit_bytes=58 << 20
        ),
        name="front",
    )(*shards, tokens, starts, scales)


def row_chunk(rows, columns, most):
    chunk = min(rows, max(16, most // columns // 16 * 16))
    while rows % chunk:
        chunk -= 16
    return chunk


def accumulate(target, source):
    *lead, rows, columns = source.shape
    chunk = row_chunk(rows, columns, 65536)
    per = rows // chunk
    many = per
    for size in lead:
        many *= size

    def step(number, carry):
        part = pl.ds(pl.multiple_of(lax.rem(number, per) * chunk, 16), chunk)
        rest, index = number // per, []
        for size in reversed(lead):
            index.insert(0, lax.rem(rest, size))
            rest = rest // size
        at = (*index, part)
        target[at] = (target[at].astype(F32) + source[at].astype(F32)).astype(target.dtype)
        return carry

    lax.fori_loop(0, many, step, 0)


RS_SEMS = 12


def reduce_ticks(me, wire, base, local, grad, quarter, held, bufs, final, squares, limit):
    from_core, from_y, from_x, from_down, from_up, from_last = bufs
    count, columns = held.shape[-2:]
    inside = count - quarter
    plane = pl.ds(pl.multiple_of(me.y * quarter, 16), inside) if quarter else pl.ds(0, count)
    mine = held.at[:, me.x, plane]
    take = pltpu.make_async_copy(grad.at[:, :, me.c], held, local)
    put_core = wire.put(grad.at[:, :, 1 - me.c], from_core, base, me.core_mate())
    got_core = wire.got(from_core, base, me.core_mate())
    put_x = wire.put(held.at[:, 1 - me.x, plane], from_x, base + 2, me.x_mate())
    got_x = wire.got(from_x, base + 2, me.x_mate())
    put_last = wire.put(mine.at[me.z], from_last, base + 3, me.y_mate())
    got_last = wire.got(from_last, base + 3, me.y_mate())
    if quarter:
        share = held.at[:, :, pl.ds(pl.multiple_of(me.y * inside, 16), quarter)]
        other = held.at[:, :, pl.ds(pl.multiple_of((1 - me.y) * inside, 16), quarter)]
        put_y = wire.put(other, from_y, base + 1, me.y_mate())
        got_y = wire.got(from_y, base + 1, me.y_mate())

    def start():
        take.start()
        put_core()

    def join_core():
        take.wait()
        got_core()
        accumulate(held, from_core)
        (put_y if quarter else put_x)()

    def join_y():
        got_y()
        accumulate(share, from_y)
        put_x()

    lines = []
    for tick in range(4):
        actions = []
        for place, sign, source, sems, onward, back in (
            (me.z, 1, from_down, 4, me.up(), me.down()),
            (3 - me.z, -1, from_up, 8, me.down(), me.up()),
        ):
            goal = me.z if tick == 3 else lax.rem(me.z + sign * (3 - tick) + 8, 4)
            sends = None if tick == 3 else both(place <= tick, place < 3)
            block, arrived = mine.at[goal], source.at[goal]
            got = wire.got(arrived, base + sems + goal, back)

            def take_in(block=block, arrived=arrived, got=got):
                got()
                accumulate(block, arrived)

            actions.append(
                functools.partial(when, both(sends, place > 0), take_in)
            )
            if sends is not None:
                actions.append(wire.put(block, arrived, base + sems + goal, onward, sends))
        lines.append(actions)

    def join_x():
        got_x()
        accumulate(mine, from_x)
        act(lines[0])

    def end_line():
        act(lines[3])
        put_last()

    def finish():
        got_last()
        own = held.at[me.z, me.x]
        middle = count - 2 * quarter
        chunk = row_chunk(middle, columns, 32768)

        def add_planes(number, carry):
            at = pl.multiple_of(quarter + number * chunk, 16)
            there = pl.multiple_of(at - (1 - me.y) * quarter, 16)
            final[pl.ds(at, chunk)] = own[pl.ds(at, chunk)].astype(F32) + from_last[
                pl.ds(there, chunk)
            ].astype(F32)
            return carry

        lax.fori_loop(0, middle // chunk, add_planes, 0)
        if quarter:
            for plane_of, at, there in ((0, 0, 0), (1, count - quarter, count - 2 * quarter)):

                def from_held(at=at):
                    final[pl.ds(at, quarter)] = own[pl.ds(at, quarter)].astype(F32)

                def from_mate(at=at, there=there):
                    final[pl.ds(at, quarter)] = from_last[pl.ds(there, quarter)].astype(F32)

                pl.when(me.y == plane_of)(from_held)
                pl.when(me.y != plane_of)(from_mate)

        def square(number, total):
            value = final[pl.ds(pl.multiple_of(number * 8, 8), 8)]
            power = value * value
            if limit % 8:
                place = number * 8 + lax.broadcasted_iota(jnp.int32, power.shape, 0)
                power = jnp.where(place < limit, power, 0.0)
            folded = power[:, :128]
            for lane in range(128, columns, 128):
                folded = folded + power[:, lane : lane + 128]
            return total + folded

        squares[...] = squares[...] + lax.fori_loop(
            0, (limit + 7) // 8, square, jnp.zeros((8, 128), F32)
        )

    return [
        start, join_core, *([join_y] if quarter else []), join_x,
        functools.partial(act, lines[1]), functools.partial(act, lines[2]), end_line, finish,
    ]


def in_rounds(sequences):
    last = max(k + len(one) for k, one in enumerate(sequences))
    rounds = []
    for number in range(last):
        actions = [
            one[number - k] for k, one in enumerate(sequences) if 0 <= number - k < len(one)
        ]
        rounds.append(functools.partial(act, actions[::-1]))
    return rounds


def reduce_kernel(pieces, *refs):
    refs = list(refs)
    arrays = 1 + max(piece[0] for piece in pieces)
    results = 1 + max(piece[5] for piece in pieces)
    count = len(pieces)
    grads, halo = refs[:arrays], refs[arrays]
    finals, (back, norm) = refs[arrays + 1 :][:results], refs[arrays + 1 + results :][:2]
    scratch = refs[arrays + 3 + results :]
    blank, passing, joined, tiles, send, recv, local = scratch[-7:]
    me = Place()
    ending = RS_SEMS * count
    blank[...] = jnp.zeros_like(blank)
    tiles[...] = jnp.zeros_like(tiles)
    clear = [
        (me.w >= 14, pltpu.make_async_copy(blank, back.at[0], local.at[count])),
        (me.c == 1, pltpu.make_async_copy(blank, back.at[1], local.at[count + 1])),
    ]
    for holds, one in clear:
        pl.when(holds)(one.start)
    steps = [me.wide(jnp.bitwise_xor(me.w, bit)) for bit in (1, 2, 4, 8)]
    wire = Wire(send, recv)
    far = me.wide(lax.rem(me.w + 14, 16))
    inner = me.w >= 2
    joins = both(me.c == 1, inner)
    load = pltpu.make_async_copy(halo.at[0], joined, local.at[count + 2])
    firsts = [
        wire.put(halo.at[0], back.at[0], ending, far, both(me.c == 0, inner)),
        wire.put(halo.at[1], back.at[1], ending + 1, me.core_mate(), me.c == 1),
        wire.put(halo.at[1], passing, ending + 2, me.core_mate(), both(me.c == 0, inner)),
    ]
    got_passing = wire.got(passing, ending + 2, me.core_mate())
    put_joined = wire.put(joined, back.at[0], ending, far, joins)
    got_back = [
        wire.got(back.at[0], ending, far, me.w < 14),
        wire.got(back.at[1], ending + 1, me.core_mate(), me.c == 0),
    ]

    def halo_start():
        act(firsts)
        pl.when(joins)(load.start)

    def halo_join():
        def join():
            load.wait()
            got_passing()
            accumulate(joined, passing)

        pl.when(joins)(join)
        put_joined()

    sequences = []
    for k, (number, first, rows, quarter, limit, result, column) in enumerate(pieces):
        here = pl.ds(first, rows)
        final = finals[result].at[here, pl.ds(column, grads[number].shape[-1])]
        sequences.append(
            reduce_ticks(
                me, wire, RS_SEMS * k, local.at[k],
                grads[number].at[:, :, :, here], quarter, scratch[7 * k],
                scratch[7 * k + 1 : 7 * k + 7], final, tiles.at[0], limit,
            )
        )
    greet(me, steps[2:])
    nothing = functools.partial(act, [])
    halo_ticks = [halo_start, halo_join, *[nothing] * 6, functools.partial(act, got_back)]
    act(in_rounds([sequences[0], halo_ticks, *sequences[1:]]))
    for k, partner in enumerate(steps):
        index = ending + 3 + k
        moved = wire.copy(tiles.at[k], tiles.at[5 + k], index, partner)
        moved.start()
        moved.wait()
        tiles[k + 1] = tiles[k] + tiles[5 + k]
    norm[...] = tiles[4]
    wire.finish()
    for holds, one in clear:
        pl.when(holds)(one.wait)


def piece_buffers(rows, columns, quarter, dtype):
    inside = rows - quarter
    some = (4, 2, quarter, columns) if quarter else (1, 1, 16, 128)
    shapes = [
        (4, 2, rows, columns),
        (4, 2, rows, columns),
        some,
        (4, inside, columns),
        (4, inside, columns),
        (4, inside, columns),
        (inside, columns),
    ]
    return [pltpu.VMEM(shape, dtype) for shape in shapes]


def reduce_all(grads, halo, pieces):
    wide = lax.axis_size("wide")
    if lax.axis_size("dp") == 2 and wide == 16:
        count = len(pieces)
        tokens = halo.shape[1:]
        sizes = {}
        for number, _, _, _, _, result, column in pieces:
            _, rows, columns = grads[number].shape
            sizes[result] = (rows, max(column + columns, sizes.get(result, (0, 0))[1]))
        out_shape = [jax.ShapeDtypeStruct(sizes[k], F32) for k in range(len(sizes))]
        out_shape.append(jax.ShapeDtypeStruct(halo.shape, halo.dtype))
        out_shape.append(jax.ShapeDtypeStruct((8, 128), F32))
        scratch = []
        for number, _, rows, quarter, *_ in pieces:
            one = grads[number]
            scratch += piece_buffers(rows, one.shape[2], quarter, one.dtype)
        sems = RS_SEMS * count + 7
        return pl.pallas_call(
            functools.partial(reduce_kernel, pieces),
            out_shape=out_shape,
            in_specs=[HBM] * (len(grads) + 1),
            out_specs=[VMEM] * len(sizes) + [HBM, VMEM],
            scratch_shapes=scratch
            + [
                pltpu.VMEM(tokens, BF16),
                pltpu.VMEM(tokens, BF16),
                pltpu.VMEM(tokens, BF16),
                pltpu.VMEM((9, 8, 128), F32),
                pltpu.SemaphoreType.DMA((sems,)),
                pltpu.SemaphoreType.DMA((sems,)),
                pltpu.SemaphoreType.DMA((count + 3,)),
            ],
            compiler_params=pltpu.CompilerParams(
                collective_id=1, has_side_effects=True, vmem_limit_bytes=60 << 20
            ),
            name="reduce_all",
        )(*[one.reshape(4, 2, 2, *one.shape[1:]) for one in grads], halo)
    whole = [
        lax.psum(
            lax.psum_scatter(one.astype(F32), "wide", scatter_dimension=0, tiled=False), "dp"
        )
        for one in grads
    ]
    totals = []
    for result in range(1 + max(piece[5] for piece in pieces)):
        columns = {piece[6]: whole[piece[0]] for piece in pieces if piece[5] == result}
        totals.append(jnp.concatenate([columns[key] for key in sorted(columns)], axis=1))
    back = jnp.stack([from_behind(halo[0], "wide", -2), from_behind(halo[1], "wide", -1)])
    squares = jnp.float32(0.0)
    for number, first, _, _, limit, *_ in pieces:
        part = whole[number][first : first + limit]
        squares = squares + jnp.sum(part * part)
    norm = jnp.zeros((8, 128), F32).at[0, 0].set(lax.psum(squares, "wide"))
    return [*totals, back, norm]


F_TILE = 256


def lane_sums(values):
    total = values[:, :128]
    for lane in range(128, values.shape[1], 128):
        total = total + values[:, lane : lane + 128]
    return total


def ffn_kernel(
    a_ref, x_ref, gy_ref, w1_ref, w2_ref, par_ref, bias_ref,
    out_ref, mid_ref, df_ref, da_ref, sums_ref,
    act, slope, grad, stats,
):
    blocks, _, units = w1_ref.shape
    tile = a_ref.shape[0]
    count = blocks * units
    first_step = pl.program_id(0) == 0

    @pl.when(first_step)
    def _():
        sums_ref[...] = jnp.zeros_like(sums_ref)

    stats[...] = jnp.zeros_like(stats)

    def columns(k):
        return pl.ds(pl.multiple_of(k * units, units), units)

    def forward(k, carry):
        pre = dot(a_ref[...], w1_ref[k]) + par_ref[2:3, columns(k)]
        half = 0.5 + 0.5 * lax.erf(pre * (0.5**0.5))
        value = pre * half
        act[k] = value
        slope[k] = half + pre * (jnp.exp(-0.5 * pre * pre) * (0.5 / jnp.pi) ** 0.5)
        stats[0] += lane_sums(value)
        stats[1] += lane_sums(value * value)
        return carry

    lax.fori_loop(0, blocks, forward, 0, unroll=2)
    mean = jnp.sum(stats[0], axis=1, keepdims=True) / count
    second = jnp.sum(stats[1], axis=1, keepdims=True) / count
    scale = lax.rsqrt(second - mean * mean + norm_epsilon)

    def middle(k, carry):
        here = columns(k)
        hat = (act[k] - mean) * scale
        mid_ref[:, here] = (hat * par_ref[0:1, here] + par_ref[1:2, here]).astype(BF16)
        down = dot(gy_ref[...], w2_ref[here, :], 1, 1)
        scaled = down * par_ref[0:1, here]
        cross = scaled * hat
        act[k] = hat
        grad[k] = scaled
        stats[2] += lane_sums(scaled)
        stats[3] += lane_sums(cross)
        sums_ref[0:1, here] += jnp.sum(down * hat, axis=0, keepdims=True)
        sums_ref[1:2, here] += jnp.sum(down, axis=0, keepdims=True)
        return carry

    lax.fori_loop(0, blocks, middle, 0, unroll=2)
    plain = jnp.sum(stats[2], axis=1, keepdims=True) / count
    crossed = jnp.sum(stats[3], axis=1, keepdims=True) / count
    width = out_ref.shape[1]
    part = min(width, 512)
    for start in range(0, width, part):
        here = slice(start, start + part)
        total = dot(mid_ref[...], w2_ref[:, here])
        out_ref[:, here] = (x_ref[:, here] + (total + bias_ref[:, here])).astype(BF16)

    def backward(k, carry):
        here = columns(k)
        back = scale * (grad[k] - plain - act[k] * crossed) * slope[k]
        low = back.astype(BF16)
        df_ref[:, here] = low
        sums_ref[2:3, here] += jnp.sum(low.astype(F32), axis=0, keepdims=True)
        return carry

    lax.fori_loop(0, blocks, backward, 0, unroll=2)
    da_ref[...] = jnp.zeros_like(da_ref)

    def back_out(k, carry):
        da_ref[...] += dot(df_ref[:, columns(k)], w1_ref[k], 1, 1)
        return carry

    lax.fori_loop(0, blocks, back_out, 0, unroll=2)


def ffn(rows, residual, out_grad, w1, w2, par, bias):
    tokens, width = rows.shape
    blocks, _, units = w1.shape
    hidden = blocks * units
    by_tile = lambda columns: pl.BlockSpec((F_TILE, columns), lambda t: (t, 0))
    once = pl.Buffered(1)
    return pl.pallas_call(
        ffn_kernel,
        grid=(tokens // F_TILE,),
        in_specs=[
            by_tile(width),
            by_tile(width),
            by_tile(width),
            pl.BlockSpec(w1.shape, lambda t: (0, 0, 0), pipeline_mode=once),
            pl.BlockSpec(w2.shape, lambda t: (0, 0), pipeline_mode=once),
            pl.BlockSpec(par.shape, lambda t: (0, 0)),
            pl.BlockSpec(bias.shape, lambda t: (0, 0)),
        ],
        out_specs=[
            by_tile(width),
            by_tile(hidden),
            by_tile(hidden),
            by_tile(width),
            pl.BlockSpec(par.shape, lambda t: (0, 0)),
        ],
        out_shape=[
            jax.ShapeDtypeStruct((tokens, width), BF16),
            jax.ShapeDtypeStruct((tokens, hidden), BF16),
            jax.ShapeDtypeStruct((tokens, hidden), BF16),
            jax.ShapeDtypeStruct((tokens, width), F32),
            jax.ShapeDtypeStruct(par.shape, F32),
        ],
        scratch_shapes=[pltpu.VMEM((blocks, F_TILE, units), F32)] * 3
        + [pltpu.VMEM((4, F_TILE, 128), F32)],
        compiler_params=pltpu.CompilerParams(vmem_limit_bytes=60 << 20),
        name="ffn",
    )(rows, residual, out_grad, w1, w2, par, bias)


def ffn_weights_kernel(a_ref, gy_ref, mid_ref, df_ref, dw1_ref, dw2_ref, a_t):
    @pl.when(pl.program_id(0) == 0)
    def _():
        a_t[...] = a_ref[...].T

    dw1_ref[0] = dot(a_t[...], df_ref[...]).astype(BF16)
    dw2_ref[0] = dot(mid_ref[...].T, gy_ref[...]).astype(BF16)


def ffn_weights(rows, out_grad, middle, pre_grad, blocks):
    tokens, width = rows.shape
    units = middle.shape[1] // blocks
    whole = pl.BlockSpec((tokens, width), lambda k: (0, 0))
    block = pl.BlockSpec((tokens, units), lambda k: (0, k))
    return pl.pallas_call(
        ffn_weights_kernel,
        grid=(blocks,),
        in_specs=[whole, whole, block, block],
        out_specs=[
            pl.BlockSpec((1, width, units), lambda k: (k, 0, 0)),
            pl.BlockSpec((1, units, width), lambda k: (k, 0, 0)),
        ],
        out_shape=[
            jax.ShapeDtypeStruct((blocks, width, units), BF16),
            jax.ShapeDtypeStruct((blocks, units, width), BF16),
        ],
        scratch_shapes=[pltpu.VMEM((width, tokens), BF16)],
        compiler_params=pltpu.CompilerParams(vmem_limit_bytes=40 << 20),
        name="ffn_weights",
    )(rows, out_grad, middle, pre_grad)


def plane_share(rows):
    return rows // 16 * 3 // 8 * 16


def pack(parts):
    flat = jnp.concatenate(parts, axis=1)
    size = -(-flat.shape[1] // 2048) * 2048
    return jnp.pad(flat, ((0, 0), (0, size - flat.shape[1]))).reshape(flat.shape[0], -1, 128)


def to_slabs(rows, wide):
    count, columns = rows.shape
    return rows.reshape(count, wide, -1).transpose(1, 0, 2).reshape(wide, -1)


def unpack_small(full, vector_shape, hidden_shape):
    wide = full.shape[0]
    count, each = vector_shape
    vectors = full[:, :count, :each].transpose(1, 0, 2).reshape(count, -1)
    rows, size = hidden_shape
    if size % 128 == 0:
        hidden = full[:, count:].reshape(wide, rows, size)
    else:
        hidden = full[:, count:, :size]
    hidden = hidden.transpose(1, 0, 2).reshape(rows, -1)
    return vectors.astype(F32), hidden.astype(F32)


def regroup(blocks, units):
    slabs, rows, columns = blocks.shape
    join = max(1, units // columns)
    if join == 1:
        return blocks
    return blocks.reshape(slabs // join, join, rows, columns).transpose(0, 2, 1, 3).reshape(
        slabs // join, rows, join * columns
    )


def ungroup(blocks, columns):
    slabs, rows, units = blocks.shape
    join = units // columns
    if join == 1:
        return blocks
    return blocks.reshape(slabs, rows, join, columns).transpose(0, 2, 1, 3).reshape(
        slabs * join, rows, columns
    )


def body(
    inputs,
    out_grad,
    doc_lengths,
    step_count,
    qkv_weight,
    qkv_first,
    qkv_second,
    out_weight,
    out_first,
    out_second,
    fc1_weight,
    fc1_first,
    fc1_second,
    fc2_weight,
    fc2_first,
    fc2_second,
    model_vectors,
    vectors_first,
    vectors_second,
    hidden_vectors,
    hidden_first,
    hidden_second,
    head_scale,
    head_first,
    head_second,
):
    tokens_dev = inputs.shape[0]
    width = inputs.shape[1]
    heads_count = head_scale.shape[0]
    head_size = width // heads_count
    wide = lax.axis_size("wide")
    hidden_width = hidden_vectors.shape[1] * wide
    vector_size, hidden_size = model_vectors.size, hidden_vectors.size

    fc1_rows, fc2_rows = fc1_weight.shape[0], fc2_weight.shape[0]
    qkv_rows, out_rows = qkv_weight.shape[0], out_weight.shape[0]
    small = jnp.concatenate(
        [
            jnp.pad(model_vectors, ((0, 0), (0, max(0, 128 - model_vectors.shape[1])))),
            hidden_vectors.reshape(-1, min(128, hidden_vectors.shape[1])),
        ]
        if hidden_vectors.shape[1] % 128 == 0
        else [
            jnp.pad(one, ((0, 0), (0, 128 - one.shape[1]))) for one in (model_vectors, hidden_vectors)
        ]
    ).astype(BF16)
    heads_low = lax.optimization_barrier(head_scale.astype(BF16)).astype(F32)
    starts = doc_starts(
        doc_lengths, lax.axis_index("dp"), lax.axis_index("wide") * tokens_dev, tokens_dev
    )
    starts = jnp.maximum(starts - (lax.axis_index("wide") - 2) * tokens_dev, 0).reshape(1, -1)
    scales = jnp.repeat(heads_low, head_size).reshape(1, width)
    gathered = front(
        [
            small,
            qkv_weight.astype(BF16),
            out_weight.astype(BF16),
            fc1_weight.astype(BF16),
            fc2_weight.astype(BF16),
        ],
        tuple(plane_share(one) for one in (0, qkv_rows, out_rows, fc1_rows, fc2_rows)),
        inputs,
        starts,
        scales,
        heads_count,
    )
    small_full, qkv_full, out_full, fc1_full, fc2_full, tokens_all, normed_low = gathered[:7]
    queries, keys_all, values_all, attended, mixed_low, log_totals = gathered[7:]
    vectors, hidden_par = unpack_small(small_full, model_vectors.shape, hidden_vectors.shape)
    qkv_full = qkv_full.reshape(width, 3 * width)
    out_full = out_full.reshape(width, width)
    fc2_full = fc2_full.reshape(hidden_width, width)

    own = slice(2 * tokens_dev, None)
    tokens_in = inputs.astype(F32)
    _, hat_in, scale_in = layer_norm(
        tokens_all.reshape(-1, width).astype(F32), vectors[0], vectors[3]
    )
    proj_out = jnp.dot(mixed_low, out_full, preferred_element_type=F32) + vectors[6]
    normed_post, hat_post, scale_post = layer_norm(proj_out, vectors[1], vectors[7])
    residual = tokens_in + normed_post
    normed_two, hat_two, scale_two = layer_norm(residual, vectors[2], vectors[8])
    rows_low = normed_two.astype(BF16)
    grad_in = out_grad.astype(F32)

    output, middle_low, pre_low, rows_grad, hidden_grad = ffn(
        rows_low, residual, out_grad, regroup(fc1_full, 256), fc2_full, hidden_par, vectors[9:10]
    )
    fc1_grad, fc2_grad = ffn_weights(rows_low, out_grad, middle_low, pre_low, hidden_width // 256)
    out_bias_total = jnp.sum(grad_in, axis=0)
    residual_grad = grad_in + norm_back(rows_grad, hat_two, scale_two, vectors[2])
    gain_two_grad = jnp.sum(rows_grad * hat_two, axis=0)
    bias_two_grad = jnp.sum(rows_grad, axis=0)
    gain_post_grad = jnp.sum(residual_grad * hat_post, axis=0)
    bias_post_grad = jnp.sum(residual_grad, axis=0)
    proj_low = norm_back(residual_grad, hat_post, scale_post, vectors[1]).astype(BF16)
    proj_bias_grad = jnp.sum(proj_low.astype(F32), axis=0)
    out_weight_grad = jnp.einsum("td,te->de", mixed_low, proj_low, preferred_element_type=F32)
    mixed_grad = jnp.einsum("te,de->td", proj_low, out_full, preferred_element_type=F32)
    head_grad = jnp.sum((mixed_grad * attended).reshape(tokens_dev, heads_count, -1), axis=(0, 2))
    attended_low = (mixed_grad * scales).astype(BF16)
    delta = (
        jnp.sum((attended_low.astype(F32) * attended).reshape(tokens_dev, heads_count, -1), axis=-1)
        .transpose(1, 0)
        .reshape(heads_count // 2, 2, tokens_dev)
    )
    query_grad, key_grad, value_grad = attend_back(
        queries, keys_all, values_all, attended_low, log_totals, delta, starts, heads_count
    )
    query_bias_grad = jnp.sum(query_grad.astype(F32), axis=0)
    value_bias_grad = jnp.sum(value_grad.astype(F32), axis=0)
    query_part = jnp.einsum("td,te->de", normed_low[own], query_grad, preferred_element_type=F32)
    key_part = jnp.einsum("td,te->de", normed_low, key_grad, preferred_element_type=F32)
    value_part = jnp.einsum("td,te->de", normed_low, value_grad, preferred_element_type=F32)
    normed_grad = jnp.einsum(
        "te,de->td", key_grad, qkv_full[:, width : 2 * width], preferred_element_type=F32
    ) + jnp.einsum("te,de->td", value_grad, qkv_full[:, 2 * width :], preferred_element_type=F32)
    halo_grad = normed_grad[: 2 * tokens_dev]
    own_grad = normed_grad[own] + jnp.einsum(
        "te,de->td", query_grad, qkv_full[:, :width], preferred_element_type=F32
    )
    gain_in_grad = jnp.sum(halo_grad * hat_in[: 2 * tokens_dev], axis=0) + jnp.sum(
        own_grad * hat_in[own], axis=0
    )
    bias_in_grad = jnp.sum(halo_grad, axis=0) + jnp.sum(own_grad, axis=0)
    vector_grad = jnp.stack(
        [
            gain_in_grad,
            gain_post_grad,
            gain_two_grad,
            bias_in_grad,
            query_bias_grad,
            value_bias_grad,
            proj_bias_grad,
            bias_post_grad,
            bias_two_grad,
            out_bias_total,
        ]
    )
    small_grad = pack(
        [
            to_slabs(vector_grad, wide),
            to_slabs(hidden_grad, wide),
            jnp.broadcast_to(head_grad[None], (wide, heads_count)),
        ]
    )
    counted = (vector_size + hidden_size) // 128
    small_part, qkv_part, out_part, fc1_part, fc2_part, halo_back, norm_tile = reduce_all(
        [
            small_grad,
            query_part.astype(BF16).reshape(wide, -1, width),
            key_part.astype(BF16).reshape(wide, -1, width),
            value_part.astype(BF16).reshape(wide, -1, width),
            out_weight_grad.astype(BF16).reshape(wide, -1, width),
            ungroup(fc1_grad, fc1_weight.shape[1]),
            fc2_grad.reshape(wide, -1, width),
        ],
        halo_grad.astype(BF16).reshape(2, tokens_dev, width),
        tuple(
            (6, k * (fc2_rows // 4), fc2_rows // 4, fc2_rows // 16, fc2_rows // 4, 4, 0)
            for k in range(4)
        )
        + tuple(
            (5, k * (fc1_rows // 4), fc1_rows // 4, plane_share(fc1_rows // 4), fc1_rows // 4, 3, 0)
            for k in range(4)
        )
        + (
            (4, 0, out_rows, out_rows // 4, out_rows, 2, 0),
            (0, 0, small_grad.shape[1], 0, counted, 0, 0),
            (1, 0, qkv_rows, qkv_rows // 4, qkv_rows, 1, 0),
            (2, 0, qkv_rows, qkv_rows // 4, qkv_rows, 1, width),
            (3, 0, qkv_rows, qkv_rows // 4, qkv_rows, 1, 2 * width),
        ),
    )
    total_grad = own_grad + halo_back[0].astype(F32) + halo_back[1].astype(F32)
    input_grad = residual_grad + norm_back(total_grad, hat_in[own], scale_in[own], vectors[0])
    flat = small_part.reshape(-1)
    vector_part = flat[:vector_size].reshape(model_vectors.shape)
    hidden_part = flat[vector_size : vector_size + hidden_size].reshape(hidden_vectors.shape)
    head_total = flat[vector_size + hidden_size :][:heads_count]
    grad_norm = jnp.sqrt(jnp.sum(norm_tile) + jnp.sum(head_total * head_total))
    factor = jnp.minimum(1.0, clip_limit / (grad_norm + 1e-06))
    step = step_count[0].astype(F32)
    grads = (qkv_part, out_part, fc1_part, fc2_part, vector_part, hidden_part, head_total)
    params = (
        qkv_weight,
        out_weight,
        fc1_weight,
        fc2_weight,
        model_vectors,
        hidden_vectors,
        head_scale,
    )
    firsts = (qkv_first, out_first, fc1_first, fc2_first, vectors_first, hidden_first, head_first)
    seconds = (
        qkv_second,
        out_second,
        fc1_second,
        fc2_second,
        vectors_second,
        hidden_second,
        head_second,
    )
    rates = (
        matrix_rate,
        matrix_rate,
        matrix_rate,
        matrix_rate,
        vector_rate,
        vector_rate,
        vector_rate,
    )
    decays = (weight_decay, weight_decay, weight_decay, weight_decay, 0.0, 0.0, 0.0)
    updated = []
    for number in range(7):
        updated.extend(
            adam_step(
                grads[number] * factor,
                params[number],
                firsts[number],
                seconds[number],
                step,
                rates[number],
                decays[number],
            )
        )
    return (
        output,
        input_grad,
        grad_norm.reshape(1),
        updated[0],
        updated[1],
        updated[2],
        updated[3],
        updated[4],
        updated[5],
        updated[6],
        updated[7],
        updated[8],
        updated[9],
        updated[10],
        updated[11],
        updated[12],
        updated[13],
        updated[14],
        updated[15],
        updated[16],
        updated[17],
        updated[18],
        updated[19],
        updated[20],
    )


def solution(mesh):
    placed = (
        P(("dp", "wide"), None),
        P(("dp", "wide"), None),
        P(),
        P(),
        P("wide", None),
        P("wide", None),
        P("wide", None),
        P("wide", None),
        P("wide", None),
        P("wide", None),
        P(None, "wide"),
        P(None, "wide"),
        P(None, "wide"),
        P("wide", None),
        P("wide", None),
        P("wide", None),
        P(None, "wide"),
        P(None, "wide"),
        P(None, "wide"),
        P(None, "wide"),
        P(None, "wide"),
        P(None, "wide"),
        P(),
        P(),
        P(),
    )
    return jax.shard_map(
        body,
        mesh=mesh,
        in_specs=placed,
        out_specs=(
            P(("dp", "wide"), None),
            P(("dp", "wide"), None),
            P(),
            P("wide", None),
            P("wide", None),
            P("wide", None),
            P("wide", None),
            P("wide", None),
            P("wide", None),
            P(None, "wide"),
            P(None, "wide"),
            P(None, "wide"),
            P("wide", None),
            P("wide", None),
            P("wide", None),
            P(None, "wide"),
            P(None, "wide"),
            P(None, "wide"),
            P(None, "wide"),
            P(None, "wide"),
            P(None, "wide"),
            P(),
            P(),
            P(),
        ),
        check_vma=False,
    )
```

```python
import functools

import jax
import jax.numpy as jnp
from jax import lax
from jax.experimental import pallas as pl
from jax.experimental.pallas import tpu as pltpu
from jax.sharding import PartitionSpec as P

DOC_MOST = 1024
MESH = pl.DeviceIdType.MESH
HBM = pl.BlockSpec(memory_space=pltpu.HBM)
VMEM = pl.BlockSpec(memory_space=pltpu.VMEM)
BF16 = jnp.bfloat16
F32 = jnp.float32

norm_epsilon = 1e-05
clip_limit = 1.0
first_decay = 0.9
second_decay = 0.98
adam_epsilon = 1e-08
matrix_rate = 0.1
vector_rate = 0.4
weight_decay = 0.1
masked_score = -1e30


def layer_norm(values_in, gain, shift):
    center = values_in - jnp.mean(values_in, axis=-1, keepdims=True)
    variance = jnp.mean(center * center, axis=-1, keepdims=True)
    scale = lax.rsqrt(variance + norm_epsilon)
    normed = center * scale
    return (normed * gain + shift, normed, scale)


def doc_starts(doc_lengths, row, first, count):
    ends = lax.dynamic_slice_in_dim(jnp.cumsum(doc_lengths, axis=1), row, 1, 0)[0]
    places = first + jnp.arange(count, dtype=jnp.int32)
    return jnp.max(jnp.where(ends[None, :] <= places[:, None], ends[None, :], 0), axis=1)


def adam_step(grad, weight, first, second, step, rate, decay):
    first_new = first_decay * first + (1.0 - first_decay) * grad
    second_new = second_decay * second + (1.0 - second_decay) * grad * grad
    fix_one = 1.0 - jnp.power(jnp.float32(first_decay), step)
    fix_two = 1.0 - jnp.power(jnp.float32(second_decay), step)
    direction = first_new / fix_one / (jnp.sqrt(second_new / fix_two) + adam_epsilon)
    weight_new = weight - rate * (direction + decay * weight)
    return (first_new, second_new, weight_new)


def from_behind(shard, axis, by):
    count = lax.axis_size(axis)
    pairs = [(i, i + by) for i in range(count) if 0 <= i + by < count]
    return lax.ppermute(shard, axis, pairs)


def dot(a, b, left=1, right=0):
    return lax.dot_general(
        a, b, (((left,), (right,)), ((), ())), preferred_element_type=F32
    )


Q_TILE = 256


def split_pair(pair, size):
    lane = lax.broadcasted_iota(jnp.int32, pair.shape, 1)
    zero = jnp.zeros_like(pair)
    return jnp.where(lane < size, pair, zero), jnp.where(lane < size, zero, pair)


def fill_mask(starts, bias, tokens, span, keys_before):
    for tile in range(tokens // Q_TILE):
        query = lax.broadcasted_iota(jnp.int32, (span, Q_TILE), 1) + tile * Q_TILE + keys_before
        key = lax.broadcasted_iota(jnp.int32, (span, Q_TILE), 0) + tile * Q_TILE
        first = starts[:, tile * Q_TILE : (tile + 1) * Q_TILE]
        seen = jnp.logical_and(key <= query, key >= first)
        bias[tile] = jnp.where(seen, 0.0, masked_score)


def attend_pair(size, q_ref, k_ref, v_ref, scale_ref, o_ref, c_ref, lse_ref, bias, vt, ot):
    tokens, window = q_ref.shape[0], k_ref.shape[0]
    span = window - tokens + Q_TILE
    vt[...] = v_ref[...].T
    for tile in range(tokens // Q_TILE):
        rows = slice(tile * Q_TILE, (tile + 1) * Q_TILE)
        keys = slice(tile * Q_TILE, tile * Q_TILE + span)
        k_pair = k_ref[keys, :]
        for head, q_one in enumerate(split_pair(q_ref[rows, :], size)):
            scores = dot(k_pair, q_one, 1, 1) + bias[tile]
            highest = jnp.max(scores, axis=0, keepdims=True)
            powers = jnp.exp(scores - highest)
            total = jnp.sum(powers, axis=0, keepdims=True)
            probs = (powers * (1.0 / total)).astype(BF16)
            lse_ref[head : head + 1, rows] = highest + jnp.log(total)
            part = slice(head * size, (head + 1) * size)
            ot[part, rows] = dot(vt[part, keys], probs)
    attended = ot[...].T
    o_ref[...] = attended
    c_ref[...] = (attended * scale_ref[...]).astype(BF16)


def attend_kernel(size, starts, scale_ref, q_ref, k_ref, v_ref, o_ref, c_ref, lse_ref, bias, vt, ot):
    tokens, window = q_ref.shape[0], k_ref.shape[0]
    before = window - tokens

    @pl.when(pl.program_id(0) == 0)
    def _():
        fill_mask(starts, bias, tokens, before + Q_TILE, before)

    attend_pair(size, q_ref, k_ref, v_ref, scale_ref, o_ref, c_ref, lse_ref.at[0], bias, vt, ot)


def attend(queries, keys, values, starts, scales, heads):
    tokens, width = queries.shape
    window = keys.shape[0]
    pairs = heads // 2
    lanes = width // pairs
    span = window - tokens + Q_TILE
    by_rows = lambda rows: pl.BlockSpec((rows, lanes), lambda p: (0, p))
    return pl.pallas_call(
        functools.partial(attend_kernel, width // heads),
        grid=(pairs,),
        in_specs=[
            pl.BlockSpec((1, tokens), lambda p: (0, 0)),
            by_rows(1),
            by_rows(tokens),
            by_rows(window),
            by_rows(window),
        ],
        out_specs=[
            by_rows(tokens),
            by_rows(tokens),
            pl.BlockSpec((1, 2, tokens), lambda p: (p, 0, 0)),
        ],
        out_shape=[
            jax.ShapeDtypeStruct((tokens, width), F32),
            jax.ShapeDtypeStruct((tokens, width), BF16),
            jax.ShapeDtypeStruct((pairs, 2, tokens), F32),
        ],
        scratch_shapes=[
            pltpu.VMEM((tokens // Q_TILE, span, Q_TILE), F32),
            pltpu.VMEM((lanes, window), BF16),
            pltpu.VMEM((lanes, tokens), F32),
        ],
        compiler_params=pltpu.CompilerParams(vmem_limit_bytes=40 << 20),
        name="attend",
    )(starts, scales, queries, keys, values)


def attend_back_pair(
    size, q_ref, k_ref, v_ref, do_ref, lse_ref, delta_ref, dq_ref, dk_ref, dv_ref, bias, dk_sum, dv_sum, kt, dqt
):
    tokens, window = q_ref.shape[0], k_ref.shape[0]
    span = window - tokens + Q_TILE
    kt[...] = k_ref[...].T
    dk_sum[...] = jnp.zeros_like(dk_sum)
    dv_sum[...] = jnp.zeros_like(dv_sum)
    for tile in range(tokens // Q_TILE):
        rows = slice(tile * Q_TILE, (tile + 1) * Q_TILE)
        keys = slice(tile * Q_TILE, tile * Q_TILE + span)
        k_pair, v_pair = k_ref[keys, :], v_ref[keys, :]
        for head, (q_one, do_one) in enumerate(
            zip(split_pair(q_ref[rows, :], size), split_pair(do_ref[rows, :], size))
        ):
            scores = dot(k_pair, q_one, 1, 1) + bias[tile]
            probs = jnp.exp(scores - lse_ref[head : head + 1, rows])
            grads = dot(v_pair, do_one, 1, 1) - delta_ref[head : head + 1, rows]
            low = (probs * grads).astype(BF16)
            dv_sum[keys, :] += dot(probs.astype(BF16), do_one)
            dk_sum[keys, :] += dot(low, q_one)
            part = slice(head * size, (head + 1) * size)
            dqt[part, rows] = dot(kt[part, keys], low)
    dq_ref[...] = (dqt[...].T * size ** (-0.5)).astype(BF16)
    dk_ref[...] = dk_sum[...].astype(BF16)
    dv_ref[...] = dv_sum[...].astype(BF16)


def attend_back_kernel(
    size, starts, q_ref, k_ref, v_ref, do_ref, lse_ref, delta_ref, dq_ref, dk_ref, dv_ref, bias, *scratch
):
    tokens, window = q_ref.shape[0], k_ref.shape[0]
    before = window - tokens

    @pl.when(pl.program_id(0) == 0)
    def _():
        fill_mask(starts, bias, tokens, before + Q_TILE, before)

    attend_back_pair(
        size, q_ref, k_ref, v_ref, do_ref, lse_ref.at[0], delta_ref.at[0], dq_ref, dk_ref, dv_ref, bias, *scratch
    )


def attend_back(queries, keys, values, outs_grad, lse, delta, starts, heads):
    tokens, width = queries.shape
    window = keys.shape[0]
    pairs = heads // 2
    lanes = width // pairs
    span = window - tokens + Q_TILE
    by_rows = lambda rows: pl.BlockSpec((rows, lanes), lambda p: (0, p))
    stats = pl.BlockSpec((1, 2, tokens), lambda p: (p, 0, 0))
    return pl.pallas_call(
        functools.partial(attend_back_kernel, width // heads),
        grid=(pairs,),
        in_specs=[
            pl.BlockSpec((1, tokens), lambda p: (0, 0)),
            by_rows(tokens),
            by_rows(window),
            by_rows(window),
            by_rows(tokens),
            stats,
            stats,
        ],
        out_specs=[
            by_rows(tokens),
            by_rows(window),
            by_rows(window),
        ],
        out_shape=[
            jax.ShapeDtypeStruct((tokens, width), BF16),
            jax.ShapeDtypeStruct((window, width), BF16),
            jax.ShapeDtypeStruct((window, width), BF16),
        ],
        scratch_shapes=[
            pltpu.VMEM((tokens // Q_TILE, span, Q_TILE), F32),
            pltpu.VMEM((window, lanes), F32),
            pltpu.VMEM((window, lanes), F32),
            pltpu.VMEM((lanes, window), BF16),
            pltpu.VMEM((lanes, tokens), F32),
        ],
        compiler_params=pltpu.CompilerParams(vmem_limit_bytes=40 << 20),
        name="attend_back",
    )(starts, queries, keys, values, outs_grad, lse, delta)


class Place:
    def __init__(self):
        self.y = lax.axis_index("dp")
        self.w = lax.axis_index("wide")
        self.z = self.w // 4
        self.x = (self.w // 2) % 2
        self.c = self.w % 2

    def slab(self, z, x, c):
        return z * 4 + x * 2 + c

    def wide(self, w):
        return (self.y, w)

    def core_mate(self):
        return self.wide(self.slab(self.z, self.x, 1 - self.c))

    def x_mate(self):
        return self.wide(self.slab(self.z, 1 - self.x, self.c))

    def y_mate(self):
        return (1 - self.y, self.w)

    def up(self):
        return self.wide(lax.rem(self.w + 4, 16))

    def down(self):
        return self.wide(lax.rem(self.w + 12, 16))


def greet(me, extra=()):
    barrier = pltpu.get_barrier_semaphore()

    def hello(target):
        pl.semaphore_signal(barrier, inc=1, device_id=target, device_id_type=MESH)

    always = [me.core_mate(), me.x_mate(), me.y_mate(), *extra]
    sometimes = [
        (me.z < 3, me.up()),
        (me.z > 0, me.down()),
        (me.w < 14, me.wide(lax.rem(me.w + 2, 16))),
        (me.w >= 2, me.wide(lax.rem(me.w + 14, 16))),
    ]
    for target in always:
        hello(target)
    for holds, target in sometimes:
        pl.when(holds)(functools.partial(hello, target))
    count = len(always) + sum(holds.astype(jnp.int32) for holds, _ in sometimes)
    pl.semaphore_wait(barrier, count)


class Wire:
    def __init__(self, send, recv):
        self.send, self.recv = send, recv
        self.planned = []

    def copy(self, source, target, index, device):
        return pltpu.make_async_remote_copy(
            src_ref=source,
            dst_ref=target,
            send_sem=self.send.at[index],
            recv_sem=self.recv.at[index],
            device_id=device,
            device_id_type=MESH,
        )

    def put(self, source, target, index, device, holds=None):
        moved = self.copy(source, target, index, device)
        self.planned.append((holds, moved))
        return lambda: when(holds, moved.start)

    def got(self, target, index, device, holds=None):
        moved = self.copy(target, target, index, device)
        return lambda: when(holds, moved.wait_recv)

    def finish(self):
        for holds, moved in self.planned:
            when(holds, moved.wait_send)


def act(actions):
    for one in actions:
        one()


def both(*conditions):
    held = [one for one in conditions if one is not None]
    total = held[0] if held else None
    for one in held[1:]:
        total = jnp.logical_and(total, one)
    return total


def when(holds, action):
    if holds is None:
        action()
    else:
        pl.when(holds)(action)


def gather_ticks(me, wire, base, own, full, third):
    rows = own.shape[0]
    plane = (
        pl.ds(pl.multiple_of(me.y * third, 16), rows - third) if third else pl.ds(0, rows)
    )
    share = pl.ds(pl.multiple_of(me.y * (rows - third), 16), third) if third else None
    other = pl.ds(pl.multiple_of((1 - me.y) * (rows - third), 16), third) if third else None
    my_slab = me.slab(me.z, me.x, me.c)
    ups, downs, xs, ys, cs, ts = (base + k for k in (0, 4, 8, 12, 20, 28))
    mine = me.z * 2 + me.x

    def pass_on(z, x, holds):
        slab = me.slab(z, x, me.c)
        place = z * 2 + x
        block = full.at[slab, plane]
        actions = []
        if third:
            piece = full.at[slab, share]
            actions.append(wire.put(piece, piece, ys + place, me.y_mate(), holds))
        actions.append(wire.put(block, block, cs + place, me.core_mate(), holds))
        return actions

    goal = full.at[my_slab, plane]
    ticks = [
        [
            wire.put(own.at[plane], goal, ups + me.z, me.up(), me.z < 3),
            wire.put(own.at[plane], goal, downs + me.z, me.down(), me.z > 0),
            wire.put(own.at[plane], goal, xs + me.z, me.x_mate()),
            wire.put(own, full.at[my_slab], cs + mine, me.core_mate()),
        ]
    ]
    for tick in range(1, 5):
        actions = []
        if tick < 4:
            for away, holds, onward, follow, sems in (
                (me.z - tick, me.z - tick >= 0, me.up(), me.z < 3, ups),
                (me.z + tick, me.z + tick <= 3, me.down(), me.z > 0, downs),
            ):
                safe = lax.rem(away + 4, 4)
                block = full.at[me.slab(safe, me.x, me.c), plane]
                actions.append(wire.got(block, sems + safe, onward, holds))
                actions.append(wire.put(block, block, sems + safe, onward, both(holds, follow)))
                actions.append(wire.put(block, block, xs + safe, me.x_mate(), holds))
                actions += pass_on(safe, me.x, holds)
        before = tick - 1
        for away, holds in (
            ((me.z, None),)
            if before == 0
            else (
                (me.z - before, me.z - before >= 0),
                (me.z + before, me.z + before <= 3),
            )
        ):
            safe = lax.rem(away + 4, 4)
            block = full.at[me.slab(safe, 1 - me.x, me.c), plane]
            actions.append(wire.got(block, xs + safe, me.x_mate(), holds))
            actions += pass_on(safe, 1 - me.x, holds)
        ticks.append(actions)
    actions = []
    if third:
        for k in range(1, 8):
            place = lax.rem(mine + k, 8)
            piece = full.at[me.slab(place // 2, place % 2, me.c), other]
            actions.append(wire.got(piece, ys + place, me.y_mate()))
            actions.append(wire.put(piece, piece, ts + place, me.core_mate()))
    ticks.append(actions)
    actions = [wire.got(full.at[me.slab(me.z, me.x, 1 - me.c)], cs + mine, me.core_mate())]
    for k in range(1, 8):
        place = lax.rem(mine + k, 8)
        slab = me.slab(place // 2, place % 2, 1 - me.c)
        actions.append(wire.got(full.at[slab, plane], cs + place, me.core_mate()))
        if third:
            actions.append(wire.got(full.at[slab, other], ts + place, me.core_mate()))
    ticks.append(actions)
    return ticks


AG_SEMS = 36


FRONT_BLOCK = 256


def front_kernel(thirds, head_size, *refs):
    owns, (tokens, starts, scale_ref) = refs[:5], refs[5:8]
    fulls, outs = refs[8:12], refs[12:19]
    xs_out, a_out, q_out, k_out, v_out, o_out, c_out = outs
    lse_ref, vecs, par = refs[19:22]
    (xs, a_all, qkv, q_all, k_all, v_all, o_all, c_all, small, bias, vt, ot, send, recv, local) = refs[22:]
    me = Place()
    count = len(owns)
    width = tokens.shape[1]
    rows = tokens.shape[0]
    window = 3 * rows
    before = window - rows
    span = before + Q_TILE
    landings = (small, qkv, *fulls[1:])
    keep = [
        pltpu.make_async_copy(own, full.at[me.w], local.at[k])
        for k, (own, full) in enumerate(zip(owns, landings))
    ] + [pltpu.make_async_copy(tokens, xs.at[2], local.at[count])]
    for one in keep:
        one.start()

    def clear(slot):
        xs[slot] = jnp.zeros((rows, width), BF16)

    pl.when(me.w < 2)(functools.partial(clear, 0))
    pl.when(me.w < 1)(functools.partial(clear, 1))
    wire = Wire(send, recv)
    first, second = AG_SEMS * count, AG_SEMS * count + 1
    ticks = [
        gather_ticks(me, wire, AG_SEMS * k, own, landing, third)
        for k, (own, landing, third) in enumerate(zip(owns, landings, thirds))
    ]
    send_block = wire.put(tokens, xs.at[0], first, me.wide(lax.rem(me.w + 2, 16)), me.w < 14)
    send_near = wire.put(tokens, xs.at[1], second, me.core_mate(), me.c == 0)
    get_block = wire.got(xs.at[0], first, me.core_mate(), me.w >= 2)
    passes = both(me.c == 1, me.w >= 2)
    pass_block = wire.copy(xs.at[0], xs.at[1], second, me.core_mate())
    get_near = wire.got(xs.at[1], second, me.core_mate(), me.w >= 1)
    greet(me)
    early, late = ticks[:2], ticks[2:]
    act(early[0][0] + early[1][0])
    send_block()
    send_near()
    for tick in range(1, 4):
        act(early[0][tick] + early[1][tick])
    for one in late:
        act(one[0])
    get_block()
    when(passes, pass_block.start)
    fill_mask(starts, bias, rows, span, before)
    for tick in range(4, 7):
        act(early[0][tick] + early[1][tick])
    get_near()
    when(passes, pass_block.wait_send)
    for one in keep:
        one.wait()
    shared = [pltpu.make_async_copy(qkv, fulls[0], local.at[1])]
    for one in shared:
        one.start()

    lane = lax.broadcasted_iota(jnp.int32, (16, 128), 1)
    for pair in range(8):
        even = small[2 * pair].astype(F32)
        odd = pltpu.roll(small[2 * pair + 1].astype(F32), 64, 1)
        vecs[:, pair * 128 : (pair + 1) * 128] = jnp.where(lane < 64, even, odd)
    for slab in range(16):
        values = small[slab].astype(F32)
        for row in range(3):
            for half in range(2):
                at = slab * 256 + half * 128
                par[row : row + 1, at : at + 128] = values[10 + 2 * row + half][None]

    def project(first_column, column, a_rows):
        weights = qkv[:, :, pl.ds(first_column + column, FRONT_BLOCK)].reshape(width, FRONT_BLOCK)
        return dot(a_rows, weights)

    per = rows // FRONT_BLOCK

    def normalize(number, carry):
        here = pl.ds(pl.multiple_of(lax.rem(number, per) * FRONT_BLOCK, FRONT_BLOCK), FRONT_BLOCK)
        there = pl.ds(pl.multiple_of(number * FRONT_BLOCK, FRONT_BLOCK), FRONT_BLOCK)
        value, hat, _ = layer_norm(xs[number // per, here].astype(F32), vecs[0:1], vecs[3:4])
        xs[number // per, here] = hat.astype(BF16)
        low = value.astype(BF16)
        a_all[there] = low
        for column in range(0, width, FRONT_BLOCK):
            columns = slice(column, column + FRONT_BLOCK)
            k_all[there, columns] = project(width, column, low).astype(BF16)
            v_all[there, columns] = (
                project(2 * width, column, low) + vecs[5:6, columns]
            ).astype(BF16)
        return carry

    lax.fori_loop(0, window // FRONT_BLOCK, normalize, 0)
    for number in range(per):
        here = pl.ds(number * FRONT_BLOCK, FRONT_BLOCK)
        low = a_all[before + number * FRONT_BLOCK : before + (number + 1) * FRONT_BLOCK]
        for column in range(0, width, FRONT_BLOCK):
            columns = slice(column, column + FRONT_BLOCK)
            query = (project(0, column, low) + vecs[4:5, columns]).astype(BF16)
            q_all[here, columns] = query * jnp.asarray(head_size ** (-0.5), BF16)
    kept = [
        pltpu.make_async_copy(one, out, local.at[2 + k])
        for k, (one, out) in enumerate(
            ((a_all, a_out), (q_all, q_out), (k_all, k_out), (v_all, v_out), (xs, xs_out))
        )
    ]
    for one in kept:
        one.start()

    def pair_step(pair, carry):
        lanes = pl.ds(pl.multiple_of(pair * 128, 128), 128)
        attend_pair(
            head_size, q_all.at[:, lanes], k_all.at[:, lanes], v_all.at[:, lanes],
            scale_ref.at[:, lanes], o_all.at[:, lanes], c_all.at[:, lanes], lse_ref.at[pair], bias, vt, ot,
        )
        for tick, when_done in ((1, 0), (2, 4)):
            pl.when(pair == when_done)(
                lambda tick=tick: act([action for one in late for action in one[tick]])
            )
        return carry

    lax.fori_loop(0, width // 128, pair_step, 0)
    results = [
        pltpu.make_async_copy(o_all, o_out, local.at[7]),
        pltpu.make_async_copy(c_all, c_out, local.at[8]),
    ]
    for one in results:
        one.start()
    for tick in range(3, 7):
        for one in late:
            act(one[tick])
    wire.finish()
    for one in shared + kept + results:
        one.wait()


def plain_front(shards, tokens, starts, scales, heads):
    width = tokens.shape[1]
    fulls = [lax.all_gather(one, "wide", axis=0, tiled=False) for one in shards]
    each, units = width // fulls[0].shape[0], shards[3].shape[1]
    vectors, par = unpack_small(fulls[0], (10, each), (3, units))
    window = jnp.stack([from_behind(tokens, "wide", 2), from_behind(tokens, "wide", 1), tokens])
    normed, hat, _ = layer_norm(window.reshape(-1, width).astype(F32), vectors[0], vectors[3])
    low = normed.astype(BF16)
    weights = fulls[1].reshape(width, 3 * width)
    queries = dot(low[-tokens.shape[0] :], weights[:, :width]) + vectors[4]
    queries = queries.astype(BF16) * jnp.asarray((width // heads) ** (-0.5), BF16)
    keys = dot(low, weights[:, width : 2 * width]).astype(BF16)
    values = (dot(low, weights[:, 2 * width :]) + vectors[5]).astype(BF16)
    attended = attend(queries, keys, values, starts, scales, heads)
    hat_low = hat.astype(BF16).reshape(window.shape)
    return [*fulls[1:], hat_low, low, queries, keys, values, *attended, vectors, par]


def front(shards, thirds, tokens, starts, scales, heads):
    rows, width = tokens.shape
    wide = lax.axis_size("wide")
    if lax.axis_size("dp") != 2 or wide != 16:
        return plain_front(shards, tokens, starts, scales, heads)
    window = 3 * rows
    like = jax.ShapeDtypeStruct
    out_shape = [like((wide, *one.shape), one.dtype) for one in shards[1:]] + [
        like((3, rows, width), BF16),
        like((window, width), BF16),
        like((rows, width), BF16),
        like((window, width), BF16),
        like((window, width), BF16),
        like((rows, width), F32),
        like((rows, width), BF16),
        like((heads // 2, 2, rows), F32),
        like((16, width), F32),
        like((8, wide * shards[3].shape[1]), F32),
    ]
    sems = AG_SEMS * len(shards) + 2
    scratch = [
        ((3, rows, width), BF16),
        ((window, width), BF16),
        ((wide, *shards[1].shape), BF16),
        ((rows, width), BF16),
        ((window, width), BF16),
        ((window, width), BF16),
        ((rows, width), F32),
        ((rows, width), BF16),
        ((wide, *shards[0].shape), BF16),
        ((rows // Q_TILE, window - rows + Q_TILE, Q_TILE), F32),
        ((128, window), BF16),
        ((128, rows), F32),
    ]
    return pl.pallas_call(
        functools.partial(front_kernel, thirds, width // heads),
        out_shape=out_shape,
        in_specs=[VMEM] * 8,
        out_specs=[HBM] * 11 + [VMEM] * 3,
        scratch_shapes=[pltpu.VMEM(shape, dtype) for shape, dtype in scratch]
        + [
            pltpu.SemaphoreType.DMA((sems,)),
            pltpu.SemaphoreType.DMA((sems,)),
            pltpu.SemaphoreType.DMA((9,)),
        ],
        compiler_params=pltpu.CompilerParams(
            collective_id=0, has_side_effects=True, vmem_limit_bytes=58 << 20
        ),
        name="front",
    )(*shards, tokens, starts, scales)


def row_chunk(rows, columns, most):
    chunk = min(rows, max(16, most // columns // 16 * 16))
    while rows % chunk:
        chunk -= 16
    return chunk


def accumulate(target, source):
    *lead, rows, columns = source.shape
    chunk = row_chunk(rows, columns, 65536)
    per = rows // chunk
    many = per
    for size in lead:
        many *= size

    def step(number, carry):
        part = pl.ds(pl.multiple_of(lax.rem(number, per) * chunk, 16), chunk)
        rest, index = number // per, []
        for size in reversed(lead):
            index.insert(0, lax.rem(rest, size))
            rest = rest // size
        at = (*index, part)
        target[at] = (target[at].astype(F32) + source[at].astype(F32)).astype(target.dtype)
        return carry

    lax.fori_loop(0, many, step, 0)


RS_SEMS = 12


def reduce_ticks(
    me, wire, base, local, grad, quarter, held, bufs, final, squares, waits_for=None, frees=None
):
    from_core, from_y, from_x, from_down, from_up, from_last = bufs
    count, columns = held.shape[-2:]
    inside = count - quarter
    plane = pl.ds(pl.multiple_of(me.y * quarter, 16), inside) if quarter else pl.ds(0, count)
    mine = held.at[:, me.x, plane]
    take = pltpu.make_async_copy(grad.at[:, :, me.c], held, local)
    put_core = wire.put(grad.at[:, :, 1 - me.c], from_core, base, me.core_mate())
    got_core = wire.got(from_core, base, me.core_mate())
    put_x = wire.put(held.at[:, 1 - me.x, plane], from_x, base + 2, me.x_mate())
    got_x = wire.got(from_x, base + 2, me.x_mate())
    put_last = wire.put(mine.at[me.z], from_last, base + 3, me.y_mate())
    got_last = wire.got(from_last, base + 3, me.y_mate())
    if quarter:
        share = held.at[:, :, pl.ds(pl.multiple_of(me.y * inside, 16), quarter)]
        other = held.at[:, :, pl.ds(pl.multiple_of((1 - me.y) * inside, 16), quarter)]
        put_y = wire.put(other, from_y, base + 1, me.y_mate())
        got_y = wire.got(from_y, base + 1, me.y_mate())

    partners = [(None, one) for one in (me.core_mate(), me.x_mate(), me.y_mate())]
    partners += [(me.z < 3, me.up()), (me.z > 0, me.down())]

    def start():
        if waits_for is not None:
            ends = (me.z < 3).astype(jnp.int32) + (me.z > 0).astype(jnp.int32)
            pl.semaphore_wait(waits_for, 3 + ends)
        take.start()
        put_core()

    def join_core():
        take.wait()
        got_core()
        accumulate(held, from_core)
        (put_y if quarter else put_x)()

    def join_y():
        got_y()
        accumulate(share, from_y)
        put_x()

    lines = []
    for tick in range(4):
        actions = []
        for place, sign, source, sems, onward, back in (
            (me.z, 1, from_down, 4, me.up(), me.down()),
            (3 - me.z, -1, from_up, 8, me.down(), me.up()),
        ):
            goal = me.z if tick == 3 else lax.rem(me.z + sign * (3 - tick) + 8, 4)
            sends = None if tick == 3 else both(place <= tick, place < 3)
            block, arrived = mine.at[goal], source.at[goal]
            got = wire.got(arrived, base + sems + goal, back)

            def take_in(block=block, arrived=arrived, got=got):
                got()
                accumulate(block, arrived)

            actions.append(
                functools.partial(when, both(sends, place > 0), take_in)
            )
            if sends is not None:
                actions.append(wire.put(block, arrived, base + sems + goal, onward, sends))
        lines.append(actions)

    def join_x():
        got_x()
        accumulate(mine, from_x)
        act(lines[0])

    def end_line():
        act(lines[3])
        put_last()

    def finish():
        got_last()
        own = held.at[me.z, me.x]
        middle = count - 2 * quarter
        chunk = row_chunk(middle, columns, 32768)

        def add_planes(number, carry):
            at = pl.multiple_of(quarter + number * chunk, 16)
            there = pl.multiple_of(at - (1 - me.y) * quarter, 16)
            final[pl.ds(at, chunk)] = own[pl.ds(at, chunk)].astype(F32) + from_last[
                pl.ds(there, chunk)
            ].astype(F32)
            return carry

        lax.fori_loop(0, middle // chunk, add_planes, 0)
        if quarter:
            for plane_of, at, there in ((0, 0, 0), (1, count - quarter, count - 2 * quarter)):

                def from_held(at=at):
                    final[pl.ds(at, quarter)] = own[pl.ds(at, quarter)].astype(F32)

                def from_mate(at=at, there=there):
                    final[pl.ds(at, quarter)] = from_last[pl.ds(there, quarter)].astype(F32)

                pl.when(me.y == plane_of)(from_held)
                pl.when(me.y != plane_of)(from_mate)

        def square(number, total):
            value = final[pl.ds(pl.multiple_of(number * 8, 8), 8)]
            return total + lane_groups(value * value)

        squares[...] = squares[...] + lax.fori_loop(
            0, count // 8, square, jnp.zeros((8, 128), F32)
        )
        if frees is not None:
            wire.finish()
            for holds, device in partners:
                when(
                    holds,
                    functools.partial(
                        pl.semaphore_signal, frees, inc=1, device_id=device, device_id_type=MESH
                    ),
                )

    return [
        start, join_core, *([join_y] if quarter else []), join_x,
        functools.partial(act, lines[1]), functools.partial(act, lines[2]), end_line, finish,
    ]


def in_rounds(sequences):
    last = max(start + len(one) for start, one in sequences)
    order = sorted(sequences, key=lambda item: -item[0])
    rounds = []
    for number in range(last):
        actions = [
            one[number - start] for start, one in order if 0 <= number - start < len(one)
        ]
        rounds.append(functools.partial(act, actions))
    return rounds


def lane_groups(values):
    total = values[:, :128]
    for lane in range(128, values.shape[1], 128):
        total = total + values[:, lane : lane + 128]
    return total


def piece_buffers(rows, columns, quarter, dtype):
    inside = rows - quarter
    some = (4, 2, quarter, columns) if quarter else (1, 1, 16, 128)
    shapes = [
        (4, 2, rows, columns),
        (4, 2, rows, columns),
        some,
        (4, inside, columns),
        (4, inside, columns),
        (4, inside, columns),
        (inside, columns),
    ]
    return [pltpu.VMEM(shape, dtype) for shape in shapes]


BACK_BLOCK = 256
DURING_PAIRS = ((0, (0, 1)), (1, (2,)), (2, (3,)), (4, (4,)), (5, (5,)), (7, (6,)))
DURING_BLOCKS = ((1, (7,)), (3, (8,)))
AFTER_BLOCKS = 9


def back_kernel(pieces, sets, head_size, *refs):
    grads, refs = refs[:3], refs[3:]
    (q_in, k_in, v_in, do_in, a_in, hat_in, w_in, starts, lse, delta, small_in), refs = refs[:11], refs[11:]
    finals, refs = refs[:4], refs[4:]
    (back_out, own_out, small_out, norm), refs = refs[:4], refs[4:]
    buffers, refs = refs[: 7 * sets], refs[7 * sets :]
    (dq, dk, dv, dw, halo, passing, small, tiles, send, recv, local, stream, freed) = refs
    me = Place()
    count = len(pieces)
    rows, width = q_in.shape
    window = k_in.shape[0]
    before = window - rows
    span = before + Q_TILE
    tiles[...] = jnp.zeros_like(tiles)
    small[0] = small_in[...]
    arrays = [*grads, *[dw.at[k] for k in range(3)]]
    wires, sequences = [], []
    last_of = {}
    for k, (number, first, size, quarter, result, column, of, start) in enumerate(pieces):
        here = pl.ds(first, size)
        wire = Wire(send, recv)
        again = of in last_of
        more = any(piece[6] == of for piece in pieces[k + 1 :])
        final = finals[result].at[here, pl.ds(column, arrays[number].shape[-1])]
        sequences.append(
            (
                start,
                reduce_ticks(
                    me, wire, RS_SEMS * k, local.at[k], arrays[number].at[:, :, :, here], quarter,
                    buffers[7 * of], buffers[7 * of + 1 : 7 * of + 7], final, tiles.at[0],
                    waits_for=freed.at[last_of[of]] if again else None,
                    frees=freed.at[k] if more else None,
                ),
            )
        )
        last_of[of] = k
        if not more:
            wires.append(wire)

    ending = RS_SEMS * count
    wire = Wire(send, recv)
    wires.append(wire)
    far = me.wide(lax.rem(me.w + 14, 16))
    inner = me.w >= 2
    joins = both(me.c == 1, inner)
    near = [
        wire.put(halo.at[1], back_out.at[1], ending + 1, me.core_mate(), me.c == 1),
        wire.put(halo.at[1], passing, ending + 2, me.core_mate(), both(me.c == 0, inner)),
    ]
    got_passing = wire.got(passing, ending + 2, me.core_mate())
    put_far = wire.put(halo.at[0], back_out.at[0], ending, far, inner)
    got_back = [
        wire.got(back_out.at[0], ending, far, me.w < 14),
        wire.got(back_out.at[1], ending + 1, me.core_mate(), me.c == 0),
    ]

    def join_halo():
        got_passing()
        accumulate(halo.at[0], passing)

    def small_step(k, partner):
        put = wire.put(small.at[k], small.at[5 + k], ending + 3 + k, partner)
        got = wire.got(small.at[5 + k], ending + 3 + k, partner)

        def take_in():
            got()
            small[k + 1] = small[k] + small[5 + k]

        return put, take_in

    steps = [me.wide(jnp.bitwise_xor(me.w, bit)) for bit in (1, 2, 4, 8)]
    smalls = [small_step(k, one) for k, one in enumerate([steps[0], me.y_mate(), *steps[1:]])]
    small_ticks = [smalls[0][0]]
    for k in range(4):
        small_ticks.append(functools.partial(act, [smalls[k][1], smalls[k + 1][0]]))
    small_ticks.append(smalls[4][1])
    last_start = pieces[-1][-1]
    computed = pieces[-3][-1]
    sequences.append((computed, small_ticks))
    sequences.append(
        (computed, [functools.partial(act, near), functools.partial(when, joins, join_halo)])
    )
    sequences.append((last_start + 3, [put_far]))
    rounds = in_rounds(sequences)
    pairs = width // 128
    blocks = width // BACK_BLOCK
    greet(me, steps[2:])

    def attention(q_two, k_two, v_two, do_two, bias, dk_sum, dv_sum, kt, dqt):
        def loads(pair, slot):
            lanes = pl.ds(pl.multiple_of(pair * 128, 128), 128)
            return [
                pltpu.make_async_copy(source.at[:, lanes], target.at[slot], stream.at[slot, k])
                for k, (source, target) in enumerate(
                    ((q_in, q_two), (k_in, k_two), (v_in, v_two), (do_in, do_two))
                )
            ]

        for one in loads(0, 0):
            one.start()
        fill_mask(starts, bias, rows, span, before)

        def pair_step(pair, carry):
            slot = lax.rem(pair, 2)
            lanes = pl.ds(pl.multiple_of(pair * 128, 128), 128)

            def prefetch():
                for one in loads(pair + 1, 1 - slot):
                    one.start()

            pl.when(pair + 1 < pairs)(prefetch)
            for k, due in DURING_PAIRS:
                pl.when(pair == k)(functools.partial(act, [rounds[number] for number in due]))
            for one in loads(pair, slot):
                one.wait()
            attend_back_pair(
                head_size, q_two.at[slot], k_two.at[slot], v_two.at[slot], do_two.at[slot],
                lse.at[pair], delta.at[pair], dq.at[:, lanes], dk.at[:, lanes], dv.at[:, lanes],
                bias, dk_sum, dv_sum, kt, dqt,
            )
            small[0, 4:5, lanes] = jnp.sum(dq[:, lanes].astype(F32), axis=0, keepdims=True)
            small[0, 5:6, lanes] = jnp.sum(dv[:, lanes].astype(F32), axis=0, keepdims=True)
            return carry

        lax.fori_loop(0, pairs, pair_step, 0)

    pl.run_scoped(
        attention,
        pltpu.VMEM((2, rows, 128), BF16),
        pltpu.VMEM((2, window, 128), BF16),
        pltpu.VMEM((2, window, 128), BF16),
        pltpu.VMEM((2, rows, 128), BF16),
        pltpu.VMEM((rows // Q_TILE, span, Q_TILE), F32),
        pltpu.VMEM((window, 128), F32),
        pltpu.VMEM((window, 128), F32),
        pltpu.VMEM((128, window), BF16),
        pltpu.VMEM((128, rows), F32),
    )

    def projections(a_two, hat_two, w_two):
        def loads(block, slot):
            here = pl.ds(pl.multiple_of(block * BACK_BLOCK, BACK_BLOCK), BACK_BLOCK)
            return [
                pltpu.make_async_copy(source, target.at[slot], stream.at[slot, k])
                for k, (source, target) in enumerate(
                    ((a_in.at[:, here], a_two), (hat_in.at[:, here], hat_two), (w_in.at[here], w_two))
                )
            ]

        for one in loads(0, 0):
            one.start()

        def block_step(block, carry):
            slot = lax.rem(block, 2)
            here = pl.ds(pl.multiple_of(block * BACK_BLOCK, BACK_BLOCK), BACK_BLOCK)

            def prefetch():
                for one in loads(block + 1, 1 - slot):
                    one.start()

            pl.when(block + 1 < blocks)(prefetch)
            for k, due in DURING_BLOCKS:
                pl.when(block == k)(functools.partial(act, [rounds[number] for number in due]))
            for one in loads(block, slot):
                one.wait()
            a_t = a_two[slot].T
            for k, made in enumerate((dot(a_t[:, before:], dq[...]), dot(a_t, dk[...]), dot(a_t, dv[...]))):
                dw[k, block] = made.astype(BF16).reshape(dw.shape[2:])
            for k in range(3):
                part = slice(k * rows, (k + 1) * rows)
                grad = dot(dk[part, :], w_two[slot, :, width : 2 * width], 1, 1) + dot(
                    dv[part, :], w_two[slot, :, 2 * width :], 1, 1
                )
                if k == 2:
                    grad = grad + dot(dq[...], w_two[slot, :, :width], 1, 1)
                    own_out[:, here] = grad
                else:
                    halo[k, :, here] = grad.astype(BF16)
                hat = hat_two[slot, part].astype(F32)
                small[0, 0:1, here] += jnp.sum(grad * hat, axis=0, keepdims=True)
                small[0, 3:4, here] += jnp.sum(grad, axis=0, keepdims=True)
            return carry

        lax.fori_loop(0, blocks, block_step, 0)

    pl.run_scoped(
        projections,
        pltpu.VMEM((2, window, BACK_BLOCK), BF16),
        pltpu.VMEM((2, window, BACK_BLOCK), BF16),
        pltpu.VMEM((2, BACK_BLOCK, 3 * width), BF16),
    )
    dq[...] = jnp.zeros_like(dq)
    clear = [
        (me.w >= 14, pltpu.make_async_copy(dq, back_out.at[0], local.at[count])),
        (me.c == 1, pltpu.make_async_copy(dq, back_out.at[1], local.at[count + 1])),
    ]
    for holds, one in clear:
        when(holds, one.start)
    act(rounds[AFTER_BLOCKS:])
    small_out[...] = small[5]
    for k, partner in enumerate(steps):
        moved = wire.copy(tiles.at[k], tiles.at[5 + k], ending + 8 + k, partner)
        moved.start()
        moved.wait()
        tiles[k + 1] = tiles[k] + tiles[5 + k]
    norm[...] = tiles[4]
    act(got_back)
    for one in wires:
        one.finish()
    for holds, one in clear:
        when(holds, one.wait)


def back(grads, attention, small, starts, stats, heads):
    queries, keys, values, outs_grad, normed, hat, weights = attention
    rows, width = queries.shape
    window = keys.shape[0]
    wide = lax.axis_size("wide")
    if lax.axis_size("dp") != 2 or wide != 16:
        return plain_back(grads, attention, small, starts, stats, heads)
    fc1, fc2, out = (one.shape for one in grads)
    tall, pieces = 4, []
    for array, shape in ((1, fc2), (0, fc1)):
        size = shape[1] // tall
        for k in range(tall):
            quarter = plane_share(size) if array == 0 else size // 4
            pieces.append((array, k * size, size, quarter, array, 0, len(pieces), len(pieces)))
    each = width // wide
    pieces.append((2, 0, each, each // 4, 2, 0, 0, 8))
    for k in range(3):
        pieces.append((3 + k, 0, each, each // 4, 3, k * width, 1 + k, AFTER_BLOCKS + k))
    pieces = tuple(pieces)
    sets = 2 * tall
    like = jax.ShapeDtypeStruct
    out_shape = [like(one.shape[1:], F32) for one in grads] + [
        like((each, 3 * width), F32),
        like((2, rows, width), BF16),
        like((rows, width), F32),
        like(small.shape, F32),
        like((8, 128), F32),
    ]
    scratch = []
    for number, _, size, quarter, *_ in pieces[:sets]:
        scratch += piece_buffers(size, grads[number].shape[2], quarter, grads[number].dtype)
    count = len(pieces)
    sems = RS_SEMS * count + 12
    return pl.pallas_call(
        functools.partial(back_kernel, pieces, sets, width // heads),
        out_shape=out_shape,
        in_specs=[HBM] * 10 + [VMEM] * 4,
        out_specs=[VMEM] * 4 + [HBM] + [VMEM] * 3,
        scratch_shapes=scratch
        + [
            pltpu.VMEM((rows, width), BF16),
            pltpu.VMEM((window, width), BF16),
            pltpu.VMEM((window, width), BF16),
            pltpu.VMEM((3, 4, 2, 2, each, width), BF16),
            pltpu.VMEM((2, rows, width), BF16),
            pltpu.VMEM((rows, width), BF16),
            pltpu.VMEM((10, *small.shape), F32),
            pltpu.VMEM((9, 8, 128), F32),
            pltpu.SemaphoreType.DMA((sems,)),
            pltpu.SemaphoreType.DMA((sems,)),
            pltpu.SemaphoreType.DMA((count + 2,)),
            pltpu.SemaphoreType.DMA((2, 4)),
            pltpu.SemaphoreType.REGULAR((count,)),
        ],
        compiler_params=pltpu.CompilerParams(
            collective_id=1, has_side_effects=True, vmem_limit_bytes=60 << 20
        ),
        name="back",
    )(
        *[one.reshape(4, 2, 2, *one.shape[1:]) for one in grads],
        queries, keys, values, outs_grad, normed, hat, weights, starts, *stats, small,
    )


def plain_back(grads, attention, small, starts, stats, heads):
    queries, keys, values, outs_grad, normed, hat, weights = attention
    rows, width = queries.shape
    wide = lax.axis_size("wide")
    dq, dk, dv = attend_back(queries, keys, values, outs_grad, *stats, starts, heads)
    earlier = dot(dk, weights[:, width : 2 * width], 1, 1) + dot(dv, weights[:, 2 * width :], 1, 1)
    own = earlier[-rows:] + dot(dq, weights[:, :width], 1, 1)
    earlier = earlier[:-rows]
    all_grad = jnp.concatenate([earlier, own])
    dw = [dot(normed[-rows:], dq, 0, 0), dot(normed, dk, 0, 0), dot(normed, dv, 0, 0)]
    grads = [*grads, jnp.concatenate(dw, axis=1).reshape(wide, -1, 3 * width)]
    totals = [
        lax.psum(
            lax.psum_scatter(one.astype(F32), "wide", scatter_dimension=0, tiled=False), "dp"
        )
        for one in grads
    ]
    sums = {
        0: jnp.sum(all_grad * hat.astype(F32), axis=0),
        3: jnp.sum(all_grad, axis=0),
        4: jnp.sum(dq.astype(F32), axis=0),
        5: jnp.sum(dv.astype(F32), axis=0),
    }
    small = jnp.concatenate(
        [sums[k][None] if k in sums else small[k : k + 1] for k in range(small.shape[0])]
    )
    low = earlier.astype(BF16).reshape(2, rows, width)
    returned = jnp.stack([from_behind(low[0], "wide", -2), from_behind(low[1], "wide", -1)])
    squares = lax.psum(sum(jnp.sum(one * one) for one in totals), "wide")
    tile = jnp.zeros((8, 128), F32).at[0, 0].set(squares)
    return [*totals, returned, own, lax.psum(small, ("dp", "wide")), tile]


F_TILE = 256


def grad_through_norm(grad, hat, scale, gain):
    scaled = grad * gain
    mean_plain = jnp.mean(scaled, axis=-1, keepdims=True)
    mean_cross = jnp.mean(scaled * hat, axis=-1, keepdims=True)
    return scale * (scaled - mean_plain - hat * mean_cross)


def down_sums(values):
    return jnp.sum(values, axis=0, keepdims=True)


def middle_kernel(
    head_size, c_ref, o_ref, x_ref, gy_ref, wo_ref, w1_ref, w2_ref, vec_ref, par_ref, scale_ref,
    out_ref, mid_ref, df_ref, a_ref, dz_ref, res_ref, do_ref, delta_ref, small_ref,
    act_all, slope, grad_all, stats, sums, x2, hat_post, hat_two, da,
):
    blocks, _, units = w1_ref.shape
    width = x_ref.shape[1]
    count = blocks * units

    @pl.when(pl.program_id(0) == 0)
    def _():
        sums[...] = jnp.zeros_like(sums)
        small_ref[...] = jnp.zeros_like(small_ref)

    stats[...] = jnp.zeros_like(stats)
    projected = dot(c_ref[...], wo_ref[...]) + vec_ref[6:7]
    value, hat, scale_post = layer_norm(projected, vec_ref[1:2], vec_ref[7:8])
    hat_post[...] = hat
    residual = x_ref[...].astype(F32) + value
    x2[...] = residual
    value, hat, scale_two = layer_norm(residual, vec_ref[2:3], vec_ref[8:9])
    hat_two[...] = hat
    a_ref[...] = value.astype(BF16)

    def columns(k):
        return pl.ds(pl.multiple_of(k * units, units), units)

    def forward(k, carry):
        pre = dot(a_ref[...], w1_ref[k]) + par_ref[2:3, columns(k)]
        half = 0.5 + 0.5 * lax.erf(pre * (0.5**0.5))
        value = pre * half
        act_all[k] = value
        slope[k] = half + pre * (jnp.exp(-0.5 * pre * pre) * (0.5 / jnp.pi) ** 0.5)
        stats[0] += lane_groups(value)
        stats[1] += lane_groups(value * value)
        return carry

    lax.fori_loop(0, blocks, forward, 0, unroll=2)
    mean = jnp.sum(stats[0], axis=1, keepdims=True) / count
    second = jnp.sum(stats[1], axis=1, keepdims=True) / count
    scale = lax.rsqrt(second - mean * mean + norm_epsilon)

    def middle(k, carry):
        here = columns(k)
        hat = (act_all[k] - mean) * scale
        mid_ref[:, here] = (hat * par_ref[0:1, here] + par_ref[1:2, here]).astype(BF16)
        down = dot(gy_ref[...], w2_ref[here, :], 1, 1)
        scaled = down * par_ref[0:1, here]
        act_all[k] = hat
        grad_all[k] = scaled
        stats[2] += lane_groups(scaled)
        stats[3] += lane_groups(scaled * hat)
        sums[0:1, here] += down_sums(down * hat)
        sums[1:2, here] += down_sums(down)
        return carry

    lax.fori_loop(0, blocks, middle, 0, unroll=2)
    plain = jnp.sum(stats[2], axis=1, keepdims=True) / count
    crossed = jnp.sum(stats[3], axis=1, keepdims=True) / count
    part = min(width, 512)
    for start in range(0, width, part):
        here = slice(start, start + part)
        total = dot(mid_ref[...], w2_ref[:, here])
        out_ref[:, here] = (x2[:, here] + (total + vec_ref[9:10, here])).astype(BF16)

    def backward(k, carry):
        here = columns(k)
        back = scale * (grad_all[k] - plain - act_all[k] * crossed) * slope[k]
        low = back.astype(BF16)
        df_ref[:, here] = low
        sums[2:3, here] += down_sums(low.astype(F32))
        return carry

    lax.fori_loop(0, blocks, backward, 0, unroll=2)
    da[...] = jnp.zeros_like(da)

    def back_out(k, carry):
        da[...] += dot(df_ref[:, columns(k)], w1_ref[k], 1, 1)
        return carry

    lax.fori_loop(0, blocks, back_out, 0, unroll=2)
    grad_in = gy_ref[...].astype(F32)
    rows_grad = da[...]
    residual_grad = grad_in + grad_through_norm(rows_grad, hat_two[...], scale_two, vec_ref[2:3])
    res_ref[...] = residual_grad
    dz = grad_through_norm(residual_grad, hat_post[...], scale_post, vec_ref[1:2]).astype(BF16)
    dz_ref[...] = dz
    for row, term in (
        (1, residual_grad * hat_post[...]),
        (2, rows_grad * hat_two[...]),
        (6, dz.astype(F32)),
        (7, residual_grad),
        (8, rows_grad),
        (9, grad_in),
    ):
        small_ref[row : row + 1] += down_sums(term)
    mixed_grad = dot(dz, wo_ref[...], 1, 1)
    outs = o_ref[...]
    low = (mixed_grad * scale_ref[...]).astype(BF16)
    do_ref[...] = low
    head_row = 10 + 3 * count // width
    small_ref[head_row : head_row + 1] += down_sums(mixed_grad * outs)
    heads = delta_ref.shape[0]
    lane = lax.broadcasted_iota(jnp.int32, (heads, width), 1)
    of = lax.broadcasted_iota(jnp.int32, (heads, width), 0) * head_size
    chosen = jnp.where(jnp.logical_and(lane >= of, lane < of + head_size), 1.0, 0.0)
    delta_ref[...] = lax.dot_general(
        chosen, low.astype(F32) * outs, (((1,), (1,)), ((), ())),
        precision=lax.Precision.HIGHEST, preferred_element_type=F32,
    )

    @pl.when(pl.program_id(0) == pl.num_programs(0) - 1)
    def _():
        for row in range(3):
            for start in range(0, count, width):
                at = 10 + (row * count + start) // width
                small_ref[at : at + 1] = sums[row : row + 1, start : start + width]


def middle_part(mixed, attended, tokens, out_grad, wo, w1, w2, vectors, par, scales, heads):
    rows, width = tokens.shape
    blocks, _, units = w1.shape
    hidden = blocks * units
    by_tile = lambda columns: pl.BlockSpec((F_TILE, columns), lambda t: (t, 0))
    once = lambda one: pl.BlockSpec(
        one.shape, lambda t: (0,) * len(one.shape), pipeline_mode=pl.Buffered(1)
    )
    small_rows = -(-(11 + 3 * hidden // width) // 8) * 8
    like = jax.ShapeDtypeStruct
    return pl.pallas_call(
        functools.partial(middle_kernel, width // heads),
        grid=(rows // F_TILE,),
        in_specs=[by_tile(width)] * 4 + [once(one) for one in (wo, w1, w2, vectors, par, scales)],
        out_specs=[
            by_tile(width),
            by_tile(hidden),
            by_tile(hidden),
            by_tile(width),
            by_tile(width),
            by_tile(width),
            by_tile(width),
            pl.BlockSpec((heads, F_TILE), lambda t: (0, t)),
            pl.BlockSpec((small_rows, width), lambda t: (0, 0)),
        ],
        out_shape=[
            like((rows, width), BF16),
            like((rows, hidden), BF16),
            like((rows, hidden), BF16),
            like((rows, width), BF16),
            like((rows, width), BF16),
            like((rows, width), F32),
            like((rows, width), BF16),
            like((heads, rows), F32),
            like((small_rows, width), F32),
        ],
        scratch_shapes=[pltpu.VMEM((blocks, F_TILE, units), F32)] * 3
        + [pltpu.VMEM((4, F_TILE, 128), F32), pltpu.VMEM((8, hidden), F32)]
        + [pltpu.VMEM((F_TILE, width), F32)] * 4,
        compiler_params=pltpu.CompilerParams(vmem_limit_bytes=60 << 20),
        name="middle_part",
    )(mixed, attended, tokens, out_grad, wo, w1, w2, vectors, par, scales)


def weights_kernel(a_ref, gy_ref, c_ref, dz_ref, mid_ref, df_ref, dw1_ref, dw2_ref, dwo_ref, a_t):
    @pl.when(pl.program_id(0) == 0)
    def _():
        a_t[...] = a_ref[...].T
        dwo_ref[...] = dot(c_ref[...].T, dz_ref[...]).astype(BF16)

    dw1_ref[0] = dot(a_t[...], df_ref[...]).astype(BF16)
    dw2_ref[0] = dot(mid_ref[...].T, gy_ref[...]).astype(BF16)


def weight_grads(rows, out_grad, mixed, proj_grad, middle, pre_grad, blocks):
    tokens, width = rows.shape
    units = middle.shape[1] // blocks
    whole = pl.BlockSpec((tokens, width), lambda k: (0, 0))
    block = pl.BlockSpec((tokens, units), lambda k: (0, k))
    return pl.pallas_call(
        weights_kernel,
        grid=(blocks,),
        in_specs=[whole] * 4 + [block, block],
        out_specs=[
            pl.BlockSpec((1, width, units), lambda k: (k, 0, 0)),
            pl.BlockSpec((1, units, width), lambda k: (k, 0, 0)),
            pl.BlockSpec((width, width), lambda k: (0, 0)),
        ],
        out_shape=[
            jax.ShapeDtypeStruct((blocks, width, units), BF16),
            jax.ShapeDtypeStruct((blocks, units, width), BF16),
            jax.ShapeDtypeStruct((width, width), BF16),
        ],
        scratch_shapes=[pltpu.VMEM((width, tokens), BF16)],
        compiler_params=pltpu.CompilerParams(vmem_limit_bytes=40 << 20),
        name="weight_grads",
    )(rows, out_grad, mixed, proj_grad, middle, pre_grad)


def plane_share(rows):
    return rows // 16 * 3 // 8 * 16


def unpack_small(full, vector_shape, hidden_shape):
    wide = full.shape[0]
    count, each = vector_shape
    vectors = full[:, :count, :each].transpose(1, 0, 2).reshape(count, -1)
    rows, size = hidden_shape
    if size % 128 == 0:
        hidden = full[:, count:].reshape(wide, rows, size)
    else:
        hidden = full[:, count:, :size]
    hidden = hidden.transpose(1, 0, 2).reshape(rows, -1)
    return vectors.astype(F32), hidden.astype(F32)


def regroup(blocks, units):
    slabs, rows, columns = blocks.shape
    join = max(1, units // columns)
    if join == 1:
        return blocks
    return blocks.reshape(slabs // join, join, rows, columns).transpose(0, 2, 1, 3).reshape(
        slabs // join, rows, join * columns
    )


def ungroup(blocks, columns):
    slabs, rows, units = blocks.shape
    join = units // columns
    if join == 1:
        return blocks
    return blocks.reshape(slabs, rows, join, columns).transpose(0, 2, 1, 3).reshape(
        slabs * join, rows, columns
    )


def body(
    inputs,
    out_grad,
    doc_lengths,
    step_count,
    qkv_weight,
    qkv_first,
    qkv_second,
    out_weight,
    out_first,
    out_second,
    fc1_weight,
    fc1_first,
    fc1_second,
    fc2_weight,
    fc2_first,
    fc2_second,
    model_vectors,
    vectors_first,
    vectors_second,
    hidden_vectors,
    hidden_first,
    hidden_second,
    head_scale,
    head_first,
    head_second,
):
    tokens_dev = inputs.shape[0]
    width = inputs.shape[1]
    heads_count = head_scale.shape[0]
    head_size = width // heads_count
    wide = lax.axis_size("wide")
    hidden_width = hidden_vectors.shape[1] * wide

    fc1_rows, fc2_rows = fc1_weight.shape[0], fc2_weight.shape[0]
    qkv_rows, out_rows = qkv_weight.shape[0], out_weight.shape[0]
    small = jnp.concatenate(
        [
            jnp.pad(model_vectors, ((0, 0), (0, max(0, 128 - model_vectors.shape[1])))),
            hidden_vectors.reshape(-1, min(128, hidden_vectors.shape[1])),
        ]
        if hidden_vectors.shape[1] % 128 == 0
        else [
            jnp.pad(one, ((0, 0), (0, 128 - one.shape[1]))) for one in (model_vectors, hidden_vectors)
        ]
    ).astype(BF16)
    heads_low = lax.optimization_barrier(head_scale.astype(BF16)).astype(F32)
    starts = doc_starts(
        doc_lengths, lax.axis_index("dp"), lax.axis_index("wide") * tokens_dev, tokens_dev
    )
    starts = jnp.maximum(starts - (lax.axis_index("wide") - 2) * tokens_dev, 0).reshape(1, -1)
    scales = jnp.repeat(heads_low, head_size).reshape(1, width)
    gathered = front(
        [
            small,
            qkv_weight.astype(BF16),
            out_weight.astype(BF16),
            fc1_weight.astype(BF16),
            fc2_weight.astype(BF16),
        ],
        tuple(plane_share(one) for one in (0, qkv_rows, out_rows, fc1_rows, fc2_rows)),
        inputs,
        starts,
        scales,
        heads_count,
    )
    qkv_full, out_full, fc1_full, fc2_full, hat_low, normed_low = gathered[:6]
    queries, keys_all, values_all, attended, mixed_low, log_totals, vectors, hidden_par = gathered[6:]
    fc2_full = fc2_full.reshape(hidden_width, width)
    output, middle_low, pre_low, rows_low, proj_low, residual_grad, attended_low, delta, small_grad = (
        middle_part(
            mixed_low,
            attended,
            inputs,
            out_grad,
            out_full.reshape(width, width),
            regroup(fc1_full, 256),
            fc2_full,
            vectors,
            hidden_par,
            scales,
            heads_count,
        )
    )
    fc1_grad, fc2_grad, out_weight_grad = weight_grads(
        rows_low, out_grad, mixed_low, proj_low, middle_low, pre_low, hidden_width // 256
    )
    fc1_part, fc2_part, out_part, qkv_part, halo_back, own_grad, small_total, norm_tile = back(
        [
            ungroup(fc1_grad, fc1_weight.shape[1]),
            fc2_grad.reshape(wide, -1, width),
            out_weight_grad.reshape(wide, -1, width),
        ],
        (
            queries,
            keys_all,
            values_all,
            attended_low,
            normed_low,
            hat_low.reshape(-1, width),
            qkv_full.reshape(width, 3 * width),
        ),
        small_grad,
        starts,
        (log_totals, delta.reshape(log_totals.shape)),
        heads_count,
    )
    total_grad = own_grad + halo_back[0].astype(F32) + halo_back[1].astype(F32)
    _, hat_in, scale_in = layer_norm(inputs.astype(F32), vectors[0], vectors[3])
    input_grad = residual_grad + grad_through_norm(total_grad, hat_in, scale_in, vectors[0])
    vector_rows = model_vectors.shape[0]
    head_row = vector_rows + hidden_vectors.shape[0] * hidden_width // width
    vector_total = small_total[:vector_rows]
    hidden_total = small_total[vector_rows:head_row].reshape(hidden_vectors.shape[0], hidden_width)
    head_total = jnp.sum(small_total[head_row].reshape(heads_count, head_size), axis=1)
    place = lax.axis_index("wide")
    vector_part = lax.dynamic_slice_in_dim(
        vector_total, place * model_vectors.shape[1], model_vectors.shape[1], 1
    )
    hidden_part = lax.dynamic_slice_in_dim(
        hidden_total, place * hidden_vectors.shape[1], hidden_vectors.shape[1], 1
    )
    small_square = jnp.sum(small_total[:head_row] ** 2) + jnp.sum(head_total**2)
    grad_norm = jnp.sqrt(jnp.sum(norm_tile) + small_square)
    factor = jnp.minimum(1.0, clip_limit / (grad_norm + 1e-06))
    step = step_count[0].astype(F32)
    grads = (qkv_part, out_part, fc1_part, fc2_part, vector_part, hidden_part, head_total)
    params = (
        qkv_weight,
        out_weight,
        fc1_weight,
        fc2_weight,
        model_vectors,
        hidden_vectors,
        head_scale,
    )
    firsts = (qkv_first, out_first, fc1_first, fc2_first, vectors_first, hidden_first, head_first)
    seconds = (
        qkv_second,
        out_second,
        fc1_second,
        fc2_second,
        vectors_second,
        hidden_second,
        head_second,
    )
    rates = (
        matrix_rate,
        matrix_rate,
        matrix_rate,
        matrix_rate,
        vector_rate,
        vector_rate,
        vector_rate,
    )
    decays = (weight_decay, weight_decay, weight_decay, weight_decay, 0.0, 0.0, 0.0)
    updated = []
    for number in range(7):
        updated.extend(
            adam_step(
                grads[number] * factor,
                params[number],
                firsts[number],
                seconds[number],
                step,
                rates[number],
                decays[number],
            )
        )
    return (
        output,
        input_grad,
        grad_norm.reshape(1),
        updated[0],
        updated[1],
        updated[2],
        updated[3],
        updated[4],
        updated[5],
        updated[6],
        updated[7],
        updated[8],
        updated[9],
        updated[10],
        updated[11],
        updated[12],
        updated[13],
        updated[14],
        updated[15],
        updated[16],
        updated[17],
        updated[18],
        updated[19],
        updated[20],
    )


def solution(mesh):
    placed = (
        P(("dp", "wide"), None),
        P(("dp", "wide"), None),
        P(),
        P(),
        P("wide", None),
        P("wide", None),
        P("wide", None),
        P("wide", None),
        P("wide", None),
        P("wide", None),
        P(None, "wide"),
        P(None, "wide"),
        P(None, "wide"),
        P("wide", None),
        P("wide", None),
        P("wide", None),
        P(None, "wide"),
        P(None, "wide"),
        P(None, "wide"),
        P(None, "wide"),
        P(None, "wide"),
        P(None, "wide"),
        P(),
        P(),
        P(),
    )
    return jax.shard_map(
        body,
        mesh=mesh,
        in_specs=placed,
        out_specs=(
            P(("dp", "wide"), None),
            P(("dp", "wide"), None),
            P(),
            P("wide", None),
            P("wide", None),
            P("wide", None),
            P("wide", None),
            P("wide", None),
            P("wide", None),
            P(None, "wide"),
            P(None, "wide"),
            P(None, "wide"),
            P("wide", None),
            P("wide", None),
            P("wide", None),
            P(None, "wide"),
            P(None, "wide"),
            P(None, "wide"),
            P(None, "wide"),
            P(None, "wide"),
            P(None, "wide"),
            P(),
            P(),
            P(),
        ),
        check_vma=False,
    )
```

```python
import functools

import jax
import jax.numpy as jnp
from jax import lax
from jax.experimental import pallas as pl
from jax.experimental.pallas import tpu as pltpu
from jax.sharding import PartitionSpec as P

DOC_MOST = 1024
MESH = pl.DeviceIdType.MESH
HBM = pl.BlockSpec(memory_space=pltpu.HBM)
VMEM = pl.BlockSpec(memory_space=pltpu.VMEM)
BF16 = jnp.bfloat16
F32 = jnp.float32

norm_epsilon = 1e-05
clip_limit = 1.0
first_decay = 0.9
second_decay = 0.98
adam_epsilon = 1e-08
matrix_rate = 0.1
vector_rate = 0.4
weight_decay = 0.1
masked_score = -1e30


def layer_norm(values_in, gain, shift):
    center = values_in - jnp.mean(values_in, axis=-1, keepdims=True)
    variance = jnp.mean(center * center, axis=-1, keepdims=True)
    scale = lax.rsqrt(variance + norm_epsilon)
    normed = center * scale
    return (normed * gain + shift, normed, scale)


def doc_starts(doc_lengths, row, first, count):
    ends = lax.dynamic_slice_in_dim(jnp.cumsum(doc_lengths, axis=1), row, 1, 0)[0]
    places = first + jnp.arange(count, dtype=jnp.int32)
    return jnp.max(jnp.where(ends[None, :] <= places[:, None], ends[None, :], 0), axis=1)


def adam_step(grad, weight, first, second, step, rate, decay):
    first_new = first_decay * first + (1.0 - first_decay) * grad
    second_new = second_decay * second + (1.0 - second_decay) * grad * grad
    fix_one = 1.0 - jnp.power(jnp.float32(first_decay), step)
    fix_two = 1.0 - jnp.power(jnp.float32(second_decay), step)
    direction = first_new / fix_one / (jnp.sqrt(second_new / fix_two) + adam_epsilon)
    weight_new = weight - rate * (direction + decay * weight)
    return (first_new, second_new, weight_new)


def from_behind(shard, axis, by):
    count = lax.axis_size(axis)
    pairs = [(i, i + by) for i in range(count) if 0 <= i + by < count]
    return lax.ppermute(shard, axis, pairs)


def dot(a, b, left=1, right=0):
    return lax.dot_general(
        a, b, (((left,), (right,)), ((), ())), preferred_element_type=F32
    )


Q_TILE = 256


def split_pair(pair, size):
    lane = lax.broadcasted_iota(jnp.int32, pair.shape, 1)
    zero = jnp.zeros_like(pair)
    return jnp.where(lane < size, pair, zero), jnp.where(lane < size, zero, pair)


def fill_mask(starts, bias, tokens, span, keys_before):
    for tile in range(tokens // Q_TILE):
        query = lax.broadcasted_iota(jnp.int32, (span, Q_TILE), 1) + tile * Q_TILE + keys_before
        key = lax.broadcasted_iota(jnp.int32, (span, Q_TILE), 0) + tile * Q_TILE
        first = starts[:, tile * Q_TILE : (tile + 1) * Q_TILE]
        seen = jnp.logical_and(key <= query, key >= first)
        bias[tile] = jnp.where(seen, 0.0, masked_score)


def attend_pair(size, q_ref, k_ref, v_ref, scale_ref, o_ref, c_ref, lse_ref, bias, vt, ot):
    tokens, window = q_ref.shape[0], k_ref.shape[0]
    span = window - tokens + Q_TILE
    vt[...] = v_ref[...].T
    for tile in range(tokens // Q_TILE):
        rows = slice(tile * Q_TILE, (tile + 1) * Q_TILE)
        keys = slice(tile * Q_TILE, tile * Q_TILE + span)
        k_pair = k_ref[keys, :]
        for head, q_one in enumerate(split_pair(q_ref[rows, :], size)):
            scores = dot(k_pair, q_one, 1, 1) + bias[tile]
            highest = jnp.max(scores, axis=0, keepdims=True)
            powers = jnp.exp(scores - highest)
            total = jnp.sum(powers, axis=0, keepdims=True)
            probs = (powers * (1.0 / total)).astype(BF16)
            lse_ref[head : head + 1, rows] = highest + jnp.log(total)
            part = slice(head * size, (head + 1) * size)
            ot[part, rows] = dot(vt[part, keys], probs)
    attended = ot[...].T
    o_ref[...] = attended
    c_ref[...] = (attended * scale_ref[...]).astype(BF16)


def attend_kernel(size, starts, scale_ref, q_ref, k_ref, v_ref, o_ref, c_ref, lse_ref, bias, vt, ot):
    tokens, window = q_ref.shape[0], k_ref.shape[0]
    before = window - tokens

    @pl.when(pl.program_id(0) == 0)
    def _():
        fill_mask(starts, bias, tokens, before + Q_TILE, before)

    attend_pair(size, q_ref, k_ref, v_ref, scale_ref, o_ref, c_ref, lse_ref.at[0], bias, vt, ot)


def attend(queries, keys, values, starts, scales, heads):
    tokens, width = queries.shape
    window = keys.shape[0]
    pairs = heads // 2
    lanes = width // pairs
    span = window - tokens + Q_TILE
    by_rows = lambda rows: pl.BlockSpec((rows, lanes), lambda p: (0, p))
    return pl.pallas_call(
        functools.partial(attend_kernel, width // heads),
        grid=(pairs,),
        in_specs=[
            pl.BlockSpec((1, tokens), lambda p: (0, 0)),
            by_rows(1),
            by_rows(tokens),
            by_rows(window),
            by_rows(window),
        ],
        out_specs=[
            by_rows(tokens),
            by_rows(tokens),
            pl.BlockSpec((1, 2, tokens), lambda p: (p, 0, 0)),
        ],
        out_shape=[
            jax.ShapeDtypeStruct((tokens, width), F32),
            jax.ShapeDtypeStruct((tokens, width), BF16),
            jax.ShapeDtypeStruct((pairs, 2, tokens), F32),
        ],
        scratch_shapes=[
            pltpu.VMEM((tokens // Q_TILE, span, Q_TILE), F32),
            pltpu.VMEM((lanes, window), BF16),
            pltpu.VMEM((lanes, tokens), F32),
        ],
        compiler_params=pltpu.CompilerParams(vmem_limit_bytes=40 << 20),
        name="attend",
    )(starts, scales, queries, keys, values)


def attend_back_pair(
    size, q_ref, k_ref, v_ref, do_ref, lse_ref, delta_ref, dq_ref, dk_ref, dv_ref, bias, dk_sum, dv_sum, kt, dqt
):
    tokens, window = q_ref.shape[0], k_ref.shape[0]
    span = window - tokens + Q_TILE
    kt[...] = k_ref[...].T
    dk_sum[...] = jnp.zeros_like(dk_sum)
    dv_sum[...] = jnp.zeros_like(dv_sum)
    for tile in range(tokens // Q_TILE):
        rows = slice(tile * Q_TILE, (tile + 1) * Q_TILE)
        keys = slice(tile * Q_TILE, tile * Q_TILE + span)
        k_pair, v_pair = k_ref[keys, :], v_ref[keys, :]
        for head, (q_one, do_one) in enumerate(
            zip(split_pair(q_ref[rows, :], size), split_pair(do_ref[rows, :], size))
        ):
            scores = dot(k_pair, q_one, 1, 1) + bias[tile]
            probs = jnp.exp(scores - lse_ref[head : head + 1, rows])
            grads = dot(v_pair, do_one, 1, 1) - delta_ref[head : head + 1, rows]
            low = (probs * grads).astype(BF16)
            dv_sum[keys, :] += dot(probs.astype(BF16), do_one)
            dk_sum[keys, :] += dot(low, q_one)
            part = slice(head * size, (head + 1) * size)
            dqt[part, rows] = dot(kt[part, keys], low)
    dq_ref[...] = (dqt[...].T * size ** (-0.5)).astype(BF16)
    dk_ref[...] = dk_sum[...].astype(BF16)
    dv_ref[...] = dv_sum[...].astype(BF16)


def attend_back_kernel(
    size, starts, q_ref, k_ref, v_ref, do_ref, lse_ref, delta_ref, dq_ref, dk_ref, dv_ref, bias, *scratch
):
    tokens, window = q_ref.shape[0], k_ref.shape[0]
    before = window - tokens

    @pl.when(pl.program_id(0) == 0)
    def _():
        fill_mask(starts, bias, tokens, before + Q_TILE, before)

    attend_back_pair(
        size, q_ref, k_ref, v_ref, do_ref, lse_ref.at[0], delta_ref.at[0], dq_ref, dk_ref, dv_ref, bias, *scratch
    )


def attend_back(queries, keys, values, outs_grad, lse, delta, starts, heads):
    tokens, width = queries.shape
    window = keys.shape[0]
    pairs = heads // 2
    lanes = width // pairs
    span = window - tokens + Q_TILE
    by_rows = lambda rows: pl.BlockSpec((rows, lanes), lambda p: (0, p))
    stats = pl.BlockSpec((1, 2, tokens), lambda p: (p, 0, 0))
    return pl.pallas_call(
        functools.partial(attend_back_kernel, width // heads),
        grid=(pairs,),
        in_specs=[
            pl.BlockSpec((1, tokens), lambda p: (0, 0)),
            by_rows(tokens),
            by_rows(window),
            by_rows(window),
            by_rows(tokens),
            stats,
            stats,
        ],
        out_specs=[
            by_rows(tokens),
            by_rows(window),
            by_rows(window),
        ],
        out_shape=[
            jax.ShapeDtypeStruct((tokens, width), BF16),
            jax.ShapeDtypeStruct((window, width), BF16),
            jax.ShapeDtypeStruct((window, width), BF16),
        ],
        scratch_shapes=[
            pltpu.VMEM((tokens // Q_TILE, span, Q_TILE), F32),
            pltpu.VMEM((window, lanes), F32),
            pltpu.VMEM((window, lanes), F32),
            pltpu.VMEM((lanes, window), BF16),
            pltpu.VMEM((lanes, tokens), F32),
        ],
        compiler_params=pltpu.CompilerParams(vmem_limit_bytes=40 << 20),
        name="attend_back",
    )(starts, queries, keys, values, outs_grad, lse, delta)


class Place:
    def __init__(self):
        self.y = lax.axis_index("dp")
        self.w = lax.axis_index("wide")
        self.z = self.w // 4
        self.x = (self.w // 2) % 2
        self.c = self.w % 2

    def slab(self, z, x, c):
        return z * 4 + x * 2 + c

    def wide(self, w):
        return (self.y, w)

    def core_mate(self):
        return self.wide(self.slab(self.z, self.x, 1 - self.c))

    def x_mate(self):
        return self.wide(self.slab(self.z, 1 - self.x, self.c))

    def y_mate(self):
        return (1 - self.y, self.w)

    def up(self):
        return self.wide(lax.rem(self.w + 4, 16))

    def down(self):
        return self.wide(lax.rem(self.w + 12, 16))


def greet(me, extra=()):
    barrier = pltpu.get_barrier_semaphore()

    def hello(target):
        pl.semaphore_signal(barrier, inc=1, device_id=target, device_id_type=MESH)

    always = [me.core_mate(), me.x_mate(), me.y_mate(), *extra]
    sometimes = [
        (me.z < 3, me.up()),
        (me.z > 0, me.down()),
        (me.w < 14, me.wide(lax.rem(me.w + 2, 16))),
        (me.w >= 2, me.wide(lax.rem(me.w + 14, 16))),
    ]
    for target in always:
        hello(target)
    for holds, target in sometimes:
        pl.when(holds)(functools.partial(hello, target))
    count = len(always) + sum(holds.astype(jnp.int32) for holds, _ in sometimes)
    pl.semaphore_wait(barrier, count)


class Wire:
    def __init__(self, send, recv):
        self.send, self.recv = send, recv
        self.planned = []

    def copy(self, source, target, index, device):
        return pltpu.make_async_remote_copy(
            src_ref=source,
            dst_ref=target,
            send_sem=self.send.at[index],
            recv_sem=self.recv.at[index],
            device_id=device,
            device_id_type=MESH,
        )

    def put(self, source, target, index, device, holds=None):
        moved = self.copy(source, target, index, device)
        self.planned.append((holds, moved))
        return lambda: when(holds, moved.start)

    def got(self, target, index, device, holds=None):
        moved = self.copy(target, target, index, device)
        return lambda: when(holds, moved.wait_recv)

    def finish(self):
        for holds, moved in self.planned:
            when(holds, moved.wait_send)


def act(actions):
    for one in actions:
        one()


def both(*conditions):
    held = [one for one in conditions if one is not None]
    total = held[0] if held else None
    for one in held[1:]:
        total = jnp.logical_and(total, one)
    return total


def when(holds, action):
    if holds is None:
        action()
    else:
        pl.when(holds)(action)


AG_SEMS = 44


def gather_ticks(me, wire, base, own, full, third, side_first):
    rows = own.shape[0]
    plane = (
        pl.ds(pl.multiple_of(me.y * third, 16), rows - third) if third else pl.ds(0, rows)
    )
    share = pl.ds(pl.multiple_of(me.y * (rows - third), 16), third) if third else None
    other = pl.ds(pl.multiple_of((1 - me.y) * (rows - third), 16), third) if third else None
    my_slab = me.slab(me.z, me.x, me.c)
    ups, downs, xs, ys, cs, ts, far_ups, far_downs = (
        base + k for k in (0, 4, 8, 12, 20, 28, 36, 40)
    )
    mine = me.z * 2 + me.x

    def pass_on(z, x, holds):
        slab = me.slab(z, x, me.c)
        place = z * 2 + x
        block = full.at[slab, plane]
        actions = []
        if third:
            piece = full.at[slab, share]
            actions.append(wire.put(piece, piece, ys + place, me.y_mate(), holds))
        actions.append(wire.put(block, block, cs + place, me.core_mate(), holds))
        return actions

    def arrivals(away):
        for z, holds, onward, follow, above in (
            (me.z - away, me.z - away >= 0, me.up(), me.z < 3, False),
            (me.z + away, me.z + away <= 3, me.down(), me.z > 0, True),
        ):
            yield lax.rem(z + 4, 4), holds, onward, follow, above

    goal = full.at[my_slab, plane]
    ticks = {
        "own": [
            wire.put(own.at[plane], goal, ups + me.z, me.up(), me.z < 3),
            wire.put(own.at[plane], goal, downs + me.z, me.down(), me.z > 0),
            wire.put(own.at[plane], goal, xs + me.z, me.x_mate()),
            wire.put(own, full.at[my_slab], cs + mine, me.core_mate()),
        ]
    }
    for tick in range(1, 5):
        actions = []
        if tick < 4:
            for z, holds, onward, follow, above in arrivals(tick):
                sems = downs if above else ups
                block = full.at[me.slab(z, me.x, me.c), plane]
                actions.append(wire.got(block, sems + z, onward, holds))
                actions.append(wire.put(block, block, sems + z, onward, both(holds, follow)))
                if not side_first:
                    actions.append(wire.put(block, block, xs + z, me.x_mate(), holds))
                actions += pass_on(z, me.x, holds)
        if side_first and tick == 1:
            block = full.at[me.slab(me.z, 1 - me.x, me.c), plane]
            actions.append(wire.got(block, xs + me.z, me.x_mate()))
            actions.append(wire.put(block, block, far_ups + me.z, me.up(), me.z < 3))
            actions.append(wire.put(block, block, far_downs + me.z, me.down(), me.z > 0))
            actions += pass_on(me.z, 1 - me.x, None)
        elif side_first:
            for z, holds, onward, follow, above in arrivals(tick - 1):
                sems = far_downs if above else far_ups
                block = full.at[me.slab(z, 1 - me.x, me.c), plane]
                actions.append(wire.got(block, sems + z, onward, holds))
                actions.append(wire.put(block, block, sems + z, onward, both(holds, follow)))
                actions += pass_on(z, 1 - me.x, holds)
        ticks["line", tick] = actions
    for away in range(4):
        actions = []
        if not side_first:
            cases = arrivals(away) if away else [(me.z, None, None, None, None)]
            for z, holds, *_ in cases:
                block = full.at[me.slab(z, 1 - me.x, me.c), plane]
                actions.append(wire.got(block, xs + z, me.x_mate(), holds))
                actions += pass_on(z, 1 - me.x, holds)
        ticks["side", away] = actions
    actions = []
    if third:
        for k in range(1, 8):
            place = lax.rem(mine + k, 8)
            piece = full.at[me.slab(place // 2, place % 2, me.c), other]
            actions.append(wire.got(piece, ys + place, me.y_mate()))
            actions.append(wire.put(piece, piece, ts + place, me.core_mate()))
    ticks["shares"] = actions
    actions = [wire.got(full.at[me.slab(me.z, me.x, 1 - me.c)], cs + mine, me.core_mate())]
    for k in range(1, 8):
        place = lax.rem(mine + k, 8)
        slab = me.slab(place // 2, place % 2, 1 - me.c)
        actions.append(wire.got(full.at[slab, plane], cs + place, me.core_mate()))
        if third:
            actions.append(wire.got(full.at[slab, other], ts + place, me.core_mate()))
    ticks["end"] = actions
    return ticks


FRONT_BLOCK = 256
FRONT_TICKS = (
    (2, (("line", 3),)),
    (5, (("line", 4), ("side", 0))),
    (7, (("side", 1),)),
)
FRONT_LAST = (("side", 2), ("side", 3))


def front_kernel(thirds, head_size, *refs):
    owns, (tokens, starts, scale_ref) = refs[:5], refs[5:8]
    fulls, outs = refs[8:12], refs[12:19]
    xs_out, a_out, q_out, k_out, v_out, o_out, c_out = outs
    lse_ref, vecs, par = refs[19:22]
    (xs, a_all, qkv, q_all, k_all, v_all, o_all, c_all, small, bias, vt, ot, send, recv, local) = refs[22:]
    me = Place()
    count = len(owns)
    width = tokens.shape[1]
    rows = tokens.shape[0]
    window = 3 * rows
    before = window - rows
    span = before + Q_TILE
    landings = (small, qkv, *fulls[1:])
    keep = [
        pltpu.make_async_copy(own, full.at[me.w], local.at[k])
        for k, (own, full) in enumerate(zip(owns, landings))
    ] + [pltpu.make_async_copy(tokens, xs.at[2], local.at[count])]
    for one in keep:
        one.start()

    def clear(slot):
        xs[slot] = jnp.zeros((rows, width), BF16)

    pl.when(me.w < 2)(functools.partial(clear, 0))
    pl.when(me.w < 1)(functools.partial(clear, 1))
    wire = Wire(send, recv)
    first, second = AG_SEMS * count, AG_SEMS * count + 1
    ticks = [
        gather_ticks(me, wire, AG_SEMS * k, own, landing, third, k == 4)
        for k, (own, landing, third) in enumerate(zip(owns, landings, thirds))
    ]
    send_block = wire.put(tokens, xs.at[0], first, me.wide(lax.rem(me.w + 2, 16)), me.w < 14)
    send_near = wire.put(tokens, xs.at[1], second, me.core_mate(), me.c == 0)
    get_block = wire.got(xs.at[0], first, me.core_mate(), me.w >= 2)
    passes = both(me.c == 1, me.w >= 2)
    pass_block = wire.copy(xs.at[0], xs.at[1], second, me.core_mate())
    get_near = wire.got(xs.at[1], second, me.core_mate(), me.w >= 1)
    greet(me)
    early, late = ticks[:2], ticks[2:]

    def go(group, *names):
        for name in names:
            for one in group:
                act(one[name])

    go(early, "own", ("line", 1), ("line", 2), ("line", 3))
    act(late[2]["own"])
    send_block()
    send_near()
    go(late[:2], "own")
    fill_mask(starts, bias, rows, span, before)
    go(early, ("side", 0), ("side", 1), ("side", 2), ("side", 3), "shares", "end")
    for one in keep:
        one.wait()
    shared = [pltpu.make_async_copy(qkv, fulls[0], local.at[1])]
    for one in shared:
        one.start()

    lane = lax.broadcasted_iota(jnp.int32, (16, 128), 1)
    for pair in range(8):
        even = small[2 * pair].astype(F32)
        odd = pltpu.roll(small[2 * pair + 1].astype(F32), 64, 1)
        vecs[:, pair * 128 : (pair + 1) * 128] = jnp.where(lane < 64, even, odd)
    for slab in range(16):
        values = small[slab].astype(F32)
        for row in range(3):
            for half in range(2):
                at = slab * 256 + half * 128
                par[row : row + 1, at : at + 128] = values[10 + 2 * row + half][None]

    def project(first_column, column, a_rows):
        weights = qkv[:, :, pl.ds(first_column + column, FRONT_BLOCK)].reshape(width, FRONT_BLOCK)
        return dot(a_rows, weights)

    per = rows // FRONT_BLOCK

    def normalize(number, carry):
        here = pl.ds(pl.multiple_of(lax.rem(number, per) * FRONT_BLOCK, FRONT_BLOCK), FRONT_BLOCK)
        there = pl.ds(pl.multiple_of(number * FRONT_BLOCK, FRONT_BLOCK), FRONT_BLOCK)
        value, hat, _ = layer_norm(xs[number // per, here].astype(F32), vecs[0:1], vecs[3:4])
        xs[number // per, here] = hat.astype(BF16)
        low = value.astype(BF16)
        a_all[there] = low
        for column in range(0, width, FRONT_BLOCK):
            columns = slice(column, column + FRONT_BLOCK)
            k_all[there, columns] = project(width, column, low).astype(BF16)
            v_all[there, columns] = (
                project(2 * width, column, low) + vecs[5:6, columns]
            ).astype(BF16)
        return carry

    lax.fori_loop(2 * per, 3 * per, normalize, 0)
    for number in range(per):
        here = pl.ds(number * FRONT_BLOCK, FRONT_BLOCK)
        low = a_all[before + number * FRONT_BLOCK : before + (number + 1) * FRONT_BLOCK]
        for column in range(0, width, FRONT_BLOCK):
            columns = slice(column, column + FRONT_BLOCK)
            query = (project(0, column, low) + vecs[4:5, columns]).astype(BF16)
            q_all[here, columns] = query * jnp.asarray(head_size ** (-0.5), BF16)
    go(late, ("line", 1))
    get_block()
    when(passes, pass_block.start)
    get_near()
    when(passes, pass_block.wait_send)
    lax.fori_loop(0, 2 * per, normalize, 0)
    go(late, ("line", 2))
    kept = [
        pltpu.make_async_copy(one, out, local.at[2 + k])
        for k, (one, out) in enumerate(
            ((a_all, a_out), (q_all, q_out), (k_all, k_out), (v_all, v_out), (xs, xs_out))
        )
    ]
    for one in kept:
        one.start()

    def pair_step(pair, carry):
        lanes = pl.ds(pl.multiple_of(pair * 128, 128), 128)
        attend_pair(
            head_size, q_all.at[:, lanes], k_all.at[:, lanes], v_all.at[:, lanes],
            scale_ref.at[:, lanes], o_all.at[:, lanes], c_all.at[:, lanes], lse_ref.at[pair], bias, vt, ot,
        )
        for due, names in FRONT_TICKS:
            pl.when(pair == due)(functools.partial(go, late, *names))
        return carry

    lax.fori_loop(0, width // 128, pair_step, 0)
    results = [
        pltpu.make_async_copy(o_all, o_out, local.at[7]),
        pltpu.make_async_copy(c_all, c_out, local.at[8]),
    ]
    for one in results:
        one.start()
    go(late, *FRONT_LAST, "shares", "end")
    wire.finish()
    for one in shared + kept + results:
        one.wait()


def plain_front(shards, tokens, starts, scales, heads):
    width = tokens.shape[1]
    fulls = [lax.all_gather(one, "wide", axis=0, tiled=False) for one in shards]
    each, units = width // fulls[0].shape[0], shards[3].shape[1]
    vectors, par = unpack_small(fulls[0], (10, each), (3, units))
    window = jnp.stack([from_behind(tokens, "wide", 2), from_behind(tokens, "wide", 1), tokens])
    normed, hat, _ = layer_norm(window.reshape(-1, width).astype(F32), vectors[0], vectors[3])
    low = normed.astype(BF16)
    weights = fulls[1].reshape(width, 3 * width)
    queries = dot(low[-tokens.shape[0] :], weights[:, :width]) + vectors[4]
    queries = queries.astype(BF16) * jnp.asarray((width // heads) ** (-0.5), BF16)
    keys = dot(low, weights[:, width : 2 * width]).astype(BF16)
    values = (dot(low, weights[:, 2 * width :]) + vectors[5]).astype(BF16)
    attended = attend(queries, keys, values, starts, scales, heads)
    hat_low = hat.astype(BF16).reshape(window.shape)
    return [*fulls[1:], hat_low, low, queries, keys, values, *attended, vectors, par]


def front(shards, thirds, tokens, starts, scales, heads):
    rows, width = tokens.shape
    wide = lax.axis_size("wide")
    if lax.axis_size("dp") != 2 or wide != 16:
        return plain_front(shards, tokens, starts, scales, heads)
    window = 3 * rows
    like = jax.ShapeDtypeStruct
    out_shape = [like((wide, *one.shape), one.dtype) for one in shards[1:]] + [
        like((3, rows, width), BF16),
        like((window, width), BF16),
        like((rows, width), BF16),
        like((window, width), BF16),
        like((window, width), BF16),
        like((rows, width), F32),
        like((rows, width), BF16),
        like((heads // 2, 2, rows), F32),
        like((16, width), F32),
        like((8, wide * shards[3].shape[1]), F32),
    ]
    sems = AG_SEMS * len(shards) + 2
    scratch = [
        ((3, rows, width), BF16),
        ((window, width), BF16),
        ((wide, *shards[1].shape), BF16),
        ((rows, width), BF16),
        ((window, width), BF16),
        ((window, width), BF16),
        ((rows, width), F32),
        ((rows, width), BF16),
        ((wide, *shards[0].shape), BF16),
        ((rows // Q_TILE, window - rows + Q_TILE, Q_TILE), F32),
        ((128, window), BF16),
        ((128, rows), F32),
    ]
    return pl.pallas_call(
        functools.partial(front_kernel, thirds, width // heads),
        out_shape=out_shape,
        in_specs=[VMEM] * 8,
        out_specs=[HBM] * 11 + [VMEM] * 3,
        scratch_shapes=[pltpu.VMEM(shape, dtype) for shape, dtype in scratch]
        + [
            pltpu.SemaphoreType.DMA((sems,)),
            pltpu.SemaphoreType.DMA((sems,)),
            pltpu.SemaphoreType.DMA((9,)),
        ],
        compiler_params=pltpu.CompilerParams(
            collective_id=0, has_side_effects=True, vmem_limit_bytes=58 << 20
        ),
        name="front",
    )(*shards, tokens, starts, scales)


def row_chunk(rows, columns, most):
    chunk = min(rows, max(16, most // columns // 16 * 16))
    while rows % chunk:
        chunk -= 16
    return chunk


def accumulate(target, source):
    *lead, rows, columns = source.shape
    chunk = row_chunk(rows, columns, 65536)
    per = rows // chunk
    many = per
    for size in lead:
        many *= size

    def step(number, carry):
        part = pl.ds(pl.multiple_of(lax.rem(number, per) * chunk, 16), chunk)
        rest, index = number // per, []
        for size in reversed(lead):
            index.insert(0, lax.rem(rest, size))
            rest = rest // size
        at = (*index, part)
        target[at] = (target[at].astype(F32) + source[at].astype(F32)).astype(target.dtype)
        return carry

    lax.fori_loop(0, many, step, 0)


RS_SEMS = 12


def reduce_ticks(
    me, wire, base, local, grad, quarter, held, bufs, final, squares, waits_for=None, frees=None
):
    from_core, from_y, from_x, from_down, from_up, from_last = bufs
    count, columns = held.shape[-2:]
    inside = count - quarter
    plane = pl.ds(pl.multiple_of(me.y * quarter, 16), inside) if quarter else pl.ds(0, count)
    mine = held.at[:, me.x, plane]
    take = pltpu.make_async_copy(grad.at[:, :, me.c], held, local)
    put_core = wire.put(grad.at[:, :, 1 - me.c], from_core, base, me.core_mate())
    got_core = wire.got(from_core, base, me.core_mate())
    put_x = wire.put(held.at[:, 1 - me.x, plane], from_x, base + 2, me.x_mate())
    got_x = wire.got(from_x, base + 2, me.x_mate())
    put_last = wire.put(mine.at[me.z], from_last, base + 3, me.y_mate())
    got_last = wire.got(from_last, base + 3, me.y_mate())
    if quarter:
        share = held.at[:, :, pl.ds(pl.multiple_of(me.y * inside, 16), quarter)]
        other = held.at[:, :, pl.ds(pl.multiple_of((1 - me.y) * inside, 16), quarter)]
        put_y = wire.put(other, from_y, base + 1, me.y_mate())
        got_y = wire.got(from_y, base + 1, me.y_mate())

    partners = [(None, one) for one in (me.core_mate(), me.x_mate(), me.y_mate())]
    partners += [(me.z < 3, me.up()), (me.z > 0, me.down())]

    def start():
        if waits_for is not None:
            ends = (me.z < 3).astype(jnp.int32) + (me.z > 0).astype(jnp.int32)
            pl.semaphore_wait(waits_for, 3 + ends)
        take.start()
        put_core()

    def join_core():
        take.wait()
        got_core()
        accumulate(held, from_core)
        (put_y if quarter else put_x)()

    def join_y():
        got_y()
        accumulate(share, from_y)
        put_x()

    lines = []
    for tick in range(4):
        actions = []
        for place, sign, source, sems, onward, back in (
            (me.z, 1, from_down, 4, me.up(), me.down()),
            (3 - me.z, -1, from_up, 8, me.down(), me.up()),
        ):
            goal = me.z if tick == 3 else lax.rem(me.z + sign * (3 - tick) + 8, 4)
            sends = None if tick == 3 else both(place <= tick, place < 3)
            block, arrived = mine.at[goal], source.at[goal]
            got = wire.got(arrived, base + sems + goal, back)

            def take_in(block=block, arrived=arrived, got=got):
                got()
                accumulate(block, arrived)

            actions.append(
                functools.partial(when, both(sends, place > 0), take_in)
            )
            if sends is not None:
                actions.append(wire.put(block, arrived, base + sems + goal, onward, sends))
        lines.append(actions)

    def join_x():
        got_x()
        accumulate(mine, from_x)
        act(lines[0])

    def end_line():
        act(lines[3])
        put_last()

    def finish():
        got_last()
        own = held.at[me.z, me.x]
        middle = count - 2 * quarter
        chunk = row_chunk(middle, columns, 32768)

        def add_planes(number, carry):
            at = pl.multiple_of(quarter + number * chunk, 16)
            there = pl.multiple_of(at - (1 - me.y) * quarter, 16)
            final[pl.ds(at, chunk)] = own[pl.ds(at, chunk)].astype(F32) + from_last[
                pl.ds(there, chunk)
            ].astype(F32)
            return carry

        lax.fori_loop(0, middle // chunk, add_planes, 0)
        if quarter:
            for plane_of, at, there in ((0, 0, 0), (1, count - quarter, count - 2 * quarter)):

                def from_held(at=at):
                    final[pl.ds(at, quarter)] = own[pl.ds(at, quarter)].astype(F32)

                def from_mate(at=at, there=there):
                    final[pl.ds(at, quarter)] = from_last[pl.ds(there, quarter)].astype(F32)

                pl.when(me.y == plane_of)(from_held)
                pl.when(me.y != plane_of)(from_mate)

        def square(number, total):
            value = final[pl.ds(pl.multiple_of(number * 8, 8), 8)]
            return total + lane_groups(value * value)

        squares[...] = squares[...] + lax.fori_loop(
            0, count // 8, square, jnp.zeros((8, 128), F32)
        )
        if frees is not None:
            wire.finish()
            for holds, device in partners:
                when(
                    holds,
                    functools.partial(
                        pl.semaphore_signal, frees, inc=1, device_id=device, device_id_type=MESH
                    ),
                )

    return [
        start, join_core, *([join_y] if quarter else []), join_x,
        functools.partial(act, lines[1]), functools.partial(act, lines[2]), end_line, finish,
    ]


def in_rounds(sequences):
    last = max(start + len(one) for start, one in sequences)
    order = sorted(sequences, key=lambda item: -item[0])
    rounds = []
    for number in range(last):
        actions = [
            one[number - start] for start, one in order if 0 <= number - start < len(one)
        ]
        rounds.append(functools.partial(act, actions))
    return rounds


def lane_groups(values):
    total = values[:, :128]
    for lane in range(128, values.shape[1], 128):
        total = total + values[:, lane : lane + 128]
    return total


def piece_buffers(rows, columns, quarter, dtype):
    inside = rows - quarter
    some = (4, 2, quarter, columns) if quarter else (1, 1, 16, 128)
    shapes = [
        (4, 2, rows, columns),
        (4, 2, rows, columns),
        some,
        (4, inside, columns),
        (4, inside, columns),
        (4, inside, columns),
        (inside, columns),
    ]
    return [pltpu.VMEM(shape, dtype) for shape in shapes]


BACK_BLOCK = 256
DURING_PAIRS = ((0, (0, 1)), (1, (2,)), (2, (3,)), (4, (4,)), (5, (5,)), (7, (6,)))
DURING_BLOCKS = ((1, (7,)), (3, (8,)))
AFTER_BLOCKS = 9


def back_kernel(pieces, sets, head_size, *refs):
    grads, refs = refs[:3], refs[3:]
    (q_in, k_in, v_in, do_in, a_in, hat_in, w_in, starts, lse, delta, small_in), refs = refs[:11], refs[11:]
    finals, refs = refs[:4], refs[4:]
    (near_out, far_out, own_out, small_out, norm), refs = refs[:5], refs[5:]
    buffers, refs = refs[: 7 * sets], refs[7 * sets :]
    (dq, dk, dv, dw, halo, passing, small, tiles, send, recv, local, stream, freed) = refs
    me = Place()
    count = len(pieces)
    rows, width = q_in.shape
    window = k_in.shape[0]
    before = window - rows
    span = before + Q_TILE
    tiles[...] = jnp.zeros_like(tiles)
    small[0] = small_in[...]
    arrays = [*grads, *[dw.at[k] for k in range(3)]]
    wires, sequences = [], []
    last_of = {}
    for k, (number, first, size, quarter, result, column, of, start) in enumerate(pieces):
        here = pl.ds(first, size)
        wire = Wire(send, recv)
        again = of in last_of
        more = any(piece[6] == of for piece in pieces[k + 1 :])
        final = finals[result].at[here, pl.ds(column, arrays[number].shape[-1])]
        sequences.append(
            (
                start,
                reduce_ticks(
                    me, wire, RS_SEMS * k, local.at[k], arrays[number].at[:, :, :, here], quarter,
                    buffers[7 * of], buffers[7 * of + 1 : 7 * of + 7], final, tiles.at[0],
                    waits_for=freed.at[last_of[of]] if again else None,
                    frees=freed.at[k] if more else None,
                ),
            )
        )
        last_of[of] = k
        if not more:
            wires.append(wire)

    ending = RS_SEMS * count
    wire = Wire(send, recv)
    wires.append(wire)
    joins = both(me.c == 1, me.w >= 2)
    near = [
        wire.put(halo.at[1], near_out, ending + 1, me.core_mate(), me.c == 1),
        wire.put(halo.at[1], passing, ending + 2, me.core_mate(), both(me.c == 0, me.w >= 2)),
    ]
    got_passing = wire.got(passing, ending + 2, me.core_mate())
    got_near = wire.got(near_out, ending + 1, me.core_mate(), me.c == 0)
    far_copy = pltpu.make_async_copy(halo.at[0], far_out, local.at[count])
    clear = pltpu.make_async_copy(dq, near_out, local.at[count + 1])

    def join_halo():
        got_passing()
        accumulate(halo.at[0], passing)

    def end_halo():
        when(joins, join_halo)
        far_copy.start()

    def small_step(k, partner):
        put = wire.put(small.at[k], small.at[5 + k], ending + 3 + k, partner)
        got = wire.got(small.at[5 + k], ending + 3 + k, partner)

        def take_in():
            got()
            small[k + 1] = small[k] + small[5 + k]

        return put, take_in

    steps = [me.wide(jnp.bitwise_xor(me.w, bit)) for bit in (1, 2, 4, 8)]
    smalls = [small_step(k, one) for k, one in enumerate([steps[0], me.y_mate(), *steps[1:]])]
    small_ticks = [smalls[0][0]]
    for k in range(4):
        small_ticks.append(functools.partial(act, [smalls[k][1], smalls[k + 1][0]]))
    small_ticks.append(smalls[4][1])
    computed = pieces[-3][-1]
    sequences.append((computed, small_ticks))
    sequences.append(
        (computed, [functools.partial(act, near), end_halo])
    )
    rounds = in_rounds(sequences)
    pairs = width // 128
    blocks = width // BACK_BLOCK
    greet(me, [*steps[2:], *(me.wide(jnp.bitwise_xor(me.w, bits)) for bits in (3, 12))])

    def attention(q_two, k_two, v_two, do_two, bias, dk_sum, dv_sum, kt, dqt):
        def loads(pair, slot):
            lanes = pl.ds(pl.multiple_of(pair * 128, 128), 128)
            return [
                pltpu.make_async_copy(source.at[:, lanes], target.at[slot], stream.at[slot, k])
                for k, (source, target) in enumerate(
                    ((q_in, q_two), (k_in, k_two), (v_in, v_two), (do_in, do_two))
                )
            ]

        for one in loads(0, 0):
            one.start()
        fill_mask(starts, bias, rows, span, before)

        def pair_step(pair, carry):
            slot = lax.rem(pair, 2)
            lanes = pl.ds(pl.multiple_of(pair * 128, 128), 128)

            def prefetch():
                for one in loads(pair + 1, 1 - slot):
                    one.start()

            pl.when(pair + 1 < pairs)(prefetch)
            for k, due in DURING_PAIRS:
                pl.when(pair == k)(functools.partial(act, [rounds[number] for number in due]))
            for one in loads(pair, slot):
                one.wait()
            attend_back_pair(
                head_size, q_two.at[slot], k_two.at[slot], v_two.at[slot], do_two.at[slot],
                lse.at[pair], delta.at[pair], dq.at[:, lanes], dk.at[:, lanes], dv.at[:, lanes],
                bias, dk_sum, dv_sum, kt, dqt,
            )
            small[0, 4:5, lanes] = jnp.sum(dq[:, lanes].astype(F32), axis=0, keepdims=True)
            small[0, 5:6, lanes] = jnp.sum(dv[:, lanes].astype(F32), axis=0, keepdims=True)
            return carry

        lax.fori_loop(0, pairs, pair_step, 0)

    pl.run_scoped(
        attention,
        pltpu.VMEM((2, rows, 128), BF16),
        pltpu.VMEM((2, window, 128), BF16),
        pltpu.VMEM((2, window, 128), BF16),
        pltpu.VMEM((2, rows, 128), BF16),
        pltpu.VMEM((rows // Q_TILE, span, Q_TILE), F32),
        pltpu.VMEM((window, 128), F32),
        pltpu.VMEM((window, 128), F32),
        pltpu.VMEM((128, window), BF16),
        pltpu.VMEM((128, rows), F32),
    )

    def projections(a_two, hat_two, w_two):
        def loads(block, slot):
            here = pl.ds(pl.multiple_of(block * BACK_BLOCK, BACK_BLOCK), BACK_BLOCK)
            return [
                pltpu.make_async_copy(source, target.at[slot], stream.at[slot, k])
                for k, (source, target) in enumerate(
                    ((a_in.at[:, here], a_two), (hat_in.at[:, here], hat_two), (w_in.at[here], w_two))
                )
            ]

        for one in loads(0, 0):
            one.start()

        def block_step(block, carry):
            slot = lax.rem(block, 2)
            here = pl.ds(pl.multiple_of(block * BACK_BLOCK, BACK_BLOCK), BACK_BLOCK)

            def prefetch():
                for one in loads(block + 1, 1 - slot):
                    one.start()

            pl.when(block + 1 < blocks)(prefetch)
            for k, due in DURING_BLOCKS:
                pl.when(block == k)(functools.partial(act, [rounds[number] for number in due]))
            for one in loads(block, slot):
                one.wait()
            a_t = a_two[slot].T
            for k, made in enumerate((dot(a_t[:, before:], dq[...]), dot(a_t, dk[...]), dot(a_t, dv[...]))):
                dw[k, block] = made.astype(BF16).reshape(dw.shape[2:])
            for k in range(3):
                part = slice(k * rows, (k + 1) * rows)
                grad = dot(dk[part, :], w_two[slot, :, width : 2 * width], 1, 1) + dot(
                    dv[part, :], w_two[slot, :, 2 * width :], 1, 1
                )
                if k == 2:
                    grad = grad + dot(dq[...], w_two[slot, :, :width], 1, 1)
                    own_out[:, here] = grad
                else:
                    halo[k, :, here] = grad.astype(BF16)
                hat = hat_two[slot, part].astype(F32)
                small[0, 0:1, here] += jnp.sum(grad * hat, axis=0, keepdims=True)
                small[0, 3:4, here] += jnp.sum(grad, axis=0, keepdims=True)
            return carry

        lax.fori_loop(0, blocks, block_step, 0)

    pl.run_scoped(
        projections,
        pltpu.VMEM((2, window, BACK_BLOCK), BF16),
        pltpu.VMEM((2, window, BACK_BLOCK), BF16),
        pltpu.VMEM((2, BACK_BLOCK, 3 * width), BF16),
    )
    dq[...] = jnp.zeros_like(dq)
    when(me.c == 1, clear.start)
    act(rounds[AFTER_BLOCKS:])
    small_out[...] = small[5]
    total = tiles.at[0]
    for half, (own_place, distances) in enumerate(((lax.rem(me.w, 4), (1, 2, 3)), (me.z, (4, 8, 12)))):
        spread = tiles.at[pl.ds(1 + 4 * half, 4)]
        spread[own_place] = total[...]
        moves = [
            wire.copy(
                total, spread.at[own_place], ending + 8 + 3 * half + k,
                me.wide(jnp.bitwise_xor(me.w, distance)),
            )
            for k, distance in enumerate(distances)
        ]
        for one in moves:
            one.start()
        for one in moves:
            one.wait()
        total = tiles.at[9 + half]
        total[...] = (spread[0] + spread[1]) + (spread[2] + spread[3])
    norm[...] = total[...]
    got_near()
    for one in wires:
        one.finish()
    far_copy.wait()
    when(me.c == 1, clear.wait)


def back(grads, attention, small, starts, stats, heads):
    queries, keys, values, outs_grad, normed, hat, weights = attention
    rows, width = queries.shape
    window = keys.shape[0]
    wide = lax.axis_size("wide")
    if lax.axis_size("dp") != 2 or wide != 16:
        return plain_back(grads, attention, small, starts, stats, heads)
    fc1, fc2, out = (one.shape for one in grads)
    tall, pieces = 4, []
    for array, shape in ((1, fc2), (0, fc1)):
        size = shape[1] // tall
        for k in range(tall):
            pieces.append((array, k * size, size, size // 4, array, 0, len(pieces), len(pieces)))
    each = width // wide
    pieces.append((2, 0, each, each // 4, 2, 0, 0, 8))
    for k in range(3):
        pieces.append((3 + k, 0, each, each // 4, 3, k * width, 1 + k, AFTER_BLOCKS + k))
    pieces = tuple(pieces)
    sets = 2 * tall
    like = jax.ShapeDtypeStruct
    out_shape = [like(one.shape[1:], F32) for one in grads] + [
        like((each, 3 * width), F32),
        like((rows, width), BF16),
        like((rows, width), BF16),
        like((rows, width), F32),
        like(small.shape, F32),
        like((8, 128), F32),
    ]
    scratch = []
    for number, _, size, quarter, *_ in pieces[:sets]:
        scratch += piece_buffers(size, grads[number].shape[2], quarter, grads[number].dtype)
    count = len(pieces)
    sems = RS_SEMS * count + 14
    *totals, near, far, own, small, norm = pl.pallas_call(
        functools.partial(back_kernel, pieces, sets, width // heads),
        out_shape=out_shape,
        in_specs=[HBM] * 10 + [VMEM] * 4,
        out_specs=[VMEM] * 4 + [HBM] * 2 + [VMEM] * 3,
        scratch_shapes=scratch
        + [
            pltpu.VMEM((rows, width), BF16),
            pltpu.VMEM((window, width), BF16),
            pltpu.VMEM((window, width), BF16),
            pltpu.VMEM((3, 4, 2, 2, each, width), BF16),
            pltpu.VMEM((2, rows, width), BF16),
            pltpu.VMEM((rows, width), BF16),
            pltpu.VMEM((10, *small.shape), F32),
            pltpu.VMEM((11, 8, 128), F32),
            pltpu.SemaphoreType.DMA((sems,)),
            pltpu.SemaphoreType.DMA((sems,)),
            pltpu.SemaphoreType.DMA((count + 2,)),
            pltpu.SemaphoreType.DMA((2, 4)),
            pltpu.SemaphoreType.REGULAR((count,)),
        ],
        compiler_params=pltpu.CompilerParams(
            collective_id=1, has_side_effects=True, vmem_limit_bytes=60 << 20
        ),
        name="back",
    )(
        *[one.reshape(4, 2, 2, *one.shape[1:]) for one in grads],
        queries, keys, values, outs_grad, normed, hat, weights, starts, *stats, small,
    )
    return [*totals, near, from_behind(far, "wide", -2), own, small, norm]


def plain_back(grads, attention, small, starts, stats, heads):
    queries, keys, values, outs_grad, normed, hat, weights = attention
    rows, width = queries.shape
    wide = lax.axis_size("wide")
    dq, dk, dv = attend_back(queries, keys, values, outs_grad, *stats, starts, heads)
    earlier = dot(dk, weights[:, width : 2 * width], 1, 1) + dot(dv, weights[:, 2 * width :], 1, 1)
    own = earlier[-rows:] + dot(dq, weights[:, :width], 1, 1)
    earlier = earlier[:-rows]
    all_grad = jnp.concatenate([earlier, own])
    dw = [dot(normed[-rows:], dq, 0, 0), dot(normed, dk, 0, 0), dot(normed, dv, 0, 0)]
    grads = [*grads, jnp.concatenate(dw, axis=1).reshape(wide, -1, 3 * width)]
    totals = [
        lax.psum(
            lax.psum_scatter(one.astype(F32), "wide", scatter_dimension=0, tiled=False), "dp"
        )
        for one in grads
    ]
    sums = {
        0: jnp.sum(all_grad * hat.astype(F32), axis=0),
        3: jnp.sum(all_grad, axis=0),
        4: jnp.sum(dq.astype(F32), axis=0),
        5: jnp.sum(dv.astype(F32), axis=0),
    }
    small = jnp.concatenate(
        [sums[k][None] if k in sums else small[k : k + 1] for k in range(small.shape[0])]
    )
    low = earlier.astype(BF16).reshape(2, rows, width)
    returned = [from_behind(low[1], "wide", -1), from_behind(low[0], "wide", -2)]
    squares = lax.psum(sum(jnp.sum(one * one) for one in totals), "wide")
    tile = jnp.zeros((8, 128), F32).at[0, 0].set(squares)
    return [*totals, *returned, own, lax.psum(small, ("dp", "wide")), tile]


F_TILE = 256


def grad_through_norm(grad, hat, scale, gain):
    scaled = grad * gain
    mean_plain = jnp.mean(scaled, axis=-1, keepdims=True)
    mean_cross = jnp.mean(scaled * hat, axis=-1, keepdims=True)
    return scale * (scaled - mean_plain - hat * mean_cross)


def down_sums(values):
    return jnp.sum(values, axis=0, keepdims=True)


def middle_kernel(
    head_size, c_ref, o_ref, x_ref, gy_ref, wo_ref, w1_ref, w2_ref, vec_ref, par_ref, scale_ref,
    out_ref, mid_ref, df_ref, a_ref, dz_ref, res_ref, do_ref, delta_ref, small_ref,
    act_all, slope, grad_all, stats, sums, x2, hat_post, hat_two, da,
):
    blocks, _, units = w1_ref.shape
    width = x_ref.shape[1]
    count = blocks * units

    @pl.when(pl.program_id(0) == 0)
    def _():
        sums[...] = jnp.zeros_like(sums)
        small_ref[...] = jnp.zeros_like(small_ref)

    stats[...] = jnp.zeros_like(stats)
    projected = dot(c_ref[...], wo_ref[...]) + vec_ref[6:7]
    value, hat, scale_post = layer_norm(projected, vec_ref[1:2], vec_ref[7:8])
    hat_post[...] = hat
    residual = x_ref[...].astype(F32) + value
    x2[...] = residual
    value, hat, scale_two = layer_norm(residual, vec_ref[2:3], vec_ref[8:9])
    hat_two[...] = hat
    a_ref[...] = value.astype(BF16)

    def columns(k):
        return pl.ds(pl.multiple_of(k * units, units), units)

    def forward(k, carry):
        pre = dot(a_ref[...], w1_ref[k]) + par_ref[2:3, columns(k)]
        half = 0.5 + 0.5 * lax.erf(pre * (0.5**0.5))
        value = pre * half
        act_all[k] = value
        slope[k] = half + pre * (jnp.exp(-0.5 * pre * pre) * (0.5 / jnp.pi) ** 0.5)
        stats[0] += lane_groups(value)
        stats[1] += lane_groups(value * value)
        return carry

    lax.fori_loop(0, blocks, forward, 0, unroll=2)
    mean = jnp.sum(stats[0], axis=1, keepdims=True) / count
    second = jnp.sum(stats[1], axis=1, keepdims=True) / count
    scale = lax.rsqrt(second - mean * mean + norm_epsilon)

    def middle(k, carry):
        here = columns(k)
        hat = (act_all[k] - mean) * scale
        mid_ref[:, here] = (hat * par_ref[0:1, here] + par_ref[1:2, here]).astype(BF16)
        down = dot(gy_ref[...], w2_ref[here, :], 1, 1)
        scaled = down * par_ref[0:1, here]
        act_all[k] = hat
        grad_all[k] = scaled
        stats[2] += lane_groups(scaled)
        stats[3] += lane_groups(scaled * hat)
        sums[0:1, here] += down_sums(down * hat)
        sums[1:2, here] += down_sums(down)
        return carry

    lax.fori_loop(0, blocks, middle, 0, unroll=2)
    plain = jnp.sum(stats[2], axis=1, keepdims=True) / count
    crossed = jnp.sum(stats[3], axis=1, keepdims=True) / count
    part = min(width, 512)
    for start in range(0, width, part):
        here = slice(start, start + part)
        total = dot(mid_ref[...], w2_ref[:, here])
        out_ref[:, here] = (x2[:, here] + (total + vec_ref[9:10, here])).astype(BF16)

    def backward(k, carry):
        here = columns(k)
        back = scale * (grad_all[k] - plain - act_all[k] * crossed) * slope[k]
        low = back.astype(BF16)
        df_ref[:, here] = low
        sums[2:3, here] += down_sums(low.astype(F32))
        return carry

    lax.fori_loop(0, blocks, backward, 0, unroll=2)
    da[...] = jnp.zeros_like(da)

    def back_out(k, carry):
        da[...] += dot(df_ref[:, columns(k)], w1_ref[k], 1, 1)
        return carry

    lax.fori_loop(0, blocks, back_out, 0, unroll=2)
    grad_in = gy_ref[...].astype(F32)
    rows_grad = da[...]
    residual_grad = grad_in + grad_through_norm(rows_grad, hat_two[...], scale_two, vec_ref[2:3])
    res_ref[...] = residual_grad
    dz = grad_through_norm(residual_grad, hat_post[...], scale_post, vec_ref[1:2]).astype(BF16)
    dz_ref[...] = dz
    for row, term in (
        (1, residual_grad * hat_post[...]),
        (2, rows_grad * hat_two[...]),
        (6, dz.astype(F32)),
        (7, residual_grad),
        (8, rows_grad),
        (9, grad_in),
    ):
        small_ref[row : row + 1] += down_sums(term)
    mixed_grad = dot(dz, wo_ref[...], 1, 1)
    outs = o_ref[...]
    low = (mixed_grad * scale_ref[...]).astype(BF16)
    do_ref[...] = low
    head_row = 10 + 3 * count // width
    small_ref[head_row : head_row + 1] += down_sums(mixed_grad * outs)
    heads = delta_ref.shape[0]
    lane = lax.broadcasted_iota(jnp.int32, (heads, width), 1)
    of = lax.broadcasted_iota(jnp.int32, (heads, width), 0) * head_size
    chosen = jnp.where(jnp.logical_and(lane >= of, lane < of + head_size), 1.0, 0.0)
    delta_ref[...] = lax.dot_general(
        chosen, low.astype(F32) * outs, (((1,), (1,)), ((), ())),
        precision=lax.Precision.HIGHEST, preferred_element_type=F32,
    )

    @pl.when(pl.program_id(0) == pl.num_programs(0) - 1)
    def _():
        for row in range(3):
            for start in range(0, count, width):
                at = 10 + (row * count + start) // width
                small_ref[at : at + 1] = sums[row : row + 1, start : start + width]


def middle_part(mixed, attended, tokens, out_grad, wo, w1, w2, vectors, par, scales, heads):
    rows, width = tokens.shape
    blocks, _, units = w1.shape
    hidden = blocks * units
    by_tile = lambda columns: pl.BlockSpec((F_TILE, columns), lambda t: (t, 0))
    once = lambda one: pl.BlockSpec(
        one.shape, lambda t: (0,) * len(one.shape), pipeline_mode=pl.Buffered(1)
    )
    small_rows = -(-(11 + 3 * hidden // width) // 8) * 8
    like = jax.ShapeDtypeStruct
    return pl.pallas_call(
        functools.partial(middle_kernel, width // heads),
        grid=(rows // F_TILE,),
        in_specs=[by_tile(width)] * 4 + [once(one) for one in (wo, w1, w2, vectors, par, scales)],
        out_specs=[
            by_tile(width),
            by_tile(hidden),
            by_tile(hidden),
            by_tile(width),
            by_tile(width),
            by_tile(width),
            by_tile(width),
            pl.BlockSpec((heads, F_TILE), lambda t: (0, t)),
            pl.BlockSpec((small_rows, width), lambda t: (0, 0)),
        ],
        out_shape=[
            like((rows, width), BF16),
            like((rows, hidden), BF16),
            like((rows, hidden), BF16),
            like((rows, width), BF16),
            like((rows, width), BF16),
            like((rows, width), F32),
            like((rows, width), BF16),
            like((heads, rows), F32),
            like((small_rows, width), F32),
        ],
        scratch_shapes=[pltpu.VMEM((blocks, F_TILE, units), F32)] * 3
        + [pltpu.VMEM((4, F_TILE, 128), F32), pltpu.VMEM((8, hidden), F32)]
        + [pltpu.VMEM((F_TILE, width), F32)] * 4,
        compiler_params=pltpu.CompilerParams(vmem_limit_bytes=60 << 20),
        name="middle_part",
    )(mixed, attended, tokens, out_grad, wo, w1, w2, vectors, par, scales)


def weights_kernel(a_ref, gy_ref, c_ref, dz_ref, mid_ref, df_ref, dw1_ref, dw2_ref, dwo_ref, a_t):
    @pl.when(pl.program_id(0) == 0)
    def _():
        a_t[...] = a_ref[...].T
        dwo_ref[...] = dot(c_ref[...].T, dz_ref[...]).astype(BF16)

    dw1_ref[0] = dot(a_t[...], df_ref[...]).astype(BF16)
    dw2_ref[0] = dot(mid_ref[...].T, gy_ref[...]).astype(BF16)


def weight_grads(rows, out_grad, mixed, proj_grad, middle, pre_grad, blocks):
    tokens, width = rows.shape
    units = middle.shape[1] // blocks
    whole = pl.BlockSpec((tokens, width), lambda k: (0, 0))
    block = pl.BlockSpec((tokens, units), lambda k: (0, k))
    return pl.pallas_call(
        weights_kernel,
        grid=(blocks,),
        in_specs=[whole] * 4 + [block, block],
        out_specs=[
            pl.BlockSpec((1, width, units), lambda k: (k, 0, 0)),
            pl.BlockSpec((1, units, width), lambda k: (k, 0, 0)),
            pl.BlockSpec((width, width), lambda k: (0, 0)),
        ],
        out_shape=[
            jax.ShapeDtypeStruct((blocks, width, units), BF16),
            jax.ShapeDtypeStruct((blocks, units, width), BF16),
            jax.ShapeDtypeStruct((width, width), BF16),
        ],
        scratch_shapes=[pltpu.VMEM((width, tokens), BF16)],
        compiler_params=pltpu.CompilerParams(vmem_limit_bytes=40 << 20),
        name="weight_grads",
    )(rows, out_grad, mixed, proj_grad, middle, pre_grad)


def plane_share(rows):
    return rows // 16 * 3 // 8 * 16


def unpack_small(full, vector_shape, hidden_shape):
    wide = full.shape[0]
    count, each = vector_shape
    vectors = full[:, :count, :each].transpose(1, 0, 2).reshape(count, -1)
    rows, size = hidden_shape
    if size % 128 == 0:
        hidden = full[:, count:].reshape(wide, rows, size)
    else:
        hidden = full[:, count:, :size]
    hidden = hidden.transpose(1, 0, 2).reshape(rows, -1)
    return vectors.astype(F32), hidden.astype(F32)


def regroup(blocks, units):
    slabs, rows, columns = blocks.shape
    join = max(1, units // columns)
    if join == 1:
        return blocks
    return blocks.reshape(slabs // join, join, rows, columns).transpose(0, 2, 1, 3).reshape(
        slabs // join, rows, join * columns
    )


def ungroup(blocks, columns):
    slabs, rows, units = blocks.shape
    join = units // columns
    if join == 1:
        return blocks
    return blocks.reshape(slabs, rows, join, columns).transpose(0, 2, 1, 3).reshape(
        slabs * join, rows, columns
    )


def body(
    inputs,
    out_grad,
    doc_lengths,
    step_count,
    qkv_weight,
    qkv_first,
    qkv_second,
    out_weight,
    out_first,
    out_second,
    fc1_weight,
    fc1_first,
    fc1_second,
    fc2_weight,
    fc2_first,
    fc2_second,
    model_vectors,
    vectors_first,
    vectors_second,
    hidden_vectors,
    hidden_first,
    hidden_second,
    head_scale,
    head_first,
    head_second,
):
    tokens_dev = inputs.shape[0]
    width = inputs.shape[1]
    heads_count = head_scale.shape[0]
    head_size = width // heads_count
    wide = lax.axis_size("wide")
    hidden_width = hidden_vectors.shape[1] * wide

    fc1_rows, fc2_rows = fc1_weight.shape[0], fc2_weight.shape[0]
    qkv_rows, out_rows = qkv_weight.shape[0], out_weight.shape[0]
    small = jnp.concatenate(
        [
            jnp.pad(model_vectors, ((0, 0), (0, max(0, 128 - model_vectors.shape[1])))),
            hidden_vectors.reshape(-1, min(128, hidden_vectors.shape[1])),
        ]
        if hidden_vectors.shape[1] % 128 == 0
        else [
            jnp.pad(one, ((0, 0), (0, 128 - one.shape[1]))) for one in (model_vectors, hidden_vectors)
        ]
    ).astype(BF16)
    heads_low = lax.optimization_barrier(head_scale.astype(BF16)).astype(F32)
    starts = doc_starts(
        doc_lengths, lax.axis_index("dp"), lax.axis_index("wide") * tokens_dev, tokens_dev
    )
    starts = jnp.maximum(starts - (lax.axis_index("wide") - 2) * tokens_dev, 0).reshape(1, -1)
    scales = jnp.repeat(heads_low, head_size).reshape(1, width)
    gathered = front(
        [
            small,
            qkv_weight.astype(BF16),
            out_weight.astype(BF16),
            fc1_weight.astype(BF16),
            fc2_weight.astype(BF16),
        ],
        (0, qkv_rows // 2, out_rows // 4, plane_share(fc1_rows), plane_share(fc2_rows)),
        inputs,
        starts,
        scales,
        heads_count,
    )
    qkv_full, out_full, fc1_full, fc2_full, hat_low, normed_low = gathered[:6]
    queries, keys_all, values_all, attended, mixed_low, log_totals, vectors, hidden_par = gathered[6:]
    fc2_full = fc2_full.reshape(hidden_width, width)
    output, middle_low, pre_low, rows_low, proj_low, residual_grad, attended_low, delta, small_grad = (
        middle_part(
            mixed_low,
            attended,
            inputs,
            out_grad,
            out_full.reshape(width, width),
            regroup(fc1_full, 256),
            fc2_full,
            vectors,
            hidden_par,
            scales,
            heads_count,
        )
    )
    fc1_grad, fc2_grad, out_weight_grad = weight_grads(
        rows_low, out_grad, mixed_low, proj_low, middle_low, pre_low, hidden_width // 256
    )
    fc1_part, fc2_part, out_part, qkv_part, near, far, own_grad, small_total, norm_tile = back(
        [
            ungroup(fc1_grad, fc1_weight.shape[1]),
            fc2_grad.reshape(wide, -1, width),
            out_weight_grad.reshape(wide, -1, width),
        ],
        (
            queries,
            keys_all,
            values_all,
            attended_low,
            normed_low,
            hat_low.reshape(-1, width),
            qkv_full.reshape(width, 3 * width),
        ),
        small_grad,
        starts,
        (log_totals, delta.reshape(log_totals.shape)),
        heads_count,
    )
    total_grad = own_grad + near.astype(F32) + far.astype(F32)
    _, hat_in, scale_in = layer_norm(inputs.astype(F32), vectors[0], vectors[3])
    input_grad = residual_grad + grad_through_norm(total_grad, hat_in, scale_in, vectors[0])
    vector_rows = model_vectors.shape[0]
    head_row = vector_rows + hidden_vectors.shape[0] * hidden_width // width
    vector_total = small_total[:vector_rows]
    hidden_total = small_total[vector_rows:head_row].reshape(hidden_vectors.shape[0], hidden_width)
    head_total = jnp.sum(small_total[head_row].reshape(heads_count, head_size), axis=1)
    place = lax.axis_index("wide")
    vector_part = lax.dynamic_slice_in_dim(
        vector_total, place * model_vectors.shape[1], model_vectors.shape[1], 1
    )
    hidden_part = lax.dynamic_slice_in_dim(
        hidden_total, place * hidden_vectors.shape[1], hidden_vectors.shape[1], 1
    )
    small_square = jnp.sum(small_total[:head_row] ** 2) + jnp.sum(head_total**2)
    grad_norm = jnp.sqrt(jnp.sum(norm_tile) + small_square)
    factor = jnp.minimum(1.0, clip_limit / (grad_norm + 1e-06))
    step = step_count[0].astype(F32)
    grads = (qkv_part, out_part, fc1_part, fc2_part, vector_part, hidden_part, head_total)
    params = (
        qkv_weight,
        out_weight,
        fc1_weight,
        fc2_weight,
        model_vectors,
        hidden_vectors,
        head_scale,
    )
    firsts = (qkv_first, out_first, fc1_first, fc2_first, vectors_first, hidden_first, head_first)
    seconds = (
        qkv_second,
        out_second,
        fc1_second,
        fc2_second,
        vectors_second,
        hidden_second,
        head_second,
    )
    rates = (
        matrix_rate,
        matrix_rate,
        matrix_rate,
        matrix_rate,
        vector_rate,
        vector_rate,
        vector_rate,
    )
    decays = (weight_decay, weight_decay, weight_decay, weight_decay, 0.0, 0.0, 0.0)
    updated = []
    for number in range(7):
        updated.extend(
            adam_step(
                grads[number] * factor,
                params[number],
                firsts[number],
                seconds[number],
                step,
                rates[number],
                decays[number],
            )
        )
    return (
        output,
        input_grad,
        grad_norm.reshape(1),
        updated[0],
        updated[1],
        updated[2],
        updated[3],
        updated[4],
        updated[5],
        updated[6],
        updated[7],
        updated[8],
        updated[9],
        updated[10],
        updated[11],
        updated[12],
        updated[13],
        updated[14],
        updated[15],
        updated[16],
        updated[17],
        updated[18],
        updated[19],
        updated[20],
    )


def solution(mesh):
    placed = (
        P(("dp", "wide"), None),
        P(("dp", "wide"), None),
        P(),
        P(),
        P("wide", None),
        P("wide", None),
        P("wide", None),
        P("wide", None),
        P("wide", None),
        P("wide", None),
        P(None, "wide"),
        P(None, "wide"),
        P(None, "wide"),
        P("wide", None),
        P("wide", None),
        P("wide", None),
        P(None, "wide"),
        P(None, "wide"),
        P(None, "wide"),
        P(None, "wide"),
        P(None, "wide"),
        P(None, "wide"),
        P(),
        P(),
        P(),
    )
    return jax.shard_map(
        body,
        mesh=mesh,
        in_specs=placed,
        out_specs=(
            P(("dp", "wide"), None),
            P(("dp", "wide"), None),
            P(),
            P("wide", None),
            P("wide", None),
            P("wide", None),
            P("wide", None),
            P("wide", None),
            P("wide", None),
            P(None, "wide"),
            P(None, "wide"),
            P(None, "wide"),
            P("wide", None),
            P("wide", None),
            P("wide", None),
            P(None, "wide"),
            P(None, "wide"),
            P(None, "wide"),
            P(None, "wide"),
            P(None, "wide"),
            P(None, "wide"),
            P(),
            P(),
            P(),
        ),
        check_vma=False,
    )
```

```python
import functools

import jax
import jax.numpy as jnp
from jax import lax
from jax.experimental import pallas as pl
from jax.experimental.pallas import tpu as pltpu
from jax.sharding import PartitionSpec as P

DOC_MOST = 1024
MESH = pl.DeviceIdType.MESH
HBM = pl.BlockSpec(memory_space=pltpu.HBM)
VMEM = pl.BlockSpec(memory_space=pltpu.VMEM)
BF16 = jnp.bfloat16
F32 = jnp.float32

norm_epsilon = 1e-05
clip_limit = 1.0
first_decay = 0.9
second_decay = 0.98
adam_epsilon = 1e-08
matrix_rate = 0.1
vector_rate = 0.4
weight_decay = 0.1
masked_score = -1e30


def layer_norm(values_in, gain, shift):
    center = values_in - jnp.mean(values_in, axis=-1, keepdims=True)
    variance = jnp.mean(center * center, axis=-1, keepdims=True)
    scale = lax.rsqrt(variance + norm_epsilon)
    normed = center * scale
    return (normed * gain + shift, normed, scale)


def doc_starts(doc_lengths, row, first, count):
    ends = lax.dynamic_slice_in_dim(jnp.cumsum(doc_lengths, axis=1), row, 1, 0)[0]
    places = first + jnp.arange(count, dtype=jnp.int32)
    return jnp.max(jnp.where(ends[None, :] <= places[:, None], ends[None, :], 0), axis=1)


def adam_step(grad, weight, first, second, step, rate, decay):
    first_new = first_decay * first + (1.0 - first_decay) * grad
    second_new = second_decay * second + (1.0 - second_decay) * grad * grad
    fix_one = 1.0 - jnp.power(jnp.float32(first_decay), step)
    fix_two = 1.0 - jnp.power(jnp.float32(second_decay), step)
    direction = first_new / fix_one / (jnp.sqrt(second_new / fix_two) + adam_epsilon)
    weight_new = weight - rate * (direction + decay * weight)
    return (first_new, second_new, weight_new)


def from_behind(shard, axis, by):
    count = lax.axis_size(axis)
    pairs = [(i, i + by) for i in range(count) if 0 <= i + by < count]
    return lax.ppermute(shard, axis, pairs)


def dot(a, b, left=1, right=0):
    return lax.dot_general(
        a, b, (((left,), (right,)), ((), ())), preferred_element_type=F32
    )


Q_TILE = 256


def split_pair(pair, size):
    lane = lax.broadcasted_iota(jnp.int32, pair.shape, 1)
    zero = jnp.zeros_like(pair)
    return jnp.where(lane < size, pair, zero), jnp.where(lane < size, zero, pair)


def fill_mask(starts, bias, tokens, span, keys_before):
    for tile in range(tokens // Q_TILE):
        query = lax.broadcasted_iota(jnp.int32, (span, Q_TILE), 1) + tile * Q_TILE + keys_before
        key = lax.broadcasted_iota(jnp.int32, (span, Q_TILE), 0) + tile * Q_TILE
        first = starts[:, tile * Q_TILE : (tile + 1) * Q_TILE]
        seen = jnp.logical_and(key <= query, key >= first)
        bias[tile] = jnp.where(seen, 0.0, masked_score)


def attend_pair(size, q_ref, k_ref, v_ref, scale_ref, o_ref, c_ref, lse_ref, bias, vt, ot):
    tokens, window = q_ref.shape[0], k_ref.shape[0]
    span = window - tokens + Q_TILE
    vt[...] = v_ref[...].T
    for tile in range(tokens // Q_TILE):
        rows = slice(tile * Q_TILE, (tile + 1) * Q_TILE)
        keys = slice(tile * Q_TILE, tile * Q_TILE + span)
        k_pair = k_ref[keys, :]
        for head, q_one in enumerate(split_pair(q_ref[rows, :], size)):
            scores = dot(k_pair, q_one, 1, 1) + bias[tile]
            highest = jnp.max(scores, axis=0, keepdims=True)
            powers = jnp.exp(scores - highest)
            total = jnp.sum(powers, axis=0, keepdims=True)
            probs = (powers * (1.0 / total)).astype(BF16)
            lse_ref[head : head + 1, rows] = highest + jnp.log(total)
            part = slice(head * size, (head + 1) * size)
            ot[part, rows] = dot(vt[part, keys], probs)
    attended = ot[...].T
    o_ref[...] = attended
    c_ref[...] = (attended * scale_ref[...]).astype(BF16)


def attend_kernel(size, starts, scale_ref, q_ref, k_ref, v_ref, o_ref, c_ref, lse_ref, bias, vt, ot):
    tokens, window = q_ref.shape[0], k_ref.shape[0]
    before = window - tokens

    @pl.when(pl.program_id(0) == 0)
    def _():
        fill_mask(starts, bias, tokens, before + Q_TILE, before)

    attend_pair(size, q_ref, k_ref, v_ref, scale_ref, o_ref, c_ref, lse_ref.at[0], bias, vt, ot)


def attend(queries, keys, values, starts, scales, heads):
    tokens, width = queries.shape
    window = keys.shape[0]
    pairs = heads // 2
    lanes = width // pairs
    span = window - tokens + Q_TILE
    by_rows = lambda rows: pl.BlockSpec((rows, lanes), lambda p: (0, p))
    return pl.pallas_call(
        functools.partial(attend_kernel, width // heads),
        grid=(pairs,),
        in_specs=[
            pl.BlockSpec((1, tokens), lambda p: (0, 0)),
            by_rows(1),
            by_rows(tokens),
            by_rows(window),
            by_rows(window),
        ],
        out_specs=[
            by_rows(tokens),
            by_rows(tokens),
            pl.BlockSpec((1, 2, tokens), lambda p: (p, 0, 0)),
        ],
        out_shape=[
            jax.ShapeDtypeStruct((tokens, width), F32),
            jax.ShapeDtypeStruct((tokens, width), BF16),
            jax.ShapeDtypeStruct((pairs, 2, tokens), F32),
        ],
        scratch_shapes=[
            pltpu.VMEM((tokens // Q_TILE, span, Q_TILE), F32),
            pltpu.VMEM((lanes, window), BF16),
            pltpu.VMEM((lanes, tokens), F32),
        ],
        compiler_params=pltpu.CompilerParams(vmem_limit_bytes=40 << 20),
        name="attend",
    )(starts, scales, queries, keys, values)


def attend_back_pair(
    size, q_ref, k_ref, v_ref, do_ref, lse_ref, delta_ref, dq_ref, dk_ref, dv_ref, bias, dk_sum, dv_sum, kt, dqt
):
    tokens, window = q_ref.shape[0], k_ref.shape[0]
    span = window - tokens + Q_TILE
    kt[...] = k_ref[...].T
    dk_sum[...] = jnp.zeros_like(dk_sum)
    dv_sum[...] = jnp.zeros_like(dv_sum)
    for tile in range(tokens // Q_TILE):
        rows = slice(tile * Q_TILE, (tile + 1) * Q_TILE)
        keys = slice(tile * Q_TILE, tile * Q_TILE + span)
        k_pair, v_pair = k_ref[keys, :], v_ref[keys, :]
        for head, (q_one, do_one) in enumerate(
            zip(split_pair(q_ref[rows, :], size), split_pair(do_ref[rows, :], size))
        ):
            scores = dot(k_pair, q_one, 1, 1) + bias[tile]
            probs = jnp.exp(scores - lse_ref[head : head + 1, rows])
            grads = dot(v_pair, do_one, 1, 1) - delta_ref[head : head + 1, rows]
            low = (probs * grads).astype(BF16)
            dv_sum[keys, :] += dot(probs.astype(BF16), do_one)
            dk_sum[keys, :] += dot(low, q_one)
            part = slice(head * size, (head + 1) * size)
            dqt[part, rows] = dot(kt[part, keys], low)
    dq_ref[...] = (dqt[...].T * size ** (-0.5)).astype(BF16)
    dk_ref[...] = dk_sum[...].astype(BF16)
    dv_ref[...] = dv_sum[...].astype(BF16)


def attend_back_kernel(
    size, starts, q_ref, k_ref, v_ref, do_ref, lse_ref, delta_ref, dq_ref, dk_ref, dv_ref, bias, *scratch
):
    tokens, window = q_ref.shape[0], k_ref.shape[0]
    before = window - tokens

    @pl.when(pl.program_id(0) == 0)
    def _():
        fill_mask(starts, bias, tokens, before + Q_TILE, before)

    attend_back_pair(
        size, q_ref, k_ref, v_ref, do_ref, lse_ref.at[0], delta_ref.at[0], dq_ref, dk_ref, dv_ref, bias, *scratch
    )


def attend_back(queries, keys, values, outs_grad, lse, delta, starts, heads):
    tokens, width = queries.shape
    window = keys.shape[0]
    pairs = heads // 2
    lanes = width // pairs
    span = window - tokens + Q_TILE
    by_rows = lambda rows: pl.BlockSpec((rows, lanes), lambda p: (0, p))
    stats = pl.BlockSpec((1, 2, tokens), lambda p: (p, 0, 0))
    return pl.pallas_call(
        functools.partial(attend_back_kernel, width // heads),
        grid=(pairs,),
        in_specs=[
            pl.BlockSpec((1, tokens), lambda p: (0, 0)),
            by_rows(tokens),
            by_rows(window),
            by_rows(window),
            by_rows(tokens),
            stats,
            stats,
        ],
        out_specs=[
            by_rows(tokens),
            by_rows(window),
            by_rows(window),
        ],
        out_shape=[
            jax.ShapeDtypeStruct((tokens, width), BF16),
            jax.ShapeDtypeStruct((window, width), BF16),
            jax.ShapeDtypeStruct((window, width), BF16),
        ],
        scratch_shapes=[
            pltpu.VMEM((tokens // Q_TILE, span, Q_TILE), F32),
            pltpu.VMEM((window, lanes), F32),
            pltpu.VMEM((window, lanes), F32),
            pltpu.VMEM((lanes, window), BF16),
            pltpu.VMEM((lanes, tokens), F32),
        ],
        compiler_params=pltpu.CompilerParams(vmem_limit_bytes=40 << 20),
        name="attend_back",
    )(starts, queries, keys, values, outs_grad, lse, delta)


class Place:
    def __init__(self):
        self.y = lax.axis_index("dp")
        self.w = lax.axis_index("wide")
        self.z = self.w // 4
        self.x = (self.w // 2) % 2
        self.c = self.w % 2

    def slab(self, z, x, c):
        return z * 4 + x * 2 + c

    def wide(self, w):
        return (self.y, w)

    def core_mate(self):
        return self.wide(self.slab(self.z, self.x, 1 - self.c))

    def x_mate(self):
        return self.wide(self.slab(self.z, 1 - self.x, self.c))

    def y_mate(self):
        return (1 - self.y, self.w)

    def up(self):
        return self.wide(lax.rem(self.w + 4, 16))

    def down(self):
        return self.wide(lax.rem(self.w + 12, 16))


def greet(me, extra=()):
    barrier = pltpu.get_barrier_semaphore()

    def hello(target):
        pl.semaphore_signal(barrier, inc=1, device_id=target, device_id_type=MESH)

    always = [me.core_mate(), me.x_mate(), me.y_mate(), *extra]
    sometimes = [
        (me.z < 3, me.up()),
        (me.z > 0, me.down()),
        (me.w < 14, me.wide(lax.rem(me.w + 2, 16))),
        (me.w >= 2, me.wide(lax.rem(me.w + 14, 16))),
    ]
    for target in always:
        hello(target)
    for holds, target in sometimes:
        pl.when(holds)(functools.partial(hello, target))
    count = len(always) + sum(holds.astype(jnp.int32) for holds, _ in sometimes)
    pl.semaphore_wait(barrier, count)


class Wire:
    def __init__(self, send, recv):
        self.send, self.recv = send, recv
        self.planned = []

    def copy(self, source, target, index, device):
        return pltpu.make_async_remote_copy(
            src_ref=source,
            dst_ref=target,
            send_sem=self.send.at[index],
            recv_sem=self.recv.at[index],
            device_id=device,
            device_id_type=MESH,
        )

    def put(self, source, target, index, device, holds=None):
        moved = self.copy(source, target, index, device)
        self.planned.append((holds, moved))
        return lambda: when(holds, moved.start)

    def got(self, target, index, device, holds=None):
        moved = self.copy(target, target, index, device)
        return lambda: when(holds, moved.wait_recv)

    def finish(self):
        for holds, moved in self.planned:
            when(holds, moved.wait_send)


def act(actions):
    for one in actions:
        one()


def both(*conditions):
    held = [one for one in conditions if one is not None]
    total = held[0] if held else None
    for one in held[1:]:
        total = jnp.logical_and(total, one)
    return total


def when(holds, action):
    if holds is None:
        action()
    else:
        pl.when(holds)(action)


AG_SEMS = 44


def gather_ticks(me, wire, base, own, full, third, side_first):
    rows = own.shape[0]
    plane = (
        pl.ds(pl.multiple_of(me.y * third, 16), rows - third) if third else pl.ds(0, rows)
    )
    share = pl.ds(pl.multiple_of(me.y * (rows - third), 16), third) if third else None
    other = pl.ds(pl.multiple_of((1 - me.y) * (rows - third), 16), third) if third else None
    my_slab = me.slab(me.z, me.x, me.c)
    ups, downs, xs, ys, cs, ts, far_ups, far_downs = (
        base + k for k in (0, 4, 8, 12, 20, 28, 36, 40)
    )
    mine = me.z * 2 + me.x

    def pass_on(z, x, holds):
        slab = me.slab(z, x, me.c)
        place = z * 2 + x
        block = full.at[slab, plane]
        actions = []
        if third:
            piece = full.at[slab, share]
            actions.append(wire.put(piece, piece, ys + place, me.y_mate(), holds))
        actions.append(wire.put(block, block, cs + place, me.core_mate(), holds))
        return actions

    def arrivals(away):
        for z, holds, onward, follow, above in (
            (me.z - away, me.z - away >= 0, me.up(), me.z < 3, False),
            (me.z + away, me.z + away <= 3, me.down(), me.z > 0, True),
        ):
            yield lax.rem(z + 4, 4), holds, onward, follow, above

    goal = full.at[my_slab, plane]
    ticks = {
        "own": [
            wire.put(own.at[plane], goal, ups + me.z, me.up(), me.z < 3),
            wire.put(own.at[plane], goal, downs + me.z, me.down(), me.z > 0),
            wire.put(own.at[plane], goal, xs + me.z, me.x_mate()),
            wire.put(own, full.at[my_slab], cs + mine, me.core_mate()),
        ]
    }
    for tick in range(1, 5):
        actions = []
        if tick < 4:
            for z, holds, onward, follow, above in arrivals(tick):
                sems = downs if above else ups
                block = full.at[me.slab(z, me.x, me.c), plane]
                actions.append(wire.got(block, sems + z, onward, holds))
                actions.append(wire.put(block, block, sems + z, onward, both(holds, follow)))
                if not side_first:
                    actions.append(wire.put(block, block, xs + z, me.x_mate(), holds))
                actions += pass_on(z, me.x, holds)
        if side_first and tick == 1:
            block = full.at[me.slab(me.z, 1 - me.x, me.c), plane]
            actions.append(wire.got(block, xs + me.z, me.x_mate()))
            actions.append(wire.put(block, block, far_ups + me.z, me.up(), me.z < 3))
            actions.append(wire.put(block, block, far_downs + me.z, me.down(), me.z > 0))
            actions += pass_on(me.z, 1 - me.x, None)
        elif side_first:
            for z, holds, onward, follow, above in arrivals(tick - 1):
                sems = far_downs if above else far_ups
                block = full.at[me.slab(z, 1 - me.x, me.c), plane]
                actions.append(wire.got(block, sems + z, onward, holds))
                actions.append(wire.put(block, block, sems + z, onward, both(holds, follow)))
                actions += pass_on(z, 1 - me.x, holds)
        ticks["line", tick] = actions
    for away in range(4):
        actions = []
        if not side_first:
            cases = arrivals(away) if away else [(me.z, None, None, None, None)]
            for z, holds, *_ in cases:
                block = full.at[me.slab(z, 1 - me.x, me.c), plane]
                actions.append(wire.got(block, xs + z, me.x_mate(), holds))
                actions += pass_on(z, 1 - me.x, holds)
        ticks["side", away] = actions
    actions = []
    if third:
        for k in range(1, 8):
            place = lax.rem(mine + k, 8)
            piece = full.at[me.slab(place // 2, place % 2, me.c), other]
            actions.append(wire.got(piece, ys + place, me.y_mate()))
            actions.append(wire.put(piece, piece, ts + place, me.core_mate()))
    ticks["shares"] = actions
    actions = [wire.got(full.at[me.slab(me.z, me.x, 1 - me.c)], cs + mine, me.core_mate())]
    for k in range(1, 8):
        place = lax.rem(mine + k, 8)
        slab = me.slab(place // 2, place % 2, 1 - me.c)
        actions.append(wire.got(full.at[slab, plane], cs + place, me.core_mate()))
        if third:
            actions.append(wire.got(full.at[slab, other], ts + place, me.core_mate()))
    ticks["end"] = actions
    return ticks


FRONT_BLOCK = 256
FRONT_TICKS = (
    (2, (("line", 3),)),
    (5, (("line", 4), ("side", 0))),
    (7, (("side", 1),)),
)
FRONT_LAST = (("side", 2), ("side", 3))


def round_rows(target, source):
    rows, columns = source.shape
    chunk = row_chunk(rows, columns, 32768)

    def step(number, carry):
        here = pl.ds(pl.multiple_of(number * chunk, 16), chunk)
        target[here] = source[here].astype(target.dtype)
        return carry

    lax.fori_loop(0, rows // chunk, step, 0)


def front_kernel(thirds, head_size, *refs):
    masters, (tokens, starts, scale_ref) = refs[:5], refs[5:8]
    fulls, outs = refs[8:12], refs[12:19]
    xs_out, a_out, q_out, k_out, v_out, o_out, c_out = outs
    lse_ref, vecs, par = refs[19:22]
    (xs, a_all, qkv, q_all, k_all, v_all, o_all, c_all, small, bias, vt, ot, *owns, send, recv, local) = refs[22:]
    for master, own in zip(masters, owns):
        round_rows(own, master)
    me = Place()
    count = len(owns)
    width = tokens.shape[1]
    rows = tokens.shape[0]
    window = 3 * rows
    before = window - rows
    span = before + Q_TILE
    landings = (small, qkv, *fulls[1:])
    keep = [
        pltpu.make_async_copy(own, full.at[me.w], local.at[k])
        for k, (own, full) in enumerate(zip(owns, landings))
    ] + [pltpu.make_async_copy(tokens, xs.at[2], local.at[count])]
    for one in keep:
        one.start()

    def clear(slot):
        xs[slot] = jnp.zeros((rows, width), BF16)

    pl.when(me.w < 2)(functools.partial(clear, 0))
    pl.when(me.w < 1)(functools.partial(clear, 1))
    wire = Wire(send, recv)
    first, second = AG_SEMS * count, AG_SEMS * count + 1
    ticks = [
        gather_ticks(me, wire, AG_SEMS * k, own, landing, third, k == 4)
        for k, (own, landing, third) in enumerate(zip(owns, landings, thirds))
    ]
    send_block = wire.put(tokens, xs.at[0], first, me.wide(lax.rem(me.w + 2, 16)), me.w < 14)
    send_near = wire.put(tokens, xs.at[1], second, me.core_mate(), me.c == 0)
    get_block = wire.got(xs.at[0], first, me.core_mate(), me.w >= 2)
    passes = both(me.c == 1, me.w >= 2)
    pass_block = wire.copy(xs.at[0], xs.at[1], second, me.core_mate())
    get_near = wire.got(xs.at[1], second, me.core_mate(), me.w >= 1)
    greet(me)
    early, late = ticks[:2], ticks[2:]

    def go(group, *names):
        for name in names:
            for one in group:
                act(one[name])

    go(early, "own", ("line", 1), ("line", 2), ("line", 3))
    act(late[2]["own"])
    send_block()
    send_near()
    go(late[:2], "own")
    fill_mask(starts, bias, rows, span, before)
    go(early, ("side", 0), ("side", 1), ("side", 2), ("side", 3), "shares", "end")
    for one in keep:
        one.wait()
    shared = [pltpu.make_async_copy(qkv, fulls[0], local.at[1])]
    for one in shared:
        one.start()

    lane = lax.broadcasted_iota(jnp.int32, (16, 128), 1)
    for pair in range(8):
        even = small[2 * pair].astype(F32)
        odd = pltpu.roll(small[2 * pair + 1].astype(F32), 64, 1)
        vecs[:, pair * 128 : (pair + 1) * 128] = jnp.where(lane < 64, even, odd)
    for slab in range(16):
        values = small[slab].astype(F32)
        for row in range(3):
            for half in range(2):
                at = slab * 256 + half * 128
                par[row : row + 1, at : at + 128] = values[10 + 2 * row + half][None]

    def project(first_column, column, a_rows):
        weights = qkv[:, :, pl.ds(first_column + column, FRONT_BLOCK)].reshape(width, FRONT_BLOCK)
        return dot(a_rows, weights)

    per = rows // FRONT_BLOCK

    def normalize(number, carry):
        here = pl.ds(pl.multiple_of(lax.rem(number, per) * FRONT_BLOCK, FRONT_BLOCK), FRONT_BLOCK)
        there = pl.ds(pl.multiple_of(number * FRONT_BLOCK, FRONT_BLOCK), FRONT_BLOCK)
        value, hat, _ = layer_norm(xs[number // per, here].astype(F32), vecs[0:1], vecs[3:4])
        xs[number // per, here] = hat.astype(BF16)
        low = value.astype(BF16)
        a_all[there] = low
        for column in range(0, width, FRONT_BLOCK):
            columns = slice(column, column + FRONT_BLOCK)
            k_all[there, columns] = project(width, column, low).astype(BF16)
            v_all[there, columns] = (
                project(2 * width, column, low) + vecs[5:6, columns]
            ).astype(BF16)
        return carry

    lax.fori_loop(2 * per, 3 * per, normalize, 0)
    for number in range(per):
        here = pl.ds(number * FRONT_BLOCK, FRONT_BLOCK)
        low = a_all[before + number * FRONT_BLOCK : before + (number + 1) * FRONT_BLOCK]
        for column in range(0, width, FRONT_BLOCK):
            columns = slice(column, column + FRONT_BLOCK)
            query = (project(0, column, low) + vecs[4:5, columns]).astype(BF16)
            q_all[here, columns] = query * jnp.asarray(head_size ** (-0.5), BF16)
    go(late, ("line", 1))
    get_block()
    when(passes, pass_block.start)
    get_near()
    when(passes, pass_block.wait_send)
    lax.fori_loop(0, 2 * per, normalize, 0)
    go(late, ("line", 2))
    kept = [
        pltpu.make_async_copy(one, out, local.at[2 + k])
        for k, (one, out) in enumerate(
            ((a_all, a_out), (q_all, q_out), (k_all, k_out), (v_all, v_out), (xs, xs_out))
        )
    ]
    for one in kept:
        one.start()

    def pair_step(pair, carry):
        lanes = pl.ds(pl.multiple_of(pair * 128, 128), 128)
        attend_pair(
            head_size, q_all.at[:, lanes], k_all.at[:, lanes], v_all.at[:, lanes],
            scale_ref.at[:, lanes], o_all.at[:, lanes], c_all.at[:, lanes], lse_ref.at[pair], bias, vt, ot,
        )
        for due, names in FRONT_TICKS:
            pl.when(pair == due)(functools.partial(go, late, *names))
        return carry

    lax.fori_loop(0, width // 128, pair_step, 0)
    results = [
        pltpu.make_async_copy(o_all, o_out, local.at[7]),
        pltpu.make_async_copy(c_all, c_out, local.at[8]),
    ]
    for one in results:
        one.start()
    go(late, *FRONT_LAST, "shares", "end")
    wire.finish()
    for one in shared + kept + results:
        one.wait()


def plain_front(shards, tokens, starts, scales, heads):
    width = tokens.shape[1]
    fulls = [lax.all_gather(one.astype(BF16), "wide", axis=0, tiled=False) for one in shards]
    each, units = width // fulls[0].shape[0], shards[3].shape[1]
    vectors, par = unpack_small(fulls[0], (10, each), (3, units))
    window = jnp.stack([from_behind(tokens, "wide", 2), from_behind(tokens, "wide", 1), tokens])
    normed, hat, _ = layer_norm(window.reshape(-1, width).astype(F32), vectors[0], vectors[3])
    low = normed.astype(BF16)
    weights = fulls[1].reshape(width, 3 * width)
    queries = dot(low[-tokens.shape[0] :], weights[:, :width]) + vectors[4]
    queries = queries.astype(BF16) * jnp.asarray((width // heads) ** (-0.5), BF16)
    keys = dot(low, weights[:, width : 2 * width]).astype(BF16)
    values = (dot(low, weights[:, 2 * width :]) + vectors[5]).astype(BF16)
    attended = attend(queries, keys, values, starts, scales, heads)
    hat_low = hat.astype(BF16).reshape(window.shape)
    return [*fulls[1:], hat_low, low, queries, keys, values, *attended, vectors, par]


def front(shards, thirds, tokens, starts, scales, heads):
    rows, width = tokens.shape
    wide = lax.axis_size("wide")
    if lax.axis_size("dp") != 2 or wide != 16:
        return plain_front(shards, tokens, starts, scales, heads)
    window = 3 * rows
    like = jax.ShapeDtypeStruct
    out_shape = [like((wide, *one.shape), BF16) for one in shards[1:]] + [
        like((3, rows, width), BF16),
        like((window, width), BF16),
        like((rows, width), BF16),
        like((window, width), BF16),
        like((window, width), BF16),
        like((rows, width), F32),
        like((rows, width), BF16),
        like((heads // 2, 2, rows), F32),
        like((16, width), F32),
        like((8, wide * shards[3].shape[1]), F32),
    ]
    sems = AG_SEMS * len(shards) + 2
    scratch = [
        ((3, rows, width), BF16),
        ((window, width), BF16),
        ((wide, *shards[1].shape), BF16),
        ((rows, width), BF16),
        ((window, width), BF16),
        ((window, width), BF16),
        ((rows, width), F32),
        ((rows, width), BF16),
        ((wide, *shards[0].shape), BF16),
        ((rows // Q_TILE, window - rows + Q_TILE, Q_TILE), F32),
        ((128, window), BF16),
        ((128, rows), F32),
        *[(one.shape, BF16) for one in shards],
    ]
    return pl.pallas_call(
        functools.partial(front_kernel, thirds, width // heads),
        out_shape=out_shape,
        in_specs=[VMEM] * 8,
        out_specs=[HBM] * 11 + [VMEM] * 3,
        scratch_shapes=[pltpu.VMEM(shape, dtype) for shape, dtype in scratch]
        + [
            pltpu.SemaphoreType.DMA((sems,)),
            pltpu.SemaphoreType.DMA((sems,)),
            pltpu.SemaphoreType.DMA((9,)),
        ],
        compiler_params=pltpu.CompilerParams(
            collective_id=0, has_side_effects=True, vmem_limit_bytes=58 << 20
        ),
        name="front",
    )(*shards, tokens, starts, scales)


def row_chunk(rows, columns, most):
    chunk = min(rows, max(16, most // columns // 16 * 16))
    while rows % chunk:
        chunk -= 16
    return chunk


def accumulate(target, source):
    *lead, rows, columns = source.shape
    chunk = row_chunk(rows, columns, 65536)
    per = rows // chunk
    many = per
    for size in lead:
        many *= size

    def step(number, carry):
        part = pl.ds(pl.multiple_of(lax.rem(number, per) * chunk, 16), chunk)
        rest, index = number // per, []
        for size in reversed(lead):
            index.insert(0, lax.rem(rest, size))
            rest = rest // size
        at = (*index, part)
        target[at] = (target[at].astype(F32) + source[at].astype(F32)).astype(target.dtype)
        return carry

    lax.fori_loop(0, many, step, 0)


RS_SEMS = 12


def reduce_ticks(
    me, wire, base, local, grad, quarter, held, bufs, final, squares, waits_for=None, frees=None
):
    from_core, from_y, from_x, from_down, from_up, from_last = bufs
    count, columns = held.shape[-2:]
    inside = count - quarter
    plane = pl.ds(pl.multiple_of(me.y * quarter, 16), inside) if quarter else pl.ds(0, count)
    mine = held.at[:, me.x, plane]
    take = pltpu.make_async_copy(grad.at[:, :, me.c], held, local)
    put_core = wire.put(grad.at[:, :, 1 - me.c], from_core, base, me.core_mate())
    got_core = wire.got(from_core, base, me.core_mate())
    put_x = wire.put(held.at[:, 1 - me.x, plane], from_x, base + 2, me.x_mate())
    got_x = wire.got(from_x, base + 2, me.x_mate())
    put_last = wire.put(mine.at[me.z], from_last, base + 3, me.y_mate())
    got_last = wire.got(from_last, base + 3, me.y_mate())
    if quarter:
        share = held.at[:, :, pl.ds(pl.multiple_of(me.y * inside, 16), quarter)]
        other = held.at[:, :, pl.ds(pl.multiple_of((1 - me.y) * inside, 16), quarter)]
        put_y = wire.put(other, from_y, base + 1, me.y_mate())
        got_y = wire.got(from_y, base + 1, me.y_mate())

    partners = [(None, one) for one in (me.core_mate(), me.x_mate(), me.y_mate())]
    partners += [(me.z < 3, me.up()), (me.z > 0, me.down())]

    def start():
        if waits_for is not None:
            ends = (me.z < 3).astype(jnp.int32) + (me.z > 0).astype(jnp.int32)
            pl.semaphore_wait(waits_for, 3 + ends)
        take.start()
        put_core()

    def join_core():
        take.wait()
        got_core()
        accumulate(held, from_core)
        (put_y if quarter else put_x)()

    def join_y():
        got_y()
        accumulate(share, from_y)
        put_x()

    lines = []
    for tick in range(4):
        actions = []
        for place, sign, source, sems, onward, back in (
            (me.z, 1, from_down, 4, me.up(), me.down()),
            (3 - me.z, -1, from_up, 8, me.down(), me.up()),
        ):
            goal = me.z if tick == 3 else lax.rem(me.z + sign * (3 - tick) + 8, 4)
            sends = None if tick == 3 else both(place <= tick, place < 3)
            block, arrived = mine.at[goal], source.at[goal]
            got = wire.got(arrived, base + sems + goal, back)

            def take_in(block=block, arrived=arrived, got=got):
                got()
                accumulate(block, arrived)

            actions.append(
                functools.partial(when, both(sends, place > 0), take_in)
            )
            if sends is not None:
                actions.append(wire.put(block, arrived, base + sems + goal, onward, sends))
        lines.append(actions)

    def join_x():
        got_x()
        accumulate(mine, from_x)
        act(lines[0])

    def end_line():
        act(lines[3])
        put_last()

    def finish():
        got_last()
        own = held.at[me.z, me.x]
        middle = count - 2 * quarter
        chunk = row_chunk(middle, columns, 32768)

        def add_planes(number, carry):
            at = pl.multiple_of(quarter + number * chunk, 16)
            there = pl.multiple_of(at - (1 - me.y) * quarter, 16)
            final[pl.ds(at, chunk)] = own[pl.ds(at, chunk)].astype(F32) + from_last[
                pl.ds(there, chunk)
            ].astype(F32)
            return carry

        lax.fori_loop(0, middle // chunk, add_planes, 0)
        if quarter:
            for plane_of, at, there in ((0, 0, 0), (1, count - quarter, count - 2 * quarter)):

                def from_held(at=at):
                    final[pl.ds(at, quarter)] = own[pl.ds(at, quarter)].astype(F32)

                def from_mate(at=at, there=there):
                    final[pl.ds(at, quarter)] = from_last[pl.ds(there, quarter)].astype(F32)

                pl.when(me.y == plane_of)(from_held)
                pl.when(me.y != plane_of)(from_mate)

        def square(number, total):
            value = final[pl.ds(pl.multiple_of(number * 8, 8), 8)]
            return total + lane_groups(value * value)

        squares[...] = squares[...] + lax.fori_loop(
            0, count // 8, square, jnp.zeros((8, 128), F32)
        )
        if frees is not None:
            wire.finish()
            for holds, device in partners:
                when(
                    holds,
                    functools.partial(
                        pl.semaphore_signal, frees, inc=1, device_id=device, device_id_type=MESH
                    ),
                )

    return [
        start, join_core, *([join_y] if quarter else []), join_x,
        functools.partial(act, lines[1]), functools.partial(act, lines[2]), end_line, finish,
    ]


def in_rounds(sequences):
    last = max(start + len(one) for start, one in sequences)
    order = sorted(sequences, key=lambda item: -item[0])
    rounds = []
    for number in range(last):
        actions = [
            one[number - start] for start, one in order if 0 <= number - start < len(one)
        ]
        rounds.append(functools.partial(act, actions))
    return rounds


def lane_groups(values):
    total = values[:, :128]
    for lane in range(128, values.shape[1], 128):
        total = total + values[:, lane : lane + 128]
    return total


def piece_buffers(rows, columns, quarter, dtype):
    inside = rows - quarter
    some = (4, 2, quarter, columns) if quarter else (1, 1, 16, 128)
    shapes = [
        (4, 2, rows, columns),
        (4, 2, rows, columns),
        some,
        (4, inside, columns),
        (4, inside, columns),
        (4, inside, columns),
        (inside, columns),
    ]
    return [pltpu.VMEM(shape, dtype) for shape in shapes]


BACK_BLOCK = 256
DURING_PAIRS = ((0, (0, 1)), (1, (2,)), (2, (3,)), (4, (4,)), (5, (5,)), (7, (6,)))
DURING_BLOCKS = ((1, (7,)), (3, (8,)))
AFTER_BLOCKS = 9


def back_kernel(pieces, sets, head_size, *refs):
    grads, refs = refs[:3], refs[3:]
    (q_in, k_in, v_in, do_in, a_in, hat_in, w_in, starts, lse, delta, small_in), refs = refs[:11], refs[11:]
    finals, refs = refs[:4], refs[4:]
    (near_out, far_out, own_out, small_out, norm), refs = refs[:5], refs[5:]
    buffers, refs = refs[: 7 * sets], refs[7 * sets :]
    (dq, dk, dv, dw, halo, passing, small, tiles, send, recv, local, stream, freed) = refs
    me = Place()
    count = len(pieces)
    rows, width = q_in.shape
    window = k_in.shape[0]
    before = window - rows
    span = before + Q_TILE
    tiles[...] = jnp.zeros_like(tiles)
    small[0] = small_in[...]
    arrays = [*grads, *[dw.at[k] for k in range(3)]]
    wires, sequences = [], []
    last_of = {}
    for k, (number, first, size, quarter, result, column, of, start) in enumerate(pieces):
        here = pl.ds(first, size)
        wire = Wire(send, recv)
        again = of in last_of
        more = any(piece[6] == of for piece in pieces[k + 1 :])
        final = finals[result].at[here, pl.ds(column, arrays[number].shape[-1])]
        sequences.append(
            (
                start,
                reduce_ticks(
                    me, wire, RS_SEMS * k, local.at[k], arrays[number].at[:, :, :, here], quarter,
                    buffers[7 * of], buffers[7 * of + 1 : 7 * of + 7], final, tiles.at[0],
                    waits_for=freed.at[last_of[of]] if again else None,
                    frees=freed.at[k] if more else None,
                ),
            )
        )
        last_of[of] = k
        if not more:
            wires.append(wire)

    ending = RS_SEMS * count
    wire = Wire(send, recv)
    wires.append(wire)
    joins = both(me.c == 1, me.w >= 2)
    near = [
        wire.put(halo.at[1], near_out, ending + 1, me.core_mate(), me.c == 1),
        wire.put(halo.at[1], passing, ending + 2, me.core_mate(), both(me.c == 0, me.w >= 2)),
    ]
    got_passing = wire.got(passing, ending + 2, me.core_mate())
    got_near = wire.got(near_out, ending + 1, me.core_mate(), me.c == 0)
    far_copy = pltpu.make_async_copy(halo.at[0], far_out, local.at[count])
    clear = pltpu.make_async_copy(dq, near_out, local.at[count + 1])

    def join_halo():
        got_passing()
        accumulate(halo.at[0], passing)

    def end_halo():
        when(joins, join_halo)
        far_copy.start()

    def small_step(k, partner):
        put = wire.put(small.at[k], small.at[5 + k], ending + 3 + k, partner)
        got = wire.got(small.at[5 + k], ending + 3 + k, partner)

        def take_in():
            got()
            small[k + 1] = small[k] + small[5 + k]

        return put, take_in

    steps = [me.wide(jnp.bitwise_xor(me.w, bit)) for bit in (1, 2, 4, 8)]
    smalls = [small_step(k, one) for k, one in enumerate([steps[0], me.y_mate(), *steps[1:]])]
    small_ticks = [smalls[0][0]]
    for k in range(4):
        small_ticks.append(functools.partial(act, [smalls[k][1], smalls[k + 1][0]]))
    small_ticks.append(smalls[4][1])
    computed = pieces[-3][-1]
    sequences.append((computed, small_ticks))
    sequences.append(
        (computed, [functools.partial(act, near), end_halo])
    )
    rounds = in_rounds(sequences)
    pairs = width // 128
    blocks = width // BACK_BLOCK
    greet(me, [*steps[2:], *(me.wide(jnp.bitwise_xor(me.w, bits)) for bits in (3, 12))])

    def attention(q_two, k_two, v_two, do_two, bias, dk_sum, dv_sum, kt, dqt):
        def loads(pair, slot):
            lanes = pl.ds(pl.multiple_of(pair * 128, 128), 128)
            return [
                pltpu.make_async_copy(source.at[:, lanes], target.at[slot], stream.at[slot, k])
                for k, (source, target) in enumerate(
                    ((q_in, q_two), (k_in, k_two), (v_in, v_two), (do_in, do_two))
                )
            ]

        for one in loads(0, 0):
            one.start()
        fill_mask(starts, bias, rows, span, before)

        def pair_step(pair, carry):
            slot = lax.rem(pair, 2)
            lanes = pl.ds(pl.multiple_of(pair * 128, 128), 128)

            def prefetch():
                for one in loads(pair + 1, 1 - slot):
                    one.start()

            pl.when(pair + 1 < pairs)(prefetch)
            for k, due in DURING_PAIRS:
                pl.when(pair == k)(functools.partial(act, [rounds[number] for number in due]))
            for one in loads(pair, slot):
                one.wait()
            attend_back_pair(
                head_size, q_two.at[slot], k_two.at[slot], v_two.at[slot], do_two.at[slot],
                lse.at[pair], delta.at[pair], dq.at[:, lanes], dk.at[:, lanes], dv.at[:, lanes],
                bias, dk_sum, dv_sum, kt, dqt,
            )
            small[0, 4:5, lanes] = jnp.sum(dq[:, lanes].astype(F32), axis=0, keepdims=True)
            small[0, 5:6, lanes] = jnp.sum(dv[:, lanes].astype(F32), axis=0, keepdims=True)
            return carry

        lax.fori_loop(0, pairs, pair_step, 0)

    pl.run_scoped(
        attention,
        pltpu.VMEM((2, rows, 128), BF16),
        pltpu.VMEM((2, window, 128), BF16),
        pltpu.VMEM((2, window, 128), BF16),
        pltpu.VMEM((2, rows, 128), BF16),
        pltpu.VMEM((rows // Q_TILE, span, Q_TILE), F32),
        pltpu.VMEM((window, 128), F32),
        pltpu.VMEM((window, 128), F32),
        pltpu.VMEM((128, window), BF16),
        pltpu.VMEM((128, rows), F32),
    )

    def projections(a_two, hat_two, w_two):
        def loads(block, slot):
            here = pl.ds(pl.multiple_of(block * BACK_BLOCK, BACK_BLOCK), BACK_BLOCK)
            return [
                pltpu.make_async_copy(source, target.at[slot], stream.at[slot, k])
                for k, (source, target) in enumerate(
                    ((a_in.at[:, here], a_two), (hat_in.at[:, here], hat_two), (w_in.at[here], w_two))
                )
            ]

        for one in loads(0, 0):
            one.start()

        def block_step(block, carry):
            slot = lax.rem(block, 2)
            here = pl.ds(pl.multiple_of(block * BACK_BLOCK, BACK_BLOCK), BACK_BLOCK)

            def prefetch():
                for one in loads(block + 1, 1 - slot):
                    one.start()

            pl.when(block + 1 < blocks)(prefetch)
            for k, due in DURING_BLOCKS:
                pl.when(block == k)(functools.partial(act, [rounds[number] for number in due]))
            for one in loads(block, slot):
                one.wait()
            a_t = a_two[slot].T
            for k, made in enumerate((dot(a_t[:, before:], dq[...]), dot(a_t, dk[...]), dot(a_t, dv[...]))):
                dw[k, block] = made.astype(BF16).reshape(dw.shape[2:])
            for k in range(3):
                part = slice(k * rows, (k + 1) * rows)
                grad = dot(dk[part, :], w_two[slot, :, width : 2 * width], 1, 1) + dot(
                    dv[part, :], w_two[slot, :, 2 * width :], 1, 1
                )
                if k == 2:
                    grad = grad + dot(dq[...], w_two[slot, :, :width], 1, 1)
                    own_out[:, here] = grad
                else:
                    halo[k, :, here] = grad.astype(BF16)
                hat = hat_two[slot, part].astype(F32)
                small[0, 0:1, here] += jnp.sum(grad * hat, axis=0, keepdims=True)
                small[0, 3:4, here] += jnp.sum(grad, axis=0, keepdims=True)
            return carry

        lax.fori_loop(0, blocks, block_step, 0)

    pl.run_scoped(
        projections,
        pltpu.VMEM((2, window, BACK_BLOCK), BF16),
        pltpu.VMEM((2, window, BACK_BLOCK), BF16),
        pltpu.VMEM((2, BACK_BLOCK, 3 * width), BF16),
    )
    dq[...] = jnp.zeros_like(dq)
    when(me.c == 1, clear.start)
    act(rounds[AFTER_BLOCKS:])
    small_out[...] = small[5]
    total = tiles.at[0]
    for half, (own_place, distances) in enumerate(((lax.rem(me.w, 4), (1, 2, 3)), (me.z, (4, 8, 12)))):
        spread = tiles.at[pl.ds(1 + 4 * half, 4)]
        spread[own_place] = total[...]
        moves = [
            wire.copy(
                total, spread.at[own_place], ending + 8 + 3 * half + k,
                me.wide(jnp.bitwise_xor(me.w, distance)),
            )
            for k, distance in enumerate(distances)
        ]
        for one in moves:
            one.start()
        for one in moves:
            one.wait()
        total = tiles.at[9 + half]
        total[...] = (spread[0] + spread[1]) + (spread[2] + spread[3])
    norm[...] = total[...]
    got_near()
    for one in wires:
        one.finish()
    far_copy.wait()
    when(me.c == 1, clear.wait)


def back(grads, attention, small, starts, stats, heads):
    queries, keys, values, outs_grad, normed, hat, weights = attention
    rows, width = queries.shape
    window = keys.shape[0]
    wide = lax.axis_size("wide")
    if lax.axis_size("dp") != 2 or wide != 16:
        return plain_back(grads, attention, small, starts, stats, heads)
    fc1, fc2, out = (one.shape for one in grads)
    tall, pieces = 4, []
    for array, shape in ((1, fc2), (0, fc1)):
        size = shape[1] // tall
        for k in range(tall):
            pieces.append((array, k * size, size, size // 4, array, 0, len(pieces), len(pieces)))
    each = width // wide
    pieces.append((2, 0, each, each // 4, 2, 0, 0, 8))
    for k in range(3):
        pieces.append((3 + k, 0, each, each // 4, 3, k * width, 1 + k, AFTER_BLOCKS + k))
    pieces = tuple(pieces)
    sets = 2 * tall
    like = jax.ShapeDtypeStruct
    out_shape = [like(one.shape[1:], F32) for one in grads] + [
        like((each, 3 * width), F32),
        like((rows, width), BF16),
        like((rows, width), BF16),
        like((rows, width), F32),
        like(small.shape, F32),
        like((8, 128), F32),
    ]
    scratch = []
    for number, _, size, quarter, *_ in pieces[:sets]:
        scratch += piece_buffers(size, grads[number].shape[2], quarter, grads[number].dtype)
    count = len(pieces)
    sems = RS_SEMS * count + 14
    *totals, near, far, own, small, norm = pl.pallas_call(
        functools.partial(back_kernel, pieces, sets, width // heads),
        out_shape=out_shape,
        in_specs=[HBM] * 10 + [VMEM] * 4,
        out_specs=[VMEM] * 4 + [HBM] * 2 + [VMEM] * 3,
        scratch_shapes=scratch
        + [
            pltpu.VMEM((rows, width), BF16),
            pltpu.VMEM((window, width), BF16),
            pltpu.VMEM((window, width), BF16),
            pltpu.VMEM((3, 4, 2, 2, each, width), BF16),
            pltpu.VMEM((2, rows, width), BF16),
            pltpu.VMEM((rows, width), BF16),
            pltpu.VMEM((10, *small.shape), F32),
            pltpu.VMEM((11, 8, 128), F32),
            pltpu.SemaphoreType.DMA((sems,)),
            pltpu.SemaphoreType.DMA((sems,)),
            pltpu.SemaphoreType.DMA((count + 2,)),
            pltpu.SemaphoreType.DMA((2, 4)),
            pltpu.SemaphoreType.REGULAR((count,)),
        ],
        compiler_params=pltpu.CompilerParams(
            collective_id=1, has_side_effects=True, vmem_limit_bytes=60 << 20
        ),
        name="back",
    )(
        *[one.reshape(4, 2, 2, *one.shape[1:]) for one in grads],
        queries, keys, values, outs_grad, normed, hat, weights, starts, *stats, small,
    )
    return [*totals, near, from_behind(far, "wide", -2), own, small, norm]


def plain_back(grads, attention, small, starts, stats, heads):
    queries, keys, values, outs_grad, normed, hat, weights = attention
    rows, width = queries.shape
    wide = lax.axis_size("wide")
    dq, dk, dv = attend_back(queries, keys, values, outs_grad, *stats, starts, heads)
    earlier = dot(dk, weights[:, width : 2 * width], 1, 1) + dot(dv, weights[:, 2 * width :], 1, 1)
    own = earlier[-rows:] + dot(dq, weights[:, :width], 1, 1)
    earlier = earlier[:-rows]
    all_grad = jnp.concatenate([earlier, own])
    dw = [dot(normed[-rows:], dq, 0, 0), dot(normed, dk, 0, 0), dot(normed, dv, 0, 0)]
    grads = [*grads, jnp.concatenate(dw, axis=1).reshape(wide, -1, 3 * width)]
    totals = [
        lax.psum(
            lax.psum_scatter(one.astype(F32), "wide", scatter_dimension=0, tiled=False), "dp"
        )
        for one in grads
    ]
    sums = {
        0: jnp.sum(all_grad * hat.astype(F32), axis=0),
        3: jnp.sum(all_grad, axis=0),
        4: jnp.sum(dq.astype(F32), axis=0),
        5: jnp.sum(dv.astype(F32), axis=0),
    }
    small = jnp.concatenate(
        [sums[k][None] if k in sums else small[k : k + 1] for k in range(small.shape[0])]
    )
    low = earlier.astype(BF16).reshape(2, rows, width)
    returned = [from_behind(low[1], "wide", -1), from_behind(low[0], "wide", -2)]
    squares = lax.psum(sum(jnp.sum(one * one) for one in totals), "wide")
    tile = jnp.zeros((8, 128), F32).at[0, 0].set(squares)
    return [*totals, *returned, own, lax.psum(small, ("dp", "wide")), tile]


F_TILE = 256


def grad_through_norm(grad, hat, scale, gain):
    scaled = grad * gain
    mean_plain = jnp.mean(scaled, axis=-1, keepdims=True)
    mean_cross = jnp.mean(scaled * hat, axis=-1, keepdims=True)
    return scale * (scaled - mean_plain - hat * mean_cross)


def down_sums(values):
    return jnp.sum(values, axis=0, keepdims=True)


def middle_kernel(
    head_size, c_ref, o_ref, x_ref, gy_ref, wo_ref, w1_ref, w2_ref, vec_ref, par_ref, scale_ref,
    out_ref, mid_ref, df_ref, a_ref, dz_ref, res_ref, do_ref, delta_ref, small_ref,
    act_all, slope, grad_all, stats, sums, x2, hat_post, hat_two, da,
):
    blocks, _, units = w1_ref.shape
    width = x_ref.shape[1]
    count = blocks * units

    @pl.when(pl.program_id(0) == 0)
    def _():
        sums[...] = jnp.zeros_like(sums)
        small_ref[...] = jnp.zeros_like(small_ref)

    stats[...] = jnp.zeros_like(stats)
    projected = dot(c_ref[...], wo_ref[...]) + vec_ref[6:7]
    value, hat, scale_post = layer_norm(projected, vec_ref[1:2], vec_ref[7:8])
    hat_post[...] = hat
    residual = x_ref[...].astype(F32) + value
    x2[...] = residual
    value, hat, scale_two = layer_norm(residual, vec_ref[2:3], vec_ref[8:9])
    hat_two[...] = hat
    a_ref[...] = value.astype(BF16)

    def columns(k):
        return pl.ds(pl.multiple_of(k * units, units), units)

    def forward(k, carry):
        pre = dot(a_ref[...], w1_ref[k]) + par_ref[2:3, columns(k)]
        half = 0.5 + 0.5 * lax.erf(pre * (0.5**0.5))
        value = pre * half
        act_all[k] = value
        slope[k] = half + pre * (jnp.exp(-0.5 * pre * pre) * (0.5 / jnp.pi) ** 0.5)
        stats[0] += lane_groups(value)
        stats[1] += lane_groups(value * value)
        return carry

    lax.fori_loop(0, blocks, forward, 0, unroll=4)
    mean = jnp.sum(stats[0], axis=1, keepdims=True) / count
    second = jnp.sum(stats[1], axis=1, keepdims=True) / count
    scale = lax.rsqrt(second - mean * mean + norm_epsilon)

    def middle(k, carry):
        here = columns(k)
        hat = (act_all[k] - mean) * scale
        mid_ref[:, here] = (hat * par_ref[0:1, here] + par_ref[1:2, here]).astype(BF16)
        down = dot(gy_ref[...], w2_ref[here, :], 1, 1)
        scaled = down * par_ref[0:1, here]
        act_all[k] = hat
        grad_all[k] = scaled
        stats[2] += lane_groups(scaled)
        stats[3] += lane_groups(scaled * hat)
        sums[0:1, here] += down_sums(down * hat)
        sums[1:2, here] += down_sums(down)
        return carry

    lax.fori_loop(0, blocks, middle, 0, unroll=4)
    plain = jnp.sum(stats[2], axis=1, keepdims=True) / count
    crossed = jnp.sum(stats[3], axis=1, keepdims=True) / count
    part = min(width, 512)
    for start in range(0, width, part):
        here = slice(start, start + part)
        total = dot(mid_ref[...], w2_ref[:, here])
        out_ref[:, here] = (x2[:, here] + (total + vec_ref[9:10, here])).astype(BF16)

    def backward(k, carry):
        here = columns(k)
        back = scale * (grad_all[k] - plain - act_all[k] * crossed) * slope[k]
        low = back.astype(BF16)
        df_ref[:, here] = low
        sums[2:3, here] += down_sums(low.astype(F32))
        return carry

    lax.fori_loop(0, blocks, backward, 0, unroll=4)
    da[...] = jnp.zeros_like(da)

    def back_out(k, carry):
        da[...] += dot(df_ref[:, columns(k)], w1_ref[k], 1, 1)
        return carry

    lax.fori_loop(0, blocks, back_out, 0, unroll=4)
    grad_in = gy_ref[...].astype(F32)
    rows_grad = da[...]
    residual_grad = grad_in + grad_through_norm(rows_grad, hat_two[...], scale_two, vec_ref[2:3])
    res_ref[...] = residual_grad
    dz = grad_through_norm(residual_grad, hat_post[...], scale_post, vec_ref[1:2]).astype(BF16)
    dz_ref[...] = dz
    for row, term in (
        (1, residual_grad * hat_post[...]),
        (2, rows_grad * hat_two[...]),
        (6, dz.astype(F32)),
        (7, residual_grad),
        (8, rows_grad),
        (9, grad_in),
    ):
        small_ref[row : row + 1] += down_sums(term)
    mixed_grad = dot(dz, wo_ref[...], 1, 1)
    outs = o_ref[...]
    low = (mixed_grad * scale_ref[...]).astype(BF16)
    do_ref[...] = low
    head_row = 10 + 3 * count // width
    small_ref[head_row : head_row + 1] += down_sums(mixed_grad * outs)
    heads = delta_ref.shape[0]
    lane = lax.broadcasted_iota(jnp.int32, (heads, width), 1)
    of = lax.broadcasted_iota(jnp.int32, (heads, width), 0) * head_size
    chosen = jnp.where(jnp.logical_and(lane >= of, lane < of + head_size), 1.0, 0.0)
    delta_ref[...] = lax.dot_general(
        chosen, low.astype(F32) * outs, (((1,), (1,)), ((), ())),
        precision=lax.Precision.HIGHEST, preferred_element_type=F32,
    )

    @pl.when(pl.program_id(0) == pl.num_programs(0) - 1)
    def _():
        for row in range(3):
            for start in range(0, count, width):
                at = 10 + (row * count + start) // width
                small_ref[at : at + 1] = sums[row : row + 1, start : start + width]


def middle_part(mixed, attended, tokens, out_grad, wo, w1, w2, vectors, par, scales, heads):
    rows, width = tokens.shape
    blocks, _, units = w1.shape
    hidden = blocks * units
    by_tile = lambda columns: pl.BlockSpec((F_TILE, columns), lambda t: (t, 0))
    once = lambda one: pl.BlockSpec(
        one.shape, lambda t: (0,) * len(one.shape), pipeline_mode=pl.Buffered(1)
    )
    small_rows = -(-(11 + 3 * hidden // width) // 8) * 8
    like = jax.ShapeDtypeStruct
    return pl.pallas_call(
        functools.partial(middle_kernel, width // heads),
        grid=(rows // F_TILE,),
        in_specs=[by_tile(width)] * 4 + [once(one) for one in (wo, w1, w2, vectors, par, scales)],
        out_specs=[
            by_tile(width),
            by_tile(hidden),
            by_tile(hidden),
            by_tile(width),
            by_tile(width),
            by_tile(width),
            by_tile(width),
            pl.BlockSpec((heads, F_TILE), lambda t: (0, t)),
            pl.BlockSpec((small_rows, width), lambda t: (0, 0)),
        ],
        out_shape=[
            like((rows, width), BF16),
            like((rows, hidden), BF16),
            like((rows, hidden), BF16),
            like((rows, width), BF16),
            like((rows, width), BF16),
            like((rows, width), F32),
            like((rows, width), BF16),
            like((heads, rows), F32),
            like((small_rows, width), F32),
        ],
        scratch_shapes=[pltpu.VMEM((blocks, F_TILE, units), F32)] * 3
        + [pltpu.VMEM((4, F_TILE, 128), F32), pltpu.VMEM((8, hidden), F32)]
        + [pltpu.VMEM((F_TILE, width), F32)] * 4,
        compiler_params=pltpu.CompilerParams(vmem_limit_bytes=60 << 20),
        name="middle_part",
    )(mixed, attended, tokens, out_grad, wo, w1, w2, vectors, par, scales)


def weights_kernel(a_ref, gy_ref, c_ref, dz_ref, mid_ref, df_ref, dw1_ref, dw2_ref, dwo_ref, a_t):
    @pl.when(pl.program_id(0) == 0)
    def _():
        a_t[...] = a_ref[...].T
        dwo_ref[...] = dot(c_ref[...].T, dz_ref[...]).astype(BF16)

    dw1_ref[0] = dot(a_t[...], df_ref[...]).astype(BF16)
    dw2_ref[0] = dot(mid_ref[...].T, gy_ref[...]).astype(BF16)


def weight_grads(rows, out_grad, mixed, proj_grad, middle, pre_grad, blocks):
    tokens, width = rows.shape
    units = middle.shape[1] // blocks
    whole = pl.BlockSpec((tokens, width), lambda k: (0, 0))
    block = pl.BlockSpec((tokens, units), lambda k: (0, k))
    return pl.pallas_call(
        weights_kernel,
        grid=(blocks,),
        in_specs=[whole] * 4 + [block, block],
        out_specs=[
            pl.BlockSpec((1, width, units), lambda k: (k, 0, 0)),
            pl.BlockSpec((1, units, width), lambda k: (k, 0, 0)),
            pl.BlockSpec((width, width), lambda k: (0, 0)),
        ],
        out_shape=[
            jax.ShapeDtypeStruct((blocks, width, units), BF16),
            jax.ShapeDtypeStruct((blocks, units, width), BF16),
            jax.ShapeDtypeStruct((width, width), BF16),
        ],
        scratch_shapes=[pltpu.VMEM((width, tokens), BF16)],
        compiler_params=pltpu.CompilerParams(vmem_limit_bytes=40 << 20),
        name="weight_grads",
    )(rows, out_grad, mixed, proj_grad, middle, pre_grad)


def plane_share(rows):
    return rows // 16 * 3 // 8 * 16


def unpack_small(full, vector_shape, hidden_shape):
    wide = full.shape[0]
    count, each = vector_shape
    vectors = full[:, :count, :each].transpose(1, 0, 2).reshape(count, -1)
    rows, size = hidden_shape
    if size % 128 == 0:
        hidden = full[:, count:].reshape(wide, rows, size)
    else:
        hidden = full[:, count:, :size]
    hidden = hidden.transpose(1, 0, 2).reshape(rows, -1)
    return vectors.astype(F32), hidden.astype(F32)


def regroup(blocks, units):
    slabs, rows, columns = blocks.shape
    join = max(1, units // columns)
    if join == 1:
        return blocks
    return blocks.reshape(slabs // join, join, rows, columns).transpose(0, 2, 1, 3).reshape(
        slabs // join, rows, join * columns
    )


def ungroup(blocks, columns):
    slabs, rows, units = blocks.shape
    join = units // columns
    if join == 1:
        return blocks
    return blocks.reshape(slabs, rows, join, columns).transpose(0, 2, 1, 3).reshape(
        slabs * join, rows, columns
    )


def body(
    inputs,
    out_grad,
    doc_lengths,
    step_count,
    qkv_weight,
    qkv_first,
    qkv_second,
    out_weight,
    out_first,
    out_second,
    fc1_weight,
    fc1_first,
    fc1_second,
    fc2_weight,
    fc2_first,
    fc2_second,
    model_vectors,
    vectors_first,
    vectors_second,
    hidden_vectors,
    hidden_first,
    hidden_second,
    head_scale,
    head_first,
    head_second,
):
    tokens_dev = inputs.shape[0]
    width = inputs.shape[1]
    heads_count = head_scale.shape[0]
    head_size = width // heads_count
    wide = lax.axis_size("wide")
    hidden_width = hidden_vectors.shape[1] * wide

    fc1_rows, fc2_rows = fc1_weight.shape[0], fc2_weight.shape[0]
    qkv_rows, out_rows = qkv_weight.shape[0], out_weight.shape[0]
    small = jnp.concatenate(
        [
            jnp.pad(model_vectors, ((0, 0), (0, max(0, 128 - model_vectors.shape[1])))),
            hidden_vectors.reshape(-1, min(128, hidden_vectors.shape[1])),
        ]
        if hidden_vectors.shape[1] % 128 == 0
        else [
            jnp.pad(one, ((0, 0), (0, 128 - one.shape[1]))) for one in (model_vectors, hidden_vectors)
        ]
    )
    heads_low = lax.optimization_barrier(head_scale.astype(BF16)).astype(F32)
    starts = doc_starts(
        doc_lengths, lax.axis_index("dp"), lax.axis_index("wide") * tokens_dev, tokens_dev
    )
    starts = jnp.maximum(starts - (lax.axis_index("wide") - 2) * tokens_dev, 0).reshape(1, -1)
    scales = jnp.repeat(heads_low, head_size).reshape(1, width)
    gathered = front(
        [
            small,
            qkv_weight,
            out_weight,
            fc1_weight,
            fc2_weight,
        ],
        (0, qkv_rows // 2, out_rows // 4, plane_share(fc1_rows), plane_share(fc2_rows)),
        inputs,
        starts,
        scales,
        heads_count,
    )
    qkv_full, out_full, fc1_full, fc2_full, hat_low, normed_low = gathered[:6]
    queries, keys_all, values_all, attended, mixed_low, log_totals, vectors, hidden_par = gathered[6:]
    fc2_full = fc2_full.reshape(hidden_width, width)
    output, middle_low, pre_low, rows_low, proj_low, residual_grad, attended_low, delta, small_grad = (
        middle_part(
            mixed_low,
            attended,
            inputs,
            out_grad,
            out_full.reshape(width, width),
            regroup(fc1_full, 256),
            fc2_full,
            vectors,
            hidden_par,
            scales,
            heads_count,
        )
    )
    fc1_grad, fc2_grad, out_weight_grad = weight_grads(
        rows_low, out_grad, mixed_low, proj_low, middle_low, pre_low, hidden_width // 256
    )
    fc1_part, fc2_part, out_part, qkv_part, near, far, own_grad, small_total, norm_tile = back(
        [
            ungroup(fc1_grad, fc1_weight.shape[1]),
            fc2_grad.reshape(wide, -1, width),
            out_weight_grad.reshape(wide, -1, width),
        ],
        (
            queries,
            keys_all,
            values_all,
            attended_low,
            normed_low,
            hat_low.reshape(-1, width),
            qkv_full.reshape(width, 3 * width),
        ),
        small_grad,
        starts,
        (log_totals, delta.reshape(log_totals.shape)),
        heads_count,
    )
    total_grad = own_grad + near.astype(F32) + far.astype(F32)
    _, hat_in, scale_in = layer_norm(inputs.astype(F32), vectors[0], vectors[3])
    input_grad = residual_grad + grad_through_norm(total_grad, hat_in, scale_in, vectors[0])
    vector_rows = model_vectors.shape[0]
    head_row = vector_rows + hidden_vectors.shape[0] * hidden_width // width
    vector_total = small_total[:vector_rows]
    hidden_total = small_total[vector_rows:head_row].reshape(hidden_vectors.shape[0], hidden_width)
    head_total = jnp.sum(small_total[head_row].reshape(heads_count, head_size), axis=1)
    place = lax.axis_index("wide")
    vector_part = lax.dynamic_slice_in_dim(
        vector_total, place * model_vectors.shape[1], model_vectors.shape[1], 1
    )
    hidden_part = lax.dynamic_slice_in_dim(
        hidden_total, place * hidden_vectors.shape[1], hidden_vectors.shape[1], 1
    )
    small_square = jnp.sum(small_total[:head_row] ** 2) + jnp.sum(head_total**2)
    grad_norm = jnp.sqrt(jnp.sum(norm_tile) + small_square)
    factor = jnp.minimum(1.0, clip_limit / (grad_norm + 1e-06))
    step = step_count[0].astype(F32)
    grads = (qkv_part, out_part, fc1_part, fc2_part, vector_part, hidden_part, head_total)
    params = (
        qkv_weight,
        out_weight,
        fc1_weight,
        fc2_weight,
        model_vectors,
        hidden_vectors,
        head_scale,
    )
    firsts = (qkv_first, out_first, fc1_first, fc2_first, vectors_first, hidden_first, head_first)
    seconds = (
        qkv_second,
        out_second,
        fc1_second,
        fc2_second,
        vectors_second,
        hidden_second,
        head_second,
    )
    rates = (
        matrix_rate,
        matrix_rate,
        matrix_rate,
        matrix_rate,
        vector_rate,
        vector_rate,
        vector_rate,
    )
    decays = (weight_decay, weight_decay, weight_decay, weight_decay, 0.0, 0.0, 0.0)
    updated = []
    for number in range(7):
        updated.extend(
            adam_step(
                grads[number] * factor,
                params[number],
                firsts[number],
                seconds[number],
                step,
                rates[number],
                decays[number],
            )
        )
    return (
        output,
        input_grad,
        grad_norm.reshape(1),
        updated[0],
        updated[1],
        updated[2],
        updated[3],
        updated[4],
        updated[5],
        updated[6],
        updated[7],
        updated[8],
        updated[9],
        updated[10],
        updated[11],
        updated[12],
        updated[13],
        updated[14],
        updated[15],
        updated[16],
        updated[17],
        updated[18],
        updated[19],
        updated[20],
    )


def solution(mesh):
    placed = (
        P(("dp", "wide"), None),
        P(("dp", "wide"), None),
        P(),
        P(),
        P("wide", None),
        P("wide", None),
        P("wide", None),
        P("wide", None),
        P("wide", None),
        P("wide", None),
        P(None, "wide"),
        P(None, "wide"),
        P(None, "wide"),
        P("wide", None),
        P("wide", None),
        P("wide", None),
        P(None, "wide"),
        P(None, "wide"),
        P(None, "wide"),
        P(None, "wide"),
        P(None, "wide"),
        P(None, "wide"),
        P(),
        P(),
        P(),
    )
    return jax.shard_map(
        body,
        mesh=mesh,
        in_specs=placed,
        out_specs=(
            P(("dp", "wide"), None),
            P(("dp", "wide"), None),
            P(),
            P("wide", None),
            P("wide", None),
            P("wide", None),
            P("wide", None),
            P("wide", None),
            P("wide", None),
            P(None, "wide"),
            P(None, "wide"),
            P(None, "wide"),
            P("wide", None),
            P("wide", None),
            P("wide", None),
            P(None, "wide"),
            P(None, "wide"),
            P(None, "wide"),
            P(None, "wide"),
            P(None, "wide"),
            P(None, "wide"),
            P(),
            P(),
            P(),
        ),
        check_vma=False,
    )
```

```python
import functools

import jax
import jax.numpy as jnp
from jax import lax
from jax.experimental import pallas as pl
from jax.experimental.pallas import tpu as pltpu
from jax.sharding import PartitionSpec as P

DOC_MOST = 1024
MESH = pl.DeviceIdType.MESH
HBM = pl.BlockSpec(memory_space=pltpu.HBM)
VMEM = pl.BlockSpec(memory_space=pltpu.VMEM)
BF16 = jnp.bfloat16
F32 = jnp.float32

norm_epsilon = 1e-05
clip_limit = 1.0
first_decay = 0.9
second_decay = 0.98
adam_epsilon = 1e-08
matrix_rate = 0.1
vector_rate = 0.4
weight_decay = 0.1
masked_score = -1e30


def layer_norm(values_in, gain, shift):
    center = values_in - jnp.mean(values_in, axis=-1, keepdims=True)
    variance = jnp.mean(center * center, axis=-1, keepdims=True)
    scale = lax.rsqrt(variance + norm_epsilon)
    normed = center * scale
    return (normed * gain + shift, normed, scale)


def doc_starts(doc_lengths, row, first, count):
    ends = lax.dynamic_slice_in_dim(jnp.cumsum(doc_lengths, axis=1), row, 1, 0)[0]
    places = first + jnp.arange(count, dtype=jnp.int32)
    return jnp.max(jnp.where(ends[None, :] <= places[:, None], ends[None, :], 0), axis=1)


def adam_step(grad, weight, first, second, step, rate, decay):
    first_new = first_decay * first + (1.0 - first_decay) * grad
    second_new = second_decay * second + (1.0 - second_decay) * grad * grad
    fix_one = 1.0 - jnp.power(jnp.float32(first_decay), step)
    fix_two = 1.0 - jnp.power(jnp.float32(second_decay), step)
    direction = first_new / fix_one / (jnp.sqrt(second_new / fix_two) + adam_epsilon)
    weight_new = weight - rate * (direction + decay * weight)
    return (first_new, second_new, weight_new)


def from_behind(shard, axis, by):
    count = lax.axis_size(axis)
    pairs = [(i, i + by) for i in range(count) if 0 <= i + by < count]
    return lax.ppermute(shard, axis, pairs)


def dot(a, b, left=1, right=0):
    return lax.dot_general(
        a, b, (((left,), (right,)), ((), ())), preferred_element_type=F32
    )


Q_TILE = 256


def split_pair(pair, size):
    lane = lax.broadcasted_iota(jnp.int32, pair.shape, 1)
    zero = jnp.zeros_like(pair)
    return jnp.where(lane < size, pair, zero), jnp.where(lane < size, zero, pair)


def fill_mask(starts, bias, tokens, span, keys_before):
    for tile in range(tokens // Q_TILE):
        query = lax.broadcasted_iota(jnp.int32, (span, Q_TILE), 1) + tile * Q_TILE + keys_before
        key = lax.broadcasted_iota(jnp.int32, (span, Q_TILE), 0) + tile * Q_TILE
        first = starts[:, tile * Q_TILE : (tile + 1) * Q_TILE]
        seen = jnp.logical_and(key <= query, key >= first)
        bias[tile] = jnp.where(seen, 0.0, masked_score)


def attend_pair(size, q_ref, k_ref, v_ref, scale_ref, o_ref, c_ref, lse_ref, bias, vt, ot):
    tokens, window = q_ref.shape[0], k_ref.shape[0]
    span = window - tokens + Q_TILE
    vt[...] = v_ref[...].T
    for tile in range(tokens // Q_TILE):
        rows = slice(tile * Q_TILE, (tile + 1) * Q_TILE)
        keys = slice(tile * Q_TILE, tile * Q_TILE + span)
        k_pair = k_ref[keys, :]
        for head, q_one in enumerate(split_pair(q_ref[rows, :], size)):
            scores = dot(k_pair, q_one, 1, 1) + bias[tile]
            highest = jnp.max(scores, axis=0, keepdims=True)
            powers = jnp.exp(scores - highest)
            total = jnp.sum(powers, axis=0, keepdims=True)
            probs = (powers * (1.0 / total)).astype(BF16)
            lse_ref[head : head + 1, rows] = highest + jnp.log(total)
            part = slice(head * size, (head + 1) * size)
            ot[part, rows] = dot(vt[part, keys], probs)
    attended = ot[...].T
    o_ref[...] = attended
    c_ref[...] = (attended * scale_ref[...]).astype(BF16)


def attend_kernel(size, starts, scale_ref, q_ref, k_ref, v_ref, o_ref, c_ref, lse_ref, bias, vt, ot):
    tokens, window = q_ref.shape[0], k_ref.shape[0]
    before = window - tokens

    @pl.when(pl.program_id(0) == 0)
    def _():
        fill_mask(starts, bias, tokens, before + Q_TILE, before)

    attend_pair(size, q_ref, k_ref, v_ref, scale_ref, o_ref, c_ref, lse_ref.at[0], bias, vt, ot)


def attend(queries, keys, values, starts, scales, heads):
    tokens, width = queries.shape
    window = keys.shape[0]
    pairs = heads // 2
    lanes = width // pairs
    span = window - tokens + Q_TILE
    by_rows = lambda rows: pl.BlockSpec((rows, lanes), lambda p: (0, p))
    return pl.pallas_call(
        functools.partial(attend_kernel, width // heads),
        grid=(pairs,),
        in_specs=[
            pl.BlockSpec((1, tokens), lambda p: (0, 0)),
            by_rows(1),
            by_rows(tokens),
            by_rows(window),
            by_rows(window),
        ],
        out_specs=[
            by_rows(tokens),
            by_rows(tokens),
            pl.BlockSpec((1, 2, tokens), lambda p: (p, 0, 0)),
        ],
        out_shape=[
            jax.ShapeDtypeStruct((tokens, width), F32),
            jax.ShapeDtypeStruct((tokens, width), BF16),
            jax.ShapeDtypeStruct((pairs, 2, tokens), F32),
        ],
        scratch_shapes=[
            pltpu.VMEM((tokens // Q_TILE, span, Q_TILE), F32),
            pltpu.VMEM((lanes, window), BF16),
            pltpu.VMEM((lanes, tokens), F32),
        ],
        compiler_params=pltpu.CompilerParams(vmem_limit_bytes=40 << 20),
        name="attend",
    )(starts, scales, queries, keys, values)


def attend_back_pair(
    size, q_ref, k_ref, v_ref, do_ref, lse_ref, delta_ref, dq_ref, dk_ref, dv_ref, bias, dk_sum, dv_sum, kt, dqt
):
    tokens, window = q_ref.shape[0], k_ref.shape[0]
    span = window - tokens + Q_TILE
    kt[...] = k_ref[...].T
    dk_sum[...] = jnp.zeros_like(dk_sum)
    dv_sum[...] = jnp.zeros_like(dv_sum)
    for tile in range(tokens // Q_TILE):
        rows = slice(tile * Q_TILE, (tile + 1) * Q_TILE)
        keys = slice(tile * Q_TILE, tile * Q_TILE + span)
        k_pair, v_pair = k_ref[keys, :], v_ref[keys, :]
        for head, (q_one, do_one) in enumerate(
            zip(split_pair(q_ref[rows, :], size), split_pair(do_ref[rows, :], size))
        ):
            scores = dot(k_pair, q_one, 1, 1) + bias[tile]
            probs = jnp.exp(scores - lse_ref[head : head + 1, rows])
            grads = dot(v_pair, do_one, 1, 1) - delta_ref[head : head + 1, rows]
            low = (probs * grads).astype(BF16)
            dv_sum[keys, :] += dot(probs.astype(BF16), do_one)
            dk_sum[keys, :] += dot(low, q_one)
            part = slice(head * size, (head + 1) * size)
            dqt[part, rows] = dot(kt[part, keys], low)
    dq_ref[...] = (dqt[...].T * size ** (-0.5)).astype(BF16)
    dk_ref[...] = dk_sum[...].astype(BF16)
    dv_ref[...] = dv_sum[...].astype(BF16)


def attend_back_kernel(
    size, starts, q_ref, k_ref, v_ref, do_ref, lse_ref, delta_ref, dq_ref, dk_ref, dv_ref, bias, *scratch
):
    tokens, window = q_ref.shape[0], k_ref.shape[0]
    before = window - tokens

    @pl.when(pl.program_id(0) == 0)
    def _():
        fill_mask(starts, bias, tokens, before + Q_TILE, before)

    attend_back_pair(
        size, q_ref, k_ref, v_ref, do_ref, lse_ref.at[0], delta_ref.at[0], dq_ref, dk_ref, dv_ref, bias, *scratch
    )


def attend_back(queries, keys, values, outs_grad, lse, delta, starts, heads):
    tokens, width = queries.shape
    window = keys.shape[0]
    pairs = heads // 2
    lanes = width // pairs
    span = window - tokens + Q_TILE
    by_rows = lambda rows: pl.BlockSpec((rows, lanes), lambda p: (0, p))
    stats = pl.BlockSpec((1, 2, tokens), lambda p: (p, 0, 0))
    return pl.pallas_call(
        functools.partial(attend_back_kernel, width // heads),
        grid=(pairs,),
        in_specs=[
            pl.BlockSpec((1, tokens), lambda p: (0, 0)),
            by_rows(tokens),
            by_rows(window),
            by_rows(window),
            by_rows(tokens),
            stats,
            stats,
        ],
        out_specs=[
            by_rows(tokens),
            by_rows(window),
            by_rows(window),
        ],
        out_shape=[
            jax.ShapeDtypeStruct((tokens, width), BF16),
            jax.ShapeDtypeStruct((window, width), BF16),
            jax.ShapeDtypeStruct((window, width), BF16),
        ],
        scratch_shapes=[
            pltpu.VMEM((tokens // Q_TILE, span, Q_TILE), F32),
            pltpu.VMEM((window, lanes), F32),
            pltpu.VMEM((window, lanes), F32),
            pltpu.VMEM((lanes, window), BF16),
            pltpu.VMEM((lanes, tokens), F32),
        ],
        compiler_params=pltpu.CompilerParams(vmem_limit_bytes=40 << 20),
        name="attend_back",
    )(starts, queries, keys, values, outs_grad, lse, delta)


class Place:
    def __init__(self):
        self.y = lax.axis_index("dp")
        self.w = lax.axis_index("wide")
        self.z = self.w // 4
        self.x = (self.w // 2) % 2
        self.c = self.w % 2

    def slab(self, z, x, c):
        return z * 4 + x * 2 + c

    def wide(self, w):
        return (self.y, w)

    def core_mate(self):
        return self.wide(self.slab(self.z, self.x, 1 - self.c))

    def x_mate(self):
        return self.wide(self.slab(self.z, 1 - self.x, self.c))

    def y_mate(self):
        return (1 - self.y, self.w)

    def up(self):
        return self.wide(lax.rem(self.w + 4, 16))

    def down(self):
        return self.wide(lax.rem(self.w + 12, 16))


def greet(me, extra=()):
    barrier = pltpu.get_barrier_semaphore()

    def hello(target):
        pl.semaphore_signal(barrier, inc=1, device_id=target, device_id_type=MESH)

    always = [me.core_mate(), me.x_mate(), me.y_mate(), *extra]
    sometimes = [
        (me.z < 3, me.up()),
        (me.z > 0, me.down()),
        (me.w < 14, me.wide(lax.rem(me.w + 2, 16))),
        (me.w >= 2, me.wide(lax.rem(me.w + 14, 16))),
    ]
    for target in always:
        hello(target)
    for holds, target in sometimes:
        pl.when(holds)(functools.partial(hello, target))
    count = len(always) + sum(holds.astype(jnp.int32) for holds, _ in sometimes)
    pl.semaphore_wait(barrier, count)


class Wire:
    def __init__(self, send, recv):
        self.send, self.recv = send, recv
        self.planned = []

    def copy(self, source, target, index, device):
        return pltpu.make_async_remote_copy(
            src_ref=source,
            dst_ref=target,
            send_sem=self.send.at[index],
            recv_sem=self.recv.at[index],
            device_id=device,
            device_id_type=MESH,
        )

    def put(self, source, target, index, device, holds=None):
        moved = self.copy(source, target, index, device)
        self.planned.append((holds, moved))
        return lambda: when(holds, moved.start)

    def got(self, target, index, device, holds=None):
        moved = self.copy(target, target, index, device)
        return lambda: when(holds, moved.wait_recv)

    def finish(self):
        for holds, moved in self.planned:
            when(holds, moved.wait_send)


def act(actions):
    for one in actions:
        one()


def both(*conditions):
    held = [one for one in conditions if one is not None]
    total = held[0] if held else None
    for one in held[1:]:
        total = jnp.logical_and(total, one)
    return total


def when(holds, action):
    if holds is None:
        action()
    else:
        pl.when(holds)(action)


AG_SEMS = 44


def gather_ticks(me, wire, base, own, full, third, side_first):
    rows = own.shape[0]
    plane = (
        pl.ds(pl.multiple_of(me.y * third, 16), rows - third) if third else pl.ds(0, rows)
    )
    share = pl.ds(pl.multiple_of(me.y * (rows - third), 16), third) if third else None
    other = pl.ds(pl.multiple_of((1 - me.y) * (rows - third), 16), third) if third else None
    my_slab = me.slab(me.z, me.x, me.c)
    ups, downs, xs, ys, cs, ts, far_ups, far_downs = (
        base + k for k in (0, 4, 8, 12, 20, 28, 36, 40)
    )
    mine = me.z * 2 + me.x

    def pass_on(z, x, holds):
        slab = me.slab(z, x, me.c)
        place = z * 2 + x
        block = full.at[slab, plane]
        actions = []
        if third:
            piece = full.at[slab, share]
            actions.append(wire.put(piece, piece, ys + place, me.y_mate(), holds))
        actions.append(wire.put(block, block, cs + place, me.core_mate(), holds))
        return actions

    def arrivals(away):
        for z, holds, onward, follow, above in (
            (me.z - away, me.z - away >= 0, me.up(), me.z < 3, False),
            (me.z + away, me.z + away <= 3, me.down(), me.z > 0, True),
        ):
            yield lax.rem(z + 4, 4), holds, onward, follow, above

    goal = full.at[my_slab, plane]
    ticks = {
        "own": [
            wire.put(own.at[plane], goal, ups + me.z, me.up(), me.z < 3),
            wire.put(own.at[plane], goal, downs + me.z, me.down(), me.z > 0),
            wire.put(own.at[plane], goal, xs + me.z, me.x_mate()),
            wire.put(own, full.at[my_slab], cs + mine, me.core_mate()),
        ]
    }
    for tick in range(1, 5):
        actions = []
        if tick < 4:
            for z, holds, onward, follow, above in arrivals(tick):
                sems = downs if above else ups
                block = full.at[me.slab(z, me.x, me.c), plane]
                actions.append(wire.got(block, sems + z, onward, holds))
                actions.append(wire.put(block, block, sems + z, onward, both(holds, follow)))
                if not side_first:
                    actions.append(wire.put(block, block, xs + z, me.x_mate(), holds))
                actions += pass_on(z, me.x, holds)
        if side_first and tick == 1:
            block = full.at[me.slab(me.z, 1 - me.x, me.c), plane]
            actions.append(wire.got(block, xs + me.z, me.x_mate()))
            actions.append(wire.put(block, block, far_ups + me.z, me.up(), me.z < 3))
            actions.append(wire.put(block, block, far_downs + me.z, me.down(), me.z > 0))
            actions += pass_on(me.z, 1 - me.x, None)
        elif side_first:
            for z, holds, onward, follow, above in arrivals(tick - 1):
                sems = far_downs if above else far_ups
                block = full.at[me.slab(z, 1 - me.x, me.c), plane]
                actions.append(wire.got(block, sems + z, onward, holds))
                actions.append(wire.put(block, block, sems + z, onward, both(holds, follow)))
                actions += pass_on(z, 1 - me.x, holds)
        ticks["line", tick] = actions
    for away in range(4):
        actions = []
        if not side_first:
            cases = arrivals(away) if away else [(me.z, None, None, None, None)]
            for z, holds, *_ in cases:
                block = full.at[me.slab(z, 1 - me.x, me.c), plane]
                actions.append(wire.got(block, xs + z, me.x_mate(), holds))
                actions += pass_on(z, 1 - me.x, holds)
        ticks["side", away] = actions
    actions = []
    if third:
        for k in range(1, 8):
            place = lax.rem(mine + k, 8)
            piece = full.at[me.slab(place // 2, place % 2, me.c), other]
            actions.append(wire.got(piece, ys + place, me.y_mate()))
            actions.append(wire.put(piece, piece, ts + place, me.core_mate()))
    ticks["shares"] = actions
    actions = [wire.got(full.at[me.slab(me.z, me.x, 1 - me.c)], cs + mine, me.core_mate())]
    for k in range(1, 8):
        place = lax.rem(mine + k, 8)
        slab = me.slab(place // 2, place % 2, 1 - me.c)
        actions.append(wire.got(full.at[slab, plane], cs + place, me.core_mate()))
        if third:
            actions.append(wire.got(full.at[slab, other], ts + place, me.core_mate()))
    ticks["end"] = actions
    return ticks


FRONT_BLOCK = 256
FRONT_TICKS = (
    (2, (("line", 3),)),
    (5, (("line", 4), ("side", 0))),
    (7, (("side", 1),)),
)
FRONT_LAST = (("side", 2), ("side", 3))


def round_rows(target, source):
    rows, columns = source.shape
    chunk = row_chunk(rows, columns, 32768)

    def step(number, carry):
        here = pl.ds(pl.multiple_of(number * chunk, 16), chunk)
        target[here] = source[here].astype(target.dtype)
        return carry

    lax.fori_loop(0, rows // chunk, step, 0)


def front_kernel(thirds, head_size, *refs):
    masters, (tokens, starts, scale_ref) = refs[:5], refs[5:8]
    fulls, outs = refs[8:12], refs[12:19]
    xs_out, a_out, q_out, k_out, v_out, o_out, c_out = outs
    lse_ref, vecs, par = refs[19:22]
    (xs, a_all, qkv, q_all, k_all, v_all, o_all, c_all, small, bias, vt, ot, *owns, send, recv, local) = refs[22:]
    for master, own in zip(masters, owns):
        round_rows(own, master)
    me = Place()
    count = len(owns)
    width = tokens.shape[1]
    rows = tokens.shape[0]
    window = 3 * rows
    before = window - rows
    span = before + Q_TILE
    landings = (small, qkv, *fulls[1:])
    keep = [
        pltpu.make_async_copy(own, full.at[me.w], local.at[k])
        for k, (own, full) in enumerate(zip(owns, landings))
    ] + [pltpu.make_async_copy(tokens, xs.at[2], local.at[count])]
    for one in keep:
        one.start()

    def clear(slot):
        xs[slot] = jnp.zeros((rows, width), BF16)

    pl.when(me.w < 2)(functools.partial(clear, 0))
    pl.when(me.w < 1)(functools.partial(clear, 1))
    wire = Wire(send, recv)
    first, second = AG_SEMS * count, AG_SEMS * count + 1
    ticks = [
        gather_ticks(me, wire, AG_SEMS * k, own, landing, third, k == 4)
        for k, (own, landing, third) in enumerate(zip(owns, landings, thirds))
    ]
    send_block = wire.put(tokens, xs.at[0], first, me.wide(lax.rem(me.w + 2, 16)), me.w < 14)
    send_near = wire.put(tokens, xs.at[1], second, me.core_mate(), me.c == 0)
    get_block = wire.got(xs.at[0], first, me.core_mate(), me.w >= 2)
    passes = both(me.c == 1, me.w >= 2)
    pass_block = wire.copy(xs.at[0], xs.at[1], second, me.core_mate())
    get_near = wire.got(xs.at[1], second, me.core_mate(), me.w >= 1)
    greet(me)
    early, late = ticks[:2], ticks[2:]

    def go(group, *names):
        for name in names:
            for one in group:
                act(one[name])

    go(early, "own", ("line", 1), ("line", 2), ("line", 3))
    act(late[2]["own"])
    send_block()
    send_near()
    go(late[:2], "own")
    fill_mask(starts, bias, rows, span, before)
    go(early, ("side", 0), ("side", 1), ("side", 2), ("side", 3), "shares", "end")
    for one in keep:
        one.wait()
    shared = [pltpu.make_async_copy(qkv, fulls[0], local.at[1])]
    for one in shared:
        one.start()

    lane = lax.broadcasted_iota(jnp.int32, (16, 128), 1)
    for pair in range(8):
        even = small[2 * pair].astype(F32)
        odd = pltpu.roll(small[2 * pair + 1].astype(F32), 64, 1)
        vecs[:, pair * 128 : (pair + 1) * 128] = jnp.where(lane < 64, even, odd)
    for slab in range(16):
        values = small[slab].astype(F32)
        for row in range(3):
            for half in range(2):
                at = slab * 256 + half * 128
                par[row : row + 1, at : at + 128] = values[10 + 2 * row + half][None]

    def project(first_column, column, a_rows):
        weights = qkv[:, :, pl.ds(first_column + column, FRONT_BLOCK)].reshape(width, FRONT_BLOCK)
        return dot(a_rows, weights)

    per = rows // FRONT_BLOCK

    def normalize(number, carry):
        here = pl.ds(pl.multiple_of(lax.rem(number, per) * FRONT_BLOCK, FRONT_BLOCK), FRONT_BLOCK)
        there = pl.ds(pl.multiple_of(number * FRONT_BLOCK, FRONT_BLOCK), FRONT_BLOCK)
        value, hat, _ = layer_norm(xs[number // per, here].astype(F32), vecs[0:1], vecs[3:4])
        xs[number // per, here] = hat.astype(BF16)
        low = value.astype(BF16)
        a_all[there] = low
        for column in range(0, width, FRONT_BLOCK):
            columns = slice(column, column + FRONT_BLOCK)
            k_all[there, columns] = project(width, column, low).astype(BF16)
            v_all[there, columns] = (
                project(2 * width, column, low) + vecs[5:6, columns]
            ).astype(BF16)
        return carry

    lax.fori_loop(2 * per, 3 * per, normalize, 0)
    for number in range(per):
        here = pl.ds(number * FRONT_BLOCK, FRONT_BLOCK)
        low = a_all[before + number * FRONT_BLOCK : before + (number + 1) * FRONT_BLOCK]
        for column in range(0, width, FRONT_BLOCK):
            columns = slice(column, column + FRONT_BLOCK)
            query = (project(0, column, low) + vecs[4:5, columns]).astype(BF16)
            q_all[here, columns] = query * jnp.asarray(head_size ** (-0.5), BF16)
    go(late, ("line", 1))
    get_block()
    when(passes, pass_block.start)
    get_near()
    when(passes, pass_block.wait_send)
    lax.fori_loop(0, 2 * per, normalize, 0)
    go(late, ("line", 2))
    kept = [
        pltpu.make_async_copy(one, out, local.at[2 + k])
        for k, (one, out) in enumerate(
            ((a_all, a_out), (q_all, q_out), (k_all, k_out), (v_all, v_out), (xs, xs_out))
        )
    ]
    for one in kept:
        one.start()

    def pair_step(pair, carry):
        lanes = pl.ds(pl.multiple_of(pair * 128, 128), 128)
        attend_pair(
            head_size, q_all.at[:, lanes], k_all.at[:, lanes], v_all.at[:, lanes],
            scale_ref.at[:, lanes], o_all.at[:, lanes], c_all.at[:, lanes], lse_ref.at[pair], bias, vt, ot,
        )
        for due, names in FRONT_TICKS:
            pl.when(pair == due)(functools.partial(go, late, *names))
        return carry

    lax.fori_loop(0, width // 128, pair_step, 0)
    results = [
        pltpu.make_async_copy(o_all, o_out, local.at[7]),
        pltpu.make_async_copy(c_all, c_out, local.at[8]),
    ]
    for one in results:
        one.start()
    go(late, *FRONT_LAST, "shares", "end")
    wire.finish()
    for one in shared + kept + results:
        one.wait()


def plain_front(shards, tokens, starts, scales, heads):
    width = tokens.shape[1]
    fulls = [lax.all_gather(one.astype(BF16), "wide", axis=0, tiled=False) for one in shards]
    each, units = width // fulls[0].shape[0], shards[3].shape[1]
    vectors, par = unpack_small(fulls[0], (10, each), (3, units))
    window = jnp.stack([from_behind(tokens, "wide", 2), from_behind(tokens, "wide", 1), tokens])
    normed, hat, _ = layer_norm(window.reshape(-1, width).astype(F32), vectors[0], vectors[3])
    low = normed.astype(BF16)
    weights = fulls[1].reshape(width, 3 * width)
    queries = dot(low[-tokens.shape[0] :], weights[:, :width]) + vectors[4]
    queries = queries.astype(BF16) * jnp.asarray((width // heads) ** (-0.5), BF16)
    keys = dot(low, weights[:, width : 2 * width]).astype(BF16)
    values = (dot(low, weights[:, 2 * width :]) + vectors[5]).astype(BF16)
    attended = attend(queries, keys, values, starts, scales, heads)
    hat_low = hat.astype(BF16).reshape(window.shape)
    return [*fulls[1:], hat_low, low, queries, keys, values, *attended, vectors, par]


def front(shards, thirds, tokens, starts, scales, heads):
    rows, width = tokens.shape
    wide = lax.axis_size("wide")
    if lax.axis_size("dp") != 2 or wide != 16:
        return plain_front(shards, tokens, starts, scales, heads)
    window = 3 * rows
    like = jax.ShapeDtypeStruct
    out_shape = [like((wide, *one.shape), BF16) for one in shards[1:]] + [
        like((3, rows, width), BF16),
        like((window, width), BF16),
        like((rows, width), BF16),
        like((window, width), BF16),
        like((window, width), BF16),
        like((rows, width), F32),
        like((rows, width), BF16),
        like((heads // 2, 2, rows), F32),
        like((16, width), F32),
        like((8, wide * shards[3].shape[1]), F32),
    ]
    sems = AG_SEMS * len(shards) + 2
    scratch = [
        ((3, rows, width), BF16),
        ((window, width), BF16),
        ((wide, *shards[1].shape), BF16),
        ((rows, width), BF16),
        ((window, width), BF16),
        ((window, width), BF16),
        ((rows, width), F32),
        ((rows, width), BF16),
        ((wide, *shards[0].shape), BF16),
        ((rows // Q_TILE, window - rows + Q_TILE, Q_TILE), F32),
        ((128, window), BF16),
        ((128, rows), F32),
        *[(one.shape, BF16) for one in shards],
    ]
    return pl.pallas_call(
        functools.partial(front_kernel, thirds, width // heads),
        out_shape=out_shape,
        in_specs=[VMEM] * 8,
        out_specs=[HBM] * 11 + [VMEM] * 3,
        scratch_shapes=[pltpu.VMEM(shape, dtype) for shape, dtype in scratch]
        + [
            pltpu.SemaphoreType.DMA((sems,)),
            pltpu.SemaphoreType.DMA((sems,)),
            pltpu.SemaphoreType.DMA((9,)),
        ],
        compiler_params=pltpu.CompilerParams(
            collective_id=0, has_side_effects=True, vmem_limit_bytes=58 << 20
        ),
        name="front",
    )(*shards, tokens, starts, scales)


def row_chunk(rows, columns, most):
    chunk = min(rows, max(16, most // columns // 16 * 16))
    while rows % chunk:
        chunk -= 16
    return chunk


def accumulate(target, source):
    *lead, rows, columns = source.shape
    chunk = row_chunk(rows, columns, 65536)
    per = rows // chunk
    many = per
    for size in lead:
        many *= size

    def step(number, carry):
        part = pl.ds(pl.multiple_of(lax.rem(number, per) * chunk, 16), chunk)
        rest, index = number // per, []
        for size in reversed(lead):
            index.insert(0, lax.rem(rest, size))
            rest = rest // size
        at = (*index, part)
        target[at] = (target[at].astype(F32) + source[at].astype(F32)).astype(target.dtype)
        return carry

    lax.fori_loop(0, many, step, 0)


RS_SEMS = 12


def reduce_ticks(
    me, wire, base, local, grad, quarter, held, bufs, final, squares, waits_for=None, frees=None
):
    from_core, from_y, from_x, from_down, from_up, from_last = bufs
    count, columns = held.shape[-2:]
    inside = count - quarter
    plane = pl.ds(pl.multiple_of(me.y * quarter, 16), inside) if quarter else pl.ds(0, count)
    mine = held.at[:, me.x, plane]
    take = pltpu.make_async_copy(grad.at[:, :, me.c], held, local)
    put_core = wire.put(grad.at[:, :, 1 - me.c], from_core, base, me.core_mate())
    got_core = wire.got(from_core, base, me.core_mate())
    put_x = wire.put(held.at[:, 1 - me.x, plane], from_x, base + 2, me.x_mate())
    got_x = wire.got(from_x, base + 2, me.x_mate())
    put_last = wire.put(mine.at[me.z], from_last, base + 3, me.y_mate())
    got_last = wire.got(from_last, base + 3, me.y_mate())
    if quarter:
        share = held.at[:, :, pl.ds(pl.multiple_of(me.y * inside, 16), quarter)]
        other = held.at[:, :, pl.ds(pl.multiple_of((1 - me.y) * inside, 16), quarter)]
        put_y = wire.put(other, from_y, base + 1, me.y_mate())
        got_y = wire.got(from_y, base + 1, me.y_mate())

    partners = [(None, one) for one in (me.core_mate(), me.x_mate(), me.y_mate())]
    partners += [(me.z < 3, me.up()), (me.z > 0, me.down())]

    def start():
        if waits_for is not None:
            ends = (me.z < 3).astype(jnp.int32) + (me.z > 0).astype(jnp.int32)
            pl.semaphore_wait(waits_for, 3 + ends)
        take.start()
        put_core()

    def join_core():
        take.wait()
        got_core()
        accumulate(held, from_core)
        (put_y if quarter else put_x)()

    def join_y():
        got_y()
        accumulate(share, from_y)
        put_x()

    lines = []
    for tick in range(4):
        actions = []
        for place, sign, source, sems, onward, back in (
            (me.z, 1, from_down, 4, me.up(), me.down()),
            (3 - me.z, -1, from_up, 8, me.down(), me.up()),
        ):
            goal = me.z if tick == 3 else lax.rem(me.z + sign * (3 - tick) + 8, 4)
            sends = None if tick == 3 else both(place <= tick, place < 3)
            block, arrived = mine.at[goal], source.at[goal]
            got = wire.got(arrived, base + sems + goal, back)

            def take_in(block=block, arrived=arrived, got=got):
                got()
                accumulate(block, arrived)

            actions.append(
                functools.partial(when, both(sends, place > 0), take_in)
            )
            if sends is not None:
                actions.append(wire.put(block, arrived, base + sems + goal, onward, sends))
        lines.append(actions)

    def join_x():
        got_x()
        accumulate(mine, from_x)
        act(lines[0])

    def end_line():
        act(lines[3])
        put_last()

    def finish():
        got_last()
        own = held.at[me.z, me.x]
        middle = count - 2 * quarter
        chunk = row_chunk(middle, columns, 32768)

        def add_planes(number, carry):
            at = pl.multiple_of(quarter + number * chunk, 16)
            there = pl.multiple_of(at - (1 - me.y) * quarter, 16)
            final[pl.ds(at, chunk)] = own[pl.ds(at, chunk)].astype(F32) + from_last[
                pl.ds(there, chunk)
            ].astype(F32)
            return carry

        lax.fori_loop(0, middle // chunk, add_planes, 0)
        if quarter:
            for plane_of, at, there in ((0, 0, 0), (1, count - quarter, count - 2 * quarter)):

                def from_held(at=at):
                    final[pl.ds(at, quarter)] = own[pl.ds(at, quarter)].astype(F32)

                def from_mate(at=at, there=there):
                    final[pl.ds(at, quarter)] = from_last[pl.ds(there, quarter)].astype(F32)

                pl.when(me.y == plane_of)(from_held)
                pl.when(me.y != plane_of)(from_mate)

        def square(number, total):
            value = final[pl.ds(pl.multiple_of(number * 8, 8), 8)]
            return total + lane_groups(value * value)

        squares[...] = squares[...] + lax.fori_loop(
            0, count // 8, square, jnp.zeros((8, 128), F32)
        )
        if frees is not None:
            wire.finish()
            for holds, device in partners:
                when(
                    holds,
                    functools.partial(
                        pl.semaphore_signal, frees, inc=1, device_id=device, device_id_type=MESH
                    ),
                )

    return [
        start, join_core, *([join_y] if quarter else []), join_x,
        functools.partial(act, lines[1]), functools.partial(act, lines[2]), end_line, finish,
    ]


def in_rounds(sequences):
    last = max(start + len(one) for start, one in sequences)
    order = sorted(sequences, key=lambda item: -item[0])
    rounds = []
    for number in range(last):
        actions = [
            one[number - start] for start, one in order if 0 <= number - start < len(one)
        ]
        rounds.append(functools.partial(act, actions))
    return rounds


def lane_groups(values):
    total = values[:, :128]
    for lane in range(128, values.shape[1], 128):
        total = total + values[:, lane : lane + 128]
    return total


def piece_buffers(rows, columns, quarter, dtype):
    inside = rows - quarter
    some = (4, 2, quarter, columns) if quarter else (1, 1, 16, 128)
    shapes = [
        (4, 2, rows, columns),
        (4, 2, rows, columns),
        some,
        (4, inside, columns),
        (4, inside, columns),
        (4, inside, columns),
        (inside, columns),
    ]
    return [pltpu.VMEM(shape, dtype) for shape in shapes]


BACK_BLOCK = 256
DURING_PAIRS = ((0, (0, 1)), (1, (2,)), (2, (3,)), (4, (4,)), (5, (5,)), (7, (6,)))
DURING_BLOCKS = ((1, (7,)), (3, (8,)))
AFTER_BLOCKS = 9


def back_kernel(pieces, sets, head_size, *refs):
    grads, refs = refs[:3], refs[3:]
    (q_in, k_in, v_in, do_in, a_in, hat_in, w_in, starts, lse, delta, small_in), refs = refs[:11], refs[11:]
    finals, refs = refs[:4], refs[4:]
    (near_out, far_out, own_out, small_out, norm), refs = refs[:5], refs[5:]
    buffers, refs = refs[: 7 * sets], refs[7 * sets :]
    (dq, dk, dv, dw, halo, passing, small, tiles, send, recv, local, stream, freed) = refs
    me = Place()
    count = len(pieces)
    rows, width = q_in.shape
    window = k_in.shape[0]
    before = window - rows
    span = before + Q_TILE
    tiles[...] = jnp.zeros_like(tiles)
    small[0] = small_in[...]
    arrays = [*grads, *[dw.at[k] for k in range(3)]]
    wires, sequences = [], []
    last_of = {}
    for k, (number, first, size, quarter, result, column, of, start) in enumerate(pieces):
        here = pl.ds(first, size)
        wire = Wire(send, recv)
        again = of in last_of
        more = any(piece[6] == of for piece in pieces[k + 1 :])
        final = finals[result].at[here, pl.ds(column, arrays[number].shape[-1])]
        sequences.append(
            (
                start,
                reduce_ticks(
                    me, wire, RS_SEMS * k, local.at[k], arrays[number].at[:, :, :, here], quarter,
                    buffers[7 * of], buffers[7 * of + 1 : 7 * of + 7], final, tiles.at[0],
                    waits_for=freed.at[last_of[of]] if again else None,
                    frees=freed.at[k] if more else None,
                ),
            )
        )
        last_of[of] = k
        if not more:
            wires.append(wire)

    ending = RS_SEMS * count
    wire = Wire(send, recv)
    wires.append(wire)
    joins = both(me.c == 1, me.w >= 2)
    near = [
        wire.put(halo.at[1], near_out, ending + 1, me.core_mate(), me.c == 1),
        wire.put(halo.at[1], passing, ending + 2, me.core_mate(), both(me.c == 0, me.w >= 2)),
    ]
    got_passing = wire.got(passing, ending + 2, me.core_mate())
    got_near = wire.got(near_out, ending + 1, me.core_mate(), me.c == 0)
    far_copy = pltpu.make_async_copy(halo.at[0], far_out, local.at[count])
    clear = pltpu.make_async_copy(dq, near_out, local.at[count + 1])

    def join_halo():
        got_passing()
        accumulate(halo.at[0], passing)

    def end_halo():
        when(joins, join_halo)
        far_copy.start()

    def small_step(k, partner):
        put = wire.put(small.at[k], small.at[5 + k], ending + 3 + k, partner)
        got = wire.got(small.at[5 + k], ending + 3 + k, partner)

        def take_in():
            got()
            small[k + 1] = small[k] + small[5 + k]

        return put, take_in

    steps = [me.wide(jnp.bitwise_xor(me.w, bit)) for bit in (1, 2, 4, 8)]
    smalls = [small_step(k, one) for k, one in enumerate([steps[0], me.y_mate(), *steps[1:]])]
    small_ticks = [smalls[0][0]]
    for k in range(4):
        small_ticks.append(functools.partial(act, [smalls[k][1], smalls[k + 1][0]]))
    small_ticks.append(smalls[4][1])
    computed = pieces[-3][-1]
    sequences.append((computed, small_ticks))
    sequences.append(
        (computed, [functools.partial(act, near), end_halo])
    )
    rounds = in_rounds(sequences)
    pairs = width // 128
    blocks = width // BACK_BLOCK
    greet(me, [*steps[2:], *(me.wide(jnp.bitwise_xor(me.w, bits)) for bits in (3, 12))])

    def attention(q_two, k_two, v_two, do_two, bias, dk_sum, dv_sum, kt, dqt):
        def loads(pair, slot):
            lanes = pl.ds(pl.multiple_of(pair * 128, 128), 128)
            return [
                pltpu.make_async_copy(source.at[:, lanes], target.at[slot], stream.at[slot, k])
                for k, (source, target) in enumerate(
                    ((q_in, q_two), (k_in, k_two), (v_in, v_two), (do_in, do_two))
                )
            ]

        for one in loads(0, 0):
            one.start()
        fill_mask(starts, bias, rows, span, before)

        def pair_step(pair, carry):
            slot = lax.rem(pair, 2)
            lanes = pl.ds(pl.multiple_of(pair * 128, 128), 128)

            def prefetch():
                for one in loads(pair + 1, 1 - slot):
                    one.start()

            pl.when(pair + 1 < pairs)(prefetch)
            for k, due in DURING_PAIRS:
                pl.when(pair == k)(functools.partial(act, [rounds[number] for number in due]))
            for one in loads(pair, slot):
                one.wait()
            attend_back_pair(
                head_size, q_two.at[slot], k_two.at[slot], v_two.at[slot], do_two.at[slot],
                lse.at[pair], delta.at[pair], dq.at[:, lanes], dk.at[:, lanes], dv.at[:, lanes],
                bias, dk_sum, dv_sum, kt, dqt,
            )
            small[0, 4:5, lanes] = jnp.sum(dq[:, lanes].astype(F32), axis=0, keepdims=True)
            small[0, 5:6, lanes] = jnp.sum(dv[:, lanes].astype(F32), axis=0, keepdims=True)
            return carry

        lax.fori_loop(0, pairs, pair_step, 0)

    pl.run_scoped(
        attention,
        pltpu.VMEM((2, rows, 128), BF16),
        pltpu.VMEM((2, window, 128), BF16),
        pltpu.VMEM((2, window, 128), BF16),
        pltpu.VMEM((2, rows, 128), BF16),
        pltpu.VMEM((rows // Q_TILE, span, Q_TILE), F32),
        pltpu.VMEM((window, 128), F32),
        pltpu.VMEM((window, 128), F32),
        pltpu.VMEM((128, window), BF16),
        pltpu.VMEM((128, rows), F32),
    )

    def projections(a_two, hat_two, w_two):
        def loads(block, slot):
            here = pl.ds(pl.multiple_of(block * BACK_BLOCK, BACK_BLOCK), BACK_BLOCK)
            return [
                pltpu.make_async_copy(source, target.at[slot], stream.at[slot, k])
                for k, (source, target) in enumerate(
                    ((a_in.at[:, here], a_two), (hat_in.at[:, here], hat_two), (w_in.at[here], w_two))
                )
            ]

        for one in loads(0, 0):
            one.start()

        def block_step(block, carry):
            slot = lax.rem(block, 2)
            here = pl.ds(pl.multiple_of(block * BACK_BLOCK, BACK_BLOCK), BACK_BLOCK)

            def prefetch():
                for one in loads(block + 1, 1 - slot):
                    one.start()

            pl.when(block + 1 < blocks)(prefetch)
            for k, due in DURING_BLOCKS:
                pl.when(block == k)(functools.partial(act, [rounds[number] for number in due]))
            for one in loads(block, slot):
                one.wait()
            a_t = a_two[slot].T
            for k, made in enumerate((dot(a_t[:, before:], dq[...]), dot(a_t, dk[...]), dot(a_t, dv[...]))):
                dw[k, block] = made.astype(BF16).reshape(dw.shape[2:])
            for k in range(3):
                part = slice(k * rows, (k + 1) * rows)
                grad = dot(dk[part, :], w_two[slot, :, width : 2 * width], 1, 1) + dot(
                    dv[part, :], w_two[slot, :, 2 * width :], 1, 1
                )
                if k == 2:
                    grad = grad + dot(dq[...], w_two[slot, :, :width], 1, 1)
                    own_out[:, here] = grad
                else:
                    halo[k, :, here] = grad.astype(BF16)
                hat = hat_two[slot, part].astype(F32)
                small[0, 0:1, here] += jnp.sum(grad * hat, axis=0, keepdims=True)
                small[0, 3:4, here] += jnp.sum(grad, axis=0, keepdims=True)
            return carry

        lax.fori_loop(0, blocks, block_step, 0)

    pl.run_scoped(
        projections,
        pltpu.VMEM((2, window, BACK_BLOCK), BF16),
        pltpu.VMEM((2, window, BACK_BLOCK), BF16),
        pltpu.VMEM((2, BACK_BLOCK, 3 * width), BF16),
    )
    dq[...] = jnp.zeros_like(dq)
    when(me.c == 1, clear.start)
    act(rounds[AFTER_BLOCKS:])
    small_out[...] = small[5]
    total = tiles.at[0]
    for half, (own_place, distances) in enumerate(((lax.rem(me.w, 4), (1, 2, 3)), (me.z, (4, 8, 12)))):
        spread = tiles.at[pl.ds(1 + 4 * half, 4)]
        spread[own_place] = total[...]
        moves = [
            wire.copy(
                total, spread.at[own_place], ending + 8 + 3 * half + k,
                me.wide(jnp.bitwise_xor(me.w, distance)),
            )
            for k, distance in enumerate(distances)
        ]
        for one in moves:
            one.start()
        for one in moves:
            one.wait()
        total = tiles.at[9 + half]
        total[...] = (spread[0] + spread[1]) + (spread[2] + spread[3])
    norm[...] = total[...]
    got_near()
    for one in wires:
        one.finish()
    far_copy.wait()
    when(me.c == 1, clear.wait)


def back(grads, attention, small, starts, stats, heads):
    queries, keys, values, outs_grad, normed, hat, weights = attention
    rows, width = queries.shape
    window = keys.shape[0]
    wide = lax.axis_size("wide")
    if lax.axis_size("dp") != 2 or wide != 16:
        return plain_back(grads, attention, small, starts, stats, heads)
    fc1, fc2, out = (one.shape for one in grads)
    tall, pieces = 4, []
    for array, shape in ((1, fc2), (0, fc1)):
        size = shape[1] // tall
        for k in range(tall):
            pieces.append((array, k * size, size, size // 4, array, 0, len(pieces), len(pieces)))
    each = width // wide
    pieces.append((2, 0, each, each // 4, 2, 0, 0, 8))
    for k in range(3):
        pieces.append((3 + k, 0, each, each // 4, 3, k * width, 1 + k, AFTER_BLOCKS + k))
    pieces = tuple(pieces)
    sets = 2 * tall
    like = jax.ShapeDtypeStruct
    out_shape = [like(one.shape[1:], F32) for one in grads] + [
        like((each, 3 * width), F32),
        like((rows, width), BF16),
        like((rows, width), BF16),
        like((rows, width), F32),
        like(small.shape, F32),
        like((8, 128), F32),
    ]
    scratch = []
    for number, _, size, quarter, *_ in pieces[:sets]:
        scratch += piece_buffers(size, grads[number].shape[2], quarter, grads[number].dtype)
    count = len(pieces)
    sems = RS_SEMS * count + 14
    *totals, near, far, own, small, norm = pl.pallas_call(
        functools.partial(back_kernel, pieces, sets, width // heads),
        out_shape=out_shape,
        in_specs=[HBM] * 10 + [VMEM] * 4,
        out_specs=[VMEM] * 4 + [HBM] * 2 + [VMEM] * 3,
        scratch_shapes=scratch
        + [
            pltpu.VMEM((rows, width), BF16),
            pltpu.VMEM((window, width), BF16),
            pltpu.VMEM((window, width), BF16),
            pltpu.VMEM((3, 4, 2, 2, each, width), BF16),
            pltpu.VMEM((2, rows, width), BF16),
            pltpu.VMEM((rows, width), BF16),
            pltpu.VMEM((10, *small.shape), F32),
            pltpu.VMEM((11, 8, 128), F32),
            pltpu.SemaphoreType.DMA((sems,)),
            pltpu.SemaphoreType.DMA((sems,)),
            pltpu.SemaphoreType.DMA((count + 2,)),
            pltpu.SemaphoreType.DMA((2, 4)),
            pltpu.SemaphoreType.REGULAR((count,)),
        ],
        compiler_params=pltpu.CompilerParams(
            collective_id=1, has_side_effects=True, vmem_limit_bytes=60 << 20
        ),
        name="back",
    )(
        *[one.reshape(4, 2, 2, *one.shape[1:]) for one in grads],
        queries, keys, values, outs_grad, normed, hat, weights, starts, *stats, small,
    )
    return [*totals, near, from_behind(far, "wide", -2), own, small, norm]


def plain_back(grads, attention, small, starts, stats, heads):
    queries, keys, values, outs_grad, normed, hat, weights = attention
    rows, width = queries.shape
    wide = lax.axis_size("wide")
    dq, dk, dv = attend_back(queries, keys, values, outs_grad, *stats, starts, heads)
    earlier = dot(dk, weights[:, width : 2 * width], 1, 1) + dot(dv, weights[:, 2 * width :], 1, 1)
    own = earlier[-rows:] + dot(dq, weights[:, :width], 1, 1)
    earlier = earlier[:-rows]
    all_grad = jnp.concatenate([earlier, own])
    dw = [dot(normed[-rows:], dq, 0, 0), dot(normed, dk, 0, 0), dot(normed, dv, 0, 0)]
    grads = [*grads, jnp.concatenate(dw, axis=1).reshape(wide, -1, 3 * width)]
    totals = [
        lax.psum(
            lax.psum_scatter(one.astype(F32), "wide", scatter_dimension=0, tiled=False), "dp"
        )
        for one in grads
    ]
    sums = {
        0: jnp.sum(all_grad * hat.astype(F32), axis=0),
        3: jnp.sum(all_grad, axis=0),
        4: jnp.sum(dq.astype(F32), axis=0),
        5: jnp.sum(dv.astype(F32), axis=0),
    }
    small = jnp.concatenate(
        [sums[k][None] if k in sums else small[k : k + 1] for k in range(small.shape[0])]
    )
    low = earlier.astype(BF16).reshape(2, rows, width)
    returned = [from_behind(low[1], "wide", -1), from_behind(low[0], "wide", -2)]
    squares = lax.psum(sum(jnp.sum(one * one) for one in totals), "wide")
    tile = jnp.zeros((8, 128), F32).at[0, 0].set(squares)
    return [*totals, *returned, own, lax.psum(small, ("dp", "wide")), tile]


F_TILE = 256


def grad_through_norm(grad, hat, scale, gain):
    scaled = grad * gain
    mean_plain = jnp.mean(scaled, axis=-1, keepdims=True)
    mean_cross = jnp.mean(scaled * hat, axis=-1, keepdims=True)
    return scale * (scaled - mean_plain - hat * mean_cross)


def down_sums(values):
    return jnp.sum(values, axis=0, keepdims=True)


def middle_kernel(
    head_size, c_ref, o_ref, x_ref, gy_ref, wo_ref, w1_ref, w2_ref, vec_ref, par_ref, scale_ref,
    out_ref, mid_ref, df_ref, a_ref, dz_ref, res_ref, do_ref, delta_ref, small_ref,
    act_all, slope, grad_all, stats, sums, x2, hat_post, hat_two, da,
):
    blocks, _, units = w1_ref.shape
    width = x_ref.shape[1]
    count = blocks * units

    @pl.when(pl.program_id(0) == 0)
    def _():
        sums[...] = jnp.zeros_like(sums)
        small_ref[...] = jnp.zeros_like(small_ref)

    stats[...] = jnp.zeros_like(stats)
    projected = dot(c_ref[...], wo_ref[...]) + vec_ref[6:7]
    value, hat, scale_post = layer_norm(projected, vec_ref[1:2], vec_ref[7:8])
    hat_post[...] = hat
    residual = x_ref[...].astype(F32) + value
    x2[...] = residual
    value, hat, scale_two = layer_norm(residual, vec_ref[2:3], vec_ref[8:9])
    hat_two[...] = hat
    a_ref[...] = value.astype(BF16)

    def columns(k):
        return pl.ds(pl.multiple_of(k * units, units), units)

    def forward(k, carry):
        pre = dot(a_ref[...], w1_ref[k]) + par_ref[2:3, columns(k)]
        half = 0.5 + 0.5 * lax.erf(pre * (0.5**0.5))
        value = pre * half
        act_all[k] = value
        slope[k] = half + pre * (jnp.exp(-0.5 * pre * pre) * (0.5 / jnp.pi) ** 0.5)
        stats[0] += lane_groups(value)
        stats[1] += lane_groups(value * value)
        return carry

    lax.fori_loop(0, blocks, forward, 0, unroll=4)
    mean = jnp.sum(stats[0], axis=1, keepdims=True) / count
    second = jnp.sum(stats[1], axis=1, keepdims=True) / count
    scale = lax.rsqrt(second - mean * mean + norm_epsilon)

    def middle(k, carry):
        here = columns(k)
        hat = (act_all[k] - mean) * scale
        mid_ref[:, here] = (hat * par_ref[0:1, here] + par_ref[1:2, here]).astype(BF16)
        down = dot(gy_ref[...], w2_ref[here, :], 1, 1)
        scaled = down * par_ref[0:1, here]
        act_all[k] = hat
        grad_all[k] = scaled
        stats[2] += lane_groups(scaled)
        stats[3] += lane_groups(scaled * hat)
        sums[0:1, here] += down_sums(down * hat)
        sums[1:2, here] += down_sums(down)
        return carry

    lax.fori_loop(0, blocks, middle, 0, unroll=4)
    plain = jnp.sum(stats[2], axis=1, keepdims=True) / count
    crossed = jnp.sum(stats[3], axis=1, keepdims=True) / count
    part = min(width, 512)
    for start in range(0, width, part):
        here = slice(start, start + part)
        total = dot(mid_ref[...], w2_ref[:, here])
        out_ref[:, here] = (x2[:, here] + (total + vec_ref[9:10, here])).astype(BF16)

    def backward(k, carry):
        here = columns(k)
        back = scale * (grad_all[k] - plain - act_all[k] * crossed) * slope[k]
        low = back.astype(BF16)
        df_ref[:, here] = low
        sums[2:3, here] += down_sums(low.astype(F32))
        return carry

    lax.fori_loop(0, blocks, backward, 0, unroll=4)
    da[...] = jnp.zeros_like(da)

    def back_out(k, carry):
        da[...] += dot(df_ref[:, columns(k)], w1_ref[k], 1, 1)
        return carry

    lax.fori_loop(0, blocks, back_out, 0, unroll=4)
    grad_in = gy_ref[...].astype(F32)
    rows_grad = da[...]
    residual_grad = grad_in + grad_through_norm(rows_grad, hat_two[...], scale_two, vec_ref[2:3])
    res_ref[...] = residual_grad
    dz = grad_through_norm(residual_grad, hat_post[...], scale_post, vec_ref[1:2]).astype(BF16)
    dz_ref[...] = dz
    for row, term in (
        (1, residual_grad * hat_post[...]),
        (2, rows_grad * hat_two[...]),
        (6, dz.astype(F32)),
        (7, residual_grad),
        (8, rows_grad),
        (9, grad_in),
    ):
        small_ref[row : row + 1] += down_sums(term)
    mixed_grad = dot(dz, wo_ref[...], 1, 1)
    outs = o_ref[...]
    low = (mixed_grad * scale_ref[...]).astype(BF16)
    do_ref[...] = low
    head_row = 10 + 3 * count // width
    small_ref[head_row : head_row + 1] += down_sums(mixed_grad * outs)
    heads = delta_ref.shape[0]
    lane = lax.broadcasted_iota(jnp.int32, (heads, width), 1)
    of = lax.broadcasted_iota(jnp.int32, (heads, width), 0) * head_size
    chosen = jnp.where(jnp.logical_and(lane >= of, lane < of + head_size), 1.0, 0.0)
    delta_ref[...] = lax.dot_general(
        chosen, low.astype(F32) * outs, (((1,), (1,)), ((), ())),
        precision=lax.Precision.HIGHEST, preferred_element_type=F32,
    )

    @pl.when(pl.program_id(0) == pl.num_programs(0) - 1)
    def _():
        for row in range(3):
            for start in range(0, count, width):
                at = 10 + (row * count + start) // width
                small_ref[at : at + 1] = sums[row : row + 1, start : start + width]


def middle_part(mixed, attended, tokens, out_grad, wo, w1, w2, vectors, par, scales, heads):
    rows, width = tokens.shape
    blocks, _, units = w1.shape
    hidden = blocks * units
    by_tile = lambda columns: pl.BlockSpec((F_TILE, columns), lambda t: (t, 0))
    once = lambda one: pl.BlockSpec(
        one.shape, lambda t: (0,) * len(one.shape), pipeline_mode=pl.Buffered(1)
    )
    small_rows = -(-(11 + 3 * hidden // width) // 8) * 8
    like = jax.ShapeDtypeStruct
    return pl.pallas_call(
        functools.partial(middle_kernel, width // heads),
        grid=(rows // F_TILE,),
        in_specs=[by_tile(width)] * 4 + [once(one) for one in (wo, w1, w2, vectors, par, scales)],
        out_specs=[
            by_tile(width),
            by_tile(hidden),
            by_tile(hidden),
            by_tile(width),
            by_tile(width),
            by_tile(width),
            by_tile(width),
            pl.BlockSpec((heads, F_TILE), lambda t: (0, t)),
            pl.BlockSpec((small_rows, width), lambda t: (0, 0)),
        ],
        out_shape=[
            like((rows, width), BF16),
            like((rows, hidden), BF16),
            like((rows, hidden), BF16),
            like((rows, width), BF16),
            like((rows, width), BF16),
            like((rows, width), F32),
            like((rows, width), BF16),
            like((heads, rows), F32),
            like((small_rows, width), F32),
        ],
        scratch_shapes=[pltpu.VMEM((blocks, F_TILE, units), F32)] * 3
        + [pltpu.VMEM((4, F_TILE, 128), F32), pltpu.VMEM((8, hidden), F32)]
        + [pltpu.VMEM((F_TILE, width), F32)] * 4,
        compiler_params=pltpu.CompilerParams(vmem_limit_bytes=60 << 20),
        name="middle_part",
    )(mixed, attended, tokens, out_grad, wo, w1, w2, vectors, par, scales)


def weights_kernel(a_ref, gy_ref, c_ref, dz_ref, mid_ref, df_ref, dw1_ref, dw2_ref, dwo_ref, a_t):
    @pl.when(pl.program_id(0) == 0)
    def _():
        a_t[...] = a_ref[...].T
        dwo_ref[...] = dot(c_ref[...].T, dz_ref[...]).astype(BF16)

    units = dw2_ref.shape[1]
    for k in range(dw1_ref.shape[0]):
        here = slice(k * units, (k + 1) * units)
        dw1_ref[k] = dot(a_t[...], df_ref[:, here]).astype(BF16)
        dw2_ref[k] = dot(mid_ref[:, here].T, gy_ref[...]).astype(BF16)


def weight_grads(rows, out_grad, mixed, proj_grad, middle, pre_grad, blocks):
    tokens, width = rows.shape
    units = middle.shape[1] // blocks
    whole = pl.BlockSpec((tokens, width), lambda k: (0, 0))
    block = pl.BlockSpec((tokens, 2 * units), lambda k: (0, k))
    return pl.pallas_call(
        weights_kernel,
        grid=(blocks // 2,),
        in_specs=[whole] * 4 + [block, block],
        out_specs=[
            pl.BlockSpec((2, width, units), lambda k: (k, 0, 0)),
            pl.BlockSpec((2, units, width), lambda k: (k, 0, 0)),
            pl.BlockSpec((width, width), lambda k: (0, 0)),
        ],
        out_shape=[
            jax.ShapeDtypeStruct((blocks, width, units), BF16),
            jax.ShapeDtypeStruct((blocks, units, width), BF16),
            jax.ShapeDtypeStruct((width, width), BF16),
        ],
        scratch_shapes=[pltpu.VMEM((width, tokens), BF16)],
        compiler_params=pltpu.CompilerParams(vmem_limit_bytes=60 << 20),
        name="weight_grads",
    )(rows, out_grad, mixed, proj_grad, middle, pre_grad)


def plane_share(rows):
    return rows // 16 * 3 // 8 * 16


def unpack_small(full, vector_shape, hidden_shape):
    wide = full.shape[0]
    count, each = vector_shape
    vectors = full[:, :count, :each].transpose(1, 0, 2).reshape(count, -1)
    rows, size = hidden_shape
    if size % 128 == 0:
        hidden = full[:, count:].reshape(wide, rows, size)
    else:
        hidden = full[:, count:, :size]
    hidden = hidden.transpose(1, 0, 2).reshape(rows, -1)
    return vectors.astype(F32), hidden.astype(F32)


def regroup(blocks, units):
    slabs, rows, columns = blocks.shape
    join = max(1, units // columns)
    if join == 1:
        return blocks
    return blocks.reshape(slabs // join, join, rows, columns).transpose(0, 2, 1, 3).reshape(
        slabs // join, rows, join * columns
    )


def ungroup(blocks, columns):
    slabs, rows, units = blocks.shape
    join = units // columns
    if join == 1:
        return blocks
    return blocks.reshape(slabs, rows, join, columns).transpose(0, 2, 1, 3).reshape(
        slabs * join, rows, columns
    )


def body(
    inputs,
    out_grad,
    doc_lengths,
    step_count,
    qkv_weight,
    qkv_first,
    qkv_second,
    out_weight,
    out_first,
    out_second,
    fc1_weight,
    fc1_first,
    fc1_second,
    fc2_weight,
    fc2_first,
    fc2_second,
    model_vectors,
    vectors_first,
    vectors_second,
    hidden_vectors,
    hidden_first,
    hidden_second,
    head_scale,
    head_first,
    head_second,
):
    tokens_dev = inputs.shape[0]
    width = inputs.shape[1]
    heads_count = head_scale.shape[0]
    head_size = width // heads_count
    wide = lax.axis_size("wide")
    hidden_width = hidden_vectors.shape[1] * wide

    fc1_rows, fc2_rows = fc1_weight.shape[0], fc2_weight.shape[0]
    qkv_rows, out_rows = qkv_weight.shape[0], out_weight.shape[0]
    small = jnp.concatenate(
        [
            jnp.pad(model_vectors, ((0, 0), (0, max(0, 128 - model_vectors.shape[1])))),
            hidden_vectors.reshape(-1, min(128, hidden_vectors.shape[1])),
        ]
        if hidden_vectors.shape[1] % 128 == 0
        else [
            jnp.pad(one, ((0, 0), (0, 128 - one.shape[1]))) for one in (model_vectors, hidden_vectors)
        ]
    )
    heads_low = lax.optimization_barrier(head_scale.astype(BF16)).astype(F32)
    starts = doc_starts(
        doc_lengths, lax.axis_index("dp"), lax.axis_index("wide") * tokens_dev, tokens_dev
    )
    starts = jnp.maximum(starts - (lax.axis_index("wide") - 2) * tokens_dev, 0).reshape(1, -1)
    scales = jnp.repeat(heads_low, head_size).reshape(1, width)
    gathered = front(
        [
            small,
            qkv_weight,
            out_weight,
            fc1_weight,
            fc2_weight,
        ],
        (0, qkv_rows // 2, out_rows // 4, plane_share(fc1_rows), plane_share(fc2_rows)),
        inputs,
        starts,
        scales,
        heads_count,
    )
    qkv_full, out_full, fc1_full, fc2_full, hat_low, normed_low = gathered[:6]
    queries, keys_all, values_all, attended, mixed_low, log_totals, vectors, hidden_par = gathered[6:]
    fc2_full = fc2_full.reshape(hidden_width, width)
    output, middle_low, pre_low, rows_low, proj_low, residual_grad, attended_low, delta, small_grad = (
        middle_part(
            mixed_low,
            attended,
            inputs,
            out_grad,
            out_full.reshape(width, width),
            regroup(fc1_full, 256),
            fc2_full,
            vectors,
            hidden_par,
            scales,
            heads_count,
        )
    )
    fc1_grad, fc2_grad, out_weight_grad = weight_grads(
        rows_low, out_grad, mixed_low, proj_low, middle_low, pre_low, hidden_width // 256
    )
    fc1_part, fc2_part, out_part, qkv_part, near, far, own_grad, small_total, norm_tile = back(
        [
            ungroup(fc1_grad, fc1_weight.shape[1]),
            fc2_grad.reshape(wide, -1, width),
            out_weight_grad.reshape(wide, -1, width),
        ],
        (
            queries,
            keys_all,
            values_all,
            attended_low,
            normed_low,
            hat_low.reshape(-1, width),
            qkv_full.reshape(width, 3 * width),
        ),
        small_grad,
        starts,
        (log_totals, delta.reshape(log_totals.shape)),
        heads_count,
    )
    total_grad = own_grad + near.astype(F32) + far.astype(F32)
    _, hat_in, scale_in = layer_norm(inputs.astype(F32), vectors[0], vectors[3])
    input_grad = residual_grad + grad_through_norm(total_grad, hat_in, scale_in, vectors[0])
    vector_rows = model_vectors.shape[0]
    head_row = vector_rows + hidden_vectors.shape[0] * hidden_width // width
    vector_total = small_total[:vector_rows]
    hidden_total = small_total[vector_rows:head_row].reshape(hidden_vectors.shape[0], hidden_width)
    head_total = jnp.sum(small_total[head_row].reshape(heads_count, head_size), axis=1)
    place = lax.axis_index("wide")
    vector_part = lax.dynamic_slice_in_dim(
        vector_total, place * model_vectors.shape[1], model_vectors.shape[1], 1
    )
    hidden_part = lax.dynamic_slice_in_dim(
        hidden_total, place * hidden_vectors.shape[1], hidden_vectors.shape[1], 1
    )
    small_square = jnp.sum(small_total[:head_row] ** 2) + jnp.sum(head_total**2)
    grad_norm = jnp.sqrt(jnp.sum(norm_tile) + small_square)
    factor = jnp.minimum(1.0, clip_limit / (grad_norm + 1e-06))
    step = step_count[0].astype(F32)
    grads = (qkv_part, out_part, fc1_part, fc2_part, vector_part, hidden_part, head_total)
    params = (
        qkv_weight,
        out_weight,
        fc1_weight,
        fc2_weight,
        model_vectors,
        hidden_vectors,
        head_scale,
    )
    firsts = (qkv_first, out_first, fc1_first, fc2_first, vectors_first, hidden_first, head_first)
    seconds = (
        qkv_second,
        out_second,
        fc1_second,
        fc2_second,
        vectors_second,
        hidden_second,
        head_second,
    )
    rates = (
        matrix_rate,
        matrix_rate,
        matrix_rate,
        matrix_rate,
        vector_rate,
        vector_rate,
        vector_rate,
    )
    decays = (weight_decay, weight_decay, weight_decay, weight_decay, 0.0, 0.0, 0.0)
    updated = []
    for number in range(7):
        updated.extend(
            adam_step(
                grads[number] * factor,
                params[number],
                firsts[number],
                seconds[number],
                step,
                rates[number],
                decays[number],
            )
        )
    return (
        output,
        input_grad,
        grad_norm.reshape(1),
        updated[0],
        updated[1],
        updated[2],
        updated[3],
        updated[4],
        updated[5],
        updated[6],
        updated[7],
        updated[8],
        updated[9],
        updated[10],
        updated[11],
        updated[12],
        updated[13],
        updated[14],
        updated[15],
        updated[16],
        updated[17],
        updated[18],
        updated[19],
        updated[20],
    )


def solution(mesh):
    placed = (
        P(("dp", "wide"), None),
        P(("dp", "wide"), None),
        P(),
        P(),
        P("wide", None),
        P("wide", None),
        P("wide", None),
        P("wide", None),
        P("wide", None),
        P("wide", None),
        P(None, "wide"),
        P(None, "wide"),
        P(None, "wide"),
        P("wide", None),
        P("wide", None),
        P("wide", None),
        P(None, "wide"),
        P(None, "wide"),
        P(None, "wide"),
        P(None, "wide"),
        P(None, "wide"),
        P(None, "wide"),
        P(),
        P(),
        P(),
    )
    return jax.shard_map(
        body,
        mesh=mesh,
        in_specs=placed,
        out_specs=(
            P(("dp", "wide"), None),
            P(("dp", "wide"), None),
            P(),
            P("wide", None),
            P("wide", None),
            P("wide", None),
            P("wide", None),
            P("wide", None),
            P("wide", None),
            P(None, "wide"),
            P(None, "wide"),
            P(None, "wide"),
            P("wide", None),
            P("wide", None),
            P("wide", None),
            P(None, "wide"),
            P(None, "wide"),
            P(None, "wide"),
            P(None, "wide"),
            P(None, "wide"),
            P(None, "wide"),
            P(),
            P(),
            P(),
        ),
        check_vma=False,
    )
```
